128 devices in a mesh: context: 32 (over z_hi, x, y), tensor: 4 (over z_lo, core).
Axes of the slice: x: 4, y: 4, z: 4 (z_hi: 2, z_lo: 2; z = z_hi * 2 + z_lo), core: 2. Of those that a mesh axis runs over, the one named last changes fastest.
Arguments:
- activations: bfloat16 [16384, 3072], P('context', 'tensor'), may hold values from -6 to 6
- qkv_weight: bfloat16 [3072, 3, 4096], P(None, None, 'tensor'), may hold values from -0.109375 to 0.109375
- log_decay: float32 [16384, 32], P('context', 'tensor'), may hold values from -1.5 to 0, as said below
- lengths: int32 [32], P('context'), may hold values from 256 to 512, as said below
- out_grad: bfloat16 [16384, 4096], P('context', 'tensor'), may hold values from -0.00036621094 to 0.00036621094
Outputs:
- weight_grad: float32 [3072, 3, 4096], P('context', None, 'tensor')
The draws below stay inside these ranges and needn't reach their ends.
Inputs may be any that keep to these rules, and one draw needn't show every extreme that they name: `log_decay`: Negative; entries vary from token to token. `lengths`: each entry is a multiple of 256; the live tokens are the first slots of their shard; in every draw at least one shard is full.
All inputs are finite; a program needn't handle non-finite values.
Results may differ from the reference program's by a relative error of at most 0.015.
Values may be sent and summed in bfloat16 or wider, within the bound.
No kernel may reach another device: no remote copies, remote signals or barrier semaphores. Data moves between devices by JAX's collectives and lax.ppermute only.
A program may use at most 128 MiB of HBM per device.

```python
import math
import jax
import jax.numpy as jnp
from jax import lax

D = 3072
HEAD = 128
BLOCK = 256
TOK_DEV = 512
HEAD_COUNT = 32
TOKEN_SLOTS = 16384


def draw_log_decay(key, part):
    random_seed_keys = jax.random.split(jax.random.fold_in(key, 17), 7)
    shard_count = TOKEN_SLOTS // TOK_DEV
    fast_share = 0.5
    is_fast = jax.random.uniform(random_seed_keys[0], (HEAD_COUNT,)) < fast_share
    fast_rate = jnp.exp(jax.random.uniform(random_seed_keys[1], (HEAD_COUNT,), minval=math.log(1.0 / 50.0), maxval=math.log(1.0 / 30.0)))
    slow_rate = jnp.exp(jax.random.uniform(random_seed_keys[2], (HEAD_COUNT,), minval=math.log(0.1), maxval=math.log(0.3))) / TOKEN_SLOTS
    head_rate = jnp.where(is_fast, fast_rate, slow_rate)
    shard_factor = jnp.exp(jax.random.uniform(random_seed_keys[3], (shard_count, HEAD_COUNT), minval=math.log(0.5), maxval=math.log(2.0)))
    token_factor = jax.random.uniform(random_seed_keys[4], (TOKEN_SLOTS, HEAD_COUNT), minval=0.7, maxval=1.4)
    baseline_decay_rate = jnp.repeat(shard_factor, TOK_DEV, axis=0) * token_factor * head_rate[None, :]
    flurry_location = jax.random.randint(random_seed_keys[5], (2,), 0, TOKEN_SLOTS)
    flurry_depth = -jnp.log(1.0 - jax.random.uniform(random_seed_keys[6], (2, HEAD_COUNT), minval=0.2, maxval=0.5))
    token_position = jnp.arange(TOKEN_SLOTS)
    flurry_list = jnp.sum((token_position[:, None, None] == flurry_location[None, :, None]) * flurry_depth[None], axis=1)
    return (-(baseline_decay_rate + flurry_list)).astype(jnp.float32)


def draw_lengths(key, part):
    random_seed_keys = jax.random.split(jax.random.fold_in(key, 29), 2)
    shard_count = TOKEN_SLOTS // TOK_DEV
    block_count = TOK_DEV // BLOCK
    block_live = jax.random.randint(random_seed_keys[0], (shard_count,), 1, block_count + 1)
    full_shard = jax.random.randint(random_seed_keys[1], (), 0, shard_count)
    block_live = jnp.where(jnp.arange(shard_count) == full_shard, block_count, block_live)
    return (block_live * BLOCK).astype(jnp.int32)


def with_spikes(values, own_key, source, target, shards_of, factor):
    owner, partner = [(jnp.arange(values.shape[position]) // (values.shape[position] // shards_of)).reshape([-1 if axis == position else 1 for axis in range(values.ndim)]) for position in (source, target)]
    chosen = jax.random.permutation(own_key, shards_of)[partner]
    strong = (owner == chosen) | (owner == (partner + shards_of // 2) % shards_of)
    return jnp.where(strong, factor * values, values)


def steps_of(rng, extent, pieces, low, largest):
    gain, own = 1.0, jax.random.fold_in(rng, 6)
    for axis_at, shards_of in pieces:
        steps = jnp.exp(jax.random.uniform(jax.random.fold_in(own, axis_at), (shards_of,), jnp.float32, low / len(pieces), largest / len(pieces)))
        gain = gain * jnp.repeat(steps, extent[axis_at] // shards_of).reshape([-1 if axis == axis_at else 1 for axis in range(len(extent))])
    return gain


def gaussian(key, shape, width, reach, pieces=(), held_as=jnp.bfloat16):
    array = width * jax.random.normal(key, shape, jnp.float32)
    if pieces:
        array = array * steps_of(key, shape, pieces, -0.22, 0.18)
    return jnp.clip(array, -reach, reach).astype(held_as)


def gaussian_with(stream_key, shape, width, most, cuts, heavy, kind=jnp.bfloat16):
    values = width * jax.random.normal(stream_key, shape, jnp.float32)
    if cuts:
        values = values * steps_of(stream_key, shape, cuts, -0.22, 0.18)
    return jnp.clip(with_spikes(values, jax.random.fold_in(stream_key, 3), *heavy), -most, most).astype(kind)


def setup_inputs(seed: int = 0) -> dict:
    splits = jax.random.split(jax.random.key(seed), 6)
    activations = gaussian_with(splits[0], (TOKEN_SLOTS, D), 1.0, 6.0, ((0, 32), (1, 4)), (0, 1, 32, 2.75))
    qkv_weight = gaussian(splits[1], (D, 3, HEAD_COUNT * HEAD), D ** -0.5, 0.109375, ((2, 4),))
    log_decay = draw_log_decay(jax.random.fold_in(splits[5], 71), 0)
    lengths = draw_lengths(jax.random.fold_in(splits[5], 71), 0)
    out_grad = gaussian(splits[4], (TOKEN_SLOTS, HEAD_COUNT * HEAD), (1.0 / TOKEN_SLOTS), 0.00036621094, ((0, 32), (1, 4)))
    return {"activations": activations, "qkv_weight": qkv_weight, "log_decay": log_decay, "lengths": lengths, "out_grad": out_grad}


def rounded(value):
    return lax.optimization_barrier(value.astype(jnp.bfloat16)).astype(jnp.float32)


def shard_sums(query, key_matrix_rows, value_matrix_rows, output_gradient, decays):
    run_sum = jnp.cumsum(decays, axis=0)
    shard_sum = run_sum[-1]
    score_scale_factor = HEAD ** -0.5
    until_finish = jnp.exp(shard_sum[None, :] - run_sum)
    decayed_key_rows = rounded(key_matrix_rows.astype(jnp.float32) * until_finish[:, :, None])
    partition_state = jnp.einsum("jla,jlu->lau", decayed_key_rows, value_matrix_rows.astype(jnp.float32)).astype(jnp.bfloat16)
    decayed_query_rows = rounded(query.astype(jnp.float32) * (score_scale_factor * jnp.exp(run_sum))[:, :, None])
    state_gradient = jnp.einsum("jla,jlu->lau", decayed_query_rows, output_gradient.astype(jnp.float32)).astype(jnp.bfloat16)
    return partition_state, state_gradient, shard_sum.astype(jnp.bfloat16)


def shard_grads(query, key_matrix_rows, value_matrix_rows, output_gradient, decays, is_live, incoming, from_later):
    run_sum = jnp.cumsum(decays, axis=0)
    shard_sum = run_sum[-1]
    score_scale_factor = HEAD ** -0.5
    token_position = jnp.arange(TOK_DEV, dtype=jnp.int32)
    causal = token_position[:, None] >= token_position[None, :]
    gap_matrix = run_sum.T[:, :, None] - run_sum.T[:, None, :]
    decay_matrix = jnp.exp(jnp.where(causal[None], gap_matrix, -jnp.inf))
    query_wide_float = query.astype(jnp.float32)
    key_wide_float = key_matrix_rows.astype(jnp.float32)
    value_wide_float = value_matrix_rows.astype(jnp.float32)
    gradient_wide_float = output_gradient.astype(jnp.float32)
    probability_wide_float = rounded(jnp.einsum("thd,shd->hts", query_wide_float, key_wide_float) * score_scale_factor * decay_matrix)
    score_wide_float = rounded(jnp.einsum("thd,shd->hts", gradient_wide_float, value_wide_float) * decay_matrix)
    arriving_wide_float = rounded(incoming)
    subsequent_wide_float = rounded(from_later)
    since_beginning = jnp.exp(run_sum)[:, :, None]
    until_finish = jnp.exp(shard_sum[None, :] - run_sum)[:, :, None]
    query_gradient = score_scale_factor * (jnp.einsum("zmb,bzw->mzw", score_wide_float, key_wide_float) + since_beginning * jnp.einsum("bzf,zof->bzo", gradient_wide_float, arriving_wide_float))
    key_gradient = score_scale_factor * jnp.einsum("rvz,vrj->zrj", score_wide_float, query_wide_float) + until_finish * jnp.einsum("bzf,zof->bzo", value_wide_float, subsequent_wide_float)
    value_gradient = jnp.einsum("rvz,vrj->zrj", probability_wide_float, gradient_wide_float) + until_finish * jnp.einsum("cnf,nfg->cng", key_wide_float, subsequent_wide_float)
    stacked = jnp.stack([query_gradient, key_gradient, value_gradient], axis=1) * is_live[:, None, None, None]
    return stacked.astype(jnp.bfloat16).reshape(TOK_DEV, 3 * HEAD_COUNT * HEAD)


def decay_step(running, shard_item):
    partition_state, shard_total = shard_item
    updated = jnp.exp(shard_total.astype(jnp.float32))[:, None, None] * running + partition_state.astype(jnp.float32)
    return updated, running


def reference(activations, qkv_weight, log_decay, lengths, out_grad):
    shards = TOKEN_SLOTS // TOK_DEV
    col_width = HEAD_COUNT * HEAD
    token_position = jnp.arange(TOKEN_SLOTS, dtype=jnp.int32)
    is_live = (token_position % TOK_DEV < jnp.repeat(lengths, TOK_DEV)).astype(jnp.float32)
    projected = jnp.dot(activations, qkv_weight.reshape(D, 3 * col_width), preferred_element_type=jnp.float32).astype(jnp.bfloat16)
    projected = (projected * is_live.astype(jnp.bfloat16)[:, None]).reshape(shards, TOK_DEV, 3, HEAD_COUNT, HEAD)
    output_gradient = out_grad.reshape(shards, TOK_DEV, HEAD_COUNT, HEAD)
    decays = (log_decay * is_live[:, None]).reshape(shards, TOK_DEV, HEAD_COUNT)
    live_shards = is_live.reshape(shards, TOK_DEV)
    input_shards = activations.reshape(shards, TOK_DEV, D)
    states, grad_states, totals = lax.map(lambda shard_item: shard_sums(shard_item[0][:, 0], shard_item[0][:, 1], shard_item[0][:, 2], shard_item[1], shard_item[2]), (projected, output_gradient, decays))
    start_state = jnp.zeros((HEAD_COUNT, HEAD, HEAD), jnp.float32)
    _, incoming = lax.scan(decay_step, start_state, (states, totals))
    _, from_later = lax.scan(decay_step, start_state, (grad_states, totals), reverse=True)

    def grads_step(running, shard_item):
        input_shard, qkv_shard, grad_shard, decay_shard, live_shard, incoming_shard, later_shard = shard_item
        qkv_grad = shard_grads(qkv_shard[:, 0], qkv_shard[:, 1], qkv_shard[:, 2], grad_shard, decay_shard, live_shard, incoming_shard, later_shard)
        partial_grad = jnp.dot(input_shard.T, qkv_grad, preferred_element_type=jnp.float32).astype(jnp.bfloat16)
        return running + partial_grad.astype(jnp.float32), None

    start_grad = jnp.zeros((D, 3 * col_width), jnp.float32)
    weight_grad, _ = lax.scan(grads_step, start_grad, (input_shards, projected, output_gradient, decays, live_shards, incoming, from_later))
    return weight_grad.reshape(D, 3, col_width)
```

```python
import functools

import jax
import jax.numpy as jnp
from jax import lax
from jax.experimental import pallas as pl
from jax.experimental.pallas import tpu as pltpu
from jax.sharding import Mesh
from jax.sharding import PartitionSpec as P

F32 = jnp.float32
BF16 = jnp.bfloat16
HEAD = 128
Z, X, Y, ZL, CO, TEN, LEN = range(7)
AB_T = (((1,), (1,)), ((), ()))
A_TB = (((0,), (0,)), ((), ()))


def dot(a, b):
    return jnp.dot(a, b, preferred_element_type=F32)


def params(mib, n=1):
    return pltpu.CompilerParams(
        dimension_semantics=("arbitrary",) * n if n else None, vmem_limit_bytes=mib << 20
    )


def cost(flops, nbytes, exps=0):
    return pl.CostEstimate(flops=int(flops), bytes_accessed=int(nbytes), transcendentals=int(exps))


def shift(axis, by):
    n = lax.axis_size(axis)
    return [(i, (i + by) % n) for i in range(n)]


def send(x, axis, by):
    return lax.ppermute(x, axis, shift(axis, by))


def project(table, shards, flips, weight, partial, last):
    n = len(shards)
    tokens, width = shards[0].shape
    cols = weight.shape[2]
    block = cols // 2

    def body(s, *refs):
        out = refs[-1]
        acc = dot(refs[0][...], refs[n][0])
        for i in range(1, n):
            acc += dot(refs[i][...], refs[n + i][0])
        if partial is not None:
            acc += refs[2 * n][0]
        if last:
            row = lax.broadcasted_iota(jnp.int32, acc.shape, 0)
            acc = jnp.where(row < s[LEN], acc, 0.0)
        out[0] = acc.astype(out.dtype)

    tile = pl.BlockSpec((1, tokens, block), lambda g, j, s: (g, 0, j))
    in_specs = [pl.BlockSpec((tokens, width), lambda g, j, s: (0, 0)) for _ in shards]
    for flip in flips:
        in_specs.append(
            pl.BlockSpec((1, width, block), lambda g, j, s, flip=flip: (g, s[TEN] ^ flip, j))
        )
    operands = [*shards, *([weight] * n)]
    if partial is not None:
        in_specs.append(tile)
        operands.append(partial)
    return pl.pallas_call(
        body,
        grid_spec=pltpu.PrefetchScalarGridSpec(
            num_scalar_prefetch=1, grid=(3, 2), in_specs=in_specs, out_specs=tile
        ),
        out_shape=jax.ShapeDtypeStruct((3, tokens, cols), BF16 if last else F32),
        compiler_params=params(40, 2),
        cost_estimate=cost(6 * n * tokens * width * cols, 8 * n * width * cols),
        name="project",
    )(table, *operands)


def shard_states(table, qkv, out_grad, cumul):
    tokens = qkv.shape[1]
    scale = HEAD**-0.5

    def body(s, qkv_ref, og_ref, cum_ref, *outs):
        r = pl.program_id(0)
        who = (s[Y] + r) % 4
        blocks, totals = [], []
        for i in range(2):
            lanes = slice(i * HEAD, (i + 1) * HEAD)
            row = cum_ref[pl.ds(who * 2 + i, 1), :]
            total = row[:, tokens - 1 : tokens]
            keys_t = qkv_ref[1, :, lanes].astype(F32).T
            query_t = qkv_ref[0, :, lanes].astype(F32).T
            keys_t = (keys_t * jnp.exp(total - row)).astype(BF16)
            query_t = (query_t * (scale * jnp.exp(row))).astype(BF16)
            blocks.append((dot(keys_t, qkv_ref[2, :, lanes]), dot(query_t, og_ref[:, lanes])))
            totals.append(total)
        at = lax.broadcasted_iota(jnp.int32, (16, HEAD), 0)
        tail = jnp.where(at == 0, totals[0], totals[1]).astype(BF16)
        for k, out in enumerate(outs):

            @pl.when(r == k)
            def _(out=out):
                for i in range(2):
                    for kind in range(2):
                        start = (2 * kind + i) * HEAD
                        out[start : start + HEAD, :] = blocks[i][kind].astype(BF16)
                out[4 * HEAD :, :] = tail

    message = jax.ShapeDtypeStruct((4 * HEAD + 16, HEAD), BF16)
    whole = pl.BlockSpec(message.shape, lambda r, s: (0, 0))
    return pl.pallas_call(
        body,
        grid_spec=pltpu.PrefetchScalarGridSpec(
            num_scalar_prefetch=1,
            grid=(4,),
            in_specs=[
                pl.BlockSpec((3, tokens, 2 * HEAD), lambda r, s: (0, 0, (s[Y] + r) % 4)),
                pl.BlockSpec((tokens, 2 * HEAD), lambda r, s: (0, (s[Y] + r) % 4)),
                pl.BlockSpec(cumul.shape, lambda r, s: (0, 0)),
            ],
            out_specs=[whole] * 4,
        ),
        out_shape=[message] * 4,
        compiler_params=params(24),
        cost_estimate=cost(32 * tokens * HEAD * HEAD, 8 * tokens * 8 * HEAD),
        name="shard_states",
    )(table, qkv, out_grad, cumul)


def in_order(refs, place, held):
    for r, ref in enumerate(refs):
        held[(place - r + 4) % 4] = ref[...]


def head_rows(first, second):
    return jnp.concatenate([first, second], axis=0)


def spread(pair):
    wide = [jnp.broadcast_to(pair[i : i + 1, :], (HEAD, HEAD)) for i in range(2)]
    return head_rows(*wide)


def ring_y(table, messages):
    half = 2 * HEAD

    def body(s, a, b, c, d, before, after, prior, later, out, held):
        in_order((a, b, c, d), s[Y], held)
        totals = [held[t, 2 * half : 2 * half + 16, :].astype(F32)[:2] for t in range(4)]
        run = jnp.zeros((half, HEAD), F32)
        reach = jnp.zeros((2, HEAD), F32)
        for t in range(4):
            before[t] = run
            prior[t] = jnp.exp(reach)
            run = spread(jnp.exp(totals[t])) * run + held[t, :half, :].astype(F32)
            reach = reach + totals[t]
        out[:half, :] = run.astype(BF16)
        whole = reach
        run = jnp.zeros((half, HEAD), F32)
        reach = jnp.zeros((2, HEAD), F32)
        for t in range(3, -1, -1):
            after[t] = run
            later[t] = jnp.exp(reach)
            run = spread(jnp.exp(totals[t])) * run + held[t, half : 2 * half, :].astype(F32)
            reach = reach + totals[t]
        out[half : 2 * half, :] = run.astype(BF16)
        high = whole.astype(BF16).astype(F32)
        low = whole - high
        at = lax.broadcasted_iota(jnp.int32, (16, HEAD), 0)
        tail = jnp.where(at == 0, high[0:1], high[1:2])
        tail = jnp.where(at == 2, low[0:1], tail)
        tail = jnp.where(at == 3, low[1:2], tail)
        out[2 * half :, :] = tail.astype(BF16)

    return pl.pallas_call(
        body,
        grid_spec=pltpu.PrefetchScalarGridSpec(
            num_scalar_prefetch=1,
            grid=(1,),
            in_specs=[pl.BlockSpec(m.shape, lambda i, s: (0, 0)) for m in messages],
            out_specs=[
                pl.BlockSpec((4, half, HEAD), lambda i, s: (0, 0, 0)),
                pl.BlockSpec((4, half, HEAD), lambda i, s: (0, 0, 0)),
                pl.BlockSpec((4, 2, HEAD), lambda i, s: (0, 0, 0)),
                pl.BlockSpec((4, 2, HEAD), lambda i, s: (0, 0, 0)),
                pl.BlockSpec(messages[0].shape, lambda i, s: (0, 0)),
            ],
            scratch_shapes=[pltpu.VMEM((4, *messages[0].shape), BF16)],
        ),
        out_shape=[
            jax.ShapeDtypeStruct((4, half, HEAD), F32),
            jax.ShapeDtypeStruct((4, half, HEAD), F32),
            jax.ShapeDtypeStruct((4, 2, HEAD), F32),
            jax.ShapeDtypeStruct((4, 2, HEAD), F32),
            jax.ShapeDtypeStruct(messages[0].shape, BF16),
        ],
        compiler_params=params(16),
        cost_estimate=cost(1 << 20, 2 << 20),
        name="ring_y",
    )(table, *messages)


def ring_x(table, messages):
    half = 2 * HEAD

    def body(s, a, b, c, d, mine, edges, out, held):
        in_order((a, b, c, d), s[X], held)
        tails = [held[t, 2 * half : 2 * half + 16, :].astype(F32) for t in range(4)]
        totals = [tail[0:2] + tail[2:4] for tail in tails]
        for kind, steps in ((0, range(4)), (1, range(3, -1, -1))):
            run = jnp.zeros((half, HEAD), F32)
            reach = jnp.zeros((2, HEAD), F32)
            for t in steps:

                @pl.when(s[X] == t)
                def _(run=run, reach=reach, kind=kind):
                    mine[kind] = run
                    edges[kind] = jnp.exp(reach)

                rows = held[t, kind * half : (kind + 1) * half, :].astype(F32)
                run = spread(jnp.exp(totals[t])) * run + rows
                reach = reach + totals[t]

            @pl.when(s[Z] == kind)
            def _(run=run):
                out[...] = run.astype(BF16)

    return pl.pallas_call(
        body,
        grid_spec=pltpu.PrefetchScalarGridSpec(
            num_scalar_prefetch=1,
            grid=(1,),
            in_specs=[pl.BlockSpec(m.shape, lambda i, s: (0, 0)) for m in messages],
            out_specs=[
                pl.BlockSpec((2, half, HEAD), lambda i, s: (0, 0, 0)),
                pl.BlockSpec((2, 2, HEAD), lambda i, s: (0, 0, 0)),
                pl.BlockSpec((half, HEAD), lambda i, s: (0, 0)),
            ],
            scratch_shapes=[pltpu.VMEM((4, *messages[0].shape), BF16)],
        ),
        out_shape=[
            jax.ShapeDtypeStruct((2, half, HEAD), F32),
            jax.ShapeDtypeStruct((2, 2, HEAD), F32),
            jax.ShapeDtypeStruct((half, HEAD), BF16),
        ],
        compiler_params=params(16),
        cost_estimate=cost(1 << 20, 2 << 20),
        name="ring_x",
    )(table, *messages)


def arrivals(table, other, mine, edges, before, after, prior, later):
    half = 2 * HEAD

    def body(s, other_ref, mine_ref, edges_ref, before_ref, after_ref, prior_ref, later_ref, *outs):
        across = other_ref[...].astype(F32)
        start = mine_ref[0] + spread(edges_ref[0]) * jnp.where(s[Z] == 1, across, 0.0)
        finish = mine_ref[1] + spread(edges_ref[1]) * jnp.where(s[Z] == 0, across, 0.0)
        for r, out in enumerate(outs):
            t = (s[Y] + r) % 4
            out[:half, :] = (before_ref[t] + spread(prior_ref[t]) * start).astype(BF16)
            out[half:, :] = (after_ref[t] + spread(later_ref[t]) * finish).astype(BF16)

    operands = (other, mine, edges, before, after, prior, later)
    message = jax.ShapeDtypeStruct((2 * half, HEAD), BF16)
    return pl.pallas_call(
        body,
        grid_spec=pltpu.PrefetchScalarGridSpec(
            num_scalar_prefetch=1,
            grid=(1,),
            in_specs=[pl.BlockSpec(m.shape, lambda i, s, n=m.ndim: (0,) * n) for m in operands],
            out_specs=[pl.BlockSpec(message.shape, lambda i, s: (0, 0))] * 4,
        ),
        out_shape=[message] * 4,
        compiler_params=params(16),
        cost_estimate=cost(1 << 20, 2 << 20),
        name="arrivals",
    )(table, *operands)


def column_of(row):
    return jnp.broadcast_to(row, (HEAD, row.shape[1])).T


def local_grads(qkv, out_grad, cumul):
    tokens = qkv.shape[1]
    heads = cumul.shape[0]
    scale = HEAD**-0.5
    size = tokens // 2

    def body(qkv_ref, og_ref, cum_ref, out):
        h = pl.program_id(0)
        row = cum_ref[pl.ds(h, 1), :]
        column = column_of(row)
        wide = jnp.concatenate([column] * (size // HEAD), axis=1)
        s_at = lax.broadcasted_iota(jnp.int32, (size, size), 0)
        t_at = lax.broadcasted_iota(jnp.int32, (size, size), 1)
        parts = [slice(0, size), slice(size, tokens)]

        def pair(t, s):
            gap = row[:, parts[t]] - wide[parts[s], :]
            if t == s:
                gap = jnp.where(s_at <= t_at, gap, -jnp.inf)
            decay = jnp.exp(gap)
            q, k, v = qkv_ref[0, parts[t], :], qkv_ref[1, parts[s], :], qkv_ref[2, parts[s], :]
            g = og_ref[parts[t], :]
            scores = lax.dot_general(k, q, AB_T, preferred_element_type=F32)
            grads = lax.dot_general(v, g, AB_T, preferred_element_type=F32)
            prob = (scores * scale * decay).astype(BF16)
            score = (grads * decay).astype(BF16)
            dq = lax.dot_general(score, k, A_TB, preferred_element_type=F32)
            return dq, dot(score, q), dot(prob, g)

        a, b, c = pair(0, 0), pair(1, 0), pair(1, 1)
        out[0, parts[0], :] = a[0] * scale
        out[0, parts[1], :] = (b[0] + c[0]) * scale
        out[1, parts[0], :] = (a[1] + b[1]) * scale
        out[1, parts[1], :] = c[1] * scale
        out[2, parts[0], :] = a[2] + b[2]
        out[2, parts[1], :] = c[2]

    tile = pl.BlockSpec((3, tokens, HEAD), lambda h: (0, 0, h))
    return pl.pallas_call(
        body,
        grid=(heads,),
        in_specs=[
            tile,
            pl.BlockSpec((tokens, HEAD), lambda h: (0, h)),
            pl.BlockSpec(cumul.shape, lambda h: (0, 0)),
        ],
        out_specs=tile,
        out_shape=jax.ShapeDtypeStruct(qkv.shape, F32),
        compiler_params=params(32),
        cost_estimate=cost(8 * 10 * tokens * tokens * HEAD, 24 * tokens * heads * HEAD, 1 << 21),
        name="local_grads",
    )(qkv, out_grad, cumul)


def whole_grads(table, local, qkv, out_grad, cumul, states):
    tokens = qkv.shape[1]
    heads = cumul.shape[0]
    scale = HEAD**-0.5
    per = heads // 2

    def head(i, s):
        return jnp.where(i < per, (1 - s[Z]) * per + i, s[Z] * per + i - per)

    def body(s, local_ref, qkv_ref, og_ref, cum_ref, a, b, c, d, *rest):
        outs, held = rest[:6], rest[6]
        i = pl.program_id(0)

        @pl.when(i == 0)
        def _():
            in_order((a, b, c, d), s[Y], held)

        h = head(i, s)
        row = cum_ref[pl.ds(h, 1), :]
        column = column_of(row)
        total = row[:, tokens - 1 : tokens]
        since = scale * jnp.exp(column)
        until = jnp.exp(total - column)
        base = pl.multiple_of((h % 2) * HEAD, HEAD)
        coming = held[h // 2, pl.ds(base, HEAD), :]
        later = held[h // 2, pl.ds(2 * HEAD + base, HEAD), :]
        live = lax.broadcasted_iota(jnp.int32, (tokens, HEAD), 0) < s[LEN]
        cross = (
            since * lax.dot_general(og_ref[...], coming, AB_T, preferred_element_type=F32),
            until * lax.dot_general(qkv_ref[2], later, AB_T, preferred_element_type=F32),
            until * dot(qkv_ref[1], later),
        )
        grads = [jnp.where(live, local_ref[j] + cross[j], 0.0).astype(BF16) for j in range(3)]

        @pl.when(i < per)
        def _():
            for j in range(3):
                outs[j][...] = grads[j]

        @pl.when(i >= per)
        def _():
            for j in range(3):
                outs[3 + j][...] = grads[j]

    tile = pl.BlockSpec((3, tokens, HEAD), lambda i, s: (0, 0, head(i, s)))
    sent = pl.BlockSpec((tokens, HEAD), lambda i, s: (0, jnp.minimum(i, per - 1)))
    kept = pl.BlockSpec((tokens, HEAD), lambda i, s: (0, jnp.maximum(i - per, 0)))
    half = jax.ShapeDtypeStruct((tokens, per * HEAD), BF16)
    return pl.pallas_call(
        body,
        grid_spec=pltpu.PrefetchScalarGridSpec(
            num_scalar_prefetch=1,
            grid=(heads,),
            in_specs=[
                tile,
                tile,
                pl.BlockSpec((tokens, HEAD), lambda i, s: (0, head(i, s))),
                pl.BlockSpec(cumul.shape, lambda i, s: (0, 0)),
                *[pl.BlockSpec(m.shape, lambda i, s: (0, 0)) for m in states],
            ],
            out_specs=[sent] * 3 + [kept] * 3,
            scratch_shapes=[pltpu.VMEM((4, *states[0].shape), BF16)],
        ),
        out_shape=[half] * 6,
        compiler_params=params(32),
        cost_estimate=cost(48 * tokens * HEAD * HEAD, 24 * tokens * heads * HEAD),
        name="whole_grads",
    )(table, local, qkv, out_grad, cumul, *states)


def turn(table, shards):
    tokens, width = shards[0].shape
    rows = 4 * width // 32

    def body(s, *refs):
        out = refs[-1]
        for k in range(4):

            @pl.when((pl.program_id(0) ^ s[TEN]) == k)
            def _(k=k):
                out[...] = refs[k][...].T.reshape(out.shape)

    return pl.pallas_call(
        body,
        grid_spec=pltpu.PrefetchScalarGridSpec(
            num_scalar_prefetch=1,
            grid=(4,),
            in_specs=[pl.BlockSpec((tokens, width), lambda i, s: (0, 0)) for _ in shards],
            out_specs=pl.BlockSpec(
                (8, 1, rows, tokens), lambda i, s: (i % 2, (i // 2) ^ s[Z], 0, 0)
            ),
        ),
        out_shape=jax.ShapeDtypeStruct((16, 2, rows, tokens), BF16),
        compiler_params=params(32),
        cost_estimate=cost(0, 16 * tokens * width),
        name="turn",
    )(table, *shards)


def weight_part(table, own, pair, kept, got):
    tokens, cols = kept.shape
    rows = own.shape[2]
    side = cols // 2

    def body(s, own_x, own_y, pair_x, pair_y, kept_ref, got_ref, left, right):
        for a, b, lanes, out in (
            (own_x, pair_x, slice(0, side), left),
            (own_y, pair_y, slice(side, cols), right),
        ):
            acc = dot(a[...].reshape(4 * rows, tokens), kept_ref[:, lanes])
            acc += dot(b[...].reshape(4 * rows, tokens), got_ref[:, lanes])
            out[0] = acc.astype(BF16)

    by_x = pl.BlockSpec((1, 4, rows, tokens), lambda r, s: ((s[X] + r) % 4, 0, 0, 0))
    by_y = pl.BlockSpec((4, 1, rows, tokens), lambda r, s: (0, (s[Y] + r) % 4, 0, 0))
    whole = pl.BlockSpec((tokens, cols), lambda r, s: (0, 0))
    out = pl.BlockSpec((1, 4 * rows, side), lambda r, s: (r, 0, 0))
    return pl.pallas_call(
        body,
        grid_spec=pltpu.PrefetchScalarGridSpec(
            num_scalar_prefetch=1,
            grid=(4,),
            in_specs=[by_x, by_y, by_x, by_y, whole, whole],
            out_specs=[out, out],
        ),
        out_shape=[jax.ShapeDtypeStruct((4, 4 * rows, side), BF16)] * 2,
        compiler_params=params(40),
        cost_estimate=cost(64 * rows * tokens * cols, 32 * rows * (tokens + cols)),
        name="weight_part",
    )(table, own, own, pair, pair, kept, got)


def ring_sum(pieces, axis):
    n = pieces.shape[1] // 2
    up = send(pieces[2, :n], axis, 1)
    down = send(pieces[2, n:], axis, -1)
    ahead = jnp.concatenate([pieces[1, :n] + up, pieces[1, n:]])
    behind = jnp.concatenate([pieces[3, :n], pieces[3, n:] + down])
    return pieces[0] + send(ahead, axis, 1) + send(behind, axis, -1)


def swap_order(piece, axis):
    blocks = piece.reshape(4, -1, piece.shape[1])
    here = lax.axis_index(axis)
    return lax.dynamic_slice_in_dim(jnp.concatenate([blocks, blocks]), here, 4)


def device_part(activations, qkv_weight, log_decay, lengths, out_grad):
    tokens = activations.shape[0]
    index = [lax.axis_index(a) for a in ("c0", "c1", "c2", "zl", "co")]
    table = jnp.stack([*index, index[3] * 2 + index[4], lengths[0]]).astype(jnp.int32)
    here_z = index[0]
    weight = jnp.transpose(qkv_weight, (1, 0, 2))

    chip = send(activations, "zl", 1)
    core = send(activations, "co", 1)
    both = send(chip, "co", 1)
    live = (jnp.arange(tokens, dtype=jnp.int32) < lengths[0]).astype(F32)
    cumul = jnp.cumsum(log_decay.T * live[None, :], axis=1)

    acc = project(table, [activations, core], (0, 1), weight, None, False)
    acc = project(table, [chip], (2,), weight, acc, False)
    qkv = project(table, [both], (3,), weight, acc, True)

    to_y = shard_states(table, qkv, out_grad, cumul)
    at_y = [to_y[0], *[send(to_y[r], "c2", r) for r in (1, 2, 3)]]
    before, after, prior, later, ring = ring_y(table, at_y)
    at_x = [ring, *[send(ring, "c1", r) for r in (1, 2, 3)]]
    mine, edges, half = ring_x(table, at_x)
    other = send(half, "c0", 1)
    back = arrivals(table, other, mine, edges, before, after, prior, later)
    states = [back[0], *[send(back[r], "c2", r) for r in (1, 2, 3)]]

    first, second, _ = lax.optimization_barrier((activations, chip, both))
    far = send(first, "c0", 1)
    far_chip = send(second, "c0", 1)
    far_core = send(far, "co", 1)
    far_both = send(far_chip, "co", 1)
    own = turn(table, [activations, core, chip, both])
    pair = turn(table, [far, far_core, far_chip, far_both])
    rows = own.shape[2]
    own = own.reshape(4, 4, 2 * rows, tokens)
    pair = pair.reshape(4, 4, 2 * rows, tokens)

    local = local_grads(qkv, out_grad, cumul)
    grads = whole_grads(table, local, qkv, out_grad, cumul, states)
    sums = []
    for j in range(3):
        got = send(grads[j], "c0", 1)
        left, right = weight_part(table, own, pair, grads[3 + j], got)
        left, right = ring_sum(left, "c1"), ring_sum(right, "c2")
        left = ring_sum(swap_order(left, "c2"), "c2")
        right = ring_sum(swap_order(right, "c1"), "c1")
        sums.append(jnp.concatenate([left, right], axis=1))
    stacked = jnp.stack(sums)
    here, there = stacked[:, :rows], stacked[:, rows:]
    there = send(there, "c0", 1)
    whole = jnp.where(
        here_z == 0,
        jnp.concatenate([here, there], axis=2),
        jnp.concatenate([there, here], axis=2),
    )
    return jnp.transpose(whole.astype(F32), (1, 0, 2))


def solution(mesh):
    finer = Mesh(mesh.devices.reshape(2, 4, 4, 2, 2), ("c0", "c1", "c2", "zl", "co"))
    context, tensor = ("c0", "c1", "c2"), ("zl", "co")
    placed = (
        P(context, tensor),
        P(None, None, tensor),
        P(context, tensor),
        P(context),
        P(context, tensor),
    )
    return jax.shard_map(
        device_part,
        mesh=finer,
        in_specs=placed,
        out_specs=P(context, None, tensor),
        check_vma=False,
    )
```

```python
import functools

import jax
import jax.numpy as jnp
from jax import lax
from jax.experimental import pallas as pl
from jax.experimental.pallas import tpu as pltpu
from jax.sharding import Mesh
from jax.sharding import PartitionSpec as P

F32 = jnp.float32
BF16 = jnp.bfloat16
HEAD = 128
Z, X, Y, ZL, CO, TEN, LEN = range(7)
AB_T = (((1,), (1,)), ((), ()))
A_TB = (((0,), (0,)), ((), ()))


def dot(a, b):
    return jnp.dot(a, b, preferred_element_type=F32)


def params(mib, n=1):
    return pltpu.CompilerParams(
        dimension_semantics=("arbitrary",) * n if n else None, vmem_limit_bytes=mib << 20
    )


def cost(flops, nbytes, exps=0):
    return pl.CostEstimate(flops=1, bytes_accessed=1, transcendentals=0)


def shift(axis, by):
    n = lax.axis_size(axis)
    return [(i, (i + by) % n) for i in range(n)]


def send(x, axis, by):
    return lax.ppermute(x, axis, shift(axis, by))


def project(table, shards, flips, weight, partial, last):
    n = len(shards)
    tokens, width = shards[0].shape
    cols = weight.shape[2]
    block = cols // 2

    def body(s, *refs):
        out = refs[-1]
        acc = dot(refs[0][...], refs[n][0])
        for i in range(1, n):
            acc += dot(refs[i][...], refs[n + i][0])
        if partial is not None:
            acc += refs[2 * n][0]
        if last:
            row = lax.broadcasted_iota(jnp.int32, acc.shape, 0)
            acc = jnp.where(row < s[LEN], acc, 0.0)
        out[0] = acc.astype(out.dtype)

    tile = pl.BlockSpec((1, tokens, block), lambda g, j, s: (g, 0, j))
    in_specs = [pl.BlockSpec((tokens, width), lambda g, j, s: (0, 0)) for _ in shards]
    for flip in flips:
        in_specs.append(
            pl.BlockSpec((1, width, block), lambda g, j, s, flip=flip: (g, s[TEN] ^ flip, j))
        )
    operands = [*shards, *([weight] * n)]
    if partial is not None:
        in_specs.append(tile)
        operands.append(partial)
    return pl.pallas_call(
        body,
        grid_spec=pltpu.PrefetchScalarGridSpec(
            num_scalar_prefetch=1, grid=(3, 2), in_specs=in_specs, out_specs=tile
        ),
        out_shape=jax.ShapeDtypeStruct((3, tokens, cols), BF16 if last else F32),
        compiler_params=params(20, 2),
        cost_estimate=cost(6 * n * tokens * width * cols, 8 * n * width * cols),
        name="project",
    )(table, *operands)


def shard_states(table, qkv, out_grad, cumul):
    tokens = qkv.shape[1]
    scale = HEAD**-0.5

    def body(s, qkv_ref, og_ref, cum_ref, *outs):
        r = pl.program_id(0)
        who = (s[Y] + r) % 4
        blocks, totals = [], []
        for i in range(2):
            lanes = slice(i * HEAD, (i + 1) * HEAD)
            row = cum_ref[pl.ds(who * 2 + i, 1), :]
            total = row[:, tokens - 1 : tokens]
            keys_t = qkv_ref[1, :, lanes].astype(F32).T
            query_t = qkv_ref[0, :, lanes].astype(F32).T
            keys_t = (keys_t * jnp.exp(total - row)).astype(BF16)
            query_t = (query_t * (scale * jnp.exp(row))).astype(BF16)
            blocks.append((dot(keys_t, qkv_ref[2, :, lanes]), dot(query_t, og_ref[:, lanes])))
            totals.append(total)
        at = lax.broadcasted_iota(jnp.int32, (16, HEAD), 0)
        tail = jnp.where(at == 0, totals[0], totals[1]).astype(BF16)
        for k, out in enumerate(outs):

            @pl.when(r == k)
            def _(out=out):
                for i in range(2):
                    for kind in range(2):
                        start = (2 * kind + i) * HEAD
                        out[start : start + HEAD, :] = blocks[i][kind].astype(BF16)
                out[4 * HEAD :, :] = tail

    message = jax.ShapeDtypeStruct((4 * HEAD + 16, HEAD), BF16)
    whole = pl.BlockSpec(message.shape, lambda r, s: (0, 0))
    return pl.pallas_call(
        body,
        grid_spec=pltpu.PrefetchScalarGridSpec(
            num_scalar_prefetch=1,
            grid=(4,),
            in_specs=[
                pl.BlockSpec((3, tokens, 2 * HEAD), lambda r, s: (0, 0, (s[Y] + r) % 4)),
                pl.BlockSpec((tokens, 2 * HEAD), lambda r, s: (0, (s[Y] + r) % 4)),
                pl.BlockSpec(cumul.shape, lambda r, s: (0, 0)),
            ],
            out_specs=[whole] * 4,
        ),
        out_shape=[message] * 4,
        compiler_params=params(12),
        cost_estimate=cost(32 * tokens * HEAD * HEAD, 8 * tokens * 8 * HEAD),
        name="shard_states",
    )(table, qkv, out_grad, cumul)


def in_order(refs, place, held):
    for r, ref in enumerate(refs):
        held[(place - r + 4) % 4] = ref[...]


def head_rows(first, second):
    return jnp.concatenate([first, second], axis=0)


def spread(pair):
    wide = [jnp.broadcast_to(pair[i : i + 1, :], (HEAD, HEAD)) for i in range(2)]
    return head_rows(*wide)


def ring_y(table, messages):
    half = 2 * HEAD

    def body(s, a, b, c, d, before, after, prior, later, out, held):
        in_order((a, b, c, d), s[Y], held)
        totals = [held[t, 2 * half : 2 * half + 16, :].astype(F32)[:2] for t in range(4)]
        run = jnp.zeros((half, HEAD), F32)
        reach = jnp.zeros((2, HEAD), F32)
        for t in range(4):
            before[t] = run
            prior[t] = jnp.exp(reach)
            run = spread(jnp.exp(totals[t])) * run + held[t, :half, :].astype(F32)
            reach = reach + totals[t]
        out[:half, :] = run.astype(BF16)
        whole = reach
        run = jnp.zeros((half, HEAD), F32)
        reach = jnp.zeros((2, HEAD), F32)
        for t in range(3, -1, -1):
            after[t] = run
            later[t] = jnp.exp(reach)
            run = spread(jnp.exp(totals[t])) * run + held[t, half : 2 * half, :].astype(F32)
            reach = reach + totals[t]
        out[half : 2 * half, :] = run.astype(BF16)
        high = whole.astype(BF16).astype(F32)
        low = whole - high
        at = lax.broadcasted_iota(jnp.int32, (16, HEAD), 0)
        tail = jnp.where(at == 0, high[0:1], high[1:2])
        tail = jnp.where(at == 2, low[0:1], tail)
        tail = jnp.where(at == 3, low[1:2], tail)
        out[2 * half :, :] = tail.astype(BF16)

    return pl.pallas_call(
        body,
        grid_spec=pltpu.PrefetchScalarGridSpec(
            num_scalar_prefetch=1,
            grid=(1,),
            in_specs=[pl.BlockSpec(m.shape, lambda i, s: (0, 0)) for m in messages],
            out_specs=[
                pl.BlockSpec((4, half, HEAD), lambda i, s: (0, 0, 0)),
                pl.BlockSpec((4, half, HEAD), lambda i, s: (0, 0, 0)),
                pl.BlockSpec((4, 2, HEAD), lambda i, s: (0, 0, 0)),
                pl.BlockSpec((4, 2, HEAD), lambda i, s: (0, 0, 0)),
                pl.BlockSpec(messages[0].shape, lambda i, s: (0, 0)),
            ],
            scratch_shapes=[pltpu.VMEM((4, *messages[0].shape), BF16)],
        ),
        out_shape=[
            jax.ShapeDtypeStruct((4, half, HEAD), F32),
            jax.ShapeDtypeStruct((4, half, HEAD), F32),
            jax.ShapeDtypeStruct((4, 2, HEAD), F32),
            jax.ShapeDtypeStruct((4, 2, HEAD), F32),
            jax.ShapeDtypeStruct(messages[0].shape, BF16),
        ],
        compiler_params=params(16),
        cost_estimate=cost(1 << 20, 2 << 20),
        name="ring_y",
    )(table, *messages)


def ring_x(table, messages):
    half = 2 * HEAD

    def body(s, a, b, c, d, mine, edges, out, held):
        in_order((a, b, c, d), s[X], held)
        tails = [held[t, 2 * half : 2 * half + 16, :].astype(F32) for t in range(4)]
        totals = [tail[0:2] + tail[2:4] for tail in tails]
        for kind, steps in ((0, range(4)), (1, range(3, -1, -1))):
            run = jnp.zeros((half, HEAD), F32)
            reach = jnp.zeros((2, HEAD), F32)
            for t in steps:

                @pl.when(s[X] == t)
                def _(run=run, reach=reach, kind=kind):
                    mine[kind] = run
                    edges[kind] = jnp.exp(reach)

                rows = held[t, kind * half : (kind + 1) * half, :].astype(F32)
                run = spread(jnp.exp(totals[t])) * run + rows
                reach = reach + totals[t]

            @pl.when(s[Z] == kind)
            def _(run=run):
                out[...] = run.astype(BF16)

    return pl.pallas_call(
        body,
        grid_spec=pltpu.PrefetchScalarGridSpec(
            num_scalar_prefetch=1,
            grid=(1,),
            in_specs=[pl.BlockSpec(m.shape, lambda i, s: (0, 0)) for m in messages],
            out_specs=[
                pl.BlockSpec((2, half, HEAD), lambda i, s: (0, 0, 0)),
                pl.BlockSpec((2, 2, HEAD), lambda i, s: (0, 0, 0)),
                pl.BlockSpec((half, HEAD), lambda i, s: (0, 0)),
            ],
            scratch_shapes=[pltpu.VMEM((4, *messages[0].shape), BF16)],
        ),
        out_shape=[
            jax.ShapeDtypeStruct((2, half, HEAD), F32),
            jax.ShapeDtypeStruct((2, 2, HEAD), F32),
            jax.ShapeDtypeStruct((half, HEAD), BF16),
        ],
        compiler_params=params(16),
        cost_estimate=cost(1 << 20, 2 << 20),
        name="ring_x",
    )(table, *messages)


def arrivals(table, other, mine, edges, before, after, prior, later):
    half = 2 * HEAD

    def body(s, other_ref, mine_ref, edges_ref, before_ref, after_ref, prior_ref, later_ref, *outs):
        across = other_ref[...].astype(F32)
        start = mine_ref[0] + spread(edges_ref[0]) * jnp.where(s[Z] == 1, across, 0.0)
        finish = mine_ref[1] + spread(edges_ref[1]) * jnp.where(s[Z] == 0, across, 0.0)
        for r, out in enumerate(outs):
            t = (s[Y] + r) % 4
            out[:half, :] = (before_ref[t] + spread(prior_ref[t]) * start).astype(BF16)
            out[half:, :] = (after_ref[t] + spread(later_ref[t]) * finish).astype(BF16)

    operands = (other, mine, edges, before, after, prior, later)
    message = jax.ShapeDtypeStruct((2 * half, HEAD), BF16)
    return pl.pallas_call(
        body,
        grid_spec=pltpu.PrefetchScalarGridSpec(
            num_scalar_prefetch=1,
            grid=(1,),
            in_specs=[pl.BlockSpec(m.shape, lambda i, s, n=m.ndim: (0,) * n) for m in operands],
            out_specs=[pl.BlockSpec(message.shape, lambda i, s: (0, 0))] * 4,
        ),
        out_shape=[message] * 4,
        compiler_params=params(16),
        cost_estimate=cost(1 << 20, 2 << 20),
        name="arrivals",
    )(table, *operands)


def column_of(row):
    return jnp.broadcast_to(row, (HEAD, row.shape[1])).T


def local_grads(qkv, out_grad, cumul, first, count, so_far):
    tokens = qkv.shape[1]
    scale = HEAD**-0.5
    size = tokens // 2

    def body(qkv_ref, og_ref, cum_ref, *refs):
        out = refs[-1]
        h = pl.program_id(0) + first
        row = cum_ref[pl.ds(h, 1), :]
        column = column_of(row)
        wide = jnp.concatenate([column] * (size // HEAD), axis=1)
        s_at = lax.broadcasted_iota(jnp.int32, (size, size), 0)
        t_at = lax.broadcasted_iota(jnp.int32, (size, size), 1)
        parts = [slice(0, size), slice(size, tokens)]

        def pair(t, s):
            gap = row[:, parts[t]] - wide[parts[s], :]
            if t == s:
                gap = jnp.where(s_at <= t_at, gap, -jnp.inf)
            decay = jnp.exp(gap)
            q, k, v = qkv_ref[0, parts[t], :], qkv_ref[1, parts[s], :], qkv_ref[2, parts[s], :]
            g = og_ref[parts[t], :]
            scores = lax.dot_general(k, q, AB_T, preferred_element_type=F32)
            grads = lax.dot_general(v, g, AB_T, preferred_element_type=F32)
            prob = (scores * scale * decay).astype(BF16)
            score = (grads * decay).astype(BF16)
            dq = lax.dot_general(score, k, A_TB, preferred_element_type=F32)
            return dq, dot(score, q), dot(prob, g)

        a, b, c = pair(0, 0), pair(1, 0), pair(1, 1)
        out[0, parts[0], :] = a[0] * scale
        out[0, parts[1], :] = (b[0] + c[0]) * scale
        out[1, parts[0], :] = (a[1] + b[1]) * scale
        out[1, parts[1], :] = c[1] * scale
        out[2, parts[0], :] = a[2] + b[2]
        out[2, parts[1], :] = c[2]

    tile = pl.BlockSpec((3, tokens, HEAD), lambda h: (0, 0, h + first))
    in_specs = [
        tile,
        pl.BlockSpec((tokens, HEAD), lambda h: (0, h + first)),
        pl.BlockSpec(cumul.shape, lambda h: (0, 0)),
    ]
    operands = [qkv, out_grad, cumul]
    if so_far is not None:
        in_specs.append(pl.BlockSpec(memory_space=pl.ANY))
        operands.append(so_far)
    return pl.pallas_call(
        body,
        grid=(count,),
        in_specs=in_specs,
        out_specs=tile,
        out_shape=jax.ShapeDtypeStruct(qkv.shape, F32),
        input_output_aliases={} if so_far is None else {3: 0},
        compiler_params=params(16),
        cost_estimate=cost(1, 1),
        name="local_grads",
    )(*operands)


def whole_grads(table, part, local, factor, cumul, states):
    tokens = local.shape[1]
    heads = cumul.shape[0]
    scale = HEAD**-0.5
    per = heads // 2
    lead = factor.ndim - 2
    at = (0, 2, 1)[part]

    def head(i, s):
        return jnp.where(i < per, (1 - s[Z]) * per + i, s[Z] * per + i - per)

    def body(s, local_ref, factor_ref, cum_ref, a, b, c, d, sent, kept, held):
        i = pl.program_id(0)

        @pl.when(i == 0)
        def _():
            in_order((a, b, c, d), s[Y], held)

        h = head(i, s)
        row = cum_ref[pl.ds(h, 1), :]
        column = column_of(row)
        base = pl.multiple_of((h % 2) * HEAD + (2 * HEAD if part else 0), HEAD)
        state = held[h // 2, pl.ds(base, HEAD), :]
        rows = factor_ref[0] if lead else factor_ref[...]
        if part < 2:
            cross = lax.dot_general(rows, state, AB_T, preferred_element_type=F32)
        else:
            cross = dot(rows, state)
        if part == 0:
            cross *= scale * jnp.exp(column)
        else:
            cross *= jnp.exp(row[:, tokens - 1 : tokens] - column)
        live = lax.broadcasted_iota(jnp.int32, (tokens, HEAD), 0) < s[LEN]
        grads = jnp.where(live, local_ref[0] + cross, 0.0).astype(BF16)

        @pl.when(i < per)
        def _():
            sent[...] = grads

        @pl.when(i >= per)
        def _():
            kept[...] = grads

    if lead:
        rows_of = pl.BlockSpec((1, tokens, HEAD), lambda i, s: (at, 0, head(i, s)))
    else:
        rows_of = pl.BlockSpec((tokens, HEAD), lambda i, s: (0, head(i, s)))
    half = jax.ShapeDtypeStruct((tokens, per * HEAD), BF16)
    return pl.pallas_call(
        body,
        grid_spec=pltpu.PrefetchScalarGridSpec(
            num_scalar_prefetch=1,
            grid=(heads,),
            in_specs=[
                pl.BlockSpec((1, tokens, HEAD), lambda i, s: (part, 0, head(i, s))),
                rows_of,
                pl.BlockSpec(cumul.shape, lambda i, s: (0, 0)),
                *[pl.BlockSpec(m.shape, lambda i, s: (0, 0)) for m in states],
            ],
            out_specs=[
                pl.BlockSpec((tokens, HEAD), lambda i, s: (0, jnp.minimum(i, per - 1))),
                pl.BlockSpec((tokens, HEAD), lambda i, s: (0, jnp.maximum(i - per, 0))),
            ],
            scratch_shapes=[pltpu.VMEM((4, *states[0].shape), BF16)],
        ),
        out_shape=[half, half],
        compiler_params=params(16),
        cost_estimate=cost(1, 1),
        name="whole_grads",
    )(table, local, factor, cumul, *states)


def turn(table, shards):
    tokens, width = shards[0].shape
    rows = 4 * width // 32

    def body(s, *refs):
        out = refs[-1]
        for k in range(4):

            @pl.when((pl.program_id(0) ^ s[TEN]) == k)
            def _(k=k):
                out[...] = refs[k][...].T.reshape(out.shape)

    return pl.pallas_call(
        body,
        grid_spec=pltpu.PrefetchScalarGridSpec(
            num_scalar_prefetch=1,
            grid=(4,),
            in_specs=[pl.BlockSpec((tokens, width), lambda i, s: (0, 0)) for _ in shards],
            out_specs=pl.BlockSpec(
                (8, 1, rows, tokens), lambda i, s: (i % 2, (i // 2) ^ s[Z], 0, 0)
            ),
        ),
        out_shape=jax.ShapeDtypeStruct((16, 2, rows, tokens), BF16),
        compiler_params=params(12),
        cost_estimate=cost(0, 16 * tokens * width),
        name="turn",
    )(table, *shards)


def weight_part(table, own, pair, kept, got):
    tokens, cols = kept.shape
    rows = own.shape[2]
    side = cols // 2

    def body(s, own_x, own_y, pair_x, pair_y, kept_ref, got_ref, left, right):
        for a, b, lanes, out in (
            (own_x, pair_x, slice(0, side), left),
            (own_y, pair_y, slice(side, cols), right),
        ):
            acc = dot(a[...].reshape(4 * rows, tokens), kept_ref[:, lanes])
            acc += dot(b[...].reshape(4 * rows, tokens), got_ref[:, lanes])
            out[0] = acc.astype(BF16)

    by_x = pl.BlockSpec((1, 4, rows, tokens), lambda r, s: ((s[X] + r) % 4, 0, 0, 0))
    by_y = pl.BlockSpec((4, 1, rows, tokens), lambda r, s: (0, (s[Y] + r) % 4, 0, 0))
    whole = pl.BlockSpec((tokens, cols), lambda r, s: (0, 0))
    out = pl.BlockSpec((1, 4 * rows, side), lambda r, s: (r, 0, 0))
    return pl.pallas_call(
        body,
        grid_spec=pltpu.PrefetchScalarGridSpec(
            num_scalar_prefetch=1,
            grid=(4,),
            in_specs=[by_x, by_y, by_x, by_y, whole, whole],
            out_specs=[out, out],
        ),
        out_shape=[jax.ShapeDtypeStruct((4, 4 * rows, side), BF16)] * 2,
        compiler_params=params(16),
        cost_estimate=cost(64 * rows * tokens * cols, 32 * rows * (tokens + cols)),
        name="weight_part",
    )(table, own, own, pair, pair, kept, got)


def ring_sum(pieces, axis):
    n = pieces[2].shape[0] // 2
    up, down = yield {(axis, 1): pieces[2][:n], (axis, -1): pieces[2][n:]}
    ahead = jnp.concatenate([pieces[1][:n] + up, pieces[1][n:]])
    behind = jnp.concatenate([pieces[3][:n], pieces[3][n:] + down])
    first, second = yield {(axis, 1): ahead, (axis, -1): behind}
    total = pieces[0].astype(F32) + first.astype(F32) + second.astype(F32)
    return total.astype(BF16)


def two_sums(pieces, first, second):
    total = yield from ring_sum(pieces, first)
    blocks = total.reshape(4, -1, total.shape[1])
    here = lax.axis_index(second)
    blocks = [
        lax.dynamic_index_in_dim(blocks, (here + r) % 4, 0, keepdims=False) for r in range(4)
    ]
    return (yield from ring_sum(blocks, second))


def one_part(left, right):
    jobs = [two_sums(left, "c1", "c2"), two_sums(right, "c2", "c1")]
    wants, done = [next(job) for job in jobs], []
    for _ in range(4):
        got = yield {link: x for want in wants for link, x in want.items()}
        answers = [[got[link] for link in want] for want in wants]
        wants, done = [], []
        for job, answer in zip(jobs, answers):
            try:
                wants.append(job.send(answer))
            except StopIteration as end:
                done.append(end.value)
    here, there = (jnp.concatenate(h) for h in zip(*[(d[: len(d) // 2], d[len(d) // 2 :]) for d in done]))
    got = yield {("c0", 1): there}
    return here, got["c0", 1]


def in_step(starters):
    job, token = starters[0](None), None
    running, results, step = [(0, job, next(job))], {}, 0
    while running:
        links = []
        for _, _, want in running:
            links += [link for link in want if link not in links]
        got = {}
        for link in links:
            messages = [want[link] for _, _, want in running if link in want]
            got[link] = send(jnp.concatenate(messages), *link)
        step += 1
        fresh = []
        if step < len(starters):
            job = starters[step](token)
            fresh = [(step, job, next(job))]
        got, fresh_wants = lax.optimization_barrier((list(got.values()), [dict(enumerate(w.values())) for _, _, w in fresh]))
        token, got = got[0], dict(zip(links, got))
        offset, still = dict.fromkeys(links, 0), []
        for at, job, want in running:
            answer = {}
            for link, x in want.items():
                answer[link] = got[link][offset[link] : offset[link] + len(x)]
                offset[link] += len(x)
            try:
                still.append((at, job, job.send(answer)))
            except StopIteration as end:
                results[at] = end.value
        for (at, job, want), held in zip(fresh, fresh_wants):
            still.append((at, job, dict(zip(want, held.values()))))
        running = still
    return [results[j] for j in range(len(starters))]


def device_part(activations, qkv_weight, log_decay, lengths, out_grad):
    after_all = lax.optimization_barrier
    tokens = activations.shape[0]
    index = [lax.axis_index(a) for a in ("c0", "c1", "c2", "zl", "co")]
    table = jnp.stack([*index, index[3] * 2 + index[4], lengths[0]]).astype(jnp.int32)
    weight = jnp.transpose(qkv_weight, (1, 0, 2))

    chip = send(activations, "zl", 1)
    core = send(activations, "co", 1)
    live = (jnp.arange(tokens, dtype=jnp.int32) < lengths[0]).astype(F32)
    cumul = jnp.cumsum(log_decay.T * live[None, :], axis=1)

    acc = project(table, [activations, core], (0, 1), weight, None, False)
    chip, acc = after_all((chip, acc))
    both = send(chip, "co", 1)
    first, second = after_all((activations, chip))
    far = send(first, "c0", 1)
    far_chip = send(second, "c0", 1)
    acc = project(table, [chip], (2,), weight, acc, False)
    both, acc = after_all((both, acc))
    qkv = project(table, [both], (3,), weight, acc, True)

    to_y = shard_states(table, qkv, out_grad, cumul)
    at_y = [send(to_y[r], "c2", r) for r in (2, 1, 3)]
    local = local_grads(qkv, out_grad, cumul, 0, 2, None)
    *at_y, local = after_all((*at_y, local))
    before, after, prior, later, ring = ring_y(table, [to_y[0], at_y[1], at_y[0], at_y[2]])
    at_x = [send(ring, "c1", r) for r in (2, 1, 3)]
    local, _ = after_all((local, ring))
    local = local_grads(qkv, out_grad, cumul, 2, 2, local)
    *at_x, local = after_all((*at_x, local))
    mine, edges, half = ring_x(table, [ring, at_x[1], at_x[0], at_x[2]])
    other = send(half, "c0", 1)
    local, _ = after_all((local, half))
    local = local_grads(qkv, out_grad, cumul, 4, 2, local)
    other, local = after_all((other, local))
    back = arrivals(table, other, mine, edges, before, after, prior, later)
    states = [send(back[r], "c2", r) for r in (2, 1, 3)]
    local, _ = after_all((local, back[0]))
    local = local_grads(qkv, out_grad, cumul, 6, 2, local)
    own = turn(table, [activations, core, chip, both])
    *states, local, own = after_all((*states, local, own))
    states = [back[0], states[1], states[0], states[2]]

    far_core = send(far, "co", 1)
    far_both = send(far_chip, "co", 1)
    pair = turn(table, [far, far_core, far_chip, far_both])
    rows = own.shape[2]
    own = own.reshape(4, 4, 2 * rows, tokens)
    pair = pair.reshape(4, 4, 2 * rows, tokens)

    sent, kept = [], []
    for j in range(3):
        if j:
            local, _ = after_all((local, kept[-1]))
        factor = out_grad if j == 0 else qkv
        halves = whole_grads(table, j, local, factor, cumul, states)
        sent.append(halves[0])
        kept.append(halves[1])
    first = send(sent[0], "c0", 1)
    first, sent[1:], kept[1:], pair = after_all((first, sent[1:], kept[1:], pair))
    second = send(sent[1], "c0", 1)

    def begin(j, token):
        if j == 2:
            got = send(after_all((sent[2], token))[0], "c0", 1)
        else:
            got = (first, second)[j]
        left, right = weight_part(table, own, pair, kept[j], got)
        return one_part([left[r] for r in range(4)], [right[r] for r in range(4)])

    starters = [functools.partial(begin, j) for j in range(3)]
    outs = []
    for here, there in in_step(starters):
        a, b = (jnp.concatenate([h[:rows], h[rows:]], axis=1) for h in (here, there))
        outs.append(
            jnp.where(
                index[0] == 0, jnp.concatenate([a, b], axis=1), jnp.concatenate([b, a], axis=1)
            )
        )
    return jnp.transpose(jnp.stack(outs).astype(F32), (1, 0, 2))


def solution(mesh):
    finer = Mesh(mesh.devices.reshape(2, 4, 4, 2, 2), ("c0", "c1", "c2", "zl", "co"))
    context, tensor = ("c0", "c1", "c2"), ("zl", "co")
    placed = (
        P(context, tensor),
        P(None, None, tensor),
        P(context, tensor),
        P(context),
        P(context, tensor),
    )
    return jax.shard_map(
        device_part,
        mesh=finer,
        in_specs=placed,
        out_specs=P(context, None, tensor),
        check_vma=False,
    )
```

```python
import jax
import jax.numpy as jnp
from jax import lax
from jax.experimental import pallas as pl
from jax.experimental.pallas import tpu as pltpu
from jax.sharding import Mesh
from jax.sharding import PartitionSpec as P

F32 = jnp.float32
BF16 = jnp.bfloat16
HEAD = 128
Z, X, Y, ZL, CO, TEN, LEN = range(7)
AB_T = (((1,), (1,)), ((), ()))
A_TB = (((0,), (0,)), ((), ()))


def dot(a, b):
    return jnp.dot(a, b, preferred_element_type=F32)


def shift(axis, by):
    n = lax.axis_size(axis)
    return [(i, (i + by) % n) for i in range(n)]


def send(x, axis, by):
    return lax.ppermute(x, axis, shift(axis, by))


def across(x):
    return lax.ppermute(x, ("c0", "zl"), [(0, 3), (1, 2), (2, 1), (3, 0)])


def whole(x):
    return pl.BlockSpec(x.shape, lambda *_, n=len(x.shape): (0,) * n)


def call(name, body, table, grid, operands, in_specs, outs, out_specs, mib, scratch=(), alias=None):
    return pl.pallas_call(
        body,
        grid_spec=pltpu.PrefetchScalarGridSpec(
            num_scalar_prefetch=1,
            grid=grid,
            in_specs=in_specs,
            out_specs=out_specs,
            scratch_shapes=scratch,
        ),
        out_shape=outs,
        input_output_aliases=alias or {},
        compiler_params=pltpu.CompilerParams(
            dimension_semantics=("arbitrary",) * len(grid), vmem_limit_bytes=mib << 20
        ),
        cost_estimate=pl.CostEstimate(flops=1, bytes_accessed=1, transcendentals=0),
        name=name,
    )(table, *operands)


def shape(dims, kind=BF16):
    return jax.ShapeDtypeStruct(dims, kind)


def project(table, shards, flips, weight, partial, last):
    n = len(shards)
    tokens, width = shards[0].shape
    cols = weight.shape[2] // 2

    def body(s, *refs):
        out = refs[-1]
        acc = dot(refs[0][...], refs[n][0])
        for i in range(1, n):
            acc += dot(refs[i][...], refs[n + i][0])
        if partial is not None:
            acc += refs[2 * n][0]
        if last:
            row = lax.broadcasted_iota(jnp.int32, acc.shape, 0)
            acc = jnp.where(row < s[LEN], acc, 0.0)
        out[0] = acc.astype(out.dtype)

    tile = pl.BlockSpec((1, tokens, cols), lambda g, s: (g, 0, 0))
    in_specs = [whole(x) for x in shards]
    for flip in flips:
        in_specs.append(
            pl.BlockSpec((1, width, cols), lambda g, s, flip=flip: (g, s[TEN] ^ flip, s[Z]))
        )
    operands = [*shards, *([weight] * n)]
    if partial is not None:
        in_specs.append(tile)
        operands.append(partial)
    out = shape((3, tokens, cols), BF16 if last else F32)
    return call("project", body, table, (3,), operands, in_specs, out, tile, 20)


def shard_states(table, qkvs, out_grads, cumul):
    tokens = qkvs[0].shape[1]
    heads = qkvs[0].shape[2] // HEAD
    scale = HEAD**-0.5

    def body(s, qkv_a, qkv_b, og_a, og_b, cum_ref, *outs):
        r = pl.program_id(0)
        who = (s[Y] + r) % 4
        blocks, totals = [], []
        for i, (qkv_ref, og_ref) in enumerate(((qkv_a, og_a), (qkv_b, og_b))):
            row = cum_ref[pl.ds(i * heads + who, 1), :]
            total = row[:, tokens - 1 : tokens]
            keys_t = qkv_ref[1].astype(F32).T
            query_t = qkv_ref[0].astype(F32).T
            keys_t = (keys_t * jnp.exp(total - row)).astype(BF16)
            query_t = (query_t * (scale * jnp.exp(row))).astype(BF16)
            blocks.append((dot(keys_t, qkv_ref[2]), dot(query_t, og_ref[...])))
            totals.append(total)
        at = lax.broadcasted_iota(jnp.int32, (16, HEAD), 0)
        tail = jnp.where(at == s[Z], totals[0], totals[1]).astype(BF16)
        for k, out in enumerate(outs):

            @pl.when(r == k)
            def _(out=out):
                for i in range(2):
                    for kind in range(2):
                        start = pl.multiple_of((2 * kind + (i ^ s[Z])) * HEAD, HEAD)
                        out[pl.ds(start, HEAD), :] = blocks[i][kind].astype(BF16)
                out[4 * HEAD :, :] = tail

    message = shape((4 * HEAD + 16, HEAD))
    qkv_tile = pl.BlockSpec((3, tokens, HEAD), lambda r, s: (0, 0, (s[Y] + r) % 4))
    og_tile = pl.BlockSpec((tokens, HEAD), lambda r, s: (0, (s[Y] + r) % 4))
    return call(
        "shard_states",
        body,
        table,
        (4,),
        (*qkvs, *out_grads, cumul),
        [qkv_tile, qkv_tile, og_tile, og_tile, whole(cumul)],
        [message] * 4,
        [whole(message)] * 4,
        12,
    )


def in_order(refs, place, held):
    for r, ref in enumerate(refs):
        held[(place - r + 4) % 4] = ref[...]


def spread(pair):
    wide = [jnp.broadcast_to(pair[i : i + 1, :], (HEAD, HEAD)) for i in range(2)]
    return jnp.concatenate(wide, axis=0)


def ring_y(table, messages):
    half = 2 * HEAD

    def body(s, a, b, c, d, before, after, prior, later, out, held):
        in_order((a, b, c, d), s[Y], held)
        totals = [held[t, 2 * half : 2 * half + 16, :].astype(F32)[:2] for t in range(4)]
        run = jnp.zeros((half, HEAD), F32)
        reach = jnp.zeros((2, HEAD), F32)
        for t in range(4):
            before[t] = run
            prior[t] = jnp.exp(reach)
            run = spread(jnp.exp(totals[t])) * run + held[t, :half, :].astype(F32)
            reach = reach + totals[t]
        out[:half, :] = run.astype(BF16)
        total = reach
        run = jnp.zeros((half, HEAD), F32)
        reach = jnp.zeros((2, HEAD), F32)
        for t in range(3, -1, -1):
            after[t] = run
            later[t] = jnp.exp(reach)
            run = spread(jnp.exp(totals[t])) * run + held[t, half : 2 * half, :].astype(F32)
            reach = reach + totals[t]
        out[half : 2 * half, :] = run.astype(BF16)
        high = total.astype(BF16).astype(F32)
        low = total - high
        at = lax.broadcasted_iota(jnp.int32, (16, HEAD), 0)
        tail = jnp.where(at == 0, high[0:1], high[1:2])
        tail = jnp.where(at == 2, low[0:1], tail)
        tail = jnp.where(at == 3, low[1:2], tail)
        out[2 * half :, :] = tail.astype(BF16)

    outs = [
        shape((4, half, HEAD), F32),
        shape((4, half, HEAD), F32),
        shape((4, 2, HEAD), F32),
        shape((4, 2, HEAD), F32),
        shape(messages[0].shape),
    ]
    return call(
        "ring_y",
        body,
        table,
        (1,),
        messages,
        [whole(m) for m in messages],
        outs,
        [whole(o) for o in outs],
        8,
        [pltpu.VMEM((4, *messages[0].shape), BF16)],
    )


def arrivals(table, messages, before, after, prior, later):
    half = 2 * HEAD

    def body(s, a, b, c, d, before_ref, after_ref, prior_ref, later_ref, *rest):
        outs, held, mine, edges = rest[:4], *rest[4:]
        in_order((a, b, c, d), s[X], held)
        tails = [held[t, 2 * half : 2 * half + 16, :].astype(F32) for t in range(4)]
        totals = [tail[0:2] + tail[2:4] for tail in tails]
        ends = []
        for kind, steps in ((0, range(4)), (1, range(3, -1, -1))):
            run = jnp.zeros((half, HEAD), F32)
            reach = jnp.zeros((2, HEAD), F32)
            for t in steps:

                @pl.when(s[X] == t)
                def _(run=run, reach=reach, kind=kind):
                    mine[kind] = run
                    edges[kind] = jnp.exp(reach)

                rows = held[t, kind * half : (kind + 1) * half, :].astype(F32)
                run = spread(jnp.exp(totals[t])) * run + rows
                reach = reach + totals[t]
            ends.append(run.astype(BF16).astype(F32))
        nothing = jnp.zeros((HEAD, HEAD), F32)
        across_up = jnp.concatenate([nothing, ends[0][:HEAD]], axis=0)
        across_down = jnp.concatenate([ends[1][HEAD:], nothing], axis=0)
        start = mine[0] + spread(edges[0]) * across_up
        finish = mine[1] + spread(edges[1]) * across_down
        for r, out in enumerate(outs):
            t = (s[Y] + r) % 4
            out[:half, :] = (before_ref[t] + spread(prior_ref[t]) * start).astype(BF16)
            out[half:, :] = (after_ref[t] + spread(later_ref[t]) * finish).astype(BF16)

    operands = (*messages, before, after, prior, later)
    message = shape((2 * half, HEAD))
    return call(
        "arrivals",
        body,
        table,
        (1,),
        operands,
        [whole(m) for m in operands],
        [message] * 4,
        [whole(message)] * 4,
        8,
        [
            pltpu.VMEM((4, *messages[0].shape), BF16),
            pltpu.VMEM((2, half, HEAD), F32),
            pltpu.VMEM((2, 2, HEAD), F32),
        ],
    )


def column_of(row):
    return jnp.broadcast_to(row, (HEAD, row.shape[1])).T


def local_grads(table, qkv, out_grad, cumul, which, first, count, so_far):
    tokens = qkv.shape[1]
    heads = qkv.shape[2] // HEAD
    scale = HEAD**-0.5
    size = tokens // 2

    def body(s, qkv_ref, og_ref, cum_ref, *refs):
        out, ready = refs[-2:]
        row = cum_ref[pl.ds(pl.program_id(0) + which * heads + first, 1), :]
        column = column_of(row)
        wide = jnp.concatenate([column] * (size // HEAD), axis=1)
        s_at = lax.broadcasted_iota(jnp.int32, (size, size), 0)
        t_at = lax.broadcasted_iota(jnp.int32, (size, size), 1)
        parts = [slice(0, size), slice(size, tokens)]

        def pair(t, s):
            gap = row[:, parts[t]] - wide[parts[s], :]
            if t == s:
                gap = jnp.where(s_at <= t_at, gap, -jnp.inf)
            decay = jnp.exp(gap)
            q, k, v = qkv_ref[0, parts[t], :], qkv_ref[1, parts[s], :], qkv_ref[2, parts[s], :]
            g = og_ref[parts[t], :]
            scores = lax.dot_general(k, q, AB_T, preferred_element_type=F32)
            grads = lax.dot_general(v, g, AB_T, preferred_element_type=F32)
            prob = (scores * scale * decay).astype(BF16)
            score = (grads * decay).astype(BF16)
            dq = lax.dot_general(score, k, A_TB, preferred_element_type=F32)
            return dq, dot(score, q), dot(prob, g)

        a, b, c = pair(0, 0), pair(1, 0), pair(1, 1)
        live = lax.broadcasted_iota(jnp.int32, (tokens, HEAD), 0) < s[LEN]
        grads = (
            jnp.concatenate([a[0], b[0] + c[0]], axis=0) * scale,
            jnp.concatenate([a[1] + b[1], c[1]], axis=0) * scale,
            jnp.concatenate([a[2] + b[2], c[2]], axis=0),
        )
        until = jnp.exp(row[:, tokens - 1 : tokens] - column)
        rows = (
            og_ref[...].astype(F32) * (scale * jnp.exp(column)),
            qkv_ref[2].astype(F32) * until,
            qkv_ref[1].astype(F32) * until,
        )
        for j in range(3):
            out[j] = jnp.where(live, grads[j], 0.0)
            ready[j] = jnp.where(live, rows[j], 0.0).astype(BF16)

    tile = pl.BlockSpec((3, tokens, HEAD), lambda h, s: (0, 0, h + first))
    in_specs = [tile, pl.BlockSpec((tokens, HEAD), lambda h, s: (0, h + first)), whole(cumul)]
    operands = [qkv, out_grad, cumul]
    if so_far is not None:
        in_specs += [pl.BlockSpec(memory_space=pl.ANY)] * 2
        operands += so_far
    return call(
        "local_grads",
        body,
        table,
        (count,),
        operands,
        in_specs,
        [shape(qkv.shape, F32), shape(qkv.shape)],
        [tile, tile],
        12,
        alias=None if so_far is None else {4: 0, 5: 1},
    )


def whole_grads(table, which, local, ready, states):
    tokens = local.shape[1]
    heads = local.shape[2] // HEAD

    def body(s, local_ref, ready_ref, a, b, c, d, left, right, held):
        h = pl.program_id(0)

        @pl.when(h == 0)
        def _():
            in_order((a, b, c, d), s[Y], held)

        base = pl.multiple_of((s[Z] ^ which) * HEAD, HEAD)
        coming = held[h, pl.ds(base, HEAD), :]
        later = held[h, pl.ds(2 * HEAD + base, HEAD), :]
        cross = (
            lax.dot_general(ready_ref[0], coming, AB_T, preferred_element_type=F32),
            lax.dot_general(ready_ref[1], later, AB_T, preferred_element_type=F32),
            dot(ready_ref[2], later),
        )
        grads = [(local_ref[j] + cross[j]).astype(BF16) for j in range(3)]
        for k in range(heads):

            @pl.when(h == k)
            def _(k=k):
                for j in range(3):
                    start = (2 * j + k % 2) * HEAD
                    (left, right)[k // 2][:, start : start + HEAD] = grads[j]

    tile = pl.BlockSpec((3, tokens, HEAD), lambda h, s: (0, 0, h))
    side = shape((tokens, 3 * heads * HEAD // 2))
    return call(
        "whole_grads",
        body,
        table,
        (heads,),
        (local, ready, *states),
        [tile, tile, *[whole(m) for m in states]],
        [side, side],
        [whole(side)] * 2,
        12,
        [pltpu.VMEM((4, *states[0].shape), BF16)],
    )


def turn(table, shards):
    tokens, width = shards[0].shape
    rows = 4 * width // 32

    def body(s, *refs):
        out = refs[-1]
        for k in range(4):

            @pl.when((pl.program_id(0) ^ s[TEN]) == k)
            def _(k=k):
                out[...] = refs[k][...].T.reshape(out.shape)

    out = shape((16, 2, rows, tokens))
    spec = pl.BlockSpec((8, 1, rows, tokens), lambda i, s: (i % 2, (i // 2) ^ s[Z], 0, 0))
    turned = call("turn", body, table, (4,), shards, [whole(x) for x in shards], out, spec, 12)
    return turned.reshape(4, 4, 2 * rows, tokens)


def weight_part(table, turned, lefts, rights, places, split):
    tokens, cols = lefts[0].shape
    rows = turned[0].shape[2]

    def body(s, own_x, own_y, pair_x, pair_y, left_a, left_b, right_a, right_b, *outs):
        r = pl.program_id(0)
        for side, (a, b, ga, gb) in enumerate(
            ((own_x, pair_x, left_a, left_b), (own_y, pair_y, right_a, right_b))
        ):
            acc = dot(a[...].reshape(4 * rows, tokens), ga[...])
            acc += dot(b[...].reshape(4 * rows, tokens), gb[...])
            acc = acc.astype(BF16)
            if split:
                outs[2 * side][...] = acc[: 2 * rows]
                outs[2 * side + 1][...] = acc[2 * rows :]
                continue
            for k in range(len(places)):

                @pl.when(r == k)
                def _(k=k, acc=acc, side=side):
                    outs[side * len(places) + k][...] = acc

    step = places[1] - places[0] if len(places) > 1 else 0
    by_x = pl.BlockSpec((1, 4, rows, tokens), lambda r, s: ((s[X] + places[0] + step * r) % 4, 0, 0, 0))
    by_y = pl.BlockSpec((4, 1, rows, tokens), lambda r, s: (0, (s[Y] + places[0] + step * r) % 4, 0, 0))
    outs = [shape((2 * rows if split else 4 * rows, cols))] * (4 if split else 2 * len(places))
    operands = (turned[0], turned[0], turned[1], turned[1], *lefts, *rights)
    return call(
        "weight_part",
        body,
        table,
        (len(places),),
        operands,
        [by_x, by_y, by_x, by_y, *[whole(x) for x in (*lefts, *rights)]],
        outs,
        [whole(o) for o in outs],
        40,
    )


def add_halves(table, near_up, near_down, up, down):
    n, cols = up.shape

    def body(s, a, b, u, d, out_a, out_b):
        out_a[...] = (a[...].astype(F32) + u[...].astype(F32)).astype(BF16)
        out_b[...] = (b[...].astype(F32) + d[...].astype(F32)).astype(BF16)

    first = pl.BlockSpec((n, cols), lambda i, s: (0, 0))
    second = pl.BlockSpec((n, cols), lambda i, s: (1, 0))
    return call(
        "add_halves",
        body,
        table,
        (1,),
        (near_up, near_down, up, down),
        [first, second, first, first],
        [shape(near_up.shape), shape(near_down.shape)],
        [first, second],
        12,
        alias={1: 0, 2: 1},
    )


def cut_blocks(table, axis, own, first, second):
    rows, cols = own.shape[0] // 4, own.shape[1]

    def body(s, a, b, c, far_up, far_down, one, three, here):
        def block(r):
            at = pl.ds(pl.multiple_of((s[axis] + r) % 4 * rows, rows), rows)
            return (a[at, :].astype(F32) + b[at, :].astype(F32) + c[at, :].astype(F32)).astype(BF16)

        far = block(2)
        far_up[...] = far[: rows // 2]
        far_down[...] = far[rows // 2 :]
        one[...] = block(1)
        three[...] = block(3)
        here[...] = block(0)

    outs = [shape((rows // 2, cols))] * 2 + [shape((rows, cols))] * 3
    operands = (own, first, second)
    return call(
        "cut_blocks",
        body,
        table,
        (1,),
        operands,
        [whole(x) for x in operands],
        outs,
        [whole(o) for o in outs],
        20,
    )


def final_sums(table, sides):
    rows, cols = sides[0][0].shape

    def body(s, *refs):
        here, there = refs[-2:]
        for k in range(2):
            a, b, c = refs[3 * k : 3 * k + 3]
            total = (a[...].astype(F32) + b[...].astype(F32) + c[...].astype(F32)).astype(BF16)
            here[k] = total[: rows // 2]
            there[k] = total[rows // 2 :]

    operands = [x for side in sides for x in side]
    outs = [shape((2, rows // 2, cols))] * 2
    return call(
        "final_sums",
        body,
        table,
        (1,),
        operands,
        [whole(x) for x in operands],
        outs,
        [whole(o) for o in outs],
        8,
    )


def finish(table, here, there):
    _, rows, cols = here.shape
    side = cols // 3

    def body(s, here_ref, there_ref, out):
        for ref, half in ((here_ref, s[Z]), (there_ref, 1 - s[Z])):
            for k in range(2):
                for j in range(3):
                    at = pl.ds(pl.multiple_of(half * 2 * side + k * side, side), side)
                    out[j, :, at] = ref[k, :, j * side : (j + 1) * side].astype(F32)

    out = shape((3, rows, 4 * side), F32)
    operands = (here, there)
    return call("finish", body, table, (1,), operands, [whole(here)] * 2, out, whole(out), 8)


def device_part(activations, qkv_weight, log_decay, lengths, out_grad):
    tied = lax.optimization_barrier
    tokens = activations.shape[0]
    heads = log_decay.shape[1]
    per = heads // 2
    index = [lax.axis_index(a) for a in ("c0", "c1", "c2", "zl", "co")]
    here_z = index[0]
    fixed = [*index, index[3] * 2 + index[4]]
    table = jnp.stack([*fixed, lengths[0]]).astype(jnp.int32)
    weight = pltpu.with_memory_space_constraint(jnp.transpose(qkv_weight, (1, 0, 2)), pltpu.HBM)

    near = send(activations, "zl", 1)
    side = across(activations)
    core = send(activations, "co", 1)

    live = (jnp.arange(tokens, dtype=jnp.int32) < lengths[0]).astype(F32)
    cumul = jnp.cumsum(log_decay.T * live[None, :], axis=1)
    size = jnp.broadcast_to(lengths.astype(F32)[:, None], (per, tokens))
    note = jnp.concatenate([lax.dynamic_slice_in_dim(cumul, (1 - here_z) * per, per), size])
    note = send(note, "c0", 1)
    width = per * HEAD
    og_own = lax.dynamic_slice_in_dim(out_grad, here_z * width, width, axis=1)
    og_other = lax.dynamic_slice_in_dim(out_grad, (1 - here_z) * width, width, axis=1)

    acc_own = project(table, [activations, core], (0, 1), weight, None, False)
    near, side, acc_own, note, og_other = tied((near, side, acc_own, note, og_other))
    cumul = jnp.concatenate([lax.dynamic_slice_in_dim(cumul, here_z * per, per), note[:per]])
    table_pair = jnp.stack([*fixed, note[per, 0].astype(jnp.int32)]).astype(jnp.int32)
    half = tokens // 2
    far = [send(side[:half], "zl", 1), across(near[half:])]
    near_core = send(near, "co", 1)
    side_core = send(side, "co", 1)
    acc_pair = project(table, [side], (2,), weight, None, False)
    near_core, side_core, acc_pair = tied((near_core, side_core, acc_pair))
    qkv_own = project(table, [near, near_core], (2, 3), weight, acc_own, True)
    *far, qkv_own = tied((*far, qkv_own))
    far = jnp.concatenate(far)
    far_core = send(far, "co", 1)
    og_pair = send(tied((og_other, far))[0], "c0", 1)
    acc_pair = project(table, [side_core, far], (3, 0), weight, acc_pair, False)
    far_core, acc_pair = tied((far_core, acc_pair))
    qkv_pair = project(table_pair, [far_core], (1,), weight, acc_pair, True)

    local_own = local_grads(table, qkv_own, og_own, cumul, 0, 0, per, None)
    og_pair, local_own, qkv_pair = tied((og_pair, local_own, qkv_pair))
    to_y = shard_states(table, (qkv_own, qkv_pair), (og_own, og_pair), cumul)
    at_y = [send(to_y[r], "c2", r) for r in (2, 1, 3)]
    local = local_grads(table_pair, qkv_pair, og_pair, cumul, 1, 0, per // 2, None)
    at_y, local = tied((at_y, local))
    before, after, prior, later, ring = ring_y(table, [to_y[0], at_y[1], at_y[0], at_y[2]])
    at_x = [send(ring, "c1", r) for r in (2, 1, 3)]
    local, _ = tied((local, ring))
    local = local_grads(table_pair, qkv_pair, og_pair, cumul, 1, per // 2, per // 2, local)
    at_x, local = tied((at_x, local))
    back = arrivals(table, [ring, at_x[1], at_x[0], at_x[2]], before, after, prior, later)
    states = [send(back[r], "c2", r) for r in (2, 1, 3)]
    first, second, _ = tied(([activations, core, near, near_core], [far, far_core, side, side_core], back[0]))
    turned = [turn(table, first), turn(table, second)]
    states, turned = tied((states, turned))
    states = [back[0], states[1], states[0], states[2]]

    left_own, right_own = whole_grads(table, 0, *local_own, states)
    left_pair, right_pair = whole_grads(table, 1, *local, states)
    lefts, rights = (left_own, left_pair), (right_own, right_pair)
    far_left, far_right = (
        lambda outs: (outs[:2], outs[2:])
    )(weight_part(table, turned, lefts, rights, (2,), True))
    l_half = [send(x, "c1", by) for x, by in zip(far_left, (1, -1))]
    r_half = [send(x, "c2", by) for x, by in zip(far_right, (1, -1))]
    turned, _ = tied((turned, far_left))
    pieces = weight_part(table, turned, lefts, rights, (1, 3), False)
    l_half, pieces = tied((l_half, pieces))
    l_near = add_halves(table, *pieces[:2], *l_half)
    l_got = [send(x, "c1", by) for x, by in zip(l_near, (1, -1))]
    r_half, _ = tied((r_half, l_near))
    r_near = add_halves(table, *pieces[2:], *r_half)
    r_got = [send(x, "c2", by) for x, by in zip(r_near, (1, -1))]
    turned, _ = tied((turned, r_near))
    own = weight_part(table, turned, lefts, rights, (0,), False)
    l_got, own = tied((l_got, own))
    l_cut = cut_blocks(table, Y, own[0], *l_got)
    r_got, _ = tied((r_got, l_cut))
    r_cut = cut_blocks(table, X, own[1], *r_got)
    l_half = [send(x, "c2", by) for x, by in zip(l_cut[:2], (1, -1))]
    r_half = [send(x, "c1", by) for x, by in zip(r_cut[:2], (1, -1))]
    l_near = add_halves(table, *l_cut[2:4], *l_half)
    l_got = [send(x, "c2", by) for x, by in zip(l_near, (1, -1))]
    r_half, _ = tied((r_half, l_near))
    r_near = add_halves(table, *r_cut[2:4], *r_half)
    r_got = [send(x, "c1", by) for x, by in zip(r_near, (1, -1))]
    here, there = final_sums(table, ((l_cut[4], *l_got), (r_cut[4], *r_got)))
    there = send(there, "c0", 1)
    return jnp.transpose(finish(table, here, there), (1, 0, 2))


def solution(mesh):
    finer = Mesh(mesh.devices.reshape(2, 4, 4, 2, 2), ("c0", "c1", "c2", "zl", "co"))
    context, tensor = ("c0", "c1", "c2"), ("zl", "co")
    placed = (
        P(context, tensor),
        P(None, None, tensor),
        P(context, tensor),
        P(context),
        P(context, tensor),
    )
    return jax.shard_map(
        device_part,
        mesh=finer,
        in_specs=placed,
        out_specs=P(context, None, tensor),
        check_vma=False,
    )
```

```python
import jax
import jax.numpy as jnp
from jax import lax
from jax.experimental import pallas as pl
from jax.experimental.pallas import tpu as pltpu
from jax.sharding import Mesh
from jax.sharding import PartitionSpec as P

F32 = jnp.float32
BF16 = jnp.bfloat16
HEAD = 128
Z, X, Y, ZL, CO, TEN, LEN = range(7)
AB_T = (((1,), (1,)), ((), ()))
A_TB = (((0,), (0,)), ((), ()))


def dot(a, b):
    return jnp.dot(a, b, preferred_element_type=F32)


def send(x, axis, by):
    return lax.ppermute(x, axis, [(i, i ^ by) for i in range(lax.axis_size(axis))])


def across(x):
    return lax.ppermute(x, ("c0", "zl"), [(0, 3), (1, 2), (2, 1), (3, 0)])


def whole(x):
    return pl.BlockSpec(x.shape, lambda *_, n=len(x.shape): (0,) * n)


def call(name, body, table, grid, operands, in_specs, outs, out_specs, mib, scratch=(), alias=None):
    return pl.pallas_call(
        body,
        grid_spec=pltpu.PrefetchScalarGridSpec(
            num_scalar_prefetch=1,
            grid=grid,
            in_specs=in_specs,
            out_specs=out_specs,
            scratch_shapes=scratch,
        ),
        out_shape=outs,
        input_output_aliases=alias or {},
        compiler_params=pltpu.CompilerParams(
            dimension_semantics=("arbitrary",) * len(grid), vmem_limit_bytes=mib << 20
        ),
        cost_estimate=pl.CostEstimate(flops=1, bytes_accessed=1, transcendentals=0),
        name=name,
    )(table, *operands)


def shape(dims, kind=BF16):
    return jax.ShapeDtypeStruct(dims, kind)


def project(table, shards, flips, weight, partial, last):
    n = len(shards)
    tokens, width = shards[0].shape
    cols = weight.shape[2] // 2

    def body(s, *refs):
        out = refs[-1]
        acc = dot(refs[0][...], refs[n][0])
        for i in range(1, n):
            acc += dot(refs[i][...], refs[n + i][0])
        if partial is not None:
            acc += refs[2 * n][0]
        if last:
            row = lax.broadcasted_iota(jnp.int32, acc.shape, 0)
            acc = jnp.where(row < s[LEN], acc, 0.0)
        out[0] = acc.astype(out.dtype)

    block = cols // 2
    tile = pl.BlockSpec((1, tokens, block), lambda g, j, s: (g, 0, j))
    in_specs = [whole(x) for x in shards]
    for flip in flips:
        in_specs.append(
            pl.BlockSpec(
                (1, width, block), lambda g, j, s, flip=flip: (g, s[TEN] ^ flip, 2 * s[Z] + j)
            )
        )
    operands = [*shards, *([weight] * n)]
    if partial is not None:
        in_specs.append(tile)
        operands.append(partial)
    out = shape((3, tokens, cols), BF16 if last else F32)
    return call("project", body, table, (3, 2), operands, in_specs, out, tile, 20)


def shard_states(table, qkv, out_grad, cumul, which, so_far):
    tokens = qkv.shape[1]
    heads = qkv.shape[2] // HEAD
    scale = HEAD**-0.5

    def body(s, qkv_ref, og_ref, cum_ref, *refs):
        outs = refs[-4:]
        r = pl.program_id(0)
        row = cum_ref[pl.ds(which * heads + (s[Y] ^ r), 1), :]
        total = row[:, tokens - 1 : tokens]
        keys_t = qkv_ref[1].T.astype(F32)
        query_t = qkv_ref[0].T.astype(F32)
        keys_t = (keys_t * jnp.exp(total - row)).astype(BF16)
        query_t = (query_t * (scale * jnp.exp(row))).astype(BF16)
        states = (dot(keys_t, qkv_ref[2]), dot(query_t, og_ref[...]))
        at = lax.broadcasted_iota(jnp.int32, (16, HEAD), 0)
        tail = jnp.broadcast_to(total, (16, HEAD)).astype(BF16)
        for k, out in enumerate(outs):

            @pl.when(r == k)
            def _(k=k, out=out):
                here = s[Z] ^ which
                if so_far is not None:
                    out[...] = refs[k][...]
                for kind in range(2):
                    start = pl.multiple_of((2 * kind + here) * HEAD, HEAD)
                    out[pl.ds(start, HEAD), :] = states[kind].astype(BF16)
                if so_far is None:
                    out[4 * HEAD :, :] = tail
                else:
                    out[4 * HEAD :, :] = jnp.where(at == here, tail, refs[k][4 * HEAD :, :])

    message = shape((4 * HEAD + 16, HEAD))
    operands = [qkv, out_grad, cumul, *(so_far or ())]
    in_specs = [
        pl.BlockSpec((3, tokens, HEAD), lambda r, s: (0, 0, s[Y] ^ r)),
        pl.BlockSpec((tokens, HEAD), lambda r, s: (0, s[Y] ^ r)),
        whole(cumul),
        *[whole(m) for m in so_far or ()],
    ]
    return call(
        "shard_states",
        body,
        table,
        (4,),
        operands,
        in_specs,
        [message] * 4,
        [whole(message)] * 4,
        12,
    )


def in_order(refs, place, held):
    for r, ref in enumerate(refs):
        held[place ^ r] = ref[...]


def spread(pair):
    wide = [jnp.broadcast_to(pair[i : i + 1, :], (HEAD, HEAD)) for i in range(2)]
    return jnp.concatenate(wide, axis=0)


def ring_y(table, messages):
    half = 2 * HEAD

    def body(s, a, b, c, d, before, after, prior, later, out, held):
        in_order((a, b, c, d), s[Y], held)
        totals = [held[t, 2 * half : 2 * half + 16, :].astype(F32)[:2] for t in range(4)]
        run = jnp.zeros((half, HEAD), F32)
        reach = jnp.zeros((2, HEAD), F32)
        for t in range(4):
            before[t] = run
            prior[t] = jnp.exp(reach)
            run = spread(jnp.exp(totals[t])) * run + held[t, :half, :].astype(F32)
            reach = reach + totals[t]
        out[:half, :] = run.astype(BF16)
        total = reach
        run = jnp.zeros((half, HEAD), F32)
        reach = jnp.zeros((2, HEAD), F32)
        for t in range(3, -1, -1):
            after[t] = run
            later[t] = jnp.exp(reach)
            run = spread(jnp.exp(totals[t])) * run + held[t, half : 2 * half, :].astype(F32)
            reach = reach + totals[t]
        out[half : 2 * half, :] = run.astype(BF16)
        high = total.astype(BF16).astype(F32)
        low = total - high
        at = lax.broadcasted_iota(jnp.int32, (16, HEAD), 0)
        tail = jnp.where(at == 0, high[0:1], high[1:2])
        tail = jnp.where(at == 2, low[0:1], tail)
        tail = jnp.where(at == 3, low[1:2], tail)
        out[2 * half :, :] = tail.astype(BF16)

    outs = [
        shape((4, half, HEAD), F32),
        shape((4, half, HEAD), F32),
        shape((4, 2, HEAD), F32),
        shape((4, 2, HEAD), F32),
        shape(messages[0].shape),
    ]
    return call(
        "ring_y",
        body,
        table,
        (1,),
        messages,
        [whole(m) for m in messages],
        outs,
        [whole(o) for o in outs],
        8,
        [pltpu.VMEM((4, *messages[0].shape), BF16)],
    )


def arrivals(table, messages, before, after, prior, later):
    half = 2 * HEAD

    def body(s, a, b, c, d, before_ref, after_ref, prior_ref, later_ref, *rest):
        outs, held, mine, edges = rest[:4], *rest[4:]
        in_order((a, b, c, d), s[X], held)
        tails = [held[t, 2 * half : 2 * half + 16, :].astype(F32) for t in range(4)]
        totals = [tail[0:2] + tail[2:4] for tail in tails]
        ends = []
        for kind, steps in ((0, range(4)), (1, range(3, -1, -1))):
            run = jnp.zeros((half, HEAD), F32)
            reach = jnp.zeros((2, HEAD), F32)
            for t in steps:

                @pl.when(s[X] == t)
                def _(run=run, reach=reach, kind=kind):
                    mine[kind] = run
                    edges[kind] = jnp.exp(reach)

                rows = held[t, kind * half : (kind + 1) * half, :].astype(F32)
                run = spread(jnp.exp(totals[t])) * run + rows
                reach = reach + totals[t]
            ends.append(run.astype(BF16).astype(F32))
        nothing = jnp.zeros((HEAD, HEAD), F32)
        across_up = jnp.concatenate([nothing, ends[0][:HEAD]], axis=0)
        across_down = jnp.concatenate([ends[1][HEAD:], nothing], axis=0)
        start = mine[0] + spread(edges[0]) * across_up
        finish = mine[1] + spread(edges[1]) * across_down
        for r, out in enumerate(outs):
            t = s[Y] ^ r
            out[:half, :] = (before_ref[t] + spread(prior_ref[t]) * start).astype(BF16)
            out[half:, :] = (after_ref[t] + spread(later_ref[t]) * finish).astype(BF16)

    operands = (*messages, before, after, prior, later)
    message = shape((2 * half, HEAD))
    return call(
        "arrivals",
        body,
        table,
        (1,),
        operands,
        [whole(m) for m in operands],
        [message] * 4,
        [whole(message)] * 4,
        8,
        [
            pltpu.VMEM((4, *messages[0].shape), BF16),
            pltpu.VMEM((2, half, HEAD), F32),
            pltpu.VMEM((2, 2, HEAD), F32),
        ],
    )


def column_of(row):
    return jnp.broadcast_to(row, (HEAD, row.shape[1])).T


def local_grads(table, qkv, out_grad, cumul, which, first, count, so_far):
    tokens = qkv.shape[1]
    heads = qkv.shape[2] // HEAD
    scale = HEAD**-0.5
    size = tokens // 2

    def body(s, qkv_ref, og_ref, cum_ref, *refs):
        out, ready = refs[-2:]
        row = cum_ref[pl.ds(pl.program_id(0) + which * heads + first, 1), :]
        column = column_of(row)
        wide = jnp.concatenate([column] * (size // HEAD), axis=1)
        s_at = lax.broadcasted_iota(jnp.int32, (size, size), 0)
        t_at = lax.broadcasted_iota(jnp.int32, (size, size), 1)
        parts = [slice(0, size), slice(size, tokens)]

        def pair(t, s):
            gap = row[:, parts[t]] - wide[parts[s], :]
            if t == s:
                gap = jnp.where(s_at <= t_at, gap, -jnp.inf)
            decay = jnp.exp(gap)
            q, k, v = qkv_ref[0, parts[t], :], qkv_ref[1, parts[s], :], qkv_ref[2, parts[s], :]
            g = og_ref[parts[t], :]
            scores = lax.dot_general(k, q, AB_T, preferred_element_type=F32)
            grads = lax.dot_general(v, g, AB_T, preferred_element_type=F32)
            prob = (scores * scale * decay).astype(BF16)
            score = (grads * decay).astype(BF16)
            dq = lax.dot_general(score, k, A_TB, preferred_element_type=F32)
            return dq, dot(score, q), dot(prob, g)

        a, b, c = pair(0, 0), pair(1, 0), pair(1, 1)
        live = lax.broadcasted_iota(jnp.int32, (tokens, HEAD), 0) < s[LEN]
        grads = (
            jnp.concatenate([a[0], b[0] + c[0]], axis=0) * scale,
            jnp.concatenate([a[1] + b[1], c[1]], axis=0) * scale,
            jnp.concatenate([a[2] + b[2], c[2]], axis=0),
        )
        until = jnp.exp(row[:, tokens - 1 : tokens] - column)
        rows = (
            og_ref[...].astype(F32) * (scale * jnp.exp(column)),
            qkv_ref[2].astype(F32) * until,
            qkv_ref[1].astype(F32) * until,
        )
        for j in range(3):
            out[j] = jnp.where(live, grads[j], 0.0)
            ready[j] = jnp.where(live, rows[j], 0.0).astype(BF16)

    tile = pl.BlockSpec((3, tokens, HEAD), lambda h, s: (0, 0, h + first))
    in_specs = [tile, pl.BlockSpec((tokens, HEAD), lambda h, s: (0, h + first)), whole(cumul)]
    operands = [qkv, out_grad, cumul]
    if so_far is not None:
        in_specs += [pl.BlockSpec(memory_space=pl.ANY)] * 2
        operands += so_far
    return call(
        "local_grads",
        body,
        table,
        (count,),
        operands,
        in_specs,
        [shape(qkv.shape, F32), shape(qkv.shape)],
        [tile, tile],
        12,
        alias=None if so_far is None else {4: 0, 5: 1},
    )


def whole_grads(table, which, local, ready, states):
    tokens = local.shape[1]
    heads = local.shape[2] // HEAD

    def body(s, local_ref, ready_ref, a, b, c, d, left, right, held):
        h = pl.program_id(0)

        @pl.when(h == 0)
        def _():
            in_order((a, b, c, d), s[Y], held)

        base = pl.multiple_of((s[Z] ^ which) * HEAD, HEAD)
        coming = held[h, pl.ds(base, HEAD), :]
        later = held[h, pl.ds(2 * HEAD + base, HEAD), :]
        cross = (
            lax.dot_general(ready_ref[0], coming, AB_T, preferred_element_type=F32),
            lax.dot_general(ready_ref[1], later, AB_T, preferred_element_type=F32),
            dot(ready_ref[2], later),
        )
        grads = [(local_ref[j] + cross[j]).astype(BF16) for j in range(3)]
        for k in range(heads):

            @pl.when(h == k)
            def _(k=k):
                for j in range(3):
                    start = (2 * j + k % 2) * HEAD
                    (left, right)[k // 2][:, start : start + HEAD] = grads[j]

    tile = pl.BlockSpec((3, tokens, HEAD), lambda h, s: (0, 0, h))
    side = shape((tokens, 3 * heads * HEAD // 2))
    return call(
        "whole_grads",
        body,
        table,
        (heads,),
        (local, ready, *states),
        [tile, tile, *[whole(m) for m in states]],
        [side, side],
        [whole(side)] * 2,
        12,
        [pltpu.VMEM((4, *states[0].shape), BF16)],
    )


def turn(table, shards):
    tokens, width = shards[0].shape
    rows = 4 * width // 32

    def body(s, *refs):
        out = refs[-1]
        for k in range(4):

            @pl.when((pl.program_id(0) ^ s[TEN]) == k)
            def _(k=k):
                out[...] = refs[k][...].T.reshape(out.shape)

    out = shape((16, 2, rows, tokens))
    spec = pl.BlockSpec((8, 1, rows, tokens), lambda i, s: (i % 2, (i // 2) ^ s[Z], 0, 0))
    turned = call("turn", body, table, (4,), shards, [whole(x) for x in shards], out, spec, 12)
    return turned.reshape(4, 4, 2 * rows, tokens)


def weight_part(table, turned, lefts, rights, places, split):
    tokens, cols = lefts[0].shape
    rows = turned[0].shape[2]

    def body(s, own_x, own_y, pair_x, pair_y, left_a, left_b, right_a, right_b, *outs):
        r = pl.program_id(0)
        for side, (a, b, ga, gb) in enumerate(
            ((own_x, pair_x, left_a, left_b), (own_y, pair_y, right_a, right_b))
        ):
            acc = dot(a[...].reshape(4 * rows, tokens), ga[...])
            acc += dot(b[...].reshape(4 * rows, tokens), gb[...])
            acc = acc.astype(BF16)
            if split:
                outs[2 * side][...] = acc[: 2 * rows]
                outs[2 * side + 1][...] = acc[2 * rows :]
                continue
            for k in range(len(places)):

                @pl.when(r == k)
                def _(k=k, acc=acc, side=side):
                    outs[side * len(places) + k][...] = acc

    step = places[1] - places[0] if len(places) > 1 else 0
    by_x = pl.BlockSpec((1, 4, rows, tokens), lambda r, s: (s[X] ^ (places[0] + step * r), 0, 0, 0))
    by_y = pl.BlockSpec((4, 1, rows, tokens), lambda r, s: (0, s[Y] ^ (places[0] + step * r), 0, 0))
    outs = [shape((2 * rows if split else 4 * rows, cols))] * (4 if split else 2 * len(places))
    operands = (turned[0], turned[0], turned[1], turned[1], *lefts, *rights)
    return call(
        "weight_part",
        body,
        table,
        (len(places),),
        operands,
        [by_x, by_y, by_x, by_y, *[whole(x) for x in (*lefts, *rights)]],
        outs,
        [whole(o) for o in outs],
        40,
    )


def add_halves(table, third, first_place, halves):
    up, down = halves
    near_up, near_down = third, first_place
    n, cols = up.shape

    def body(s, a, b, u, d, out_a, out_b):
        out_a[...] = (a[...].astype(F32) + u[...].astype(F32)).astype(BF16)
        out_b[...] = (b[...].astype(F32) + d[...].astype(F32)).astype(BF16)

    first = pl.BlockSpec((n, cols), lambda i, s: (0, 0))
    second = pl.BlockSpec((n, cols), lambda i, s: (1, 0))
    return call(
        "add_halves",
        body,
        table,
        (1,),
        (near_up, near_down, up, down),
        [first, second, first, first],
        [shape(near_up.shape), shape(near_down.shape)],
        [first, second],
        12,
        alias={1: 0, 2: 1},
    )


def cut_blocks(table, axis, own, first, second):
    rows, cols = own.shape[0] // 4, own.shape[1]

    def body(s, a, b, c, far_up, far_down, one, three, here):
        def block(r):
            at = pl.ds(pl.multiple_of((s[axis] ^ r) * rows, rows), rows)
            return (a[at, :].astype(F32) + b[at, :].astype(F32) + c[at, :].astype(F32)).astype(BF16)

        far = block(2)
        far_up[...] = far[: rows // 2]
        far_down[...] = far[rows // 2 :]
        one[...] = block(1)
        three[...] = block(3)
        here[...] = block(0)

    outs = [shape((rows // 2, cols))] * 2 + [shape((rows, cols))] * 3
    operands = (own, first, second)
    return call(
        "cut_blocks",
        body,
        table,
        (1,),
        operands,
        [whole(x) for x in operands],
        outs,
        [whole(o) for o in outs],
        20,
    )


def final_sums(table, sides):
    rows, cols = sides[0][0].shape

    def body(s, *refs):
        here, there = refs[-2:]
        for k in range(2):
            a, b, c = refs[3 * k : 3 * k + 3]
            total = (a[...].astype(F32) + b[...].astype(F32) + c[...].astype(F32)).astype(BF16)
            here[k] = total[: rows // 2]
            there[k] = total[rows // 2 :]

    operands = [x for side in sides for x in side]
    outs = [shape((2, rows // 2, cols))] * 2
    return call(
        "final_sums",
        body,
        table,
        (1,),
        operands,
        [whole(x) for x in operands],
        outs,
        [whole(o) for o in outs],
        8,
    )


def finish(table, here, there):
    _, rows, cols = here.shape
    side = cols // 3

    def body(s, here_ref, there_ref, out):
        for ref, half in ((here_ref, s[Z]), (there_ref, 1 - s[Z])):
            for k in range(2):
                for j in range(3):
                    at = pl.ds(pl.multiple_of(half * 2 * side + k * side, side), side)
                    out[j, :, at] = ref[k, :, j * side : (j + 1) * side].astype(F32)

    out = shape((3, rows, 4 * side), F32)
    operands = (here, there)
    return call("finish", body, table, (1,), operands, [whole(here)] * 2, out, whole(out), 8)


def swaps(pieces, left, right):
    a, c = send(pieces[0], left, 1), send(pieces[2], right, 1)
    b, d = send(pieces[1], left, 3), send(pieces[3], right, 3)
    return [a, b], [c, d]


def device_part(activations, qkv_weight, log_decay, lengths, out_grad):
    tied = lax.optimization_barrier
    tokens = activations.shape[0]
    heads = log_decay.shape[1]
    per = heads // 2
    index = [lax.axis_index(a) for a in ("c0", "c1", "c2", "zl", "co")]
    here_z = index[0]
    fixed = [*index, index[3] * 2 + index[4]]
    table = jnp.stack([*fixed, lengths[0]]).astype(jnp.int32)
    weight = pltpu.with_memory_space_constraint(jnp.transpose(qkv_weight, (1, 0, 2)), pltpu.HBM)

    near = send(activations, "zl", 1)
    side = across(activations)
    core = send(activations, "co", 1)

    live = (jnp.arange(tokens, dtype=jnp.int32) < lengths[0]).astype(F32)
    cumul = jnp.cumsum(log_decay.T * live[None, :], axis=1)
    size = jnp.broadcast_to(lengths.astype(F32)[:, None], (per, tokens))
    note = jnp.concatenate([lax.dynamic_slice_in_dim(cumul, (1 - here_z) * per, per), size])
    note = send(note, "c0", 1)
    width = per * HEAD
    og_own = lax.dynamic_slice_in_dim(out_grad, here_z * width, width, axis=1)
    og_other = lax.dynamic_slice_in_dim(out_grad, (1 - here_z) * width, width, axis=1)

    acc_own = project(table, [activations, core], (0, 1), weight, None, False)
    near, side, acc_own = tied((near, side, acc_own))
    half = tokens // 2
    near_core = send(near, "co", 1)
    side_core = send(side, "co", 1)
    far = [send(side[:half], "zl", 1), across(near[half:])]
    qkv_own = project(table, [near, near_core], (2, 3), weight, acc_own, True)
    side_core, note, og_other, qkv_own = tied((side_core, note, og_other, qkv_own))
    acc_pair = project(table, [side, side_core], (2, 3), weight, None, False)
    cumul = jnp.concatenate([lax.dynamic_slice_in_dim(cumul, here_z * per, per), note[:per]])
    table_pair = jnp.stack([*fixed, note[per, 0].astype(jnp.int32)]).astype(jnp.int32)
    *far, acc_pair = tied((*far, acc_pair))
    far = jnp.concatenate(far)
    far_core = send(far, "co", 1)
    og_pair = send(tied((og_other, far))[0], "c0", 1)
    first, _ = tied(([activations, core, near, near_core], far))
    turned = [turn(table, first)]
    to_y = shard_states(table, qkv_own, og_own, cumul, 0, None)
    far_core, acc_pair, to_y, turned = tied((far_core, acc_pair, to_y, turned))
    qkv_pair = project(table_pair, [far, far_core], (0, 1), weight, acc_pair, True)

    to_y = shard_states(table, qkv_pair, og_pair, cumul, 1, to_y)
    at_y = [send(to_y[r], "c2", r) for r in (1, 3, 2)]
    qkv_own, _ = tied((qkv_own, to_y[0]))
    local_own = local_grads(table, qkv_own, og_own, cumul, 0, 0, per, None)
    at_y, local_own = tied((at_y, local_own))
    before, after, prior, later, ring = ring_y(table, [to_y[0], at_y[0], at_y[2], at_y[1]])
    at_x = [send(ring, "c1", r) for r in (1, 3, 2)]
    qkv_pair, _ = tied((qkv_pair, ring))
    local = local_grads(table_pair, qkv_pair, og_pair, cumul, 1, 0, per // 2, None)
    at_x, local = tied((at_x, local))
    back = arrivals(table, [ring, at_x[0], at_x[2], at_x[1]], before, after, prior, later)
    states = [send(back[r], "c2", r) for r in (1, 3, 2)]
    local, _ = tied((local, back[0]))
    local = local_grads(table_pair, qkv_pair, og_pair, cumul, 1, per // 2, per // 2, local)
    second, _ = tied(([far, far_core, side, side_core], back[0]))
    turned.append(turn(table, second))
    states, turned, local = tied((states, turned, local))
    states = [back[0], states[0], states[2], states[1]]

    left_own, right_own = whole_grads(table, 0, *local_own, states)
    left_pair, right_pair = whole_grads(table, 1, *local, states)
    lefts, rights = (left_own, left_pair), (right_own, right_pair)
    far_piece = weight_part(table, turned, lefts, rights, (2,), True)
    l_half, r_half = swaps(far_piece, "c1", "c2")
    turned, _ = tied((turned, far_piece[0]))
    l_one, l_three, r_one, r_three = weight_part(table, turned, lefts, rights, (1, 3), False)
    l_half, l_one = tied((l_half, l_one))
    l_three, l_one = add_halves(table, l_three, l_one, l_half)
    l_got = [send(l_one, "c1", 1), send(l_three, "c1", 3)]
    r_half, _ = tied((r_half, l_one))
    r_three, r_one = add_halves(table, r_three, r_one, r_half)
    r_got = [send(r_one, "c2", 1), send(r_three, "c2", 3)]
    turned, _ = tied((turned, r_one))
    own = weight_part(table, turned, lefts, rights, (0,), False)
    l_got, own = tied((l_got, own))
    l_cut = cut_blocks(table, Y, own[0], *l_got)
    r_got, _ = tied((r_got, l_cut))
    r_cut = cut_blocks(table, X, own[1], *r_got)
    l_half = [send(x, "c2", by) for x, by in zip(l_cut[:2], (1, 3))]
    r_half = [send(x, "c1", by) for x, by in zip(r_cut[:2], (1, 3))]
    l_three, l_one = add_halves(table, l_cut[3], l_cut[2], l_half)
    l_got = [send(l_one, "c2", 1), send(l_three, "c2", 3)]
    r_half, _ = tied((r_half, l_one))
    r_three, r_one = add_halves(table, r_cut[3], r_cut[2], r_half)
    r_got = [send(r_one, "c1", 1), send(r_three, "c1", 3)]
    here, there = final_sums(table, ((l_cut[4], *l_got), (r_cut[4], *r_got)))
    there = send(there, "c0", 1)
    return jnp.transpose(finish(table, here, there), (1, 0, 2))


def solution(mesh):
    finer = Mesh(mesh.devices.reshape(2, 4, 4, 2, 2), ("c0", "c1", "c2", "zl", "co"))
    context, tensor = ("c0", "c1", "c2"), ("zl", "co")
    placed = (
        P(context, tensor),
        P(None, None, tensor),
        P(context, tensor),
        P(context),
        P(context, tensor),
    )
    return jax.shard_map(
        device_part,
        mesh=finer,
        in_specs=placed,
        out_specs=P(context, None, tensor),
        check_vma=False,
    )
```

```python
import jax
import jax.numpy as jnp
from jax import lax
from jax.experimental import pallas as pl
from jax.experimental.pallas import tpu as pltpu
from jax.sharding import Mesh
from jax.sharding import PartitionSpec as P

F32 = jnp.float32
BF16 = jnp.bfloat16
HEAD = 128
Z, X, Y, ZL, CO, TEN, LEN = range(7)
AB_T = (((1,), (1,)), ((), ()))
A_TB = (((0,), (0,)), ((), ()))


def dot(a, b):
    return jnp.dot(a, b, preferred_element_type=F32)


def send(x, axis, by):
    return lax.ppermute(x, axis, [(i, i ^ by) for i in range(lax.axis_size(axis))])


def across(x):
    return lax.ppermute(x, ("c0", "zl"), [(0, 3), (1, 2), (2, 1), (3, 0)])


def whole(x):
    return pl.BlockSpec(x.shape, lambda *_, n=len(x.shape): (0,) * n)


def call(name, body, table, grid, operands, in_specs, outs, out_specs, mib, scratch=(), alias=None):
    return pl.pallas_call(
        body,
        grid_spec=pltpu.PrefetchScalarGridSpec(
            num_scalar_prefetch=1,
            grid=grid,
            in_specs=in_specs,
            out_specs=out_specs,
            scratch_shapes=scratch,
        ),
        out_shape=outs,
        input_output_aliases=alias or {},
        compiler_params=pltpu.CompilerParams(
            dimension_semantics=("arbitrary",) * len(grid), vmem_limit_bytes=mib << 20
        ),
        cost_estimate=pl.CostEstimate(flops=1, bytes_accessed=1, transcendentals=0),
        name=name,
    )(table, *operands)


def shape(dims, kind=BF16):
    return jax.ShapeDtypeStruct(dims, kind)


def joined(refs):
    parts = [ref[...] for ref in refs]
    return parts[0] if len(parts) == 1 else jnp.concatenate(parts, axis=0)


def project(table, shards, flips, weight, partial, last):
    n, counts = len(shards), [len(x) for x in shards]
    flat = [part for x in shards for part in x]
    tokens, width = sum(part.shape[0] for part in shards[0]), flat[0].shape[1]
    cols = weight.shape[2] // 2

    def body(s, *refs):
        out, rest = refs[-1], list(refs)
        acc = None
        for i, count in enumerate(counts):
            rows = joined([rest.pop(0) for _ in range(count)])
            term = dot(rows, refs[len(flat) + i][0])
            acc = term if acc is None else acc + term
        if partial is not None:
            acc += refs[len(flat) + n][0]
        if last:
            row = lax.broadcasted_iota(jnp.int32, acc.shape, 0)
            acc = jnp.where(row < s[LEN], acc, 0.0)
        out[0] = acc.astype(out.dtype)

    tile = pl.BlockSpec((1, tokens, cols), lambda g, s: (g, 0, 0))
    in_specs = [whole(x) for x in flat]
    for flip in flips:
        in_specs.append(
            pl.BlockSpec((1, width, cols), lambda g, s, flip=flip: (g, s[TEN] ^ flip, s[Z]))
        )
    operands = [*flat, *([weight] * n)]
    if partial is not None:
        in_specs.append(tile)
        operands.append(partial)
    out = shape((3, tokens, cols), BF16 if last else F32)
    return call("project", body, table, (3,), operands, in_specs, out, tile, 24)


def shard_states(table, qkv, out_grad, cumul, which, so_far):
    tokens = qkv.shape[1]
    heads = qkv.shape[2] // HEAD
    scale = HEAD**-0.5

    def body(s, qkv_ref, og_ref, cum_ref, *refs):
        outs = refs[-4:]
        r = pl.program_id(0)
        row = cum_ref[pl.ds(which * heads + (s[Y] ^ r), 1), :]
        total = row[:, tokens - 1 : tokens]
        keys_t = qkv_ref[1].T.astype(F32)
        query_t = qkv_ref[0].T.astype(F32)
        keys_t = (keys_t * jnp.exp(total - row)).astype(BF16)
        query_t = (query_t * (scale * jnp.exp(row))).astype(BF16)
        states = (dot(keys_t, qkv_ref[2]), dot(query_t, og_ref[...]))
        at = lax.broadcasted_iota(jnp.int32, (16, HEAD), 0)
        tail = jnp.broadcast_to(total, (16, HEAD)).astype(BF16)
        for k, out in enumerate(outs):

            @pl.when(r == k)
            def _(k=k, out=out):
                here = s[Z] ^ which
                if so_far is not None:
                    out[...] = refs[k][...]
                for kind in range(2):
                    start = pl.multiple_of((2 * kind + here) * HEAD, HEAD)
                    out[pl.ds(start, HEAD), :] = states[kind].astype(BF16)
                if so_far is None:
                    out[4 * HEAD :, :] = tail
                else:
                    out[4 * HEAD :, :] = jnp.where(at == here, tail, refs[k][4 * HEAD :, :])

    message = shape((4 * HEAD + 16, HEAD))
    operands = [qkv, out_grad, cumul, *(so_far or ())]
    in_specs = [
        pl.BlockSpec((3, tokens, HEAD), lambda r, s: (0, 0, s[Y] ^ r)),
        pl.BlockSpec((tokens, HEAD), lambda r, s: (0, s[Y] ^ r)),
        whole(cumul),
        *[whole(m) for m in so_far or ()],
    ]
    return call(
        "shard_states",
        body,
        table,
        (4,),
        operands,
        in_specs,
        [message] * 4,
        [whole(message)] * 4,
        12,
    )


def in_order(refs, place, held):
    for r, ref in enumerate(refs):
        held[place ^ r] = ref[...]


def spread(pair):
    wide = [jnp.broadcast_to(pair[i : i + 1, :], (HEAD, HEAD)) for i in range(2)]
    return jnp.concatenate(wide, axis=0)


def ring_y(table, messages):
    half = 2 * HEAD

    def body(s, a, b, c, d, before, after, prior, later, out, held):
        in_order((a, b, c, d), s[Y], held)
        totals = [held[t, 2 * half : 2 * half + 16, :].astype(F32)[:2] for t in range(4)]
        run = jnp.zeros((half, HEAD), F32)
        reach = jnp.zeros((2, HEAD), F32)
        for t in range(4):
            before[t] = run
            prior[t] = jnp.exp(reach)
            run = spread(jnp.exp(totals[t])) * run + held[t, :half, :].astype(F32)
            reach = reach + totals[t]
        out[:half, :] = run.astype(BF16)
        total = reach
        run = jnp.zeros((half, HEAD), F32)
        reach = jnp.zeros((2, HEAD), F32)
        for t in range(3, -1, -1):
            after[t] = run
            later[t] = jnp.exp(reach)
            run = spread(jnp.exp(totals[t])) * run + held[t, half : 2 * half, :].astype(F32)
            reach = reach + totals[t]
        out[half : 2 * half, :] = run.astype(BF16)
        high = total.astype(BF16).astype(F32)
        low = total - high
        at = lax.broadcasted_iota(jnp.int32, (16, HEAD), 0)
        tail = jnp.where(at == 0, high[0:1], high[1:2])
        tail = jnp.where(at == 2, low[0:1], tail)
        tail = jnp.where(at == 3, low[1:2], tail)
        out[2 * half :, :] = tail.astype(BF16)

    outs = [
        shape((4, half, HEAD), F32),
        shape((4, half, HEAD), F32),
        shape((4, 2, HEAD), F32),
        shape((4, 2, HEAD), F32),
        shape(messages[0].shape),
    ]
    return call(
        "ring_y",
        body,
        table,
        (1,),
        messages,
        [whole(m) for m in messages],
        outs,
        [whole(o) for o in outs],
        8,
        [pltpu.VMEM((4, *messages[0].shape), BF16)],
    )


def arrivals(table, messages, before, after, prior, later):
    half = 2 * HEAD

    def body(s, a, b, c, d, before_ref, after_ref, prior_ref, later_ref, *rest):
        outs, held, mine, edges = rest[:4], *rest[4:]
        in_order((a, b, c, d), s[X], held)
        tails = [held[t, 2 * half : 2 * half + 16, :].astype(F32) for t in range(4)]
        totals = [tail[0:2] + tail[2:4] for tail in tails]
        ends = []
        for kind, steps in ((0, range(4)), (1, range(3, -1, -1))):
            run = jnp.zeros((half, HEAD), F32)
            reach = jnp.zeros((2, HEAD), F32)
            for t in steps:

                @pl.when(s[X] == t)
                def _(run=run, reach=reach, kind=kind):
                    mine[kind] = run
                    edges[kind] = jnp.exp(reach)

                rows = held[t, kind * half : (kind + 1) * half, :].astype(F32)
                run = spread(jnp.exp(totals[t])) * run + rows
                reach = reach + totals[t]
            ends.append(run.astype(BF16).astype(F32))
        nothing = jnp.zeros((HEAD, HEAD), F32)
        across_up = jnp.concatenate([nothing, ends[0][:HEAD]], axis=0)
        across_down = jnp.concatenate([ends[1][HEAD:], nothing], axis=0)
        start = mine[0] + spread(edges[0]) * across_up
        finish = mine[1] + spread(edges[1]) * across_down
        for r, out in enumerate(outs):
            t = s[Y] ^ r
            out[:half, :] = (before_ref[t] + spread(prior_ref[t]) * start).astype(BF16)
            out[half:, :] = (after_ref[t] + spread(later_ref[t]) * finish).astype(BF16)

    operands = (*messages, before, after, prior, later)
    message = shape((2 * half, HEAD))
    return call(
        "arrivals",
        body,
        table,
        (1,),
        operands,
        [whole(m) for m in operands],
        [message] * 4,
        [whole(message)] * 4,
        8,
        [
            pltpu.VMEM((4, *messages[0].shape), BF16),
            pltpu.VMEM((2, half, HEAD), F32),
            pltpu.VMEM((2, 2, HEAD), F32),
        ],
    )


def column_of(row):
    return jnp.broadcast_to(row, (HEAD, row.shape[1])).T


def local_grads(table, qkv, out_grad, cumul, which, first, count, so_far):
    tokens = qkv.shape[1]
    heads = qkv.shape[2] // HEAD
    scale = HEAD**-0.5
    size = tokens // 2

    def body(s, qkv_ref, og_ref, cum_ref, *refs):
        out, ready = refs[-2:]
        row = cum_ref[pl.ds(pl.program_id(0) + which * heads + first, 1), :]
        column = column_of(row)
        wide = jnp.concatenate([column] * (size // HEAD), axis=1)
        s_at = lax.broadcasted_iota(jnp.int32, (size, size), 0)
        t_at = lax.broadcasted_iota(jnp.int32, (size, size), 1)
        parts = [slice(0, size), slice(size, tokens)]

        def pair(t, s):
            if t == s:
                gap = row[:, parts[t]] - wide[parts[s], :]
                decay = jnp.exp(jnp.where(s_at <= t_at, gap, -jnp.inf))
            else:
                middle = row[:, size - 1 : size]
                to_middle = jnp.exp(middle - column[parts[s], :])
                decay = jnp.concatenate([to_middle] * (size // HEAD), axis=1)
                decay *= jnp.exp(row[:, parts[t]] - middle)
            q, k, v = qkv_ref[0, parts[t], :], qkv_ref[1, parts[s], :], qkv_ref[2, parts[s], :]
            g = og_ref[parts[t], :]
            scores = lax.dot_general(k, q, AB_T, preferred_element_type=F32)
            grads = lax.dot_general(v, g, AB_T, preferred_element_type=F32)
            prob = (scores * decay).astype(BF16)
            score = (grads * decay).astype(BF16)
            dq = lax.dot_general(score, k, A_TB, preferred_element_type=F32)
            return dq, dot(score, q), dot(prob, g)

        a, b, c = pair(0, 0), pair(1, 0), pair(1, 1)
        live = lax.broadcasted_iota(jnp.int32, (tokens, HEAD), 0) < s[LEN]
        grads = (
            jnp.concatenate([a[0], b[0] + c[0]], axis=0) * scale,
            jnp.concatenate([a[1] + b[1], c[1]], axis=0) * scale,
            jnp.concatenate([a[2] + b[2], c[2]], axis=0) * scale,
        )
        until = jnp.exp(row[:, tokens - 1 : tokens] - column)
        rows = (
            og_ref[...].astype(F32) * (scale * jnp.exp(column)),
            qkv_ref[2].astype(F32) * until,
            qkv_ref[1].astype(F32) * until,
        )
        for j in range(3):
            out[j] = jnp.where(live, grads[j], 0.0)
            ready[j] = jnp.where(live, rows[j], 0.0).astype(BF16)

    tile = pl.BlockSpec((3, tokens, HEAD), lambda h, s: (0, 0, h + first))
    in_specs = [tile, pl.BlockSpec((tokens, HEAD), lambda h, s: (0, h + first)), whole(cumul)]
    operands = [qkv, out_grad, cumul]
    if so_far is not None:
        in_specs += [pl.BlockSpec(memory_space=pl.ANY)] * 2
        operands += so_far
    return call(
        "local_grads",
        body,
        table,
        (count,),
        operands,
        in_specs,
        [shape(qkv.shape, F32), shape(qkv.shape)],
        [tile, tile],
        12,
        alias=None if so_far is None else {4: 0, 5: 1},
    )


def whole_grads(table, which, local, ready, states):
    tokens = local.shape[1]
    heads = local.shape[2] // HEAD

    def body(s, local_ref, ready_ref, a, b, c, d, left, right, held):
        h = pl.program_id(0)

        @pl.when(h == 0)
        def _():
            in_order((a, b, c, d), s[Y], held)

        base = pl.multiple_of((s[Z] ^ which) * HEAD, HEAD)
        coming = held[h, pl.ds(base, HEAD), :]
        later = held[h, pl.ds(2 * HEAD + base, HEAD), :]
        cross = (
            lax.dot_general(ready_ref[0], coming, AB_T, preferred_element_type=F32),
            lax.dot_general(ready_ref[1], later, AB_T, preferred_element_type=F32),
            dot(ready_ref[2], later),
        )
        grads = [(local_ref[j] + cross[j]).astype(BF16) for j in range(3)]
        for k in range(heads):

            @pl.when(h == k)
            def _(k=k):
                for j in range(3):
                    start = (2 * j + k % 2) * HEAD
                    (left, right)[k // 2][:, start : start + HEAD] = grads[j]

    tile = pl.BlockSpec((3, tokens, HEAD), lambda h, s: (0, 0, h))
    side = shape((tokens, 3 * heads * HEAD // 2))
    return call(
        "whole_grads",
        body,
        table,
        (heads,),
        (local, ready, *states),
        [tile, tile, *[whole(m) for m in states]],
        [side, side],
        [whole(side)] * 2,
        12,
        [pltpu.VMEM((4, *states[0].shape), BF16)],
    )


def turn(table, shards):
    counts = [len(x) for x in shards]
    flat = [part for x in shards for part in x]
    tokens, width = sum(part.shape[0] for part in shards[0]), flat[0].shape[1]
    rows = 4 * width // 32

    def body(s, *refs):
        out, at = refs[-1], 0
        for k, count in enumerate(counts):
            mine, at = refs[at : at + count], at + count

            @pl.when((pl.program_id(0) ^ s[TEN]) == k)
            def _(mine=mine):
                out[...] = joined(mine).T.reshape(out.shape)

    out = shape((16, 2, rows, tokens))
    spec = pl.BlockSpec((8, 1, rows, tokens), lambda i, s: (i % 2, (i // 2) ^ s[Z], 0, 0))
    turned = call("turn", body, table, (4,), flat, [whole(x) for x in flat], out, spec, 12)
    return turned.reshape(4, 4, 2 * rows, tokens)


def weight_part(table, turned, lefts, rights, places, split):
    tokens, cols = lefts[0].shape
    rows = turned[0].shape[2]

    def body(s, own_x, own_y, pair_x, pair_y, left_a, left_b, right_a, right_b, *outs):
        r = pl.program_id(0)
        for side, (a, b, ga, gb) in enumerate(
            ((own_x, pair_x, left_a, left_b), (own_y, pair_y, right_a, right_b))
        ):
            acc = dot(a[...].reshape(4 * rows, tokens), ga[...])
            acc += dot(b[...].reshape(4 * rows, tokens), gb[...])
            acc = acc.astype(BF16)
            if split:
                outs[2 * side][...] = acc[: 2 * rows]
                outs[2 * side + 1][...] = acc[2 * rows :]
                continue
            for k in range(len(places)):

                @pl.when(r == k)
                def _(k=k, acc=acc, side=side):
                    outs[side * len(places) + k][...] = acc

    step = places[1] - places[0] if len(places) > 1 else 0
    by_x = pl.BlockSpec((1, 4, rows, tokens), lambda r, s: (s[X] ^ (places[0] + step * r), 0, 0, 0))
    by_y = pl.BlockSpec((4, 1, rows, tokens), lambda r, s: (0, s[Y] ^ (places[0] + step * r), 0, 0))
    outs = [shape((2 * rows if split else 4 * rows, cols))] * (4 if split else 2 * len(places))
    operands = (turned[0], turned[0], turned[1], turned[1], *lefts, *rights)
    return call(
        "weight_part",
        body,
        table,
        (len(places),),
        operands,
        [by_x, by_y, by_x, by_y, *[whole(x) for x in (*lefts, *rights)]],
        outs,
        [whole(o) for o in outs],
        30,
    )


def add_halves(table, third, first_place, halves):
    up, down = halves
    near_up, near_down = third, first_place
    n, cols = up.shape

    def body(s, a, b, u, d, out_a, out_b):
        out_a[...] = (a[...].astype(F32) + u[...].astype(F32)).astype(BF16)
        out_b[...] = (b[...].astype(F32) + d[...].astype(F32)).astype(BF16)

    first = pl.BlockSpec((n, cols), lambda i, s: (0, 0))
    second = pl.BlockSpec((n, cols), lambda i, s: (1, 0))
    return call(
        "add_halves",
        body,
        table,
        (1,),
        (near_up, near_down, up, down),
        [first, second, first, first],
        [shape(near_up.shape), shape(near_down.shape)],
        [first, second],
        12,
        alias={1: 0, 2: 1},
    )


def cut_blocks(table, axis, own, first, second):
    rows, cols = own.shape[0] // 4, own.shape[1]

    def body(s, a, b, c, *outs):
        for r, out in zip((1, 3, 2, 0), outs):
            at = pl.ds(pl.multiple_of((s[axis] ^ r) * rows, rows), rows)
            total = a[at, :].astype(F32) + b[at, :].astype(F32) + c[at, :].astype(F32)
            out[...] = total.astype(BF16)

    outs = [shape((rows, cols))] * 4
    operands = (own, first, second)
    return call(
        "cut_blocks",
        body,
        table,
        (1,),
        operands,
        [whole(x) for x in operands],
        outs,
        [whole(o) for o in outs],
        20,
    )


def final_sums(table, sides):
    rows, cols = sides[0][0].shape

    def body(s, *refs):
        here, there = refs[-2:]
        for k in range(2):
            total = sum(ref[...].astype(F32) for ref in refs[4 * k : 4 * k + 4]).astype(BF16)
            here[k] = total[: rows // 2]
            there[k] = total[rows // 2 :]

    operands = [x for side in sides for x in side]
    outs = [shape((2, rows // 2, cols))] * 2
    return call(
        "final_sums",
        body,
        table,
        (1,),
        operands,
        [whole(x) for x in operands],
        outs,
        [whole(o) for o in outs],
        12,
    )


def finish(table, here, there):
    _, rows, cols = here.shape
    side = cols // 3

    def body(s, here_ref, there_ref, out):
        for ref, half in ((here_ref, s[Z]), (there_ref, 1 - s[Z])):
            for k in range(2):
                for j in range(3):
                    at = pl.ds(pl.multiple_of(half * 2 * side + k * side, side), side)
                    out[j, :, at] = ref[k, :, j * side : (j + 1) * side].astype(F32)

    out = shape((3, rows, 4 * side), F32)
    operands = (here, there)
    return call("finish", body, table, (1,), operands, [whole(here)] * 2, out, whole(out), 8)


def swaps(pieces, left, right):
    a, c = send(pieces[0], left, 1), send(pieces[2], right, 1)
    b, d = send(pieces[1], left, 3), send(pieces[3], right, 3)
    return [a, b], [c, d]


def device_part(activations, qkv_weight, log_decay, lengths, out_grad):
    tied = lax.optimization_barrier
    tokens = activations.shape[0]
    heads = log_decay.shape[1]
    per = heads // 2
    index = [lax.axis_index(a) for a in ("c0", "c1", "c2", "zl", "co")]
    here_z = index[0]
    fixed = [*index, index[3] * 2 + index[4]]
    table = jnp.stack([*fixed, lengths[0]]).astype(jnp.int32)
    weight = pltpu.with_memory_space_constraint(jnp.transpose(qkv_weight, (1, 0, 2)), pltpu.HBM)

    near = send(activations, "zl", 1)
    side = across(activations)
    core = send(activations, "co", 1)

    live = (jnp.arange(tokens, dtype=jnp.int32) < lengths[0]).astype(F32)
    cumul = jnp.cumsum(log_decay.T * live[None, :], axis=1)
    size = jnp.broadcast_to(lengths.astype(F32)[:, None], (per, tokens))
    note = jnp.concatenate([lax.dynamic_slice_in_dim(cumul, (1 - here_z) * per, per), size])
    note = send(note, "c0", 1)
    width = per * HEAD
    og_own = lax.dynamic_slice_in_dim(out_grad, here_z * width, width, axis=1)
    og_other = lax.dynamic_slice_in_dim(out_grad, (1 - here_z) * width, width, axis=1)

    acc_own = project(table, [[activations], [core]], (0, 1), weight, None, False)
    near, side, acc_own, note, og_other = tied((near, side, acc_own, note, og_other))
    half = tokens // 2
    far = [send(side[:half], "zl", 1), across(near[half:])]
    near_core = send(near, "co", 1)
    side_core = send(side, "co", 1)
    cumul = jnp.concatenate([lax.dynamic_slice_in_dim(cumul, here_z * per, per), note[:per]])
    table_pair = jnp.stack([*fixed, note[per, 0].astype(jnp.int32)]).astype(jnp.int32)
    acc_pair = project(table, [[side]], (2,), weight, None, False)
    near_core, acc_pair = tied((near_core, acc_pair))
    qkv_own = project(table, [[near], [near_core]], (2, 3), weight, acc_own, True)
    far, side_core, qkv_own, table_pair, cumul = tied((far, side_core, qkv_own, table_pair, cumul))
    far_core = [send(x, "co", 1) for x in far]
    og_pair = send(tied((og_other, far))[0], "c0", 1)
    to_y = shard_states(table, qkv_own, og_own, cumul, 0, None)
    far_core, to_y = tied((far_core, to_y))
    qkv_pair = project(table_pair, [[side_core], far, far_core], (3, 0, 1), weight, acc_pair, True)
    turned = [turn(table, tied(([[activations], [core], [near], [near_core]], qkv_pair))[0])]
    og_pair, qkv_pair, turned = tied((og_pair, qkv_pair, turned))

    to_y = shard_states(table, qkv_pair, og_pair, cumul, 1, to_y)
    at_y = [send(to_y[r], "c2", r) for r in (1, 3, 2)]
    qkv_own, _ = tied((qkv_own, to_y[0]))
    local_own = local_grads(table, qkv_own, og_own, cumul, 0, 0, per, None)
    at_y, local_own = tied((at_y, local_own))
    before, after, prior, later, ring = ring_y(table, [to_y[0], at_y[0], at_y[2], at_y[1]])
    at_x = [send(ring, "c1", r) for r in (1, 3, 2)]
    qkv_pair, _ = tied((qkv_pair, ring))
    local = local_grads(table_pair, qkv_pair, og_pair, cumul, 1, 0, per // 2, None)
    at_x, local = tied((at_x, local))
    back = arrivals(table, [ring, at_x[0], at_x[2], at_x[1]], before, after, prior, later)
    states = [send(back[r], "c2", r) for r in (1, 3, 2)]
    local, _ = tied((local, back[0]))
    local = local_grads(table_pair, qkv_pair, og_pair, cumul, 1, per // 2, per // 2, local)
    second, _ = tied(([far, far_core, [side], [side_core]], back[0]))
    turned.append(turn(table, second))
    states, turned, local = tied((states, turned, local))
    states = [back[0], states[0], states[2], states[1]]

    left_own, right_own = whole_grads(table, 0, *local_own, states)
    left_pair, right_pair = whole_grads(table, 1, *local, states)
    lefts, rights = (left_own, left_pair), (right_own, right_pair)
    far_piece = weight_part(table, turned, lefts, rights, (2,), True)
    l_half, r_half = swaps(far_piece, "c1", "c2")
    turned, _ = tied((turned, far_piece[0]))
    l_one, l_three, r_one, r_three = weight_part(table, turned, lefts, rights, (1, 3), False)
    l_half, l_one = tied((l_half, l_one))
    l_three, l_one = add_halves(table, l_three, l_one, l_half)
    l_got = [send(l_one, "c1", 1), send(l_three, "c1", 3)]
    r_half, _ = tied((r_half, l_one))
    r_three, r_one = add_halves(table, r_three, r_one, r_half)
    r_got = [send(r_one, "c2", 1), send(r_three, "c2", 3)]
    turned, _ = tied((turned, r_one))
    own = weight_part(table, turned, lefts, rights, (0,), False)
    l_got, own = tied((l_got, own))
    l_cut = cut_blocks(table, Y, own[0], *l_got)
    r_got, _ = tied((r_got, l_cut))
    r_cut = cut_blocks(table, X, own[1], *r_got)
    l_got = [send(x, "c2", by) for x, by in zip(l_cut, (1, 3, 2))]
    r_got = [send(x, "c1", by) for x, by in zip(r_cut, (1, 3, 2))]
    here, there = final_sums(table, ((l_cut[3], *l_got), (r_cut[3], *r_got)))
    there = send(there, "c0", 1)
    return jnp.transpose(finish(table, here, there), (1, 0, 2))


def solution(mesh):
    finer = Mesh(mesh.devices.reshape(2, 4, 4, 2, 2), ("c0", "c1", "c2", "zl", "co"))
    context, tensor = ("c0", "c1", "c2"), ("zl", "co")
    placed = (
        P(context, tensor),
        P(None, None, tensor),
        P(context, tensor),
        P(context),
        P(context, tensor),
    )
    return jax.shard_map(
        device_part,
        mesh=finer,
        in_specs=placed,
        out_specs=P(context, None, tensor),
        check_vma=False,
    )
```

```python
import jax
import jax.numpy as jnp
from jax import lax
from jax.experimental import pallas as pl
from jax.experimental.pallas import tpu as pltpu
from jax.sharding import Mesh
from jax.sharding import PartitionSpec as P

F32 = jnp.float32
BF16 = jnp.bfloat16
HEAD = 128
Z, X, Y, ZL, CO, TEN, LEN = range(7)
AB_T = (((1,), (1,)), ((), ()))
A_TB = (((0,), (0,)), ((), ()))


def dot(a, b):
    return jnp.dot(a, b, preferred_element_type=F32)


def send(x, axis, by):
    return lax.ppermute(x, axis, [(i, i ^ by) for i in range(lax.axis_size(axis))])


def across(x):
    return lax.ppermute(x, ("c0", "zl"), [(0, 3), (1, 2), (2, 1), (3, 0)])


def whole(x):
    return pl.BlockSpec(x.shape, lambda *_, n=len(x.shape): (0,) * n)


def call(name, body, table, grid, operands, in_specs, outs, out_specs, mib, scratch=(), alias=None):
    return pl.pallas_call(
        body,
        grid_spec=pltpu.PrefetchScalarGridSpec(
            num_scalar_prefetch=1,
            grid=grid,
            in_specs=in_specs,
            out_specs=out_specs,
            scratch_shapes=scratch,
        ),
        out_shape=outs,
        input_output_aliases=alias or {},
        compiler_params=pltpu.CompilerParams(
            dimension_semantics=("arbitrary",) * len(grid), vmem_limit_bytes=mib << 20
        ),
        cost_estimate=pl.CostEstimate(flops=1, bytes_accessed=1, transcendentals=0),
        name=name,
    )(table, *operands)


def in_hbm(xs):
    return [pltpu.with_memory_space_constraint(x, pltpu.HBM) for x in xs]


def shape(dims, kind=BF16):
    return jax.ShapeDtypeStruct(dims, kind)


def joined(refs):
    parts = [ref[...] for ref in refs]
    return parts[0] if len(parts) == 1 else jnp.concatenate(parts, axis=0)


def project(table, shards, flips, weight, partial, last):
    n, counts = len(shards), [len(x) for x in shards]
    flat = [part for x in shards for part in x]
    tokens, width = sum(part.shape[0] for part in shards[0]), flat[0].shape[1]
    cols = weight.shape[2]

    def body(s, *refs):
        out, rest = refs[-1], list(refs)
        acc = None
        for i, count in enumerate(counts):
            rows = joined([rest.pop(0) for _ in range(count)])
            term = dot(rows, refs[len(flat) + i][0])
            acc = term if acc is None else acc + term
        if partial is not None:
            acc += refs[len(flat) + n][0]
        if last:
            row = lax.broadcasted_iota(jnp.int32, acc.shape, 0)
            acc = jnp.where(row < s[LEN], acc, 0.0)
        out[0] = acc.astype(out.dtype)

    tile = pl.BlockSpec((1, tokens, cols), lambda g, s: (g, 0, 0))
    in_specs = [whole(x) for x in flat]
    for flip in flips:
        in_specs.append(
            pl.BlockSpec((1, width, cols), lambda g, s, flip=flip: (g, s[TEN] ^ flip, 0))
        )
    operands = [*flat, *([weight] * n)]
    if partial is not None:
        in_specs.append(tile)
        operands.append(partial)
    out = shape((3, tokens, cols)) if last else pltpu.HBM((3, tokens, cols), F32)
    return call("project", body, table, (3,), in_hbm(operands), in_specs, out, tile, 24)


def shard_states(table, qkv, out_grad, cumul, which, so_far):
    tokens = qkv.shape[1]
    heads = qkv.shape[2] // HEAD
    scale = HEAD**-0.5

    def body(s, qkv_ref, og_ref, cum_ref, *refs):
        outs = refs[-4:]
        r = pl.program_id(0)
        row = cum_ref[pl.ds(which * heads + (s[Y] ^ r), 1), :]
        total = row[:, tokens - 1 : tokens]
        keys_t = qkv_ref[1].T.astype(F32)
        query_t = qkv_ref[0].T.astype(F32)
        keys_t = (keys_t * jnp.exp(total - row)).astype(BF16)
        query_t = (query_t * (scale * jnp.exp(row))).astype(BF16)
        states = (dot(keys_t, qkv_ref[2]), dot(query_t, og_ref[...]))
        at = lax.broadcasted_iota(jnp.int32, (16, HEAD), 0)
        tail = jnp.broadcast_to(total, (16, HEAD)).astype(BF16)
        for k, out in enumerate(outs):

            @pl.when(r == k)
            def _(k=k, out=out):
                here = s[Z] ^ which
                if so_far is not None:
                    out[...] = refs[k][...]
                for kind in range(2):
                    start = pl.multiple_of((2 * kind + here) * HEAD, HEAD)
                    out[pl.ds(start, HEAD), :] = states[kind].astype(BF16)
                if so_far is None:
                    out[4 * HEAD :, :] = tail
                else:
                    out[4 * HEAD :, :] = jnp.where(at == here, tail, refs[k][4 * HEAD :, :])

    message = shape((4 * HEAD + 16, HEAD))
    operands = [qkv, out_grad, cumul, *(so_far or ())]
    in_specs = [
        pl.BlockSpec((3, tokens, HEAD), lambda r, s: (0, 0, s[Y] ^ r)),
        pl.BlockSpec((tokens, HEAD), lambda r, s: (0, s[Y] ^ r)),
        whole(cumul),
        *[whole(m) for m in so_far or ()],
    ]
    return call(
        "shard_states",
        body,
        table,
        (4,),
        operands,
        in_specs,
        [message] * 4,
        [whole(message)] * 4,
        12,
    )


def in_order(refs, place, held):
    for r, ref in enumerate(refs):
        held[place ^ r] = ref[...]


def spread(pair):
    wide = [jnp.broadcast_to(pair[i : i + 1, :], (HEAD, HEAD)) for i in range(2)]
    return jnp.concatenate(wide, axis=0)


def ring_y(table, messages):
    half = 2 * HEAD

    def body(s, a, b, c, d, before, after, prior, later, out, held):
        in_order((a, b, c, d), s[Y], held)
        totals = [held[t, 2 * half : 2 * half + 16, :].astype(F32)[:2] for t in range(4)]
        run = jnp.zeros((half, HEAD), F32)
        reach = jnp.zeros((2, HEAD), F32)
        for t in range(4):
            before[t] = run
            prior[t] = jnp.exp(reach)
            run = spread(jnp.exp(totals[t])) * run + held[t, :half, :].astype(F32)
            reach = reach + totals[t]
        out[:half, :] = run.astype(BF16)
        total = reach
        run = jnp.zeros((half, HEAD), F32)
        reach = jnp.zeros((2, HEAD), F32)
        for t in range(3, -1, -1):
            after[t] = run
            later[t] = jnp.exp(reach)
            run = spread(jnp.exp(totals[t])) * run + held[t, half : 2 * half, :].astype(F32)
            reach = reach + totals[t]
        out[half : 2 * half, :] = run.astype(BF16)
        high = total.astype(BF16).astype(F32)
        low = total - high
        at = lax.broadcasted_iota(jnp.int32, (16, HEAD), 0)
        tail = jnp.where(at == 0, high[0:1], high[1:2])
        tail = jnp.where(at == 2, low[0:1], tail)
        tail = jnp.where(at == 3, low[1:2], tail)
        out[2 * half :, :] = tail.astype(BF16)

    outs = [
        shape((4, half, HEAD), F32),
        shape((4, half, HEAD), F32),
        shape((4, 2, HEAD), F32),
        shape((4, 2, HEAD), F32),
        shape(messages[0].shape),
    ]
    return call(
        "ring_y",
        body,
        table,
        (1,),
        messages,
        [whole(m) for m in messages],
        outs,
        [whole(o) for o in outs],
        8,
        [pltpu.VMEM((4, *messages[0].shape), BF16)],
    )


def arrivals(table, messages, before, after, prior, later):
    half = 2 * HEAD

    def body(s, a, b, c, d, before_ref, after_ref, prior_ref, later_ref, *rest):
        outs, held, mine, edges = rest[:4], *rest[4:]
        in_order((a, b, c, d), s[X], held)
        tails = [held[t, 2 * half : 2 * half + 16, :].astype(F32) for t in range(4)]
        totals = [tail[0:2] + tail[2:4] for tail in tails]
        ends = []
        for kind, steps in ((0, range(4)), (1, range(3, -1, -1))):
            run = jnp.zeros((half, HEAD), F32)
            reach = jnp.zeros((2, HEAD), F32)
            for t in steps:

                @pl.when(s[X] == t)
                def _(run=run, reach=reach, kind=kind):
                    mine[kind] = run
                    edges[kind] = jnp.exp(reach)

                rows = held[t, kind * half : (kind + 1) * half, :].astype(F32)
                run = spread(jnp.exp(totals[t])) * run + rows
                reach = reach + totals[t]
            ends.append(run.astype(BF16).astype(F32))
        nothing = jnp.zeros((HEAD, HEAD), F32)
        across_up = jnp.concatenate([nothing, ends[0][:HEAD]], axis=0)
        across_down = jnp.concatenate([ends[1][HEAD:], nothing], axis=0)
        start = mine[0] + spread(edges[0]) * across_up
        finish = mine[1] + spread(edges[1]) * across_down
        for r, out in enumerate(outs):
            t = s[Y] ^ r
            out[:half, :] = (before_ref[t] + spread(prior_ref[t]) * start).astype(BF16)
            out[half:, :] = (after_ref[t] + spread(later_ref[t]) * finish).astype(BF16)

    operands = (*messages, before, after, prior, later)
    message = shape((2 * half, HEAD))
    return call(
        "arrivals",
        body,
        table,
        (1,),
        operands,
        [whole(m) for m in operands],
        [message] * 4,
        [whole(message)] * 4,
        8,
        [
            pltpu.VMEM((4, *messages[0].shape), BF16),
            pltpu.VMEM((2, half, HEAD), F32),
            pltpu.VMEM((2, 2, HEAD), F32),
        ],
    )


def column_of(row):
    return jnp.broadcast_to(row, (HEAD, row.shape[1])).T


def local_grads(table, qkv, out_grad, cumul, which, first, count, so_far):
    tokens = qkv.shape[1]
    heads = qkv.shape[2] // HEAD
    scale = HEAD**-0.5
    size = tokens // 2

    def body(s, qkv_ref, og_ref, cum_ref, *refs):
        out, ready = refs[-2:]
        row = cum_ref[pl.ds(pl.program_id(0) + which * heads + first, 1), :]
        column = column_of(row)
        wide = jnp.concatenate([column] * (size // HEAD), axis=1)
        s_at = lax.broadcasted_iota(jnp.int32, (size, size), 0)
        t_at = lax.broadcasted_iota(jnp.int32, (size, size), 1)
        parts = [slice(0, size), slice(size, tokens)]

        def pair(t, s):
            if t == s:
                gap = row[:, parts[t]] - wide[parts[s], :]
                decay = jnp.exp(jnp.where(s_at <= t_at, gap, -jnp.inf))
            else:
                middle = row[:, size - 1 : size]
                to_middle = jnp.exp(middle - column[parts[s], :])
                decay = jnp.concatenate([to_middle] * (size // HEAD), axis=1)
                decay *= jnp.exp(row[:, parts[t]] - middle)
            q, k, v = qkv_ref[0, parts[t], :], qkv_ref[1, parts[s], :], qkv_ref[2, parts[s], :]
            g = og_ref[parts[t], :]
            scores = lax.dot_general(k, q, AB_T, preferred_element_type=F32)
            grads = lax.dot_general(v, g, AB_T, preferred_element_type=F32)
            prob = (scores * decay).astype(BF16)
            score = (grads * decay).astype(BF16)
            dq = lax.dot_general(score, k, A_TB, preferred_element_type=F32)
            return dq, dot(score, q), dot(prob, g)

        a, b, c = pair(0, 0), pair(1, 0), pair(1, 1)
        live = lax.broadcasted_iota(jnp.int32, (tokens, HEAD), 0) < s[LEN]
        grads = (
            jnp.concatenate([a[0], b[0] + c[0]], axis=0) * scale,
            jnp.concatenate([a[1] + b[1], c[1]], axis=0) * scale,
            jnp.concatenate([a[2] + b[2], c[2]], axis=0) * scale,
        )
        until = jnp.exp(row[:, tokens - 1 : tokens] - column)
        rows = (
            og_ref[...].astype(F32) * (scale * jnp.exp(column)),
            qkv_ref[2].astype(F32) * until,
            qkv_ref[1].astype(F32) * until,
        )
        for j in range(3):
            out[j] = jnp.where(live, grads[j], 0.0).astype(BF16)
            ready[j] = jnp.where(live, rows[j], 0.0).astype(BF16)

    tile = pl.BlockSpec((3, tokens, HEAD), lambda h, s: (0, 0, h + first))
    in_specs = [tile, pl.BlockSpec((tokens, HEAD), lambda h, s: (0, h + first)), whole(cumul)]
    operands = [qkv, out_grad, cumul]
    if so_far is not None:
        in_specs += [pl.BlockSpec(memory_space=pl.ANY)] * 2
        operands += so_far
    return call(
        "local_grads",
        body,
        table,
        (count,),
        operands,
        in_specs,
        [shape(qkv.shape), shape(qkv.shape)],
        [tile, tile],
        12,
        alias=None if so_far is None else {4: 0, 5: 1},
    )


def whole_grads(table, which, local, ready, states):
    tokens = local.shape[1]
    heads = local.shape[2] // HEAD

    def body(s, local_ref, ready_ref, a, b, c, d, left, right, held):
        h = pl.program_id(0)

        @pl.when(h == 0)
        def _():
            in_order((a, b, c, d), s[Y], held)

        base = pl.multiple_of((s[Z] ^ which) * HEAD, HEAD)
        coming = held[h, pl.ds(base, HEAD), :]
        later = held[h, pl.ds(2 * HEAD + base, HEAD), :]
        cross = (
            lax.dot_general(ready_ref[0], coming, AB_T, preferred_element_type=F32),
            lax.dot_general(ready_ref[1], later, AB_T, preferred_element_type=F32),
            dot(ready_ref[2], later),
        )
        grads = [(local_ref[j].astype(F32) + cross[j]).astype(BF16) for j in range(3)]
        for k in range(heads):

            @pl.when(h == k)
            def _(k=k):
                for j in range(3):
                    start = (2 * j + k % 2) * HEAD
                    (left, right)[k // 2][:, start : start + HEAD] = grads[j]

    tile = pl.BlockSpec((3, tokens, HEAD), lambda h, s: (0, 0, h))
    side = shape((tokens, 3 * heads * HEAD // 2))
    return call(
        "whole_grads",
        body,
        table,
        (heads,),
        (local, ready, *states),
        [tile, tile, *[whole(m) for m in states]],
        [side, side],
        [whole(side)] * 2,
        12,
        [pltpu.VMEM((4, *states[0].shape), BF16)],
    )


def turn(table, shards, base, so_far):
    tokens, width = shards[0].shape
    n, rows = len(shards), 4 * width // 32

    def body(s, *refs):
        out = refs[-1]
        for k in range(n):

            @pl.when(pl.program_id(0) == k)
            def _(k=k):
                out[...] = refs[k][...].T.reshape(out.shape)

    def place(i, s):
        i = s[TEN] ^ (base + i)
        return i % 2, (i // 2) ^ s[Z], 0, 0

    out = shape((16, 2, rows, tokens))
    spec = pl.BlockSpec((8, 1, rows, tokens), place)
    operands, in_specs = in_hbm(shards), [whole(x) for x in shards]
    if so_far is not None:
        operands.append(so_far)
        in_specs.append(pl.BlockSpec(memory_space=pl.ANY))
    return call(
        "turn",
        body,
        table,
        (n,),
        operands,
        in_specs,
        out,
        spec,
        12,
        alias=None if so_far is None else {n + 1: 0},
    )


def weight_part(table, turned, lefts, rights, places, split):
    tokens, cols = lefts[0].shape
    rows = turned[0].shape[2]

    def body(s, own_x, own_y, pair_x, pair_y, left_a, left_b, right_a, right_b, *outs):
        r = pl.program_id(0)
        for side, (a, b, ga, gb) in enumerate(
            ((own_x, pair_x, left_a, left_b), (own_y, pair_y, right_a, right_b))
        ):
            acc = dot(a[...].reshape(4 * rows, tokens), ga[...])
            acc += dot(b[...].reshape(4 * rows, tokens), gb[...])
            acc = acc.astype(BF16)
            if split:
                outs[2 * side][...] = acc[: 2 * rows]
                outs[2 * side + 1][...] = acc[2 * rows :]
                continue
            for k in range(len(places)):

                @pl.when(r == k)
                def _(k=k, acc=acc, side=side):
                    outs[side * len(places) + k][...] = acc

    step = places[1] - places[0] if len(places) > 1 else 0
    by_x = pl.BlockSpec((1, 4, rows, tokens), lambda r, s: (s[X] ^ (places[0] + step * r), 0, 0, 0))
    by_y = pl.BlockSpec((4, 1, rows, tokens), lambda r, s: (0, s[Y] ^ (places[0] + step * r), 0, 0))
    outs = [shape((2 * rows if split else 4 * rows, cols))] * (4 if split else 2 * len(places))
    operands = (turned[0], turned[0], turned[1], turned[1], *lefts, *rights)
    return call(
        "weight_part",
        body,
        table,
        (len(places),),
        operands,
        [by_x, by_y, by_x, by_y, *[whole(x) for x in (*lefts, *rights)]],
        outs,
        [whole(o) for o in outs],
        30,
    )


def add_halves(table, third, first_place, halves):
    up, down = halves
    near_up, near_down = third, first_place
    n, cols = up.shape

    def body(s, a, b, u, d, out_a, out_b):
        out_a[...] = (a[...].astype(F32) + u[...].astype(F32)).astype(BF16)
        out_b[...] = (b[...].astype(F32) + d[...].astype(F32)).astype(BF16)

    first = pl.BlockSpec((n, cols), lambda i, s: (0, 0))
    second = pl.BlockSpec((n, cols), lambda i, s: (1, 0))
    return call(
        "add_halves",
        body,
        table,
        (1,),
        (near_up, near_down, up, down),
        [first, second, first, first],
        [shape(near_up.shape), shape(near_down.shape)],
        [first, second],
        12,
        alias={1: 0, 2: 1},
    )


def cut_blocks(table, left, right):
    rows, cols = left[0].shape[0] // 4, left[0].shape[1]

    def body(s, *refs):
        for k, axis in enumerate((Y, X)):
            a, b, c = refs[3 * k : 3 * k + 3]
            for r, out in zip((1, 3, 2, 0), refs[6 + 4 * k : 10 + 4 * k]):
                at = pl.ds(pl.multiple_of((s[axis] ^ r) * rows, rows), rows)
                total = a[at, :].astype(F32) + b[at, :].astype(F32) + c[at, :].astype(F32)
                out[...] = total.astype(BF16)

    outs = [shape((rows, cols))] * 8
    operands = (*left, *right)
    cut = call(
        "cut_blocks",
        body,
        table,
        (1,),
        operands,
        [whole(x) for x in operands],
        outs,
        [whole(o) for o in outs],
        24,
    )
    return cut[:4], cut[4:]


def final_sums(table, sides):
    rows, cols = sides[0][0].shape

    def body(s, *refs):
        here, there = refs[-2:]
        for k in range(2):
            total = sum(ref[...].astype(F32) for ref in refs[4 * k : 4 * k + 4]).astype(BF16)
            here[k] = total[: rows // 2]
            there[k] = total[rows // 2 :]

    operands = [x for side in sides for x in side]
    outs = [shape((2, rows // 2, cols))] * 2
    return call(
        "final_sums",
        body,
        table,
        (1,),
        operands,
        [whole(x) for x in operands],
        outs,
        [whole(o) for o in outs],
        12,
    )


def finish(table, here, there):
    _, rows, cols = here.shape
    side = cols // 3

    def body(s, here_ref, there_ref, out):
        for ref, half in ((here_ref, s[Z]), (there_ref, 1 - s[Z])):
            for k in range(2):
                for j in range(3):
                    at = pl.ds(pl.multiple_of(half * 2 * side + k * side, side), side)
                    out[j, :, at] = ref[k, :, j * side : (j + 1) * side].astype(F32)

    out = shape((3, rows, 4 * side), F32)
    operands = (here, there)
    return call("finish", body, table, (1,), operands, [whole(here)] * 2, out, whole(out), 8)


def swaps(pieces, left, right):
    a, c = send(pieces[0], left, 1), send(pieces[2], right, 1)
    b, d = send(pieces[1], left, 3), send(pieces[3], right, 3)
    return [a, b], [c, d]


def device_part(activations, qkv_weight, log_decay, lengths, out_grad):
    tied = lax.optimization_barrier
    tokens = activations.shape[0]
    heads = log_decay.shape[1]
    per = heads // 2
    index = [lax.axis_index(a) for a in ("c0", "c1", "c2", "zl", "co")]
    here_z = index[0]
    fixed = [*index, index[3] * 2 + index[4]]
    table = jnp.stack([*fixed, lengths[0]]).astype(jnp.int32)
    weight = jnp.transpose(qkv_weight, (1, 0, 2))
    width = per * HEAD
    weight = lax.dynamic_slice_in_dim(weight, here_z * width, width, axis=2)

    near = send(activations, "zl", 1)
    side = across(activations)
    core = send(activations, "co", 1)

    live = (jnp.arange(tokens, dtype=jnp.int32) < lengths[0]).astype(F32)
    cumul = jnp.cumsum(log_decay.T * live[None, :], axis=1)
    size = jnp.broadcast_to(lengths.astype(F32)[:, None], (per, tokens))
    note = jnp.concatenate([lax.dynamic_slice_in_dim(cumul, (1 - here_z) * per, per), size])
    og_own = lax.dynamic_slice_in_dim(out_grad, here_z * width, width, axis=1)
    og_other = lax.dynamic_slice_in_dim(out_grad, (1 - here_z) * width, width, axis=1)

    acc_own = project(table, [[activations], [core]], (0, 1), weight, None, False)
    turned = turn(table, [activations, core], 0, None)
    near, side, acc_own, note, og_other, turned = tied((near, side, acc_own, note, og_other, turned))
    note = send(note, "c0", 1)
    near_core = send(near, "co", 1)
    side_core = send(side, "co", 1)
    far = send(tied((activations, near, side))[0], "c0", 1)
    acc_pair = project(table, [[side]], (2,), weight, None, False)
    near_core, acc_pair = tied((near_core, acc_pair))
    qkv_own = project(table, [[near], [near_core]], (2, 3), weight, acc_own, True)
    turned = [turn(table, tied(([near, near_core], qkv_own))[0], 2, turned)]
    note, side_core, qkv_own, far, turned = tied((note, side_core, qkv_own, far, turned))
    cumul = jnp.concatenate([lax.dynamic_slice_in_dim(cumul, here_z * per, per), note[:per]])
    table_pair = jnp.stack([*fixed, note[per, 0].astype(jnp.int32)]).astype(jnp.int32)
    far_core = send(far, "co", 1)
    og_pair = send(tied((og_other, far))[0], "c0", 1)
    to_y = shard_states(table, qkv_own, og_own, cumul, 0, None)
    far_core, to_y = tied((far_core, to_y))
    qkv_pair = project(table_pair, [[side_core], [far], [far_core]], (3, 0, 1), weight, acc_pair, True)
    og_pair, qkv_pair = tied((og_pair, qkv_pair))

    to_y = shard_states(table, qkv_pair, og_pair, cumul, 1, to_y)
    at_y = [send(to_y[r], "c2", r) for r in (1, 3, 2)]
    qkv_own, _ = tied((qkv_own, to_y[0]))
    local_own = local_grads(table, qkv_own, og_own, cumul, 0, 0, per, None)
    at_y, local_own = tied((at_y, local_own))
    before, after, prior, later, ring = ring_y(table, [to_y[0], at_y[0], at_y[2], at_y[1]])
    at_x = [send(ring, "c1", r) for r in (1, 3, 2)]
    qkv_pair, _ = tied((qkv_pair, ring))
    local = local_grads(table_pair, qkv_pair, og_pair, cumul, 1, 0, per // 2, None)
    at_x, local = tied((at_x, local))
    back = arrivals(table, [ring, at_x[0], at_x[2], at_x[1]], before, after, prior, later)
    states = [send(back[r], "c2", r) for r in (1, 3, 2)]
    local, _ = tied((local, back[0]))
    local = local_grads(table_pair, qkv_pair, og_pair, cumul, 1, per // 2, per // 2, local)
    second, _ = tied(([far, far_core, side, side_core], back[0]))
    turned.append(turn(table, second, 0, None))
    states, turned, local = tied((states, turned, local))
    states = [back[0], states[0], states[2], states[1]]
    turned = [t.reshape(4, 4, -1, tokens) for t in turned]

    left_own, right_own = whole_grads(table, 0, *local_own, states)
    left_pair, right_pair = whole_grads(table, 1, *local, states)
    lefts, rights = (left_own, left_pair), (right_own, right_pair)
    far_piece = weight_part(table, turned, lefts, rights, (2,), True)
    l_half, r_half = swaps(far_piece, "c1", "c2")
    turned, _ = tied((turned, far_piece[0]))
    l_one, l_three, r_one, r_three = weight_part(table, turned, lefts, rights, (1, 3), False)
    l_half, l_one = tied((l_half, l_one))
    l_three, l_one = add_halves(table, l_three, l_one, l_half)
    l_got = [send(l_one, "c1", 1), send(l_three, "c1", 3)]
    r_half, _ = tied((r_half, l_one))
    r_three, r_one = add_halves(table, r_three, r_one, r_half)
    r_got = [send(r_one, "c2", 1), send(r_three, "c2", 3)]
    turned, _ = tied((turned, r_one))
    own = weight_part(table, turned, lefts, rights, (0,), False)
    l_got, own = tied((l_got, own))
    l_cut, r_cut = cut_blocks(table, (own[0], *l_got), (own[1], *r_got))
    l_got = [send(x, "c2", by) for x, by in zip(l_cut, (1, 3, 2))]
    r_got = [send(x, "c1", by) for x, by in zip(r_cut, (1, 3, 2))]
    here, there = final_sums(table, ((l_cut[3], *l_got), (r_cut[3], *r_got)))
    there = send(there, "c0", 1)
    return jnp.transpose(finish(table, here, there), (1, 0, 2))


def solution(mesh):
    finer = Mesh(mesh.devices.reshape(2, 4, 4, 2, 2), ("c0", "c1", "c2", "zl", "co"))
    context, tensor = ("c0", "c1", "c2"), ("zl", "co")
    placed = (
        P(context, tensor),
        P(None, None, tensor),
        P(context, tensor),
        P(context),
        P(context, tensor),
    )
    return jax.shard_map(
        device_part,
        mesh=finer,
        in_specs=placed,
        out_specs=P(context, None, tensor),
        check_vma=False,
    )
```

```python
import jax
import jax.numpy as jnp
from jax import lax
from jax.experimental import pallas as pl
from jax.experimental.pallas import tpu as pltpu
from jax.sharding import Mesh
from jax.sharding import PartitionSpec as P

F32 = jnp.float32
BF16 = jnp.bfloat16
HEAD = 128
PROJ = 24
Z, X, Y, ZL, CO, TEN, LEN = range(7)
AB_T = (((1,), (1,)), ((), ()))
A_TB = (((0,), (0,)), ((), ()))


def dot(a, b):
    return jnp.dot(a, b, preferred_element_type=F32)


def send(x, axis, by):
    return lax.ppermute(x, axis, [(i, i ^ by) for i in range(lax.axis_size(axis))])


def across(x):
    return lax.ppermute(x, ("c0", "zl"), [(0, 3), (1, 2), (2, 1), (3, 0)])


def whole(x):
    return pl.BlockSpec(x.shape, lambda *_, n=len(x.shape): (0,) * n)


def call(name, body, table, grid, operands, in_specs, outs, out_specs, mib, scratch=(), alias=None):
    return pl.pallas_call(
        body,
        grid_spec=pltpu.PrefetchScalarGridSpec(
            num_scalar_prefetch=1,
            grid=grid,
            in_specs=in_specs,
            out_specs=out_specs,
            scratch_shapes=scratch,
        ),
        out_shape=outs,
        input_output_aliases=alias or {},
        compiler_params=pltpu.CompilerParams(
            dimension_semantics=("arbitrary",) * len(grid), vmem_limit_bytes=mib << 20
        ),
        cost_estimate=pl.CostEstimate(flops=1, bytes_accessed=1, transcendentals=0),
        name=name,
    )(table, *operands)


def shape(dims, kind=BF16):
    return jax.ShapeDtypeStruct(dims, kind)


def joined(refs):
    parts = [ref[...] for ref in refs]
    return parts[0] if len(parts) == 1 else jnp.concatenate(parts, axis=0)


def project(table, shards, flips, weight, partial, last):
    n, counts = len(shards), [len(x) for x in shards]
    flat = [part for x in shards for part in x]
    tokens, width = sum(part.shape[0] for part in shards[0]), flat[0].shape[1]
    cols = weight.shape[2] // 2

    def body(s, *refs):
        out, rest = refs[-1], list(refs)
        acc = None
        for i, count in enumerate(counts):
            rows = joined([rest.pop(0) for _ in range(count)])
            term = dot(rows, refs[len(flat) + i][0])
            acc = term if acc is None else acc + term
        if partial is not None:
            acc += refs[len(flat) + n][0]
        if last:
            row = lax.broadcasted_iota(jnp.int32, acc.shape, 0)
            acc = jnp.where(row < s[LEN], acc, 0.0)
        out[0] = acc.astype(out.dtype)

    tile = pl.BlockSpec((1, tokens, cols), lambda g, s: (g, 0, 0))
    in_specs = [whole(x) for x in flat]
    for flip in flips:
        in_specs.append(
            pl.BlockSpec((1, width, cols), lambda g, s, flip=flip: (g, s[TEN] ^ flip, s[Z]))
        )
    operands = [*flat, *([weight] * n)]
    if partial is not None:
        in_specs.append(tile)
        operands.append(partial)
    out = shape((3, tokens, cols), BF16 if last else F32)
    return call("project", body, table, (3,), operands, in_specs, out, tile, PROJ)


def shard_states(table, qkv, out_grad, cumul, which, so_far):
    tokens = qkv.shape[1]
    heads = qkv.shape[2] // HEAD
    scale = HEAD**-0.5

    def body(s, qkv_ref, og_ref, cum_ref, *refs):
        outs = refs[-4:]
        r = pl.program_id(0)
        row = cum_ref[pl.ds(which * heads + (s[Y] ^ r), 1), :]
        total = row[:, tokens - 1 : tokens]
        keys_t = qkv_ref[1].T.astype(F32)
        query_t = qkv_ref[0].T.astype(F32)
        keys_t = (keys_t * jnp.exp(total - row)).astype(BF16)
        query_t = (query_t * (scale * jnp.exp(row))).astype(BF16)
        states = (dot(keys_t, qkv_ref[2]), dot(query_t, og_ref[...]))
        at = lax.broadcasted_iota(jnp.int32, (16, HEAD), 0)
        tail = jnp.broadcast_to(total, (16, HEAD)).astype(BF16)
        for k, out in enumerate(outs):

            @pl.when(r == k)
            def _(k=k, out=out):
                here = s[Z] ^ which
                if so_far is not None:
                    out[...] = refs[k][...]
                for kind in range(2):
                    start = pl.multiple_of((2 * kind + here) * HEAD, HEAD)
                    out[pl.ds(start, HEAD), :] = states[kind].astype(BF16)
                if so_far is None:
                    out[4 * HEAD :, :] = tail
                else:
                    out[4 * HEAD :, :] = jnp.where(at == here, tail, refs[k][4 * HEAD :, :])

    message = shape((4 * HEAD + 16, HEAD))
    operands = [qkv, out_grad, cumul, *(so_far or ())]
    in_specs = [
        pl.BlockSpec((3, tokens, HEAD), lambda r, s: (0, 0, s[Y] ^ r)),
        pl.BlockSpec((tokens, HEAD), lambda r, s: (0, s[Y] ^ r)),
        whole(cumul),
        *[whole(m) for m in so_far or ()],
    ]
    return call(
        "shard_states",
        body,
        table,
        (4,),
        operands,
        in_specs,
        [message] * 4,
        [whole(message)] * 4,
        12,
    )


def in_order(refs, place, held):
    for r, ref in enumerate(refs):
        held[place ^ r] = ref[...]


def spread(pair):
    wide = [jnp.broadcast_to(pair[i : i + 1, :], (HEAD, HEAD)) for i in range(2)]
    return jnp.concatenate(wide, axis=0)


def ring_y(table, messages):
    half = 2 * HEAD

    def body(s, a, b, c, d, before, after, prior, later, out, held):
        in_order((a, b, c, d), s[Y], held)
        totals = [held[t, 2 * half : 2 * half + 16, :].astype(F32)[:2] for t in range(4)]
        run = jnp.zeros((half, HEAD), F32)
        reach = jnp.zeros((2, HEAD), F32)
        for t in range(4):
            before[t] = run
            prior[t] = jnp.exp(reach)
            run = spread(jnp.exp(totals[t])) * run + held[t, :half, :].astype(F32)
            reach = reach + totals[t]
        out[:half, :] = run.astype(BF16)
        total = reach
        run = jnp.zeros((half, HEAD), F32)
        reach = jnp.zeros((2, HEAD), F32)
        for t in range(3, -1, -1):
            after[t] = run
            later[t] = jnp.exp(reach)
            run = spread(jnp.exp(totals[t])) * run + held[t, half : 2 * half, :].astype(F32)
            reach = reach + totals[t]
        out[half : 2 * half, :] = run.astype(BF16)
        high = total.astype(BF16).astype(F32)
        low = total - high
        at = lax.broadcasted_iota(jnp.int32, (16, HEAD), 0)
        tail = jnp.where(at == 0, high[0:1], high[1:2])
        tail = jnp.where(at == 2, low[0:1], tail)
        tail = jnp.where(at == 3, low[1:2], tail)
        out[2 * half :, :] = tail.astype(BF16)

    outs = [
        shape((4, half, HEAD), F32),
        shape((4, half, HEAD), F32),
        shape((4, 2, HEAD), F32),
        shape((4, 2, HEAD), F32),
        shape(messages[0].shape),
    ]
    return call(
        "ring_y",
        body,
        table,
        (1,),
        messages,
        [whole(m) for m in messages],
        outs,
        [whole(o) for o in outs],
        8,
        [pltpu.VMEM((4, *messages[0].shape), BF16)],
    )


def arrivals(table, messages, before, after, prior, later):
    half = 2 * HEAD

    def body(s, a, b, c, d, before_ref, after_ref, prior_ref, later_ref, *rest):
        outs, held, mine, edges = rest[:4], *rest[4:]
        in_order((a, b, c, d), s[X], held)
        tails = [held[t, 2 * half : 2 * half + 16, :].astype(F32) for t in range(4)]
        totals = [tail[0:2] + tail[2:4] for tail in tails]
        ends = []
        for kind, steps in ((0, range(4)), (1, range(3, -1, -1))):
            run = jnp.zeros((half, HEAD), F32)
            reach = jnp.zeros((2, HEAD), F32)
            for t in steps:

                @pl.when(s[X] == t)
                def _(run=run, reach=reach, kind=kind):
                    mine[kind] = run
                    edges[kind] = jnp.exp(reach)

                rows = held[t, kind * half : (kind + 1) * half, :].astype(F32)
                run = spread(jnp.exp(totals[t])) * run + rows
                reach = reach + totals[t]
            ends.append(run.astype(BF16).astype(F32))
        nothing = jnp.zeros((HEAD, HEAD), F32)
        across_up = jnp.concatenate([nothing, ends[0][:HEAD]], axis=0)
        across_down = jnp.concatenate([ends[1][HEAD:], nothing], axis=0)
        start = mine[0] + spread(edges[0]) * across_up
        finish = mine[1] + spread(edges[1]) * across_down
        for r, out in enumerate(outs):
            t = s[Y] ^ r
            out[:half, :] = (before_ref[t] + spread(prior_ref[t]) * start).astype(BF16)
            out[half:, :] = (after_ref[t] + spread(later_ref[t]) * finish).astype(BF16)

    operands = (*messages, before, after, prior, later)
    message = shape((2 * half, HEAD))
    return call(
        "arrivals",
        body,
        table,
        (1,),
        operands,
        [whole(m) for m in operands],
        [message] * 4,
        [whole(message)] * 4,
        8,
        [
            pltpu.VMEM((4, *messages[0].shape), BF16),
            pltpu.VMEM((2, half, HEAD), F32),
            pltpu.VMEM((2, 2, HEAD), F32),
        ],
    )


def column_of(row):
    return jnp.broadcast_to(row, (HEAD, row.shape[1])).T


def local_grads(table, qkv, out_grad, cumul, which, first, count, so_far):
    tokens = qkv.shape[1]
    heads = qkv.shape[2] // HEAD
    scale = HEAD**-0.5
    size = tokens // 2

    def body(s, qkv_ref, og_ref, cum_ref, *refs):
        out, ready = refs[-2:]
        row = cum_ref[pl.ds(pl.program_id(0) + which * heads + first, 1), :]
        column = column_of(row)
        wide = jnp.concatenate([column] * (size // HEAD), axis=1)
        s_at = lax.broadcasted_iota(jnp.int32, (size, size), 0)
        t_at = lax.broadcasted_iota(jnp.int32, (size, size), 1)
        parts = [slice(0, size), slice(size, tokens)]

        def pair(t, s):
            if t == s:
                gap = row[:, parts[t]] - wide[parts[s], :]
                decay = jnp.exp(jnp.where(s_at <= t_at, gap, -jnp.inf))
            else:
                middle = row[:, size - 1 : size]
                to_middle = jnp.exp(middle - column[parts[s], :])
                decay = jnp.concatenate([to_middle] * (size // HEAD), axis=1)
                decay *= jnp.exp(row[:, parts[t]] - middle)
            q, k, v = qkv_ref[0, parts[t], :], qkv_ref[1, parts[s], :], qkv_ref[2, parts[s], :]
            g = og_ref[parts[t], :]
            scores = lax.dot_general(k, q, AB_T, preferred_element_type=F32)
            grads = lax.dot_general(v, g, AB_T, preferred_element_type=F32)
            prob = (scores * decay).astype(BF16)
            score = (grads * decay).astype(BF16)
            dq = lax.dot_general(score, k, A_TB, preferred_element_type=F32)
            return dq, dot(score, q), dot(prob, g)

        a, b, c = pair(0, 0), pair(1, 0), pair(1, 1)
        live = lax.broadcasted_iota(jnp.int32, (tokens, HEAD), 0) < s[LEN]
        grads = (
            jnp.concatenate([a[0], b[0] + c[0]], axis=0) * scale,
            jnp.concatenate([a[1] + b[1], c[1]], axis=0) * scale,
            jnp.concatenate([a[2] + b[2], c[2]], axis=0) * scale,
        )
        until = jnp.exp(row[:, tokens - 1 : tokens] - column)
        rows = (
            og_ref[...].astype(F32) * (scale * jnp.exp(column)),
            qkv_ref[2].astype(F32) * until,
            qkv_ref[1].astype(F32) * until,
        )
        for j in range(3):
            out[j] = jnp.where(live, grads[j], 0.0).astype(BF16)
            ready[j] = jnp.where(live, rows[j], 0.0).astype(BF16)

    tile = pl.BlockSpec((3, tokens, HEAD), lambda h, s: (0, 0, h + first))
    in_specs = [tile, pl.BlockSpec((tokens, HEAD), lambda h, s: (0, h + first)), whole(cumul)]
    operands = [qkv, out_grad, cumul]
    if so_far is not None:
        in_specs += [pl.BlockSpec(memory_space=pl.ANY)] * 2
        operands += so_far
    return call(
        "local_grads",
        body,
        table,
        (count,),
        operands,
        in_specs,
        [shape(qkv.shape), shape(qkv.shape)],
        [tile, tile],
        12,
        alias=None if so_far is None else {4: 0, 5: 1},
    )


def whole_grads(table, which, local, ready, states):
    tokens = local.shape[1]
    heads = local.shape[2] // HEAD

    def body(s, local_ref, ready_ref, a, b, c, d, left, right, held):
        h = pl.program_id(0)

        @pl.when(h == 0)
        def _():
            in_order((a, b, c, d), s[Y], held)

        base = pl.multiple_of((s[Z] ^ which) * HEAD, HEAD)
        coming = held[h, pl.ds(base, HEAD), :]
        later = held[h, pl.ds(2 * HEAD + base, HEAD), :]
        cross = (
            lax.dot_general(ready_ref[0], coming, AB_T, preferred_element_type=F32),
            lax.dot_general(ready_ref[1], later, AB_T, preferred_element_type=F32),
            dot(ready_ref[2], later),
        )
        grads = [(local_ref[j].astype(F32) + cross[j]).astype(BF16) for j in range(3)]
        for k in range(heads):

            @pl.when(h == k)
            def _(k=k):
                for j in range(3):
                    start = (2 * j + k % 2) * HEAD
                    (left, right)[k // 2][:, start : start + HEAD] = grads[j]

    tile = pl.BlockSpec((3, tokens, HEAD), lambda h, s: (0, 0, h))
    side = shape((tokens, 3 * heads * HEAD // 2))
    return call(
        "whole_grads",
        body,
        table,
        (heads,),
        (local, ready, *states),
        [tile, tile, *[whole(m) for m in states]],
        [side, side],
        [whole(side)] * 2,
        12,
        [pltpu.VMEM((4, *states[0].shape), BF16)],
    )


def turn(table, shards, base, so_far):
    flat = [part for x in shards for part in x]
    tokens, width = sum(part.shape[0] for part in shards[0]), flat[0].shape[1]
    n, rows = len(shards), 4 * width // 32

    def body(s, *refs):
        out, at = refs[-1], 0
        for k, x in enumerate(shards):
            mine, at = refs[at : at + len(x)], at + len(x)

            @pl.when(pl.program_id(0) == k)
            def _(mine=mine):
                out[...] = joined(mine).T.reshape(out.shape)

    def place(i, s):
        i = s[TEN] ^ (base + i)
        return i % 2, (i // 2) ^ s[Z], 0, 0

    out = shape((16, 2, rows, tokens))
    spec = pl.BlockSpec((8, 1, rows, tokens), place)
    operands, in_specs = list(flat), [whole(x) for x in flat]
    if so_far is not None:
        operands.append(so_far)
        in_specs.append(pl.BlockSpec(memory_space=pl.ANY))
    return call(
        "turn",
        body,
        table,
        (n,),
        operands,
        in_specs,
        out,
        spec,
        12,
        alias=None if so_far is None else {len(flat) + 1: 0},
    )


def weight_part(table, turned, lefts, rights, places, split):
    tokens, cols = lefts[0].shape
    rows = turned[0].shape[2]

    def body(s, own_x, own_y, pair_x, pair_y, left_a, left_b, right_a, right_b, *outs):
        r = pl.program_id(0)
        for side, (a, b, ga, gb) in enumerate(
            ((own_x, pair_x, left_a, left_b), (own_y, pair_y, right_a, right_b))
        ):
            acc = dot(a[...].reshape(4 * rows, tokens), ga[...])
            acc += dot(b[...].reshape(4 * rows, tokens), gb[...])
            acc = acc.astype(BF16)
            if split:
                outs[2 * side][...] = acc[: 2 * rows]
                outs[2 * side + 1][...] = acc[2 * rows :]
                continue
            for k in range(len(places)):

                @pl.when(r == k)
                def _(k=k, acc=acc, side=side):
                    outs[side * len(places) + k][...] = acc

    step = places[1] - places[0] if len(places) > 1 else 0
    by_x = pl.BlockSpec((1, 4, rows, tokens), lambda r, s: (s[X] ^ (places[0] + step * r), 0, 0, 0))
    by_y = pl.BlockSpec((4, 1, rows, tokens), lambda r, s: (0, s[Y] ^ (places[0] + step * r), 0, 0))
    outs = [shape((2 * rows if split else 4 * rows, cols))] * (4 if split else 2 * len(places))
    operands = (turned[0], turned[0], turned[1], turned[1], *lefts, *rights)
    return call(
        "weight_part",
        body,
        table,
        (len(places),),
        operands,
        [by_x, by_y, by_x, by_y, *[whole(x) for x in (*lefts, *rights)]],
        outs,
        [whole(o) for o in outs],
        30,
    )


def add_halves(table, third, first_place, halves):
    up, down = halves
    near_up, near_down = third, first_place
    n, cols = up.shape

    def body(s, a, b, u, d, out_a, out_b):
        out_a[...] = (a[...].astype(F32) + u[...].astype(F32)).astype(BF16)
        out_b[...] = (b[...].astype(F32) + d[...].astype(F32)).astype(BF16)

    first = pl.BlockSpec((n, cols), lambda i, s: (0, 0))
    second = pl.BlockSpec((n, cols), lambda i, s: (1, 0))
    return call(
        "add_halves",
        body,
        table,
        (1,),
        (near_up, near_down, up, down),
        [first, second, first, first],
        [shape(near_up.shape), shape(near_down.shape)],
        [first, second],
        12,
        alias={1: 0, 2: 1},
    )


def cut_blocks(table, left, right):
    rows, cols = left[0].shape[0] // 4, left[0].shape[1]

    def body(s, *refs):
        for k, axis in enumerate((Y, X)):
            a, b, c = refs[3 * k : 3 * k + 3]
            for r, out in zip((1, 3, 2, 0), refs[6 + 4 * k : 10 + 4 * k]):
                at = pl.ds(pl.multiple_of((s[axis] ^ r) * rows, rows), rows)
                total = a[at, :].astype(F32) + b[at, :].astype(F32) + c[at, :].astype(F32)
                out[...] = total.astype(BF16)

    outs = [shape((rows, cols))] * 8
    operands = (*left, *right)
    cut = call(
        "cut_blocks",
        body,
        table,
        (1,),
        operands,
        [whole(x) for x in operands],
        outs,
        [whole(o) for o in outs],
        24,
    )
    return cut[:4], cut[4:]


def final_sums(table, sides):
    rows, cols = sides[0][0].shape

    def body(s, *refs):
        here, there = refs[-2:]
        for k in range(2):
            total = sum(ref[...].astype(F32) for ref in refs[4 * k : 4 * k + 4]).astype(BF16)
            here[k] = total[: rows // 2]
            there[k] = total[rows // 2 :]

    operands = [x for side in sides for x in side]
    outs = [shape((2, rows // 2, cols))] * 2
    return call(
        "final_sums",
        body,
        table,
        (1,),
        operands,
        [whole(x) for x in operands],
        outs,
        [whole(o) for o in outs],
        12,
    )


def finish(table, here, there):
    _, rows, cols = here.shape
    side = cols // 3

    def body(s, here_ref, there_ref, out):
        for ref, half in ((here_ref, s[Z]), (there_ref, 1 - s[Z])):
            for k in range(2):
                for j in range(3):
                    at = pl.ds(pl.multiple_of(half * 2 * side + k * side, side), side)
                    out[j, :, at] = ref[k, :, j * side : (j + 1) * side].astype(F32)

    out = shape((3, rows, 4 * side), F32)
    operands = (here, there)
    return call("finish", body, table, (1,), operands, [whole(here)] * 2, out, whole(out), 8)


def swaps(pieces, left, right):
    a, c = send(pieces[0], left, 1), send(pieces[2], right, 1)
    b, d = send(pieces[1], left, 3), send(pieces[3], right, 3)
    return [a, b], [c, d]


def device_part(activations, qkv_weight, log_decay, lengths, out_grad):
    tied = lax.optimization_barrier
    tokens = activations.shape[0]
    heads = log_decay.shape[1]
    per = heads // 2
    index = [lax.axis_index(a) for a in ("c0", "c1", "c2", "zl", "co")]
    here_z = index[0]
    fixed = [*index, index[3] * 2 + index[4]]
    table = jnp.stack([*fixed, lengths[0]]).astype(jnp.int32)
    weight = pltpu.with_memory_space_constraint(jnp.transpose(qkv_weight, (1, 0, 2)), pltpu.HBM)
    width = per * HEAD

    half = tokens // 2
    rows = [activations[:half], activations[half:]]
    near = [send(x, "zl", 1) for x in rows]
    side = [across(x) for x in rows]
    core = send(activations, "co", 1)

    live = (jnp.arange(tokens, dtype=jnp.int32) < lengths[0]).astype(F32)
    cumul = jnp.cumsum(log_decay.T * live[None, :], axis=1)
    size = jnp.broadcast_to(lengths.astype(F32)[:, None], (per, tokens))
    note = jnp.concatenate([lax.dynamic_slice_in_dim(cumul, (1 - here_z) * per, per), size])
    og_own = lax.dynamic_slice_in_dim(out_grad, here_z * width, width, axis=1)
    og_other = lax.dynamic_slice_in_dim(out_grad, (1 - here_z) * width, width, axis=1)

    acc_own = project(table, [[activations], [core]], (0, 1), weight, None, False)
    turned = turn(table, [[activations], [core]], 0, None)
    near, side, acc_own, note, og_other, turned = tied((near, side, acc_own, note, og_other, turned))
    note = send(note, "c0", 1)
    far = [send(side[0], "zl", 1), across(near[1])]
    near_core = [send(x, "co", 1) for x in near]
    side_core = [send(x, "co", 1) for x in side]
    qkv_own = project(table, [near, near_core], (2, 3), weight, acc_own, True)
    side_core, qkv_own = tied((side_core, qkv_own))
    acc_pair = project(table, [side, side_core], (2, 3), weight, None, False)
    note, far, acc_pair = tied((note, far, acc_pair))
    cumul = jnp.concatenate([lax.dynamic_slice_in_dim(cumul, here_z * per, per), note[:per]])
    table_pair = jnp.stack([*fixed, note[per, 0].astype(jnp.int32)]).astype(jnp.int32)
    far_core = [send(x, "co", 1) for x in far]
    og_pair = send(tied((og_other, far))[0], "c0", 1)
    to_y = shard_states(table, qkv_own, og_own, cumul, 0, None)
    far_core, to_y = tied((far_core, to_y))
    qkv_pair = project(table_pair, [far, far_core], (0, 1), weight, acc_pair, True)
    turned = [turn(table, tied(([near, near_core], qkv_pair))[0], 2, turned)]
    og_pair, qkv_pair, turned = tied((og_pair, qkv_pair, turned))

    to_y = shard_states(table, qkv_pair, og_pair, cumul, 1, to_y)
    at_y = [send(to_y[r], "c2", r) for r in (1, 3, 2)]
    qkv_own, _ = tied((qkv_own, to_y[0]))
    local_own = local_grads(table, qkv_own, og_own, cumul, 0, 0, per, None)
    at_y, local_own = tied((at_y, local_own))
    before, after, prior, later, ring = ring_y(table, [to_y[0], at_y[0], at_y[2], at_y[1]])
    at_x = [send(ring, "c1", r) for r in (1, 3, 2)]
    qkv_pair, _ = tied((qkv_pair, ring))
    local = local_grads(table_pair, qkv_pair, og_pair, cumul, 1, 0, per // 2, None)
    at_x, local = tied((at_x, local))
    back = arrivals(table, [ring, at_x[0], at_x[2], at_x[1]], before, after, prior, later)
    states = [send(back[r], "c2", r) for r in (1, 3, 2)]
    local, _ = tied((local, back[0]))
    local = local_grads(table_pair, qkv_pair, og_pair, cumul, 1, per // 2, per // 2, local)
    second, _ = tied(([far, far_core, side, side_core], back[0]))
    turned.append(turn(table, second, 0, None))
    states, turned, local = tied((states, turned, local))
    states = [back[0], states[0], states[2], states[1]]
    turned = [t.reshape(4, 4, -1, tokens) for t in turned]

    left_own, right_own = whole_grads(table, 0, *local_own, states)
    left_pair, right_pair = whole_grads(table, 1, *local, states)
    lefts, rights = (left_own, left_pair), (right_own, right_pair)
    far_piece = weight_part(table, turned, lefts, rights, (2,), True)
    l_half, r_half = swaps(far_piece, "c1", "c2")
    turned, _ = tied((turned, far_piece[0]))
    l_one, l_three, r_one, r_three = weight_part(table, turned, lefts, rights, (1, 3), False)
    l_half, l_one = tied((l_half, l_one))
    l_three, l_one = add_halves(table, l_three, l_one, l_half)
    l_got = [send(l_one, "c1", 1), send(l_three, "c1", 3)]
    r_half, _ = tied((r_half, l_one))
    r_three, r_one = add_halves(table, r_three, r_one, r_half)
    r_got = [send(r_one, "c2", 1), send(r_three, "c2", 3)]
    turned, _ = tied((turned, r_one))
    own = weight_part(table, turned, lefts, rights, (0,), False)
    l_got, own = tied((l_got, own))
    l_cut, r_cut = cut_blocks(table, (own[0], *l_got), (own[1], *r_got))
    l_got = [send(x, "c2", by) for x, by in zip(l_cut, (1, 3, 2))]
    r_got = [send(x, "c1", by) for x, by in zip(r_cut, (1, 3, 2))]
    here, there = final_sums(table, ((l_cut[3], *l_got), (r_cut[3], *r_got)))
    there = send(there, "c0", 1)
    return jnp.transpose(finish(table, here, there), (1, 0, 2))


def solution(mesh):
    finer = Mesh(mesh.devices.reshape(2, 4, 4, 2, 2), ("c0", "c1", "c2", "zl", "co"))
    context, tensor = ("c0", "c1", "c2"), ("zl", "co")
    placed = (
        P(context, tensor),
        P(None, None, tensor),
        P(context, tensor),
        P(context),
        P(context, tensor),
    )
    return jax.shard_map(
        device_part,
        mesh=finer,
        in_specs=placed,
        out_specs=P(context, None, tensor),
        check_vma=False,
    )
```

```python
import jax
import jax.numpy as jnp
from jax import lax
from jax.experimental import pallas as pl
from jax.experimental.pallas import tpu as pltpu
from jax.sharding import Mesh
from jax.sharding import PartitionSpec as P

F32 = jnp.float32
BF16 = jnp.bfloat16
HEAD = 128
Z, X, Y, ZL, CO, TEN, LEN = range(7)
AB_T = (((1,), (1,)), ((), ()))
A_TB = (((0,), (0,)), ((), ()))


def dot(a, b):
    return jnp.dot(a, b, preferred_element_type=F32)


def send(x, axis, by):
    return lax.ppermute(x, axis, [(i, i ^ by) for i in range(lax.axis_size(axis))])


def across(x):
    return lax.ppermute(x, ("c0", "zl"), [(0, 3), (1, 2), (2, 1), (3, 0)])


def whole(x):
    return pl.BlockSpec(x.shape, lambda *_, n=len(x.shape): (0,) * n)


def call(name, body, table, grid, operands, in_specs, outs, out_specs, mib, scratch=(), alias=None):
    return pl.pallas_call(
        body,
        grid_spec=pltpu.PrefetchScalarGridSpec(
            num_scalar_prefetch=1,
            grid=grid,
            in_specs=in_specs,
            out_specs=out_specs,
            scratch_shapes=scratch,
        ),
        out_shape=outs,
        input_output_aliases=alias or {},
        compiler_params=pltpu.CompilerParams(
            dimension_semantics=("arbitrary",) * len(grid), vmem_limit_bytes=mib << 20
        ),
        cost_estimate=pl.CostEstimate(flops=1, bytes_accessed=1, transcendentals=0),
        name=name,
    )(table, *operands)


def shape(dims, kind=BF16):
    return jax.ShapeDtypeStruct(dims, kind)


def joined(refs):
    parts = [ref[...] for ref in refs]
    return parts[0] if len(parts) == 1 else jnp.concatenate(parts, axis=0)


def project(table, shards, flips, weight, partial, last):
    n, counts = len(shards), [len(x) for x in shards]
    flat = [part for x in shards for part in x]
    tokens, width = sum(part.shape[0] for part in shards[0]), flat[0].shape[1]
    cols = weight.shape[2] // 2

    def body(s, *refs):
        out, rest = refs[-1], list(refs)
        acc = None
        for i, count in enumerate(counts):
            rows = joined([rest.pop(0) for _ in range(count)])
            term = dot(rows, refs[len(flat) + i][0])
            acc = term if acc is None else acc + term
        if partial is not None:
            acc += refs[len(flat) + n][0]
        if last:
            row = lax.broadcasted_iota(jnp.int32, acc.shape, 0)
            acc = jnp.where(row < s[LEN], acc, 0.0)
        out[0] = acc.astype(out.dtype)

    tile = pl.BlockSpec((1, tokens, cols), lambda g, s: (g, 0, 0))
    in_specs = [whole(x) for x in flat]
    for flip in flips:
        in_specs.append(
            pl.BlockSpec((1, width, cols), lambda g, s, flip=flip: (g, s[TEN] ^ flip, s[Z]))
        )
    operands = [*flat, *([weight] * n)]
    if partial is not None:
        in_specs.append(tile)
        operands.append(partial)
    out = shape((3, tokens, cols), BF16 if last else F32)
    return call("project", body, table, (3,), operands, in_specs, out, tile, 24)


def shard_states(table, qkv, out_grad, cumul, which, so_far):
    tokens = qkv.shape[1]
    heads = qkv.shape[2] // HEAD
    scale = HEAD**-0.5

    def body(s, qkv_ref, og_ref, cum_ref, *refs):
        outs = refs[-4:]
        r = pl.program_id(0)
        row = cum_ref[pl.ds(which * heads + (s[Y] ^ r), 1), :]
        total = row[:, tokens - 1 : tokens]
        keys_t = qkv_ref[1].T.astype(F32)
        query_t = qkv_ref[0].T.astype(F32)
        keys_t = (keys_t * jnp.exp(total - row)).astype(BF16)
        query_t = (query_t * (scale * jnp.exp(row))).astype(BF16)
        states = (dot(keys_t, qkv_ref[2]), dot(query_t, og_ref[...]))
        at = lax.broadcasted_iota(jnp.int32, (16, HEAD), 0)
        tail = jnp.broadcast_to(total, (16, HEAD)).astype(BF16)
        for k, out in enumerate(outs):

            @pl.when(r == k)
            def _(k=k, out=out):
                here = s[Z] ^ which
                if so_far is not None:
                    out[...] = refs[k][...]
                for kind in range(2):
                    start = pl.multiple_of((2 * kind + here) * HEAD, HEAD)
                    out[pl.ds(start, HEAD), :] = states[kind].astype(BF16)
                if so_far is None:
                    out[4 * HEAD :, :] = tail
                else:
                    out[4 * HEAD :, :] = jnp.where(at == here, tail, refs[k][4 * HEAD :, :])

    message = shape((4 * HEAD + 16, HEAD))
    operands = [qkv, out_grad, cumul, *(so_far or ())]
    in_specs = [
        pl.BlockSpec((3, tokens, HEAD), lambda r, s: (0, 0, s[Y] ^ r)),
        pl.BlockSpec((tokens, HEAD), lambda r, s: (0, s[Y] ^ r)),
        whole(cumul),
        *[whole(m) for m in so_far or ()],
    ]
    return call(
        "shard_states",
        body,
        table,
        (4,),
        operands,
        in_specs,
        [message] * 4,
        [whole(message)] * 4,
        12,
    )


def in_order(refs, place, held):
    for r, ref in enumerate(refs):
        held[place ^ r] = ref[...]


def spread(pair):
    wide = [jnp.broadcast_to(pair[i : i + 1, :], (HEAD, HEAD)) for i in range(2)]
    return jnp.concatenate(wide, axis=0)


def ring_y(table, messages):
    half = 2 * HEAD

    def body(s, a, b, c, d, before, after, prior, later, out, held):
        in_order((a, b, c, d), s[Y], held)
        totals = [held[t, 2 * half : 2 * half + 16, :].astype(F32)[:2] for t in range(4)]
        run = jnp.zeros((half, HEAD), F32)
        reach = jnp.zeros((2, HEAD), F32)
        for t in range(4):
            before[t] = run
            prior[t] = jnp.exp(reach)
            run = spread(jnp.exp(totals[t])) * run + held[t, :half, :].astype(F32)
            reach = reach + totals[t]
        out[:half, :] = run.astype(BF16)
        total = reach
        run = jnp.zeros((half, HEAD), F32)
        reach = jnp.zeros((2, HEAD), F32)
        for t in range(3, -1, -1):
            after[t] = run
            later[t] = jnp.exp(reach)
            run = spread(jnp.exp(totals[t])) * run + held[t, half : 2 * half, :].astype(F32)
            reach = reach + totals[t]
        out[half : 2 * half, :] = run.astype(BF16)
        high = total.astype(BF16).astype(F32)
        low = total - high
        at = lax.broadcasted_iota(jnp.int32, (16, HEAD), 0)
        tail = jnp.where(at == 0, high[0:1], high[1:2])
        tail = jnp.where(at == 2, low[0:1], tail)
        tail = jnp.where(at == 3, low[1:2], tail)
        out[2 * half :, :] = tail.astype(BF16)

    outs = [
        shape((4, half, HEAD), F32),
        shape((4, half, HEAD), F32),
        shape((4, 2, HEAD), F32),
        shape((4, 2, HEAD), F32),
        shape(messages[0].shape),
    ]
    return call(
        "ring_y",
        body,
        table,
        (1,),
        messages,
        [whole(m) for m in messages],
        outs,
        [whole(o) for o in outs],
        8,
        [pltpu.VMEM((4, *messages[0].shape), BF16)],
    )


def arrivals(table, messages, before, after, prior, later):
    half = 2 * HEAD

    def body(s, a, b, c, d, before_ref, after_ref, prior_ref, later_ref, *rest):
        outs, held, mine, edges = rest[:4], *rest[4:]
        in_order((a, b, c, d), s[X], held)
        tails = [held[t, 2 * half : 2 * half + 16, :].astype(F32) for t in range(4)]
        totals = [tail[0:2] + tail[2:4] for tail in tails]
        ends = []
        for kind, steps in ((0, range(4)), (1, range(3, -1, -1))):
            run = jnp.zeros((half, HEAD), F32)
            reach = jnp.zeros((2, HEAD), F32)
            for t in steps:

                @pl.when(s[X] == t)
                def _(run=run, reach=reach, kind=kind):
                    mine[kind] = run
                    edges[kind] = jnp.exp(reach)

                rows = held[t, kind * half : (kind + 1) * half, :].astype(F32)
                run = spread(jnp.exp(totals[t])) * run + rows
                reach = reach + totals[t]
            ends.append(run.astype(BF16).astype(F32))
        nothing = jnp.zeros((HEAD, HEAD), F32)
        across_up = jnp.concatenate([nothing, ends[0][:HEAD]], axis=0)
        across_down = jnp.concatenate([ends[1][HEAD:], nothing], axis=0)
        start = mine[0] + spread(edges[0]) * across_up
        finish = mine[1] + spread(edges[1]) * across_down
        for r, out in enumerate(outs):
            t = s[Y] ^ r
            out[:half, :] = (before_ref[t] + spread(prior_ref[t]) * start).astype(BF16)
            out[half:, :] = (after_ref[t] + spread(later_ref[t]) * finish).astype(BF16)

    operands = (*messages, before, after, prior, later)
    message = shape((2 * half, HEAD))
    return call(
        "arrivals",
        body,
        table,
        (1,),
        operands,
        [whole(m) for m in operands],
        [message] * 4,
        [whole(message)] * 4,
        8,
        [
            pltpu.VMEM((4, *messages[0].shape), BF16),
            pltpu.VMEM((2, half, HEAD), F32),
            pltpu.VMEM((2, 2, HEAD), F32),
        ],
    )


def column_of(row):
    return jnp.broadcast_to(row, (HEAD, row.shape[1])).T


def local_grads(table, qkv, out_grad, cumul, which, first, count, so_far):
    tokens = qkv.shape[1]
    heads = qkv.shape[2] // HEAD
    scale = HEAD**-0.5
    size = tokens // 2

    def body(s, qkv_ref, og_ref, cum_ref, *refs):
        out, ready = refs[-2:]
        row = cum_ref[pl.ds(pl.program_id(0) + which * heads + first, 1), :]
        column = column_of(row)
        wide = jnp.concatenate([column] * (size // HEAD), axis=1)
        s_at = lax.broadcasted_iota(jnp.int32, (size, size), 0)
        t_at = lax.broadcasted_iota(jnp.int32, (size, size), 1)
        parts = [slice(0, size), slice(size, tokens)]

        def pair(t, s):
            if t == s:
                gap = row[:, parts[t]] - wide[parts[s], :]
                decay = jnp.exp(jnp.where(s_at <= t_at, gap, -jnp.inf))
            else:
                middle = row[:, size - 1 : size]
                to_middle = jnp.exp(middle - column[parts[s], :])
                decay = jnp.concatenate([to_middle] * (size // HEAD), axis=1)
                decay *= jnp.exp(row[:, parts[t]] - middle)
            q, k, v = qkv_ref[0, parts[t], :], qkv_ref[1, parts[s], :], qkv_ref[2, parts[s], :]
            g = og_ref[parts[t], :]
            scores = lax.dot_general(k, q, AB_T, preferred_element_type=F32)
            grads = lax.dot_general(v, g, AB_T, preferred_element_type=F32)
            prob = (scores * decay).astype(BF16)
            score = (grads * decay).astype(BF16)
            dq = lax.dot_general(score, k, A_TB, preferred_element_type=F32)
            return dq, dot(score, q), dot(prob, g)

        a, b, c = pair(0, 0), pair(1, 0), pair(1, 1)
        live = lax.broadcasted_iota(jnp.int32, (tokens, HEAD), 0) < s[LEN]
        grads = (
            jnp.concatenate([a[0], b[0] + c[0]], axis=0) * scale,
            jnp.concatenate([a[1] + b[1], c[1]], axis=0) * scale,
            jnp.concatenate([a[2] + b[2], c[2]], axis=0) * scale,
        )
        until = jnp.exp(row[:, tokens - 1 : tokens] - column)
        rows = (
            og_ref[...].astype(F32) * (scale * jnp.exp(column)),
            qkv_ref[2].astype(F32) * until,
            qkv_ref[1].astype(F32) * until,
        )
        for j in range(3):
            out[j] = jnp.where(live, grads[j], 0.0).astype(BF16)
            ready[j] = jnp.where(live, rows[j], 0.0).astype(BF16)

    tile = pl.BlockSpec((3, tokens, HEAD), lambda h, s: (0, 0, h + first))
    in_specs = [tile, pl.BlockSpec((tokens, HEAD), lambda h, s: (0, h + first)), whole(cumul)]
    operands = [qkv, out_grad, cumul]
    if so_far is not None:
        in_specs += [pl.BlockSpec(memory_space=pl.ANY)] * 2
        operands += so_far
    return call(
        "local_grads",
        body,
        table,
        (count,),
        operands,
        in_specs,
        [shape(qkv.shape), shape(qkv.shape)],
        [tile, tile],
        12,
        alias=None if so_far is None else {4: 0, 5: 1},
    )


def whole_grads(table, which, local, ready, states):
    tokens = local.shape[1]
    heads = local.shape[2] // HEAD

    def body(s, local_ref, ready_ref, a, b, c, d, left, right, held):
        h = pl.program_id(0)

        @pl.when(h == 0)
        def _():
            in_order((a, b, c, d), s[Y], held)

        base = pl.multiple_of((s[Z] ^ which) * HEAD, HEAD)
        coming = held[h, pl.ds(base, HEAD), :]
        later = held[h, pl.ds(2 * HEAD + base, HEAD), :]
        cross = (
            lax.dot_general(ready_ref[0], coming, AB_T, preferred_element_type=F32),
            lax.dot_general(ready_ref[1], later, AB_T, preferred_element_type=F32),
            dot(ready_ref[2], later),
        )
        grads = [(local_ref[j].astype(F32) + cross[j]).astype(BF16) for j in range(3)]
        for k in range(heads):

            @pl.when(h == k)
            def _(k=k):
                for j in range(3):
                    start = (2 * j + k % 2) * HEAD
                    (left, right)[k // 2][:, start : start + HEAD] = grads[j]

    tile = pl.BlockSpec((3, tokens, HEAD), lambda h, s: (0, 0, h))
    side = shape((tokens, 3 * heads * HEAD // 2))
    return call(
        "whole_grads",
        body,
        table,
        (heads,),
        (local, ready, *states),
        [tile, tile, *[whole(m) for m in states]],
        [side, side],
        [whole(side)] * 2,
        12,
        [pltpu.VMEM((4, *states[0].shape), BF16)],
    )


def turn(table, shards):
    counts = [len(x) for x in shards]
    flat = [part for x in shards for part in x]
    tokens, width = sum(part.shape[0] for part in shards[0]), flat[0].shape[1]
    rows = 4 * width // 32

    def body(s, *refs):
        out, at = refs[-1], 0
        for k, count in enumerate(counts):
            mine, at = refs[at : at + count], at + count

            @pl.when((pl.program_id(0) ^ s[TEN]) == k)
            def _(mine=mine):
                out[...] = joined(mine).T.reshape(out.shape)

    out = shape((16, 2, rows, tokens))
    spec = pl.BlockSpec((8, 1, rows, tokens), lambda i, s: (i % 2, (i // 2) ^ s[Z], 0, 0))
    turned = call("turn", body, table, (4,), flat, [whole(x) for x in flat], out, spec, 12)
    return turned.reshape(4, 4, 2 * rows, tokens)


def weight_part(table, turned, lefts, rights, places, split):
    tokens, cols = lefts[0].shape
    rows = turned[0].shape[2]

    def body(s, own_x, own_y, pair_x, pair_y, left_a, left_b, right_a, right_b, *outs):
        r = pl.program_id(0)
        for side, (a, b, ga, gb) in enumerate(
            ((own_x, pair_x, left_a, left_b), (own_y, pair_y, right_a, right_b))
        ):
            acc = dot(a[...].reshape(4 * rows, tokens), ga[...])
            acc += dot(b[...].reshape(4 * rows, tokens), gb[...])
            acc = acc.astype(BF16)
            if split:
                outs[2 * side][...] = acc[: 2 * rows]
                outs[2 * side + 1][...] = acc[2 * rows :]
                continue
            for k in range(len(places)):

                @pl.when(r == k)
                def _(k=k, acc=acc, side=side):
                    outs[side * len(places) + k][...] = acc

    step = places[1] - places[0] if len(places) > 1 else 0
    by_x = pl.BlockSpec((1, 4, rows, tokens), lambda r, s: (s[X] ^ (places[0] + step * r), 0, 0, 0))
    by_y = pl.BlockSpec((4, 1, rows, tokens), lambda r, s: (0, s[Y] ^ (places[0] + step * r), 0, 0))
    outs = [shape((2 * rows if split else 4 * rows, cols))] * (4 if split else 2 * len(places))
    operands = (turned[0], turned[0], turned[1], turned[1], *lefts, *rights)
    return call(
        "weight_part",
        body,
        table,
        (len(places),),
        operands,
        [by_x, by_y, by_x, by_y, *[whole(x) for x in (*lefts, *rights)]],
        outs,
        [whole(o) for o in outs],
        30,
    )


def add_halves(table, third, first_place, halves):
    up, down = halves
    near_up, near_down = third, first_place
    n, cols = up.shape

    def body(s, a, b, u, d, out_a, out_b):
        out_a[...] = (a[...].astype(F32) + u[...].astype(F32)).astype(BF16)
        out_b[...] = (b[...].astype(F32) + d[...].astype(F32)).astype(BF16)

    first = pl.BlockSpec((n, cols), lambda i, s: (0, 0))
    second = pl.BlockSpec((n, cols), lambda i, s: (1, 0))
    return call(
        "add_halves",
        body,
        table,
        (1,),
        (near_up, near_down, up, down),
        [first, second, first, first],
        [shape(near_up.shape), shape(near_down.shape)],
        [first, second],
        12,
        alias={1: 0, 2: 1},
    )


def cut_blocks(table, left, right):
    rows, cols = left[0].shape[0] // 4, left[0].shape[1]

    def body(s, *refs):
        for k, axis in enumerate((Y, X)):
            a, b, c = refs[3 * k : 3 * k + 3]
            for r, out in zip((1, 3, 2, 0), refs[6 + 4 * k : 10 + 4 * k]):
                at = pl.ds(pl.multiple_of((s[axis] ^ r) * rows, rows), rows)
                total = a[at, :].astype(F32) + b[at, :].astype(F32) + c[at, :].astype(F32)
                out[...] = total.astype(BF16)

    outs = [shape((rows, cols))] * 8
    operands = (*left, *right)
    cut = call(
        "cut_blocks",
        body,
        table,
        (1,),
        operands,
        [whole(x) for x in operands],
        outs,
        [whole(o) for o in outs],
        24,
    )
    return cut[:4], cut[4:]


def final_sums(table, sides):
    rows, cols = sides[0][0].shape

    def body(s, *refs):
        here, there = refs[-2:]
        for k in range(2):
            total = sum(ref[...].astype(F32) for ref in refs[4 * k : 4 * k + 4]).astype(BF16)
            here[k] = total[: rows // 2]
            there[k] = total[rows // 2 :]

    operands = [x for side in sides for x in side]
    outs = [shape((2, rows // 2, cols))] * 2
    return call(
        "final_sums",
        body,
        table,
        (1,),
        operands,
        [whole(x) for x in operands],
        outs,
        [whole(o) for o in outs],
        12,
    )


def finish(table, here, there):
    _, rows, cols = here.shape
    side = cols // 3

    def body(s, here_ref, there_ref, out):
        for ref, half in ((here_ref, s[Z]), (there_ref, 1 - s[Z])):
            for k in range(2):
                for j in range(3):
                    at = pl.ds(pl.multiple_of(half * 2 * side + k * side, side), side)
                    out[j, :, at] = ref[k, :, j * side : (j + 1) * side].astype(F32)

    out = shape((3, rows, 4 * side), F32)
    operands = (here, there)
    return call("finish", body, table, (1,), operands, [whole(here)] * 2, out, whole(out), 8)


def swaps(pieces, left, right):
    a, c = send(pieces[0], left, 1), send(pieces[2], right, 1)
    b, d = send(pieces[1], left, 3), send(pieces[3], right, 3)
    return [a, b], [c, d]


def device_part(activations, qkv_weight, log_decay, lengths, out_grad):
    tied = lax.optimization_barrier
    tokens = activations.shape[0]
    heads = log_decay.shape[1]
    per = heads // 2
    index = [lax.axis_index(a) for a in ("c0", "c1", "c2", "zl", "co")]
    here_z = index[0]
    fixed = [*index, index[3] * 2 + index[4]]
    table = jnp.stack([*fixed, lengths[0]]).astype(jnp.int32)
    weight = pltpu.with_memory_space_constraint(jnp.transpose(qkv_weight, (1, 0, 2)), pltpu.HBM)

    near = send(activations, "zl", 1)
    side = across(activations)
    core = send(activations, "co", 1)

    live = (jnp.arange(tokens, dtype=jnp.int32) < lengths[0]).astype(F32)
    cumul = jnp.cumsum(log_decay.T * live[None, :], axis=1)
    size = jnp.broadcast_to(lengths.astype(F32)[:, None], (per, tokens))
    note = jnp.concatenate([lax.dynamic_slice_in_dim(cumul, (1 - here_z) * per, per), size])
    note = send(note, "c0", 1)
    width = per * HEAD
    og_own = lax.dynamic_slice_in_dim(out_grad, here_z * width, width, axis=1)
    og_other = lax.dynamic_slice_in_dim(out_grad, (1 - here_z) * width, width, axis=1)

    acc_own = project(table, [[activations], [core]], (0, 1), weight, None, False)
    near, side, acc_own, note, og_other = tied((near, side, acc_own, note, og_other))
    half = tokens // 2
    far = [send(side[:half], "zl", 1), across(near[half:])]
    near_core = send(near, "co", 1)
    side_core = send(side, "co", 1)
    cumul = jnp.concatenate([lax.dynamic_slice_in_dim(cumul, here_z * per, per), note[:per]])
    table_pair = jnp.stack([*fixed, note[per, 0].astype(jnp.int32)]).astype(jnp.int32)
    qkv_own = project(table, [[near], [near_core]], (2, 3), weight, acc_own, True)
    turned = [turn(table, tied(([[activations], [core], [near], [near_core]], qkv_own))[0])]
    far, side_core, qkv_own, table_pair, cumul, turned = tied(
        (far, side_core, qkv_own, table_pair, cumul, turned)
    )
    far_core = [send(x, "co", 1) for x in far]
    og_pair = send(tied((og_other, far))[0], "c0", 1)
    local_own = local_grads(table, qkv_own, og_own, cumul, 0, 0, per // 2, None)
    far_core, local_own = tied((far_core, local_own))
    qkv_pair = project(
        table_pair, [[side], [side_core], far, far_core], (2, 3, 0, 1), weight, None, True
    )
    qkv_own, _ = tied((qkv_own, qkv_pair))
    to_y = shard_states(table, qkv_own, og_own, cumul, 0, None)
    og_pair, qkv_pair, to_y = tied((og_pair, qkv_pair, to_y))

    to_y = shard_states(table, qkv_pair, og_pair, cumul, 1, to_y)
    at_y = [send(to_y[r], "c2", r) for r in (1, 3, 2)]
    qkv_own, _ = tied((qkv_own, to_y[0]))
    local_own = local_grads(table, qkv_own, og_own, cumul, 0, per // 2, per // 2, local_own)
    at_y, local_own = tied((at_y, local_own))
    before, after, prior, later, ring = ring_y(table, [to_y[0], at_y[0], at_y[2], at_y[1]])
    at_x = [send(ring, "c1", r) for r in (1, 3, 2)]
    qkv_pair, _ = tied((qkv_pair, ring))
    local = local_grads(table_pair, qkv_pair, og_pair, cumul, 1, 0, per // 2, None)
    at_x, local = tied((at_x, local))
    back = arrivals(table, [ring, at_x[0], at_x[2], at_x[1]], before, after, prior, later)
    states = [send(back[r], "c2", r) for r in (1, 3, 2)]
    local, _ = tied((local, back[0]))
    local = local_grads(table_pair, qkv_pair, og_pair, cumul, 1, per // 2, per // 2, local)
    second, _ = tied(([far, far_core, [side], [side_core]], back[0]))
    turned.append(turn(table, second))
    states, turned, local = tied((states, turned, local))
    states = [back[0], states[0], states[2], states[1]]

    left_own, right_own = whole_grads(table, 0, *local_own, states)
    left_pair, right_pair = whole_grads(table, 1, *local, states)
    lefts, rights = (left_own, left_pair), (right_own, right_pair)
    far_piece = weight_part(table, turned, lefts, rights, (2,), True)
    l_half, r_half = swaps(far_piece, "c1", "c2")
    turned, _ = tied((turned, far_piece[0]))
    l_one, l_three, r_one, r_three = weight_part(table, turned, lefts, rights, (1, 3), False)
    l_half, l_one = tied((l_half, l_one))
    l_three, l_one = add_halves(table, l_three, l_one, l_half)
    l_got = [send(l_one, "c1", 1), send(l_three, "c1", 3)]
    r_half, _ = tied((r_half, l_one))
    r_three, r_one = add_halves(table, r_three, r_one, r_half)
    r_got = [send(r_one, "c2", 1), send(r_three, "c2", 3)]
    turned, _ = tied((turned, r_one))
    own = weight_part(table, turned, lefts, rights, (0,), False)
    l_got, own = tied((l_got, own))
    l_cut, r_cut = cut_blocks(table, (own[0], *l_got), (own[1], *r_got))
    l_got = [send(x, "c2", by) for x, by in zip(l_cut, (1, 3, 2))]
    r_got = [send(x, "c1", by) for x, by in zip(r_cut, (1, 3, 2))]
    here, there = final_sums(table, ((l_cut[3], *l_got), (r_cut[3], *r_got)))
    there = send(there, "c0", 1)
    return jnp.transpose(finish(table, here, there), (1, 0, 2))


def solution(mesh):
    finer = Mesh(mesh.devices.reshape(2, 4, 4, 2, 2), ("c0", "c1", "c2", "zl", "co"))
    context, tensor = ("c0", "c1", "c2"), ("zl", "co")
    placed = (
        P(context, tensor),
        P(None, None, tensor),
        P(context, tensor),
        P(context),
        P(context, tensor),
    )
    return jax.shard_map(
        device_part,
        mesh=finer,
        in_specs=placed,
        out_specs=P(context, None, tensor),
        check_vma=False,
    )
```

```python
import jax
import jax.numpy as jnp
from jax import lax
from jax.experimental import pallas as pl
from jax.experimental.pallas import tpu as pltpu
from jax.sharding import Mesh
from jax.sharding import PartitionSpec as P

F32 = jnp.float32
BF16 = jnp.bfloat16
HEAD = 128
HEADS = 4
Z, X, Y, ZL, CO, TEN = range(6)
AB_T = (((1,), (1,)), ((), ()))
A_TB = (((0,), (0,)), ((), ()))


def dot(a, b):
    return jnp.dot(a, b, preferred_element_type=F32)


def send(x, axis, by):
    return lax.ppermute(x, axis, [(i, i ^ by) for i in range(lax.axis_size(axis))])


def across(x):
    return lax.ppermute(x, ("c0", "zl"), [(0, 3), (1, 2), (2, 1), (3, 0)])


def whole(x):
    return pl.BlockSpec(x.shape, lambda *_, n=len(x.shape): (0,) * n)


def call(name, body, table, grid, operands, in_specs, outs, out_specs, mib, scratch=(), alias=None):
    return pl.pallas_call(
        body,
        grid_spec=pltpu.PrefetchScalarGridSpec(
            num_scalar_prefetch=1,
            grid=grid,
            in_specs=in_specs,
            out_specs=out_specs,
            scratch_shapes=scratch,
        ),
        out_shape=outs,
        input_output_aliases=alias or {},
        compiler_params=pltpu.CompilerParams(
            dimension_semantics=("arbitrary",) * len(grid), vmem_limit_bytes=mib << 20
        ),
        cost_estimate=pl.CostEstimate(flops=1, bytes_accessed=1, transcendentals=0),
        name=name,
    )(table, *operands)


def shape(dims, kind=BF16):
    return jax.ShapeDtypeStruct(dims, kind)


def joined(refs):
    parts = [ref[...] for ref in refs]
    return parts[0] if len(parts) == 1 else jnp.concatenate(parts, axis=0)


def living(info, dims):
    row = lax.broadcasted_iota(jnp.int32, dims, 0).astype(F32)
    return row < info[HEADS : HEADS + 1, :1]


def project(table, shards, flips, weight, partial, info):
    last = info is not None
    n, counts = len(shards), [len(x) for x in shards]
    flat = [part for x in shards for part in x]
    tokens, width = sum(part.shape[0] for part in shards[0]), flat[0].shape[1]
    cols = weight.shape[2] // 2

    def body(s, *refs):
        out, rest = refs[-1], list(refs)
        acc = None
        for i, count in enumerate(counts):
            rows = joined([rest.pop(0) for _ in range(count)])
            term = dot(rows, refs[len(flat) + i][0])
            acc = term if acc is None else acc + term
        if partial is not None:
            acc += refs[len(flat) + n][0]
        if last:
            acc = jnp.where(living(refs[-2], acc.shape), acc, 0.0)
        out[0] = acc.astype(out.dtype)

    tile = pl.BlockSpec((1, tokens, cols), lambda g, s: (g, 0, 0))
    in_specs = [whole(x) for x in flat]
    for flip in flips:
        in_specs.append(
            pl.BlockSpec((1, width, cols), lambda g, s, flip=flip: (g, s[TEN] ^ flip, s[Z]))
        )
    operands = [*flat, *([weight] * n)]
    if partial is not None:
        in_specs.append(tile)
        operands.append(partial)
    if last:
        in_specs.append(whole(info))
        operands.append(info)
    out = shape((3, tokens, cols), BF16 if last else F32)
    return call("project", body, table, (3,), operands, in_specs, out, tile, 24)


def shard_states(table, qkv, out_grad, cumul, which, so_far):
    tokens = qkv.shape[1]
    scale = HEAD**-0.5

    def body(s, qkv_ref, og_ref, cum_ref, *refs):
        outs = refs[-4:]
        r = pl.program_id(0)
        row = cum_ref[pl.ds(s[Y] ^ r, 1), :]
        total = row[:, tokens - 1 : tokens]
        keys_t = qkv_ref[1].T.astype(F32)
        query_t = qkv_ref[0].T.astype(F32)
        keys_t = (keys_t * jnp.exp(total - row)).astype(BF16)
        query_t = (query_t * (scale * jnp.exp(row))).astype(BF16)
        states = (dot(keys_t, qkv_ref[2]), dot(query_t, og_ref[...]))
        at = lax.broadcasted_iota(jnp.int32, (16, HEAD), 0)
        tail = jnp.broadcast_to(total, (16, HEAD)).astype(BF16)
        for k, out in enumerate(outs):

            @pl.when(r == k)
            def _(k=k, out=out):
                here = s[Z] ^ which
                if so_far is not None:
                    out[...] = refs[k][...]
                for kind in range(2):
                    start = pl.multiple_of((2 * kind + here) * HEAD, HEAD)
                    out[pl.ds(start, HEAD), :] = states[kind].astype(BF16)
                if so_far is None:
                    out[4 * HEAD :, :] = tail
                else:
                    out[4 * HEAD :, :] = jnp.where(at == here, tail, refs[k][4 * HEAD :, :])

    message = shape((4 * HEAD + 16, HEAD))
    operands = [qkv, out_grad, cumul, *(so_far or ())]
    in_specs = [
        pl.BlockSpec((3, tokens, HEAD), lambda r, s: (0, 0, s[Y] ^ r)),
        pl.BlockSpec((tokens, HEAD), lambda r, s: (0, s[Y] ^ r)),
        whole(cumul),
        *[whole(m) for m in so_far or ()],
    ]
    return call(
        "shard_states",
        body,
        table,
        (4,),
        operands,
        in_specs,
        [message] * 4,
        [whole(message)] * 4,
        12,
    )


def in_order(refs, place, held):
    for r, ref in enumerate(refs):
        held[place ^ r] = ref[...]


def spread(pair):
    wide = [jnp.broadcast_to(pair[i : i + 1, :], (HEAD, HEAD)) for i in range(2)]
    return jnp.concatenate(wide, axis=0)


def ring_y(table, messages):
    half = 2 * HEAD

    def body(s, a, b, c, d, before, after, prior, later, out, held):
        in_order((a, b, c, d), s[Y], held)
        totals = [held[t, 2 * half : 2 * half + 16, :].astype(F32)[:2] for t in range(4)]
        run = jnp.zeros((half, HEAD), F32)
        reach = jnp.zeros((2, HEAD), F32)
        for t in range(4):
            before[t] = run
            prior[t] = jnp.exp(reach)
            run = spread(jnp.exp(totals[t])) * run + held[t, :half, :].astype(F32)
            reach = reach + totals[t]
        out[:half, :] = run.astype(BF16)
        total = reach
        run = jnp.zeros((half, HEAD), F32)
        reach = jnp.zeros((2, HEAD), F32)
        for t in range(3, -1, -1):
            after[t] = run
            later[t] = jnp.exp(reach)
            run = spread(jnp.exp(totals[t])) * run + held[t, half : 2 * half, :].astype(F32)
            reach = reach + totals[t]
        out[half : 2 * half, :] = run.astype(BF16)
        high = total.astype(BF16).astype(F32)
        low = total - high
        at = lax.broadcasted_iota(jnp.int32, (16, HEAD), 0)
        tail = jnp.where(at == 0, high[0:1], high[1:2])
        tail = jnp.where(at == 2, low[0:1], tail)
        tail = jnp.where(at == 3, low[1:2], tail)
        out[2 * half :, :] = tail.astype(BF16)

    outs = [
        shape((4, half, HEAD), F32),
        shape((4, half, HEAD), F32),
        shape((4, 2, HEAD), F32),
        shape((4, 2, HEAD), F32),
        shape(messages[0].shape),
    ]
    return call(
        "ring_y",
        body,
        table,
        (1,),
        messages,
        [whole(m) for m in messages],
        outs,
        [whole(o) for o in outs],
        8,
        [pltpu.VMEM((4, *messages[0].shape), BF16)],
    )


def arrivals(table, messages, before, after, prior, later):
    half = 2 * HEAD

    def body(s, a, b, c, d, before_ref, after_ref, prior_ref, later_ref, *rest):
        outs, held, mine, edges = rest[:4], *rest[4:]
        in_order((a, b, c, d), s[X], held)
        tails = [held[t, 2 * half : 2 * half + 16, :].astype(F32) for t in range(4)]
        totals = [tail[0:2] + tail[2:4] for tail in tails]
        ends = []
        for kind, steps in ((0, range(4)), (1, range(3, -1, -1))):
            run = jnp.zeros((half, HEAD), F32)
            reach = jnp.zeros((2, HEAD), F32)
            for t in steps:

                @pl.when(s[X] == t)
                def _(run=run, reach=reach, kind=kind):
                    mine[kind] = run
                    edges[kind] = jnp.exp(reach)

                rows = held[t, kind * half : (kind + 1) * half, :].astype(F32)
                run = spread(jnp.exp(totals[t])) * run + rows
                reach = reach + totals[t]
            ends.append(run.astype(BF16).astype(F32))
        nothing = jnp.zeros((HEAD, HEAD), F32)
        across_up = jnp.concatenate([nothing, ends[0][:HEAD]], axis=0)
        across_down = jnp.concatenate([ends[1][HEAD:], nothing], axis=0)
        start = mine[0] + spread(edges[0]) * across_up
        finish = mine[1] + spread(edges[1]) * across_down
        for r, out in enumerate(outs):
            t = s[Y] ^ r
            out[:half, :] = (before_ref[t] + spread(prior_ref[t]) * start).astype(BF16)
            out[half:, :] = (after_ref[t] + spread(later_ref[t]) * finish).astype(BF16)

    operands = (*messages, before, after, prior, later)
    message = shape((2 * half, HEAD))
    return call(
        "arrivals",
        body,
        table,
        (1,),
        operands,
        [whole(m) for m in operands],
        [message] * 4,
        [whole(message)] * 4,
        8,
        [
            pltpu.VMEM((4, *messages[0].shape), BF16),
            pltpu.VMEM((2, half, HEAD), F32),
            pltpu.VMEM((2, 2, HEAD), F32),
        ],
    )


def column_of(row):
    return jnp.broadcast_to(row, (HEAD, row.shape[1])).T


def local_grads(table, qkv, out_grad, cumul, first, count, so_far):
    tokens = qkv.shape[1]
    scale = HEAD**-0.5
    size = tokens // 2

    def body(s, qkv_ref, og_ref, cum_ref, *refs):
        out, ready = refs[-2:]
        row = cum_ref[pl.ds(pl.program_id(0) + first, 1), :]
        column = column_of(row)
        wide = jnp.concatenate([column] * (size // HEAD), axis=1)
        s_at = lax.broadcasted_iota(jnp.int32, (size, size), 0)
        t_at = lax.broadcasted_iota(jnp.int32, (size, size), 1)
        parts = [slice(0, size), slice(size, tokens)]

        def pair(t, s):
            if t == s:
                gap = row[:, parts[t]] - wide[parts[s], :]
                decay = jnp.exp(jnp.where(s_at <= t_at, gap, -jnp.inf))
            else:
                middle = row[:, size - 1 : size]
                to_middle = jnp.exp(middle - column[parts[s], :])
                decay = jnp.concatenate([to_middle] * (size // HEAD), axis=1)
                decay *= jnp.exp(row[:, parts[t]] - middle)
            q, k, v = qkv_ref[0, parts[t], :], qkv_ref[1, parts[s], :], qkv_ref[2, parts[s], :]
            g = og_ref[parts[t], :]
            scores = lax.dot_general(k, q, AB_T, preferred_element_type=F32)
            grads = lax.dot_general(v, g, AB_T, preferred_element_type=F32)
            prob = (scores * decay).astype(BF16)
            score = (grads * decay).astype(BF16)
            dq = lax.dot_general(score, k, A_TB, preferred_element_type=F32)
            return dq, dot(score, q), dot(prob, g)

        a, b, c = pair(0, 0), pair(1, 0), pair(1, 1)
        live = living(cum_ref, (tokens, HEAD))
        grads = (
            jnp.concatenate([a[0], b[0] + c[0]], axis=0) * scale,
            jnp.concatenate([a[1] + b[1], c[1]], axis=0) * scale,
            jnp.concatenate([a[2] + b[2], c[2]], axis=0) * scale,
        )
        until = jnp.exp(row[:, tokens - 1 : tokens] - column)
        rows = (
            og_ref[...].astype(F32) * (scale * jnp.exp(column)),
            qkv_ref[2].astype(F32) * until,
            qkv_ref[1].astype(F32) * until,
        )
        for j in range(3):
            out[j] = jnp.where(live, grads[j], 0.0).astype(BF16)
            ready[j] = jnp.where(live, rows[j], 0.0).astype(BF16)

    tile = pl.BlockSpec((3, tokens, HEAD), lambda h, s: (0, 0, h + first))
    in_specs = [tile, pl.BlockSpec((tokens, HEAD), lambda h, s: (0, h + first)), whole(cumul)]
    operands = [qkv, out_grad, cumul]
    if so_far is not None:
        in_specs += [pl.BlockSpec(memory_space=pl.ANY)] * 2
        operands += so_far
    return call(
        "local_grads",
        body,
        table,
        (count,),
        operands,
        in_specs,
        [shape(qkv.shape), shape(qkv.shape)],
        [tile, tile],
        12,
        alias=None if so_far is None else {4: 0, 5: 1},
    )


def whole_grads(table, which, local, ready, states):
    tokens = local.shape[1]
    heads = local.shape[2] // HEAD

    def body(s, local_ref, ready_ref, a, b, c, d, left, right, held):
        h = pl.program_id(0)

        @pl.when(h == 0)
        def _():
            in_order((a, b, c, d), s[Y], held)

        base = pl.multiple_of((s[Z] ^ which) * HEAD, HEAD)
        coming = held[h, pl.ds(base, HEAD), :]
        later = held[h, pl.ds(2 * HEAD + base, HEAD), :]
        cross = (
            lax.dot_general(ready_ref[0], coming, AB_T, preferred_element_type=F32),
            lax.dot_general(ready_ref[1], later, AB_T, preferred_element_type=F32),
            dot(ready_ref[2], later),
        )
        grads = [(local_ref[j].astype(F32) + cross[j]).astype(BF16) for j in range(3)]
        for k in range(heads):

            @pl.when(h == k)
            def _(k=k):
                for j in range(3):
                    start = (2 * j + k % 2) * HEAD
                    (left, right)[k // 2][:, start : start + HEAD] = grads[j]

    tile = pl.BlockSpec((3, tokens, HEAD), lambda h, s: (0, 0, h))
    side = shape((tokens, 3 * heads * HEAD // 2))
    return call(
        "whole_grads",
        body,
        table,
        (heads,),
        (local, ready, *states),
        [tile, tile, *[whole(m) for m in states]],
        [side, side],
        [whole(side)] * 2,
        12,
        [pltpu.VMEM((4, *states[0].shape), BF16)],
    )


def split(table, first, second):
    tokens, width = first.shape

    def body(s, a, b, out_a, out_b):
        out_a[...] = a[...]
        out_b[...] = b[...]

    halves = [pl.BlockSpec((tokens // 2, width), lambda i, s, k=k: (k, 0)) for k in range(2)]
    out = shape((tokens // 2, width))
    return call("split", body, table, (1,), (first, second), halves, [out] * 2, [whole(out)] * 2, 8)


def turn(table, shards):
    counts = [len(x) for x in shards]
    flat = [part for x in shards for part in x]
    tokens, width = sum(part.shape[0] for part in shards[0]), flat[0].shape[1]
    rows = 4 * width // 32

    def body(s, *refs):
        out, at = refs[-1], 0
        for k, count in enumerate(counts):
            mine, at = refs[at : at + count], at + count

            @pl.when((pl.program_id(0) ^ s[TEN]) == k)
            def _(mine=mine):
                out[...] = joined(mine).T.reshape(out.shape)

    out = shape((16, 2, rows, tokens))
    spec = pl.BlockSpec((8, 1, rows, tokens), lambda i, s: (i % 2, (i // 2) ^ s[Z], 0, 0))
    turned = call("turn", body, table, (4,), flat, [whole(x) for x in flat], out, spec, 12)
    return turned.reshape(4, 4, 2 * rows, tokens)


def weight_part(table, turned, lefts, rights, places, split):
    tokens, cols = lefts[0].shape
    rows = turned[0].shape[2]

    def body(s, own_x, own_y, pair_x, pair_y, left_a, left_b, right_a, right_b, *outs):
        r = pl.program_id(0)
        for side, (a, b, ga, gb) in enumerate(
            ((own_x, pair_x, left_a, left_b), (own_y, pair_y, right_a, right_b))
        ):
            acc = dot(a[...].reshape(4 * rows, tokens), ga[...])
            acc += dot(b[...].reshape(4 * rows, tokens), gb[...])
            acc = acc.astype(BF16)
            if split:
                outs[2 * side][...] = acc[: 2 * rows]
                outs[2 * side + 1][...] = acc[2 * rows :]
                continue
            for k in range(len(places)):

                @pl.when(r == k)
                def _(k=k, acc=acc, side=side):
                    outs[side * len(places) + k][...] = acc

    step = places[1] - places[0] if len(places) > 1 else 0
    by_x = pl.BlockSpec((1, 4, rows, tokens), lambda r, s: (s[X] ^ (places[0] + step * r), 0, 0, 0))
    by_y = pl.BlockSpec((4, 1, rows, tokens), lambda r, s: (0, s[Y] ^ (places[0] + step * r), 0, 0))
    outs = [shape((2 * rows if split else 4 * rows, cols))] * (4 if split else 2 * len(places))
    operands = (turned[0], turned[0], turned[1], turned[1], *lefts, *rights)
    return call(
        "weight_part",
        body,
        table,
        (len(places),),
        operands,
        [by_x, by_y, by_x, by_y, *[whole(x) for x in (*lefts, *rights)]],
        outs,
        [whole(o) for o in outs],
        30,
    )


def add_halves(table, third, first_place, halves):
    up, down = halves
    near_up, near_down = third, first_place
    n, cols = up.shape

    def body(s, a, b, u, d, out_a, out_b):
        out_a[...] = (a[...].astype(F32) + u[...].astype(F32)).astype(BF16)
        out_b[...] = (b[...].astype(F32) + d[...].astype(F32)).astype(BF16)

    first = pl.BlockSpec((n, cols), lambda i, s: (0, 0))
    second = pl.BlockSpec((n, cols), lambda i, s: (1, 0))
    return call(
        "add_halves",
        body,
        table,
        (1,),
        (near_up, near_down, up, down),
        [first, second, first, first],
        [shape(near_up.shape), shape(near_down.shape)],
        [first, second],
        12,
        alias={1: 0, 2: 1},
    )


def cut_blocks(table, left, right):
    rows, cols = left[0].shape[0] // 4, left[0].shape[1]

    def body(s, *refs):
        for k, axis in enumerate((Y, X)):
            a, b, c = refs[3 * k : 3 * k + 3]
            for r, out in zip((1, 3, 2, 0), refs[6 + 4 * k : 10 + 4 * k]):
                at = pl.ds(pl.multiple_of((s[axis] ^ r) * rows, rows), rows)
                total = a[at, :].astype(F32) + b[at, :].astype(F32) + c[at, :].astype(F32)
                out[...] = total.astype(BF16)

    outs = [shape((rows, cols))] * 8
    operands = (*left, *right)
    cut = call(
        "cut_blocks",
        body,
        table,
        (1,),
        operands,
        [whole(x) for x in operands],
        outs,
        [whole(o) for o in outs],
        24,
    )
    return cut[:4], cut[4:]


def final_sums(table, sides):
    rows, cols = sides[0][0].shape

    def body(s, *refs):
        here, there = refs[-2:]
        for k in range(2):
            total = sum(ref[...].astype(F32) for ref in refs[k:8:2]).astype(BF16)
            here[k] = total[: rows // 2]
            there[k] = total[rows // 2 :]

    operands = [x for both in zip(*sides) for x in both]
    outs = [shape((2, rows // 2, cols))] * 2
    return call(
        "final_sums",
        body,
        table,
        (1,),
        operands,
        [whole(x) for x in operands],
        outs,
        [whole(o) for o in outs],
        12,
    )


def finish(table, here, there):
    _, rows, cols = here.shape
    side = cols // 3

    def body(s, here_ref, there_ref, out):
        for ref, half in ((here_ref, s[Z]), (there_ref, 1 - s[Z])):
            for k in range(2):
                for j in range(3):
                    at = pl.ds(pl.multiple_of(half * 2 * side + k * side, side), side)
                    out[j, :, at] = ref[k, :, j * side : (j + 1) * side].astype(F32)

    out = shape((3, rows, 4 * side), F32)
    operands = (here, there)
    return call("finish", body, table, (1,), operands, [whole(here)] * 2, out, whole(out), 8)


def swaps(pieces, left, right):
    a, c = send(pieces[0], left, 1), send(pieces[2], right, 1)
    b, d = send(pieces[1], left, 3), send(pieces[3], right, 3)
    return [a, b], [c, d]


def device_part(activations, qkv_weight, log_decay, lengths, out_grad):
    tied = lax.optimization_barrier
    tokens = activations.shape[0]
    heads = log_decay.shape[1]
    per = heads // 2
    index = [lax.axis_index(a) for a in ("c0", "c1", "c2", "zl", "co")]
    here_z = index[0]
    fixed = [*index, index[3] * 2 + index[4]]
    table = jnp.stack(fixed).astype(jnp.int32)
    weight = pltpu.with_memory_space_constraint(jnp.transpose(qkv_weight, (1, 0, 2)), pltpu.HBM)

    near = send(activations, "zl", 1)
    side = across(activations)
    core = send(activations, "co", 1)

    live = (jnp.arange(tokens, dtype=jnp.int32) < lengths[0]).astype(F32)
    cumul = jnp.cumsum(log_decay.T * live[None, :], axis=1)
    size = jnp.broadcast_to(lengths.astype(F32)[:, None], (per, tokens))
    info, note = (
        jnp.concatenate([lax.dynamic_slice_in_dim(cumul, z * per, per), size])
        for z in (here_z, 1 - here_z)
    )
    note = send(note, "c0", 1)
    width = per * HEAD
    og_own = lax.dynamic_slice_in_dim(out_grad, here_z * width, width, axis=1)
    og_other = lax.dynamic_slice_in_dim(out_grad, (1 - here_z) * width, width, axis=1)

    acc_own = project(table, [[activations], [core]], (0, 1), weight, None, None)
    near, side, acc_own, note, og_other, info = tied((near, side, acc_own, note, og_other, info))
    far = split(table, side, near)
    far = [send(far[0], "zl", 1), across(far[1])]
    near_core = send(near, "co", 1)
    side_core = send(side, "co", 1)
    qkv_own = project(table, [[near], [near_core]], (2, 3), weight, acc_own, info)
    turned = [turn(table, tied(([[activations], [core], [near], [near_core]], qkv_own))[0])]
    far, side_core, qkv_own, turned = tied((far, side_core, qkv_own, turned))
    far_core = [send(x, "co", 1) for x in far]
    og_pair = send(tied((og_other, far))[0], "c0", 1)
    local_own = local_grads(table, qkv_own, og_own, info, 0, per // 2, None)
    far_core, local_own = tied((far_core, local_own))
    qkv_pair = project(
        table, [[side], [side_core], far, far_core], (2, 3, 0, 1), weight, None, note
    )
    qkv_own, _ = tied((qkv_own, qkv_pair))
    to_y = shard_states(table, qkv_own, og_own, info, 0, None)
    og_pair, qkv_pair, to_y = tied((og_pair, qkv_pair, to_y))

    to_y = shard_states(table, qkv_pair, og_pair, note, 1, to_y)
    at_y = [send(to_y[r], "c2", r) for r in (1, 3, 2)]
    qkv_own, _ = tied((qkv_own, to_y[0]))
    local_own = local_grads(table, qkv_own, og_own, info, per // 2, per // 2, local_own)
    second, _ = tied(([far, far_core, [side], [side_core]], to_y[0]))
    turned.append(turn(table, second))
    at_y, local_own, turned = tied((at_y, local_own, turned))
    before, after, prior, later, ring = ring_y(table, [to_y[0], at_y[0], at_y[2], at_y[1]])
    at_x = [send(ring, "c1", r) for r in (1, 3, 2)]
    qkv_pair, _ = tied((qkv_pair, ring))
    local = local_grads(table, qkv_pair, og_pair, note, 0, per // 2, None)
    at_x, local = tied((at_x, local))
    back = arrivals(table, [ring, at_x[0], at_x[2], at_x[1]], before, after, prior, later)
    states = [send(back[r], "c2", r) for r in (1, 3, 2)]
    local, _ = tied((local, back[0]))
    local = local_grads(table, qkv_pair, og_pair, note, per // 2, per // 2, local)
    states, turned, local = tied((states, turned, local))
    states = [back[0], states[0], states[2], states[1]]

    left_own, right_own = whole_grads(table, 0, *local_own, states)
    left_pair, right_pair = whole_grads(table, 1, *local, states)
    lefts, rights = (left_own, left_pair), (right_own, right_pair)
    far_piece = weight_part(table, turned, lefts, rights, (2,), True)
    l_half, r_half = swaps(far_piece, "c1", "c2")
    turned, _ = tied((turned, far_piece[0]))
    l_one, l_three, r_one, r_three = weight_part(table, turned, lefts, rights, (1, 3), False)
    l_half, l_one = tied((l_half, l_one))
    l_three, l_one = add_halves(table, l_three, l_one, l_half)
    l_got = [send(l_one, "c1", 1), send(l_three, "c1", 3)]
    r_half, _ = tied((r_half, l_one))
    r_three, r_one = add_halves(table, r_three, r_one, r_half)
    r_got = [send(r_one, "c2", 1), send(r_three, "c2", 3)]
    turned, _ = tied((turned, r_one))
    own = weight_part(table, turned, lefts, rights, (0,), False)
    l_got, own = tied((l_got, own))
    l_cut, r_cut = cut_blocks(table, (own[0], *l_got), (own[1], *r_got))
    l_got, r_got = [], []
    for k, by in enumerate((1, 3, 2)):
        l_got.append(send(l_cut[k], "c2", by))
        r_got.append(send(r_cut[k], "c1", by))
    here, there = final_sums(table, ((l_cut[3], *l_got), (r_cut[3], *r_got)))
    there = send(there, "c0", 1)
    return jnp.transpose(finish(table, here, there), (1, 0, 2))


def solution(mesh):
    finer = Mesh(mesh.devices.reshape(2, 4, 4, 2, 2), ("c0", "c1", "c2", "zl", "co"))
    context, tensor = ("c0", "c1", "c2"), ("zl", "co")
    placed = (
        P(context, tensor),
        P(None, None, tensor),
        P(context, tensor),
        P(context),
        P(context, tensor),
    )
    return jax.shard_map(
        device_part,
        mesh=finer,
        in_specs=placed,
        out_specs=P(context, None, tensor),
        check_vma=False,
    )
```

```python
import jax
import jax.numpy as jnp
from jax import lax
from jax.experimental import pallas as pl
from jax.experimental.pallas import tpu as pltpu
from jax.sharding import Mesh
from jax.sharding import PartitionSpec as P

F32 = jnp.float32
BF16 = jnp.bfloat16
HEAD = 128
HEADS = 4
Z, X, Y, ZL, CO, TEN = range(6)
AB_T = (((1,), (1,)), ((), ()))
A_TB = (((0,), (0,)), ((), ()))


def dot(a, b):
    return jnp.dot(a, b, preferred_element_type=F32)


def send(x, axis, by):
    return lax.ppermute(x, axis, [(i, i ^ by) for i in range(lax.axis_size(axis))])


def across(x):
    return lax.ppermute(x, ("c0", "zl"), [(0, 3), (1, 2), (2, 1), (3, 0)])


def whole(x):
    return pl.BlockSpec(x.shape, lambda *_, n=len(x.shape): (0,) * n)


def call(name, body, table, grid, operands, in_specs, outs, out_specs, mib, scratch=(), alias=None):
    return pl.pallas_call(
        body,
        grid_spec=pltpu.PrefetchScalarGridSpec(
            num_scalar_prefetch=1,
            grid=grid,
            in_specs=in_specs,
            out_specs=out_specs,
            scratch_shapes=scratch,
        ),
        out_shape=outs,
        input_output_aliases=alias or {},
        compiler_params=pltpu.CompilerParams(
            dimension_semantics=("arbitrary",) * len(grid), vmem_limit_bytes=mib << 20
        ),
        cost_estimate=pl.CostEstimate(flops=1, bytes_accessed=1, transcendentals=0),
        name=name,
    )(table, *operands)


def shape(dims, kind=BF16):
    return jax.ShapeDtypeStruct(dims, kind)


def joined(refs):
    parts = [ref[...] for ref in refs]
    return parts[0] if len(parts) == 1 else jnp.concatenate(parts, axis=0)


def living(info, dims):
    row = lax.broadcasted_iota(jnp.int32, dims, 0).astype(F32)
    return row < info[HEADS : HEADS + 1, :1]


def project(table, shards, flips, weight, partial, info):
    last = info is not None
    n, counts = len(shards), [len(x) for x in shards]
    flat = [part for x in shards for part in x]
    tokens, width = sum(part.shape[0] for part in shards[0]), flat[0].shape[1]
    cols = weight.shape[2] // 2

    def body(s, *refs):
        out, rest = refs[-1], list(refs)
        acc = None
        for i, count in enumerate(counts):
            rows = joined([rest.pop(0) for _ in range(count)])
            term = dot(rows, refs[len(flat) + i][0])
            acc = term if acc is None else acc + term
        if partial is not None:
            acc += refs[len(flat) + n][0]
        if last:
            acc = jnp.where(living(refs[-2], acc.shape), acc, 0.0)
        out[0] = acc.astype(out.dtype)

    tile = pl.BlockSpec((1, tokens, cols), lambda g, s: (g, 0, 0))
    in_specs = [whole(x) for x in flat]
    for flip in flips:
        in_specs.append(
            pl.BlockSpec((1, width, cols), lambda g, s, flip=flip: (g, s[TEN] ^ flip, s[Z]))
        )
    operands = [*flat, *([weight] * n)]
    if partial is not None:
        in_specs.append(tile)
        operands.append(partial)
    if last:
        in_specs.append(whole(info))
        operands.append(info)
    out = shape((3, tokens, cols), BF16 if last else F32)
    return call("project", body, table, (3,), operands, in_specs, out, tile, 24)


def shard_states(table, qkv, out_grad, cumul, which, so_far):
    tokens = qkv.shape[1]
    scale = HEAD**-0.5

    def body(s, qkv_ref, og_ref, cum_ref, *refs):
        outs = refs[-4:]
        r = pl.program_id(0)
        row = cum_ref[pl.ds(s[Y] ^ r, 1), :]
        total = row[:, tokens - 1 : tokens]
        keys_t = qkv_ref[1].T.astype(F32)
        query_t = qkv_ref[0].T.astype(F32)
        keys_t = (keys_t * jnp.exp(total - row)).astype(BF16)
        query_t = (query_t * (scale * jnp.exp(row))).astype(BF16)
        states = (dot(keys_t, qkv_ref[2]), dot(query_t, og_ref[...]))
        at = lax.broadcasted_iota(jnp.int32, (16, HEAD), 0)
        tail = jnp.broadcast_to(total, (16, HEAD)).astype(BF16)
        for k, out in enumerate(outs):

            @pl.when(r == k)
            def _(k=k, out=out):
                here = s[Z] ^ which
                if so_far is not None:
                    out[...] = refs[k][...]
                for kind in range(2):
                    start = pl.multiple_of((2 * kind + here) * HEAD, HEAD)
                    out[pl.ds(start, HEAD), :] = states[kind].astype(BF16)
                if so_far is None:
                    out[4 * HEAD :, :] = tail
                else:
                    out[4 * HEAD :, :] = jnp.where(at == here, tail, refs[k][4 * HEAD :, :])

    message = shape((4 * HEAD + 16, HEAD))
    operands = [qkv, out_grad, cumul, *(so_far or ())]
    in_specs = [
        pl.BlockSpec((3, tokens, HEAD), lambda r, s: (0, 0, s[Y] ^ r)),
        pl.BlockSpec((tokens, HEAD), lambda r, s: (0, s[Y] ^ r)),
        whole(cumul),
        *[whole(m) for m in so_far or ()],
    ]
    return call(
        "shard_states",
        body,
        table,
        (4,),
        operands,
        in_specs,
        [message] * 4,
        [whole(message)] * 4,
        12,
    )


def in_order(refs, place, held):
    for r, ref in enumerate(refs):
        held[place ^ r] = ref[...]


def spread(pair):
    wide = [jnp.broadcast_to(pair[i : i + 1, :], (HEAD, HEAD)) for i in range(2)]
    return jnp.concatenate(wide, axis=0)


def ring_y(table, messages):
    half = 2 * HEAD

    def body(s, a, b, c, d, before, after, prior, later, out, held):
        in_order((a, b, c, d), s[Y], held)
        totals = [held[t, 2 * half : 2 * half + 16, :].astype(F32)[:2] for t in range(4)]
        run = jnp.zeros((half, HEAD), F32)
        reach = jnp.zeros((2, HEAD), F32)
        for t in range(4):
            before[t] = run
            prior[t] = jnp.exp(reach)
            run = spread(jnp.exp(totals[t])) * run + held[t, :half, :].astype(F32)
            reach = reach + totals[t]
        out[:half, :] = run.astype(BF16)
        total = reach
        run = jnp.zeros((half, HEAD), F32)
        reach = jnp.zeros((2, HEAD), F32)
        for t in range(3, -1, -1):
            after[t] = run
            later[t] = jnp.exp(reach)
            run = spread(jnp.exp(totals[t])) * run + held[t, half : 2 * half, :].astype(F32)
            reach = reach + totals[t]
        out[half : 2 * half, :] = run.astype(BF16)
        high = total.astype(BF16).astype(F32)
        low = total - high
        at = lax.broadcasted_iota(jnp.int32, (16, HEAD), 0)
        tail = jnp.where(at == 0, high[0:1], high[1:2])
        tail = jnp.where(at == 2, low[0:1], tail)
        tail = jnp.where(at == 3, low[1:2], tail)
        out[2 * half :, :] = tail.astype(BF16)

    outs = [
        shape((4, half, HEAD), F32),
        shape((4, half, HEAD), F32),
        shape((4, 2, HEAD), F32),
        shape((4, 2, HEAD), F32),
        shape(messages[0].shape),
    ]
    return call(
        "ring_y",
        body,
        table,
        (1,),
        messages,
        [whole(m) for m in messages],
        outs,
        [whole(o) for o in outs],
        8,
        [pltpu.VMEM((4, *messages[0].shape), BF16)],
    )


def arrivals(table, messages, before, after, prior, later):
    half = 2 * HEAD

    def body(s, a, b, c, d, before_ref, after_ref, prior_ref, later_ref, *rest):
        outs, held, mine, edges = rest[:4], *rest[4:]
        in_order((a, b, c, d), s[X], held)
        tails = [held[t, 2 * half : 2 * half + 16, :].astype(F32) for t in range(4)]
        totals = [tail[0:2] + tail[2:4] for tail in tails]
        ends = []
        for kind, steps in ((0, range(4)), (1, range(3, -1, -1))):
            run = jnp.zeros((half, HEAD), F32)
            reach = jnp.zeros((2, HEAD), F32)
            for t in steps:

                @pl.when(s[X] == t)
                def _(run=run, reach=reach, kind=kind):
                    mine[kind] = run
                    edges[kind] = jnp.exp(reach)

                rows = held[t, kind * half : (kind + 1) * half, :].astype(F32)
                run = spread(jnp.exp(totals[t])) * run + rows
                reach = reach + totals[t]
            ends.append(run.astype(BF16).astype(F32))
        nothing = jnp.zeros((HEAD, HEAD), F32)
        across_up = jnp.concatenate([nothing, ends[0][:HEAD]], axis=0)
        across_down = jnp.concatenate([ends[1][HEAD:], nothing], axis=0)
        start = mine[0] + spread(edges[0]) * across_up
        finish = mine[1] + spread(edges[1]) * across_down
        for r, out in enumerate(outs):
            t = s[Y] ^ r
            out[:half, :] = (before_ref[t] + spread(prior_ref[t]) * start).astype(BF16)
            out[half:, :] = (after_ref[t] + spread(later_ref[t]) * finish).astype(BF16)

    operands = (*messages, before, after, prior, later)
    message = shape((2 * half, HEAD))
    return call(
        "arrivals",
        body,
        table,
        (1,),
        operands,
        [whole(m) for m in operands],
        [message] * 4,
        [whole(message)] * 4,
        8,
        [
            pltpu.VMEM((4, *messages[0].shape), BF16),
            pltpu.VMEM((2, half, HEAD), F32),
            pltpu.VMEM((2, 2, HEAD), F32),
        ],
    )


def column_of(row):
    return jnp.broadcast_to(row, (HEAD, row.shape[1])).T


def local_grads(table, qkv, out_grad, cumul, first, count, so_far):
    tokens = qkv.shape[1]
    scale = HEAD**-0.5
    size = tokens // 2

    def body(s, qkv_ref, og_ref, cum_ref, *refs):
        out, ready = refs[-2:]
        row = cum_ref[pl.ds(pl.program_id(0) + first, 1), :]
        column = column_of(row)
        wide = jnp.concatenate([column] * (size // HEAD), axis=1)
        s_at = lax.broadcasted_iota(jnp.int32, (size, size), 0)
        t_at = lax.broadcasted_iota(jnp.int32, (size, size), 1)
        parts = [slice(0, size), slice(size, tokens)]

        def pair(t, s):
            if t == s:
                gap = row[:, parts[t]] - wide[parts[s], :]
                decay = jnp.exp(jnp.where(s_at <= t_at, gap, -jnp.inf))
            else:
                middle = row[:, size - 1 : size]
                to_middle = jnp.exp(middle - column[parts[s], :])
                decay = jnp.concatenate([to_middle] * (size // HEAD), axis=1)
                decay *= jnp.exp(row[:, parts[t]] - middle)
            q, k, v = qkv_ref[0, parts[t], :], qkv_ref[1, parts[s], :], qkv_ref[2, parts[s], :]
            g = og_ref[parts[t], :]
            scores = lax.dot_general(k, q, AB_T, preferred_element_type=F32)
            grads = lax.dot_general(v, g, AB_T, preferred_element_type=F32)
            prob = (scores * decay).astype(BF16)
            score = (grads * decay).astype(BF16)
            dq = lax.dot_general(score, k, A_TB, preferred_element_type=F32)
            return dq, dot(score, q), dot(prob, g)

        a, b, c = pair(0, 0), pair(1, 0), pair(1, 1)
        live = living(cum_ref, (tokens, HEAD))
        grads = (
            jnp.concatenate([a[0], b[0] + c[0]], axis=0) * scale,
            jnp.concatenate([a[1] + b[1], c[1]], axis=0) * scale,
            jnp.concatenate([a[2] + b[2], c[2]], axis=0) * scale,
        )
        until = jnp.exp(row[:, tokens - 1 : tokens] - column)
        rows = (
            og_ref[...].astype(F32) * (scale * jnp.exp(column)),
            qkv_ref[2].astype(F32) * until,
            qkv_ref[1].astype(F32) * until,
        )
        for j in range(3):
            out[j] = jnp.where(live, grads[j], 0.0).astype(BF16)
            ready[j] = jnp.where(live, rows[j], 0.0).astype(BF16)

    tile = pl.BlockSpec((3, tokens, HEAD), lambda h, s: (0, 0, h + first))
    in_specs = [tile, pl.BlockSpec((tokens, HEAD), lambda h, s: (0, h + first)), whole(cumul)]
    operands = [qkv, out_grad, cumul]
    if so_far is not None:
        in_specs += [pl.BlockSpec(memory_space=pl.ANY)] * 2
        operands += so_far
    return call(
        "local_grads",
        body,
        table,
        (count,),
        operands,
        in_specs,
        [shape(qkv.shape), shape(qkv.shape)],
        [tile, tile],
        12,
        alias=None if so_far is None else {4: 0, 5: 1},
    )


def whole_grads(table, own, pair, states):
    tokens, heads = own[0].shape[1], HEADS

    def body(s, local_a, ready_a, local_b, ready_b, a, b, c, d, *rest):
        outs, held = rest[:4], rest[4]
        i = pl.program_id(0)

        @pl.when(i == 0)
        def _():
            in_order((a, b, c, d), s[Y], held)

        for which, (local_ref, ready_ref) in enumerate(((local_a, ready_a), (local_b, ready_b))):
            for k in range(heads):

                @pl.when(i == which * heads + k)
                def _(k=k, which=which, local_ref=local_ref, ready_ref=ready_ref):
                    base = pl.multiple_of((s[Z] ^ which) * HEAD, HEAD)
                    coming = held[k, pl.ds(base, HEAD), :]
                    later = held[k, pl.ds(2 * HEAD + base, HEAD), :]
                    cross = (
                        lax.dot_general(ready_ref[0], coming, AB_T, preferred_element_type=F32),
                        lax.dot_general(ready_ref[1], later, AB_T, preferred_element_type=F32),
                        dot(ready_ref[2], later),
                    )
                    out = outs[2 * which + k // 2]
                    for j in range(3):
                        start = (2 * j + k % 2) * HEAD
                        total = local_ref[j].astype(F32) + cross[j]
                        out[:, start : start + HEAD] = total.astype(BF16)

    first = pl.BlockSpec((3, tokens, HEAD), lambda i, s: (0, 0, jnp.minimum(i, heads - 1)))
    second = pl.BlockSpec((3, tokens, HEAD), lambda i, s: (0, 0, jnp.maximum(i - heads, 0)))
    side = shape((tokens, 3 * heads * HEAD // 2))
    return call(
        "whole_grads",
        body,
        table,
        (2 * heads,),
        (*own, *pair, *states),
        [first, first, second, second, *[whole(m) for m in states]],
        [side] * 4,
        [whole(side)] * 4,
        16,
        [pltpu.VMEM((4, *states[0].shape), BF16)],
    )


def split(table, first, second):
    tokens, width = first.shape

    def body(s, a, b, out_a, out_b):
        out_a[...] = a[...]
        out_b[...] = b[...]

    halves = [pl.BlockSpec((tokens // 2, width), lambda i, s, k=k: (k, 0)) for k in range(2)]
    out = shape((tokens // 2, width))
    return call("split", body, table, (1,), (first, second), halves, [out] * 2, [whole(out)] * 2, 8)


def turn(table, shards):
    counts = [len(x) for x in shards]
    flat = [part for x in shards for part in x]
    tokens, width = sum(part.shape[0] for part in shards[0]), flat[0].shape[1]
    rows = 4 * width // 32

    def body(s, *refs):
        out, at = refs[-1], 0
        for k, count in enumerate(counts):
            mine, at = refs[at : at + count], at + count

            @pl.when((pl.program_id(0) ^ s[TEN]) == k)
            def _(mine=mine):
                out[...] = joined(mine).T.reshape(out.shape)

    out = shape((16, 2, rows, tokens))
    spec = pl.BlockSpec((8, 1, rows, tokens), lambda i, s: (i % 2, (i // 2) ^ s[Z], 0, 0))
    turned = call("turn", body, table, (4,), flat, [whole(x) for x in flat], out, spec, 12)
    return turned.reshape(4, 4, 2 * rows, tokens)


def weight_part(table, turned, lefts, rights, places, split):
    tokens, cols = lefts[0].shape
    rows = turned[0].shape[2]

    def body(s, own_x, own_y, pair_x, pair_y, left_a, left_b, right_a, right_b, *outs):
        r = pl.program_id(0)
        for side, (a, b, ga, gb) in enumerate(
            ((own_x, pair_x, left_a, left_b), (own_y, pair_y, right_a, right_b))
        ):
            acc = dot(a[...].reshape(4 * rows, tokens), ga[...])
            acc += dot(b[...].reshape(4 * rows, tokens), gb[...])
            acc = acc.astype(BF16)
            if split:
                outs[2 * side][...] = acc[: 2 * rows]
                outs[2 * side + 1][...] = acc[2 * rows :]
                continue
            for k in range(len(places)):

                @pl.when(r == k)
                def _(k=k, acc=acc, side=side):
                    outs[side * len(places) + k][...] = acc

    step = places[1] - places[0] if len(places) > 1 else 0
    by_x = pl.BlockSpec((1, 4, rows, tokens), lambda r, s: (s[X] ^ (places[0] + step * r), 0, 0, 0))
    by_y = pl.BlockSpec((4, 1, rows, tokens), lambda r, s: (0, s[Y] ^ (places[0] + step * r), 0, 0))
    outs = [shape((2 * rows if split else 4 * rows, cols))] * (4 if split else 2 * len(places))
    operands = (turned[0], turned[0], turned[1], turned[1], *lefts, *rights)
    return call(
        "weight_part",
        body,
        table,
        (len(places),),
        operands,
        [by_x, by_y, by_x, by_y, *[whole(x) for x in (*lefts, *rights)]],
        outs,
        [whole(o) for o in outs],
        30,
    )


def add_halves(table, third, first_place, halves):
    up, down = halves
    near_up, near_down = third, first_place
    n, cols = up.shape

    def body(s, a, b, u, d, out_a, out_b):
        out_a[...] = (a[...].astype(F32) + u[...].astype(F32)).astype(BF16)
        out_b[...] = (b[...].astype(F32) + d[...].astype(F32)).astype(BF16)

    first = pl.BlockSpec((n, cols), lambda i, s: (0, 0))
    second = pl.BlockSpec((n, cols), lambda i, s: (1, 0))
    return call(
        "add_halves",
        body,
        table,
        (1,),
        (near_up, near_down, up, down),
        [first, second, first, first],
        [shape(near_up.shape), shape(near_down.shape)],
        [first, second],
        12,
        alias={1: 0, 2: 1},
    )


def cut_blocks(table, left, right):
    rows, cols = left[0].shape[0] // 4, left[0].shape[1]

    def body(s, *refs):
        for k, axis in enumerate((Y, X)):
            a, b, c = refs[3 * k : 3 * k + 3]
            for r, out in zip((1, 3, 2, 0), refs[6 + 4 * k : 10 + 4 * k]):
                at = pl.ds(pl.multiple_of((s[axis] ^ r) * rows, rows), rows)
                total = a[at, :].astype(F32) + b[at, :].astype(F32) + c[at, :].astype(F32)
                out[...] = total.astype(BF16)

    outs = [shape((rows, cols))] * 8
    operands = (*left, *right)
    cut = call(
        "cut_blocks",
        body,
        table,
        (1,),
        operands,
        [whole(x) for x in operands],
        outs,
        [whole(o) for o in outs],
        24,
    )
    return cut[:4], cut[4:]


def final_sums(table, parts):
    rows, cols = parts[0].shape

    def body(s, a, b, c, d, here, there):
        total = sum(ref[...].astype(F32) for ref in (a, b, c, d)).astype(BF16)
        here[...] = total[: rows // 2]
        there[...] = total[rows // 2 :]

    outs = [shape((rows // 2, cols))] * 2
    return call(
        "final_sums",
        body,
        table,
        (1,),
        parts,
        [whole(x) for x in parts],
        outs,
        [whole(o) for o in outs],
        8,
    )


def finish(table, here, there):
    rows, cols = here[0].shape
    side = cols // 3

    def body(s, *refs):
        out = refs[-1]
        for i, half in enumerate((s[Z], 1 - s[Z])):
            for k in range(2):
                for j in range(3):
                    at = pl.ds(pl.multiple_of(half * 2 * side + k * side, side), side)
                    out[j, :, at] = refs[2 * i + k][:, j * side : (j + 1) * side].astype(F32)

    out = shape((3, rows, 4 * side), F32)
    operands = (*here, *there)
    return call("finish", body, table, (1,), operands, [whole(x) for x in operands], out, whole(out), 8)


def swaps(pieces, left, right):
    a, c = send(pieces[0], left, 1), send(pieces[2], right, 1)
    b, d = send(pieces[1], left, 3), send(pieces[3], right, 3)
    return [a, b], [c, d]


def device_part(activations, qkv_weight, log_decay, lengths, out_grad):
    tied = lax.optimization_barrier
    tokens = activations.shape[0]
    heads = log_decay.shape[1]
    per = heads // 2
    index = [lax.axis_index(a) for a in ("c0", "c1", "c2", "zl", "co")]
    here_z = index[0]
    fixed = [*index, index[3] * 2 + index[4]]
    table = jnp.stack(fixed).astype(jnp.int32)
    weight = pltpu.with_memory_space_constraint(jnp.transpose(qkv_weight, (1, 0, 2)), pltpu.HBM)

    near = send(activations, "zl", 1)
    side = across(activations)
    core = send(activations, "co", 1)

    live = (jnp.arange(tokens, dtype=jnp.int32) < lengths[0]).astype(F32)
    cumul = jnp.cumsum(log_decay.T * live[None, :], axis=1)
    size = jnp.broadcast_to(lengths.astype(F32)[:, None], (per, tokens))
    info, note = (
        jnp.concatenate([lax.dynamic_slice_in_dim(cumul, z * per, per), size])
        for z in (here_z, 1 - here_z)
    )
    note = send(note, "c0", 1)
    width = per * HEAD
    og_own = lax.dynamic_slice_in_dim(out_grad, here_z * width, width, axis=1)
    og_other = lax.dynamic_slice_in_dim(out_grad, (1 - here_z) * width, width, axis=1)

    acc_own = project(table, [[activations], [core]], (0, 1), weight, None, None)
    near, side, acc_own, note, og_other, info = tied((near, side, acc_own, note, og_other, info))
    far = split(table, side, near)
    far = [send(far[0], "zl", 1), across(far[1])]
    near_core = send(near, "co", 1)
    side_core = send(side, "co", 1)
    qkv_own = project(table, [[near], [near_core]], (2, 3), weight, acc_own, info)
    turned = [turn(table, tied(([[activations], [core], [near], [near_core]], qkv_own))[0])]
    far, side_core, qkv_own, turned = tied((far, side_core, qkv_own, turned))
    far_core = [send(x, "co", 1) for x in far]
    og_pair = send(tied((og_other, far))[0], "c0", 1)
    qkv_pair = project(
        table, [[side], [side_core], far, far_core], (2, 3, 0, 1), weight, None, note
    )
    qkv_own, _ = tied((qkv_own, qkv_pair))
    to_y = shard_states(table, qkv_own, og_own, info, 0, None)
    og_pair, qkv_pair, to_y = tied((og_pair, qkv_pair, to_y))

    to_y = shard_states(table, qkv_pair, og_pair, note, 1, to_y)
    at_y = [send(to_y[r], "c2", r) for r in (1, 3, 2)]
    qkv_own, _ = tied((qkv_own, to_y[0]))
    local_own = local_grads(table, qkv_own, og_own, info, 0, per, None)
    at_y, local_own = tied((at_y, local_own))
    before, after, prior, later, ring = ring_y(table, [to_y[0], at_y[0], at_y[2], at_y[1]])
    at_x = [send(ring, "c1", r) for r in (1, 3, 2)]
    qkv_pair, _ = tied((qkv_pair, ring))
    local = local_grads(table, qkv_pair, og_pair, note, 0, per // 2, None)
    second, _ = tied(([far, far_core, [side], [side_core]], ring))
    turned.append(turn(table, second))
    at_x, local, turned = tied((at_x, local, turned))
    back = arrivals(table, [ring, at_x[0], at_x[2], at_x[1]], before, after, prior, later)
    states = [send(back[r], "c2", r) for r in (1, 3, 2)]
    local, _ = tied((local, back[0]))
    local = local_grads(table, qkv_pair, og_pair, note, per // 2, per // 2, local)
    states, turned, local = tied((states, turned, local))
    states = [back[0], states[0], states[2], states[1]]

    left_own, right_own, left_pair, right_pair = whole_grads(table, local_own, local, states)
    lefts, rights = (left_own, left_pair), (right_own, right_pair)
    far_piece = weight_part(table, turned, lefts, rights, (2,), True)
    l_half, r_half = swaps(far_piece, "c1", "c2")
    turned, _ = tied((turned, far_piece[0]))
    l_one, l_three, r_one, r_three = weight_part(table, turned, lefts, rights, (1, 3), False)
    l_half, l_one = tied((l_half, l_one))
    l_three, l_one = add_halves(table, l_three, l_one, l_half)
    l_got = [send(l_one, "c1", 1), send(l_three, "c1", 3)]
    r_half, _ = tied((r_half, l_one))
    r_three, r_one = add_halves(table, r_three, r_one, r_half)
    r_got = [send(r_one, "c2", 1), send(r_three, "c2", 3)]
    turned, _ = tied((turned, r_one))
    own = weight_part(table, turned, lefts, rights, (0,), False)
    l_got, own = tied((l_got, own))
    l_cut, r_cut = cut_blocks(table, (own[0], *l_got), (own[1], *r_got))
    l_got = [send(x, "c2", by) for x, by in zip(l_cut, (1, 3, 2))]
    r_got = [send(x, "c1", by) for x, by in zip(r_cut, (1, 3, 2))]
    l_here, l_there = final_sums(table, (l_cut[3], *l_got))
    r_got, _ = tied((r_got, l_here))
    r_here, r_there = final_sums(table, (r_cut[3], *r_got))
    there = [send(x, "c0", 1) for x in (l_there, r_there)]
    return jnp.transpose(finish(table, (l_here, r_here), there), (1, 0, 2))


def solution(mesh):
    finer = Mesh(mesh.devices.reshape(2, 4, 4, 2, 2), ("c0", "c1", "c2", "zl", "co"))
    context, tensor = ("c0", "c1", "c2"), ("zl", "co")
    placed = (
        P(context, tensor),
        P(None, None, tensor),
        P(context, tensor),
        P(context),
        P(context, tensor),
    )
    return jax.shard_map(
        device_part,
        mesh=finer,
        in_specs=placed,
        out_specs=P(context, None, tensor),
        check_vma=False,
    )
```

```python
import jax
import jax.numpy as jnp
from jax import lax
from jax.experimental import pallas as pl
from jax.experimental.pallas import tpu as pltpu
from jax.sharding import Mesh
from jax.sharding import PartitionSpec as P

F32 = jnp.float32
BF16 = jnp.bfloat16
HEAD = 128
HEADS = 4
Z, X, Y, ZL, CO, TEN = range(6)
AB_T = (((1,), (1,)), ((), ()))
A_TB = (((0,), (0,)), ((), ()))


def dot(a, b):
    return jnp.dot(a, b, preferred_element_type=F32)


def send(x, axis, by):
    return lax.ppermute(x, axis, [(i, i ^ by) for i in range(lax.axis_size(axis))])


def across(x):
    return lax.ppermute(x, ("c0", "zl"), [(0, 3), (1, 2), (2, 1), (3, 0)])


def whole(x):
    return pl.BlockSpec(x.shape, lambda *_, n=len(x.shape): (0,) * n)


def call(name, body, table, grid, operands, in_specs, outs, out_specs, mib, scratch=(), alias=None):
    return pl.pallas_call(
        body,
        grid_spec=pltpu.PrefetchScalarGridSpec(
            num_scalar_prefetch=1,
            grid=grid,
            in_specs=in_specs,
            out_specs=out_specs,
            scratch_shapes=scratch,
        ),
        out_shape=outs,
        input_output_aliases=alias or {},
        compiler_params=pltpu.CompilerParams(
            dimension_semantics=("arbitrary",) * len(grid), vmem_limit_bytes=mib << 20
        ),
        cost_estimate=pl.CostEstimate(flops=1, bytes_accessed=1, transcendentals=0),
        name=name,
    )(table, *operands)


def shape(dims, kind=BF16):
    return jax.ShapeDtypeStruct(dims, kind)


def joined(refs):
    parts = [ref[...] for ref in refs]
    return parts[0] if len(parts) == 1 else jnp.concatenate(parts, axis=0)


def living(info, dims):
    row = lax.broadcasted_iota(jnp.int32, dims, 0).astype(F32)
    return row < info[HEADS : HEADS + 1, :1]


def project(table, shards, flips, weight, partial, info):
    last = info is not None
    n, counts = len(shards), [len(x) for x in shards]
    flat = [part for x in shards for part in x]
    tokens, width = sum(part.shape[0] for part in shards[0]), flat[0].shape[1]
    cols = weight.shape[2] // 2

    def body(s, *refs):
        out, rest = refs[-1], list(refs)
        acc = None
        for i, count in enumerate(counts):
            rows = joined([rest.pop(0) for _ in range(count)])
            term = dot(rows, refs[len(flat) + i][0])
            acc = term if acc is None else acc + term
        if partial is not None:
            acc += refs[len(flat) + n][0]
        if last:
            acc = jnp.where(living(refs[-2], acc.shape), acc, 0.0)
        out[0] = acc.astype(out.dtype)

    tile = pl.BlockSpec((1, tokens, cols), lambda g, s: (g, 0, 0))
    in_specs = [whole(x) for x in flat]
    for flip in flips:
        in_specs.append(
            pl.BlockSpec((1, width, cols), lambda g, s, flip=flip: (g, s[TEN] ^ flip, s[Z]))
        )
    operands = [*flat, *([weight] * n)]
    if partial is not None:
        in_specs.append(tile)
        operands.append(partial)
    if last:
        in_specs.append(whole(info))
        operands.append(info)
    out = shape((3, tokens, cols), BF16 if last else F32)
    return call("project", body, table, (3,), operands, in_specs, out, tile, 24)


def shard_states(table, qkv, out_grad, cumul, which, so_far):
    tokens = qkv.shape[1]
    scale = HEAD**-0.5

    def body(s, qkv_ref, og_ref, cum_ref, *refs):
        outs = refs[-4:]
        r = pl.program_id(0)
        row = cum_ref[pl.ds(s[Y] ^ r, 1), :]
        total = row[:, tokens - 1 : tokens]
        keys_t = qkv_ref[1].T.astype(F32)
        query_t = qkv_ref[0].T.astype(F32)
        keys_t = (keys_t * jnp.exp(total - row)).astype(BF16)
        query_t = (query_t * (scale * jnp.exp(row))).astype(BF16)
        states = (dot(keys_t, qkv_ref[2]), dot(query_t, og_ref[...]))
        at = lax.broadcasted_iota(jnp.int32, (16, HEAD), 0)
        tail = jnp.broadcast_to(total, (16, HEAD)).astype(BF16)
        for k, out in enumerate(outs):

            @pl.when(r == k)
            def _(k=k, out=out):
                here = s[Z] ^ which
                if so_far is not None:
                    out[...] = refs[k][...]
                for kind in range(2):
                    start = pl.multiple_of((2 * kind + here) * HEAD, HEAD)
                    out[pl.ds(start, HEAD), :] = states[kind].astype(BF16)
                if so_far is None:
                    out[4 * HEAD :, :] = tail
                else:
                    out[4 * HEAD :, :] = jnp.where(at == here, tail, refs[k][4 * HEAD :, :])

    message = shape((4 * HEAD + 16, HEAD))
    operands = [qkv, out_grad, cumul, *(so_far or ())]
    in_specs = [
        pl.BlockSpec((3, tokens, HEAD), lambda r, s: (0, 0, s[Y] ^ r)),
        pl.BlockSpec((tokens, HEAD), lambda r, s: (0, s[Y] ^ r)),
        whole(cumul),
        *[whole(m) for m in so_far or ()],
    ]
    return call(
        "shard_states",
        body,
        table,
        (4,),
        operands,
        in_specs,
        [message] * 4,
        [whole(message)] * 4,
        12,
    )


def in_order(refs, place, held):
    for r, ref in enumerate(refs):
        held[place ^ r] = ref[...]


def spread(pair):
    wide = [jnp.broadcast_to(pair[i : i + 1, :], (HEAD, HEAD)) for i in range(2)]
    return jnp.concatenate(wide, axis=0)


def ring_y(table, messages):
    half = 2 * HEAD

    def body(s, a, b, c, d, before, after, prior, later, out, held):
        in_order((a, b, c, d), s[Y], held)
        totals = [held[t, 2 * half : 2 * half + 16, :].astype(F32)[:2] for t in range(4)]
        run = jnp.zeros((half, HEAD), F32)
        reach = jnp.zeros((2, HEAD), F32)
        for t in range(4):
            before[t] = run
            prior[t] = jnp.exp(reach)
            run = spread(jnp.exp(totals[t])) * run + held[t, :half, :].astype(F32)
            reach = reach + totals[t]
        out[:half, :] = run.astype(BF16)
        total = reach
        run = jnp.zeros((half, HEAD), F32)
        reach = jnp.zeros((2, HEAD), F32)
        for t in range(3, -1, -1):
            after[t] = run
            later[t] = jnp.exp(reach)
            run = spread(jnp.exp(totals[t])) * run + held[t, half : 2 * half, :].astype(F32)
            reach = reach + totals[t]
        out[half : 2 * half, :] = run.astype(BF16)
        high = total.astype(BF16).astype(F32)
        low = total - high
        at = lax.broadcasted_iota(jnp.int32, (16, HEAD), 0)
        tail = jnp.where(at == 0, high[0:1], high[1:2])
        tail = jnp.where(at == 2, low[0:1], tail)
        tail = jnp.where(at == 3, low[1:2], tail)
        out[2 * half :, :] = tail.astype(BF16)

    outs = [
        shape((4, half, HEAD), F32),
        shape((4, half, HEAD), F32),
        shape((4, 2, HEAD), F32),
        shape((4, 2, HEAD), F32),
        shape(messages[0].shape),
    ]
    return call(
        "ring_y",
        body,
        table,
        (1,),
        messages,
        [whole(m) for m in messages],
        outs,
        [whole(o) for o in outs],
        8,
        [pltpu.VMEM((4, *messages[0].shape), BF16)],
    )


def arrivals(table, messages, before, after, prior, later):
    half = 2 * HEAD

    def body(s, a, b, c, d, before_ref, after_ref, prior_ref, later_ref, *rest):
        outs, held, mine, edges = rest[:4], *rest[4:]
        in_order((a, b, c, d), s[X], held)
        tails = [held[t, 2 * half : 2 * half + 16, :].astype(F32) for t in range(4)]
        totals = [tail[0:2] + tail[2:4] for tail in tails]
        ends = []
        for kind, steps in ((0, range(4)), (1, range(3, -1, -1))):
            run = jnp.zeros((half, HEAD), F32)
            reach = jnp.zeros((2, HEAD), F32)
            for t in steps:

                @pl.when(s[X] == t)
                def _(run=run, reach=reach, kind=kind):
                    mine[kind] = run
                    edges[kind] = jnp.exp(reach)

                rows = held[t, kind * half : (kind + 1) * half, :].astype(F32)
                run = spread(jnp.exp(totals[t])) * run + rows
                reach = reach + totals[t]
            ends.append(run.astype(BF16).astype(F32))
        nothing = jnp.zeros((HEAD, HEAD), F32)
        across_up = jnp.concatenate([nothing, ends[0][:HEAD]], axis=0)
        across_down = jnp.concatenate([ends[1][HEAD:], nothing], axis=0)
        start = mine[0] + spread(edges[0]) * across_up
        finish = mine[1] + spread(edges[1]) * across_down
        for r, out in enumerate(outs):
            t = s[Y] ^ r
            out[:half, :] = (before_ref[t] + spread(prior_ref[t]) * start).astype(BF16)
            out[half:, :] = (after_ref[t] + spread(later_ref[t]) * finish).astype(BF16)

    operands = (*messages, before, after, prior, later)
    message = shape((2 * half, HEAD))
    return call(
        "arrivals",
        body,
        table,
        (1,),
        operands,
        [whole(m) for m in operands],
        [message] * 4,
        [whole(message)] * 4,
        8,
        [
            pltpu.VMEM((4, *messages[0].shape), BF16),
            pltpu.VMEM((2, half, HEAD), F32),
            pltpu.VMEM((2, 2, HEAD), F32),
        ],
    )


def column_of(row):
    return jnp.broadcast_to(row, (HEAD, row.shape[1])).T


def local_grads(table, qkv, out_grad, cumul, first, count, so_far):
    tokens = qkv.shape[1]
    scale = HEAD**-0.5
    size = tokens // 2

    def body(s, qkv_ref, og_ref, cum_ref, *refs):
        out, ready = refs[-2:]
        row = cum_ref[pl.ds(pl.program_id(0) + first, 1), :]
        column = column_of(row)
        wide = jnp.concatenate([column] * (size // HEAD), axis=1)
        s_at = lax.broadcasted_iota(jnp.int32, (size, size), 0)
        t_at = lax.broadcasted_iota(jnp.int32, (size, size), 1)
        parts = [slice(0, size), slice(size, tokens)]

        def pair(t, s):
            if t == s:
                gap = row[:, parts[t]] - wide[parts[s], :]
                decay = jnp.exp(jnp.where(s_at <= t_at, gap, -jnp.inf))
            else:
                middle = row[:, size - 1 : size]
                to_middle = jnp.exp(middle - column[parts[s], :])
                decay = jnp.concatenate([to_middle] * (size // HEAD), axis=1)
                decay *= jnp.exp(row[:, parts[t]] - middle)
            q, k, v = qkv_ref[0, parts[t], :], qkv_ref[1, parts[s], :], qkv_ref[2, parts[s], :]
            g = og_ref[parts[t], :]
            scores = lax.dot_general(k, q, AB_T, preferred_element_type=F32)
            grads = lax.dot_general(v, g, AB_T, preferred_element_type=F32)
            prob = (scores * decay).astype(BF16)
            score = (grads * decay).astype(BF16)
            dq = lax.dot_general(score, k, A_TB, preferred_element_type=F32)
            return dq, dot(score, q), dot(prob, g)

        a, b, c = pair(0, 0), pair(1, 0), pair(1, 1)
        live = living(cum_ref, (tokens, HEAD))
        grads = (
            jnp.concatenate([a[0], b[0] + c[0]], axis=0) * scale,
            jnp.concatenate([a[1] + b[1], c[1]], axis=0) * scale,
            jnp.concatenate([a[2] + b[2], c[2]], axis=0) * scale,
        )
        until = jnp.exp(row[:, tokens - 1 : tokens] - column)
        rows = (
            og_ref[...].astype(F32) * (scale * jnp.exp(column)),
            qkv_ref[2].astype(F32) * until,
            qkv_ref[1].astype(F32) * until,
        )
        for j in range(3):
            out[j] = jnp.where(live, grads[j], 0.0).astype(BF16)
            ready[j] = jnp.where(live, rows[j], 0.0).astype(BF16)

    tile = pl.BlockSpec((3, tokens, HEAD), lambda h, s: (0, 0, h + first))
    in_specs = [tile, pl.BlockSpec((tokens, HEAD), lambda h, s: (0, h + first)), whole(cumul)]
    operands = [qkv, out_grad, cumul]
    if so_far is not None:
        in_specs += [pl.BlockSpec(memory_space=pl.ANY)] * 2
        operands += so_far
    return call(
        "local_grads",
        body,
        table,
        (count,),
        operands,
        in_specs,
        [shape(qkv.shape), shape(qkv.shape)],
        [tile, tile],
        12,
        alias=None if so_far is None else {4: 0, 5: 1},
    )


def whole_grads(table, own, pair, states):
    tokens, heads = own[0].shape[1], HEADS

    def body(s, local_a, ready_a, local_b, ready_b, a, b, c, d, *rest):
        outs, held = rest[:4], rest[4]
        i = pl.program_id(0)

        @pl.when(i == 0)
        def _():
            in_order((a, b, c, d), s[Y], held)

        for which, (local_ref, ready_ref) in enumerate(((local_a, ready_a), (local_b, ready_b))):
            for k in range(heads):

                @pl.when(i == which * heads + k)
                def _(k=k, which=which, local_ref=local_ref, ready_ref=ready_ref):
                    base = pl.multiple_of((s[Z] ^ which) * HEAD, HEAD)
                    coming = held[k, pl.ds(base, HEAD), :]
                    later = held[k, pl.ds(2 * HEAD + base, HEAD), :]
                    cross = (
                        lax.dot_general(ready_ref[0], coming, AB_T, preferred_element_type=F32),
                        lax.dot_general(ready_ref[1], later, AB_T, preferred_element_type=F32),
                        dot(ready_ref[2], later),
                    )
                    out = outs[2 * which + k // 2]
                    for j in range(3):
                        start = (2 * j + k % 2) * HEAD
                        total = local_ref[j].astype(F32) + cross[j]
                        out[:, start : start + HEAD] = total.astype(BF16)

    first = pl.BlockSpec((3, tokens, HEAD), lambda i, s: (0, 0, jnp.minimum(i, heads - 1)))
    second = pl.BlockSpec((3, tokens, HEAD), lambda i, s: (0, 0, jnp.maximum(i - heads, 0)))
    side = shape((tokens, 3 * heads * HEAD // 2))
    return call(
        "whole_grads",
        body,
        table,
        (2 * heads,),
        (*own, *pair, *states),
        [first, first, second, second, *[whole(m) for m in states]],
        [side] * 4,
        [whole(side)] * 4,
        16,
        [pltpu.VMEM((4, *states[0].shape), BF16)],
    )


def split(table, first, second):
    tokens, width = first.shape

    def body(s, a, b, out_a, out_b):
        out_a[...] = a[...]
        out_b[...] = b[...]

    halves = [pl.BlockSpec((tokens // 2, width), lambda i, s, k=k: (k, 0)) for k in range(2)]
    out = shape((tokens // 2, width))
    return call("split", body, table, (1,), (first, second), halves, [out] * 2, [whole(out)] * 2, 8)


def turn(table, shards):
    counts = [len(x) for x in shards]
    flat = [part for x in shards for part in x]
    tokens, width = sum(part.shape[0] for part in shards[0]), flat[0].shape[1]
    rows = 4 * width // 32

    def body(s, *refs):
        out, at = refs[-1], 0
        for k, count in enumerate(counts):
            mine, at = refs[at : at + count], at + count

            @pl.when((pl.program_id(0) ^ s[TEN]) == k)
            def _(mine=mine):
                out[...] = joined(mine).T.reshape(out.shape)

    out = shape((16, 2, rows, tokens))
    spec = pl.BlockSpec((8, 1, rows, tokens), lambda i, s: (i % 2, (i // 2) ^ s[Z], 0, 0))
    turned = call("turn", body, table, (4,), flat, [whole(x) for x in flat], out, spec, 12)
    return turned.reshape(4, 4, 2 * rows, tokens)


def weight_part(table, turned, lefts, rights, places, split):
    tokens, cols = lefts[0].shape
    rows = turned[0].shape[2]

    def body(s, own_x, own_y, pair_x, pair_y, left_a, left_b, right_a, right_b, *outs):
        r = pl.program_id(0)
        for side, (a, b, ga, gb) in enumerate(
            ((own_x, pair_x, left_a, left_b), (own_y, pair_y, right_a, right_b))
        ):
            acc = dot(a[...].reshape(4 * rows, tokens), ga[...])
            acc += dot(b[...].reshape(4 * rows, tokens), gb[...])
            acc = acc.astype(BF16)
            if split:
                outs[2 * side][...] = acc[: 2 * rows]
                outs[2 * side + 1][...] = acc[2 * rows :]
                continue
            for k in range(len(places)):

                @pl.when(r == k)
                def _(k=k, acc=acc, side=side):
                    outs[side * len(places) + k][...] = acc

    step = places[1] - places[0] if len(places) > 1 else 0
    by_x = pl.BlockSpec((1, 4, rows, tokens), lambda r, s: (s[X] ^ (places[0] + step * r), 0, 0, 0))
    by_y = pl.BlockSpec((4, 1, rows, tokens), lambda r, s: (0, s[Y] ^ (places[0] + step * r), 0, 0))
    outs = [shape((2 * rows if split else 4 * rows, cols))] * (4 if split else 2 * len(places))
    operands = (turned[0], turned[0], turned[1], turned[1], *lefts, *rights)
    return call(
        "weight_part",
        body,
        table,
        (len(places),),
        operands,
        [by_x, by_y, by_x, by_y, *[whole(x) for x in (*lefts, *rights)]],
        outs,
        [whole(o) for o in outs],
        30,
    )


def add_halves(table, third, first_place, halves):
    up, down = halves
    near_up, near_down = third, first_place
    n, cols = up.shape

    def body(s, a, b, u, d, out_a, out_b):
        out_a[...] = (a[...].astype(F32) + u[...].astype(F32)).astype(BF16)
        out_b[...] = (b[...].astype(F32) + d[...].astype(F32)).astype(BF16)

    first = pl.BlockSpec((n, cols), lambda i, s: (0, 0))
    second = pl.BlockSpec((n, cols), lambda i, s: (1, 0))
    return call(
        "add_halves",
        body,
        table,
        (1,),
        (near_up, near_down, up, down),
        [first, second, first, first],
        [shape(near_up.shape), shape(near_down.shape)],
        [first, second],
        12,
        alias={1: 0, 2: 1},
    )


def cut_blocks(table, axis, parts):
    rows, cols = parts[0].shape[0] // 4, parts[0].shape[1]

    def body(s, a, b, c, *outs):
        for r, out in zip((1, 3, 2, 0), outs):
            at = pl.ds(pl.multiple_of((s[axis] ^ r) * rows, rows), rows)
            total = a[at, :].astype(F32) + b[at, :].astype(F32) + c[at, :].astype(F32)
            out[...] = total.astype(BF16)

    outs = [shape((rows, cols))] * 4
    return call(
        "cut_blocks",
        body,
        table,
        (1,),
        parts,
        [whole(x) for x in parts],
        outs,
        [whole(o) for o in outs],
        16,
    )


def final_sums(table, parts):
    rows, cols = parts[0].shape

    def body(s, a, b, c, d, here, there):
        total = sum(ref[...].astype(F32) for ref in (a, b, c, d)).astype(BF16)
        here[...] = total[: rows // 2]
        there[...] = total[rows // 2 :]

    outs = [shape((rows // 2, cols))] * 2
    return call(
        "final_sums",
        body,
        table,
        (1,),
        parts,
        [whole(x) for x in parts],
        outs,
        [whole(o) for o in outs],
        8,
    )


def finish(table, here, there):
    rows, cols = here[0].shape
    side = cols // 3

    def body(s, *refs):
        out = refs[-1]
        for i, half in enumerate((s[Z], 1 - s[Z])):
            for k in range(2):
                for j in range(3):
                    at = pl.ds(pl.multiple_of(half * 2 * side + k * side, side), side)
                    out[j, :, at] = refs[2 * i + k][:, j * side : (j + 1) * side].astype(F32)

    out = shape((3, rows, 4 * side), F32)
    operands = (*here, *there)
    return call("finish", body, table, (1,), operands, [whole(x) for x in operands], out, whole(out), 8)


def swaps(pieces, left, right):
    a, c = send(pieces[0], left, 1), send(pieces[2], right, 1)
    b, d = send(pieces[1], left, 3), send(pieces[3], right, 3)
    return [a, b], [c, d]


def device_part(activations, qkv_weight, log_decay, lengths, out_grad):
    tied = lax.optimization_barrier
    tokens = activations.shape[0]
    heads = log_decay.shape[1]
    per = heads // 2
    index = [lax.axis_index(a) for a in ("c0", "c1", "c2", "zl", "co")]
    here_z = index[0]
    fixed = [*index, index[3] * 2 + index[4]]
    table = jnp.stack(fixed).astype(jnp.int32)
    weight = pltpu.with_memory_space_constraint(jnp.transpose(qkv_weight, (1, 0, 2)), pltpu.HBM)

    near = send(activations, "zl", 1)
    side = across(activations)
    core = send(activations, "co", 1)

    live = (jnp.arange(tokens, dtype=jnp.int32) < lengths[0]).astype(F32)
    cumul = jnp.cumsum(log_decay.T * live[None, :], axis=1)
    size = jnp.broadcast_to(lengths.astype(F32)[:, None], (per, tokens))
    info, note = (
        jnp.concatenate([lax.dynamic_slice_in_dim(cumul, z * per, per), size])
        for z in (here_z, 1 - here_z)
    )
    note = send(note, "c0", 1)
    width = per * HEAD
    og_own = lax.dynamic_slice_in_dim(out_grad, here_z * width, width, axis=1)
    og_other = lax.dynamic_slice_in_dim(out_grad, (1 - here_z) * width, width, axis=1)

    acc_own = project(table, [[activations], [core]], (0, 1), weight, None, None)
    near, side, acc_own, note, og_other, info = tied((near, side, acc_own, note, og_other, info))
    far = split(table, side, near)
    far = [send(far[0], "zl", 1), across(far[1])]
    near_core = send(near, "co", 1)
    side_core = send(side, "co", 1)
    qkv_own = project(table, [[near], [near_core]], (2, 3), weight, acc_own, info)
    turned = [turn(table, tied(([[activations], [core], [near], [near_core]], qkv_own))[0])]
    far, side_core, qkv_own, turned = tied((far, side_core, qkv_own, turned))
    far_core = [send(x, "co", 1) for x in far]
    og_pair = send(tied((og_other, far))[0], "c0", 1)
    to_y = shard_states(table, qkv_own, og_own, info, 0, None)
    far_core, to_y = tied((far_core, to_y))
    qkv_pair = project(
        table, [[side], [side_core], far, far_core], (2, 3, 0, 1), weight, None, note
    )
    og_pair, qkv_pair = tied((og_pair, qkv_pair))

    to_y = shard_states(table, qkv_pair, og_pair, note, 1, to_y)
    at_y = [send(to_y[r], "c2", r) for r in (1, 3, 2)]
    qkv_own, _ = tied((qkv_own, to_y[0]))
    local_own = local_grads(table, qkv_own, og_own, info, 0, per, None)
    at_y, local_own = tied((at_y, local_own))
    before, after, prior, later, ring = ring_y(table, [to_y[0], at_y[0], at_y[2], at_y[1]])
    at_x = [send(ring, "c1", r) for r in (1, 3, 2)]
    qkv_pair, _ = tied((qkv_pair, ring))
    local = local_grads(table, qkv_pair, og_pair, note, 0, per // 2, None)
    second, _ = tied(([far, far_core, [side], [side_core]], ring))
    turned.append(turn(table, second))
    at_x, local, turned = tied((at_x, local, turned))
    back = arrivals(table, [ring, at_x[0], at_x[2], at_x[1]], before, after, prior, later)
    states = [send(back[r], "c2", r) for r in (1, 3, 2)]
    local, _ = tied((local, back[0]))
    local = local_grads(table, qkv_pair, og_pair, note, per // 2, per // 2, local)
    states, turned, local = tied((states, turned, local))
    states = [back[0], states[0], states[2], states[1]]

    left_own, right_own, left_pair, right_pair = whole_grads(table, local_own, local, states)
    lefts, rights = (left_own, left_pair), (right_own, right_pair)
    far_piece = weight_part(table, turned, lefts, rights, (2,), True)
    l_half, r_half = swaps(far_piece, "c1", "c2")
    turned, _ = tied((turned, far_piece[0]))
    l_one, l_three, r_one, r_three = weight_part(table, turned, lefts, rights, (1, 3), False)
    l_half, l_one = tied((l_half, l_one))
    l_three, l_one = add_halves(table, l_three, l_one, l_half)
    l_got = [send(l_one, "c1", 1), send(l_three, "c1", 3)]
    r_half, _ = tied((r_half, l_one))
    r_three, r_one = add_halves(table, r_three, r_one, r_half)
    r_got = [send(r_one, "c2", 1), send(r_three, "c2", 3)]
    turned, _ = tied((turned, r_one))
    own = weight_part(table, turned, lefts, rights, (0,), False)
    l_got, own = tied((l_got, own))
    l_cut = cut_blocks(table, Y, (own[0], *l_got))
    r_got, _ = tied((r_got, l_cut[3]))
    r_cut = cut_blocks(table, X, (own[1], *r_got))
    l_got = [send(x, "c2", by) for x, by in zip(l_cut, (1, 3, 2))]
    r_got = [send(x, "c1", by) for x, by in zip(r_cut, (1, 3, 2))]
    l_got, _ = tied((l_got, r_cut[3]))
    l_here, l_there = final_sums(table, (l_cut[3], *l_got))
    r_got, _ = tied((r_got, l_here))
    r_here, r_there = final_sums(table, (r_cut[3], *r_got))
    l_there = send(l_there, "c0", 1)
    l_there, r_there = tied((l_there, r_there))
    there = [l_there, send(r_there, "c0", 1)]
    return jnp.transpose(finish(table, (l_here, r_here), there), (1, 0, 2))


def solution(mesh):
    finer = Mesh(mesh.devices.reshape(2, 4, 4, 2, 2), ("c0", "c1", "c2", "zl", "co"))
    context, tensor = ("c0", "c1", "c2"), ("zl", "co")
    placed = (
        P(context, tensor),
        P(None, None, tensor),
        P(context, tensor),
        P(context),
        P(context, tensor),
    )
    return jax.shard_map(
        device_part,
        mesh=finer,
        in_specs=placed,
        out_specs=P(context, None, tensor),
        check_vma=False,
    )
```

```python
import jax
import jax.numpy as jnp
from jax import lax
from jax.experimental import pallas as pl
from jax.experimental.pallas import tpu as pltpu
from jax.sharding import Mesh
from jax.sharding import PartitionSpec as P

F32 = jnp.float32
BF16 = jnp.bfloat16
HEAD = 128
HEADS = 4
Z, X, Y, ZL, CO, TEN = range(6)
AB_T = (((1,), (1,)), ((), ()))
A_TB = (((0,), (0,)), ((), ()))


def dot(a, b):
    return jnp.dot(a, b, preferred_element_type=F32)


def send(x, axis, by):
    return lax.ppermute(x, axis, [(i, i ^ by) for i in range(lax.axis_size(axis))])


def across(x):
    return lax.ppermute(x, ("c0", "zl"), [(0, 3), (1, 2), (2, 1), (3, 0)])


def whole(x):
    return pl.BlockSpec(x.shape, lambda *_, n=len(x.shape): (0,) * n)


def call(name, body, table, grid, operands, in_specs, outs, out_specs, mib, scratch=(), alias=None):
    return pl.pallas_call(
        body,
        grid_spec=pltpu.PrefetchScalarGridSpec(
            num_scalar_prefetch=1,
            grid=grid,
            in_specs=in_specs,
            out_specs=out_specs,
            scratch_shapes=scratch,
        ),
        out_shape=outs,
        input_output_aliases=alias or {},
        compiler_params=pltpu.CompilerParams(
            dimension_semantics=("arbitrary",) * len(grid), vmem_limit_bytes=mib << 20
        ),
        cost_estimate=pl.CostEstimate(flops=1, bytes_accessed=1, transcendentals=0),
        name=name,
    )(table, *operands)


def shape(dims, kind=BF16):
    return jax.ShapeDtypeStruct(dims, kind)


def joined(refs):
    parts = [ref[...] for ref in refs]
    return parts[0] if len(parts) == 1 else jnp.concatenate(parts, axis=0)


def living(info, dims):
    row = lax.broadcasted_iota(jnp.int32, dims, 0).astype(F32)
    return row < info[HEADS : HEADS + 1, :1]


def project(table, shards, flips, weight, partial, info):
    last = info is not None
    n, counts = len(shards), [len(x) for x in shards]
    flat = [part for x in shards for part in x]
    tokens, width = sum(part.shape[0] for part in shards[0]), flat[0].shape[1]
    cols = weight.shape[2] // 2

    def body(s, *refs):
        out, rest = refs[-1], list(refs)
        acc = None
        for i, count in enumerate(counts):
            rows = joined([rest.pop(0) for _ in range(count)])
            term = dot(rows, refs[len(flat) + i][0])
            acc = term if acc is None else acc + term
        if partial is not None:
            acc += refs[len(flat) + n][0]
        if last:
            acc = jnp.where(living(refs[-2], acc.shape), acc, 0.0)
        out[0] = acc.astype(out.dtype)

    tile = pl.BlockSpec((1, tokens, cols), lambda g, s: (g, 0, 0))
    in_specs = [whole(x) for x in flat]
    for flip in flips:
        in_specs.append(
            pl.BlockSpec((1, width, cols), lambda g, s, flip=flip: (g, s[TEN] ^ flip, s[Z]))
        )
    operands = [*flat, *([weight] * n)]
    if partial is not None:
        in_specs.append(tile)
        operands.append(partial)
    if last:
        in_specs.append(whole(info))
        operands.append(info)
    out = shape((3, tokens, cols), BF16 if last else F32)
    return call("project", body, table, (3,), operands, in_specs, out, tile, 24)


def shard_states(table, qkv, out_grad, cumul, which, so_far):
    tokens = qkv.shape[1]
    scale = HEAD**-0.5

    def body(s, qkv_ref, og_ref, cum_ref, *refs):
        outs = refs[-4:]
        r = pl.program_id(0)
        row = cum_ref[pl.ds(s[Y] ^ r, 1), :]
        total = row[:, tokens - 1 : tokens]
        keys_t = qkv_ref[1].T.astype(F32)
        query_t = qkv_ref[0].T.astype(F32)
        keys_t = (keys_t * jnp.exp(total - row)).astype(BF16)
        query_t = (query_t * (scale * jnp.exp(row))).astype(BF16)
        states = (dot(keys_t, qkv_ref[2]), dot(query_t, og_ref[...]))
        at = lax.broadcasted_iota(jnp.int32, (16, HEAD), 0)
        tail = jnp.broadcast_to(total, (16, HEAD)).astype(BF16)
        for k, out in enumerate(outs):

            @pl.when(r == k)
            def _(k=k, out=out):
                here = s[Z] ^ which
                if so_far is not None:
                    out[...] = refs[k][...]
                for kind in range(2):
                    start = pl.multiple_of((2 * kind + here) * HEAD, HEAD)
                    out[pl.ds(start, HEAD), :] = states[kind].astype(BF16)
                if so_far is None:
                    out[4 * HEAD :, :] = tail
                else:
                    out[4 * HEAD :, :] = jnp.where(at == here, tail, refs[k][4 * HEAD :, :])

    message = shape((4 * HEAD + 16, HEAD))
    operands = [qkv, out_grad, cumul, *(so_far or ())]
    in_specs = [
        pl.BlockSpec((3, tokens, HEAD), lambda r, s: (0, 0, s[Y] ^ r)),
        pl.BlockSpec((tokens, HEAD), lambda r, s: (0, s[Y] ^ r)),
        whole(cumul),
        *[whole(m) for m in so_far or ()],
    ]
    return call(
        "shard_states",
        body,
        table,
        (4,),
        operands,
        in_specs,
        [message] * 4,
        [whole(message)] * 4,
        12,
    )


def in_order(refs, place, held):
    for r, ref in enumerate(refs):
        held[place ^ r] = ref[...]


def spread(pair):
    wide = [jnp.broadcast_to(pair[i : i + 1, :], (HEAD, HEAD)) for i in range(2)]
    return jnp.concatenate(wide, axis=0)


def ring_y(table, messages):
    half = 2 * HEAD

    def body(s, a, b, c, d, before, after, prior, later, out, held):
        in_order((a, b, c, d), s[Y], held)
        totals = [held[t, 2 * half : 2 * half + 16, :].astype(F32)[:2] for t in range(4)]
        run = jnp.zeros((half, HEAD), F32)
        reach = jnp.zeros((2, HEAD), F32)
        for t in range(4):
            before[t] = run
            prior[t] = jnp.exp(reach)
            run = spread(jnp.exp(totals[t])) * run + held[t, :half, :].astype(F32)
            reach = reach + totals[t]
        out[:half, :] = run.astype(BF16)
        total = reach
        run = jnp.zeros((half, HEAD), F32)
        reach = jnp.zeros((2, HEAD), F32)
        for t in range(3, -1, -1):
            after[t] = run
            later[t] = jnp.exp(reach)
            run = spread(jnp.exp(totals[t])) * run + held[t, half : 2 * half, :].astype(F32)
            reach = reach + totals[t]
        out[half : 2 * half, :] = run.astype(BF16)
        high = total.astype(BF16).astype(F32)
        low = total - high
        at = lax.broadcasted_iota(jnp.int32, (16, HEAD), 0)
        tail = jnp.where(at == 0, high[0:1], high[1:2])
        tail = jnp.where(at == 2, low[0:1], tail)
        tail = jnp.where(at == 3, low[1:2], tail)
        out[2 * half :, :] = tail.astype(BF16)

    outs = [
        shape((4, half, HEAD), F32),
        shape((4, half, HEAD), F32),
        shape((4, 2, HEAD), F32),
        shape((4, 2, HEAD), F32),
        shape(messages[0].shape),
    ]
    return call(
        "ring_y",
        body,
        table,
        (1,),
        messages,
        [whole(m) for m in messages],
        outs,
        [whole(o) for o in outs],
        8,
        [pltpu.VMEM((4, *messages[0].shape), BF16)],
    )


def arrivals(table, messages, before, after, prior, later):
    half = 2 * HEAD

    def body(s, a, b, c, d, before_ref, after_ref, prior_ref, later_ref, *rest):
        outs, held, mine, edges = rest[:4], *rest[4:]
        in_order((a, b, c, d), s[X], held)
        tails = [held[t, 2 * half : 2 * half + 16, :].astype(F32) for t in range(4)]
        totals = [tail[0:2] + tail[2:4] for tail in tails]
        ends = []
        for kind, steps in ((0, range(4)), (1, range(3, -1, -1))):
            run = jnp.zeros((half, HEAD), F32)
            reach = jnp.zeros((2, HEAD), F32)
            for t in steps:

                @pl.when(s[X] == t)
                def _(run=run, reach=reach, kind=kind):
                    mine[kind] = run
                    edges[kind] = jnp.exp(reach)

                rows = held[t, kind * half : (kind + 1) * half, :].astype(F32)
                run = spread(jnp.exp(totals[t])) * run + rows
                reach = reach + totals[t]
            ends.append(run.astype(BF16).astype(F32))
        nothing = jnp.zeros((HEAD, HEAD), F32)
        across_up = jnp.concatenate([nothing, ends[0][:HEAD]], axis=0)
        across_down = jnp.concatenate([ends[1][HEAD:], nothing], axis=0)
        start = mine[0] + spread(edges[0]) * across_up
        finish = mine[1] + spread(edges[1]) * across_down
        for r, out in enumerate(outs):
            t = s[Y] ^ r
            out[:half, :] = (before_ref[t] + spread(prior_ref[t]) * start).astype(BF16)
            out[half:, :] = (after_ref[t] + spread(later_ref[t]) * finish).astype(BF16)

    operands = (*messages, before, after, prior, later)
    message = shape((2 * half, HEAD))
    return call(
        "arrivals",
        body,
        table,
        (1,),
        operands,
        [whole(m) for m in operands],
        [message] * 4,
        [whole(message)] * 4,
        8,
        [
            pltpu.VMEM((4, *messages[0].shape), BF16),
            pltpu.VMEM((2, half, HEAD), F32),
            pltpu.VMEM((2, 2, HEAD), F32),
        ],
    )


def column_of(row):
    return jnp.broadcast_to(row, (HEAD, row.shape[1])).T


def local_grads(table, qkv, out_grad, cumul, first, count, so_far):
    tokens = qkv.shape[1]
    scale = HEAD**-0.5
    size = tokens // 2

    def body(s, qkv_ref, og_ref, cum_ref, *refs):
        out, ready = refs[-2:]
        row = cum_ref[pl.ds(pl.program_id(0) + first, 1), :]
        column = column_of(row)
        wide = jnp.concatenate([column] * (size // HEAD), axis=1)
        s_at = lax.broadcasted_iota(jnp.int32, (size, size), 0)
        t_at = lax.broadcasted_iota(jnp.int32, (size, size), 1)
        parts = [slice(0, size), slice(size, tokens)]

        def pair(t, s):
            if t == s:
                gap = row[:, parts[t]] - wide[parts[s], :]
                decay = jnp.exp(jnp.where(s_at <= t_at, gap, -jnp.inf))
            else:
                middle = row[:, size - 1 : size]
                to_middle = jnp.exp(middle - column[parts[s], :])
                decay = jnp.concatenate([to_middle] * (size // HEAD), axis=1)
                decay *= jnp.exp(row[:, parts[t]] - middle)
            q, k, v = qkv_ref[0, parts[t], :], qkv_ref[1, parts[s], :], qkv_ref[2, parts[s], :]
            g = og_ref[parts[t], :]
            scores = lax.dot_general(k, q, AB_T, preferred_element_type=F32)
            grads = lax.dot_general(v, g, AB_T, preferred_element_type=F32)
            prob = (scores * decay).astype(BF16)
            score = (grads * decay).astype(BF16)
            dq = lax.dot_general(score, k, A_TB, preferred_element_type=F32)
            return dq, dot(score, q), dot(prob, g)

        a, b, c = pair(0, 0), pair(1, 0), pair(1, 1)
        live = living(cum_ref, (tokens, HEAD))
        grads = (
            jnp.concatenate([a[0], b[0] + c[0]], axis=0) * scale,
            jnp.concatenate([a[1] + b[1], c[1]], axis=0) * scale,
            jnp.concatenate([a[2] + b[2], c[2]], axis=0) * scale,
        )
        until = jnp.exp(row[:, tokens - 1 : tokens] - column)
        rows = (
            og_ref[...].astype(F32) * (scale * jnp.exp(column)),
            qkv_ref[2].astype(F32) * until,
            qkv_ref[1].astype(F32) * until,
        )
        for j in range(3):
            out[j] = jnp.where(live, grads[j], 0.0).astype(BF16)
            ready[j] = jnp.where(live, rows[j], 0.0).astype(BF16)

    tile = pl.BlockSpec((3, tokens, HEAD), lambda h, s: (0, 0, h + first))
    in_specs = [tile, pl.BlockSpec((tokens, HEAD), lambda h, s: (0, h + first)), whole(cumul)]
    operands = [qkv, out_grad, cumul]
    if so_far is not None:
        in_specs += [pl.BlockSpec(memory_space=pl.ANY)] * 2
        operands += so_far
    return call(
        "local_grads",
        body,
        table,
        (count,),
        operands,
        in_specs,
        [shape(qkv.shape), shape(qkv.shape)],
        [tile, tile],
        12,
        alias=None if so_far is None else {4: 0, 5: 1},
    )


def whole_grads(table, own, pair, states):
    tokens, heads = own[0].shape[1], HEADS

    def body(s, local_a, ready_a, local_b, ready_b, a, b, c, d, *rest):
        outs, held = rest[:4], rest[4]
        i = pl.program_id(0)

        @pl.when(i == 0)
        def _():
            in_order((a, b, c, d), s[Y], held)

        for which, (local_ref, ready_ref) in enumerate(((local_a, ready_a), (local_b, ready_b))):
            for k in range(heads):

                @pl.when(i == which * heads + k)
                def _(k=k, which=which, local_ref=local_ref, ready_ref=ready_ref):
                    base = pl.multiple_of((s[Z] ^ which) * HEAD, HEAD)
                    coming = held[k, pl.ds(base, HEAD), :]
                    later = held[k, pl.ds(2 * HEAD + base, HEAD), :]
                    cross = (
                        lax.dot_general(ready_ref[0], coming, AB_T, preferred_element_type=F32),
                        lax.dot_general(ready_ref[1], later, AB_T, preferred_element_type=F32),
                        dot(ready_ref[2], later),
                    )
                    out = outs[2 * which + k // 2]
                    for j in range(3):
                        start = (2 * j + k % 2) * HEAD
                        total = local_ref[j].astype(F32) + cross[j]
                        out[:, start : start + HEAD] = total.astype(BF16)

    first = pl.BlockSpec((3, tokens, HEAD), lambda i, s: (0, 0, jnp.minimum(i, heads - 1)))
    second = pl.BlockSpec((3, tokens, HEAD), lambda i, s: (0, 0, jnp.maximum(i - heads, 0)))
    side = shape((tokens, 3 * heads * HEAD // 2))
    return call(
        "whole_grads",
        body,
        table,
        (2 * heads,),
        (*own, *pair, *states),
        [first, first, second, second, *[whole(m) for m in states]],
        [side] * 4,
        [whole(side)] * 4,
        16,
        [pltpu.VMEM((4, *states[0].shape), BF16)],
    )


def split(table, first, second):
    tokens, width = first.shape

    def body(s, a, b, out_a, out_b):
        out_a[...] = a[...]
        out_b[...] = b[...]

    halves = [pl.BlockSpec((tokens // 2, width), lambda i, s, k=k: (k, 0)) for k in range(2)]
    out = shape((tokens // 2, width))
    return call("split", body, table, (1,), (first, second), halves, [out] * 2, [whole(out)] * 2, 8)


def turn(table, shards):
    counts = [len(x) for x in shards]
    flat = [part for x in shards for part in x]
    tokens, width = sum(part.shape[0] for part in shards[0]), flat[0].shape[1]
    rows = 4 * width // 32

    def body(s, *refs):
        out, at = refs[-1], 0
        for k, count in enumerate(counts):
            mine, at = refs[at : at + count], at + count

            @pl.when((pl.program_id(0) ^ s[TEN]) == k)
            def _(mine=mine):
                out[...] = joined(mine).T.reshape(out.shape)

    out = shape((16, 2, rows, tokens))
    spec = pl.BlockSpec((8, 1, rows, tokens), lambda i, s: (i % 2, (i // 2) ^ s[Z], 0, 0))
    turned = call("turn", body, table, (4,), flat, [whole(x) for x in flat], out, spec, 12)
    return turned.reshape(4, 4, 2 * rows, tokens)


def weight_part(table, turned, lefts, rights, places, split):
    tokens, cols = lefts[0].shape
    rows = turned[0].shape[2]

    def body(s, own_x, own_y, pair_x, pair_y, left_a, left_b, right_a, right_b, *outs):
        r = pl.program_id(0)
        for side, (a, b, ga, gb) in enumerate(
            ((own_x, pair_x, left_a, left_b), (own_y, pair_y, right_a, right_b))
        ):
            acc = dot(a[...].reshape(4 * rows, tokens), ga[...])
            acc += dot(b[...].reshape(4 * rows, tokens), gb[...])
            acc = acc.astype(BF16)
            if split:
                outs[2 * side][...] = acc[: 2 * rows]
                outs[2 * side + 1][...] = acc[2 * rows :]
                continue
            for k in range(len(places)):

                @pl.when(r == k)
                def _(k=k, acc=acc, side=side):
                    outs[side * len(places) + k][...] = acc

    step = places[1] - places[0] if len(places) > 1 else 0
    by_x = pl.BlockSpec((1, 4, rows, tokens), lambda r, s: (s[X] ^ (places[0] + step * r), 0, 0, 0))
    by_y = pl.BlockSpec((4, 1, rows, tokens), lambda r, s: (0, s[Y] ^ (places[0] + step * r), 0, 0))
    outs = [shape((2 * rows if split else 4 * rows, cols))] * (4 if split else 2 * len(places))
    operands = (turned[0], turned[0], turned[1], turned[1], *lefts, *rights)
    return call(
        "weight_part",
        body,
        table,
        (len(places),),
        operands,
        [by_x, by_y, by_x, by_y, *[whole(x) for x in (*lefts, *rights)]],
        outs,
        [whole(o) for o in outs],
        30,
    )


def add_halves(table, third, first_place, halves):
    up, down = halves
    near_up, near_down = third, first_place
    n, cols = up.shape

    def body(s, a, b, u, d, out_a, out_b):
        out_a[...] = (a[...].astype(F32) + u[...].astype(F32)).astype(BF16)
        out_b[...] = (b[...].astype(F32) + d[...].astype(F32)).astype(BF16)

    steps = 4
    first = pl.BlockSpec((n // steps, cols), lambda i, s: (i, 0))
    second = pl.BlockSpec((n // steps, cols), lambda i, s: (i + steps, 0))
    return call(
        "add_halves",
        body,
        table,
        (steps,),
        (near_up, near_down, up, down),
        [first, second, first, first],
        [shape(near_up.shape), shape(near_down.shape)],
        [first, second],
        12,
        alias={1: 0, 2: 1},
    )


def cut_blocks(table, axis, parts):
    rows, cols = parts[0].shape[0] // 4, parts[0].shape[1]

    def body(s, a, b, c, *outs):
        for r, out in zip((1, 3, 2, 0), outs):
            at = pl.ds(pl.multiple_of((s[axis] ^ r) * rows, rows), rows)
            total = a[at, :].astype(F32) + b[at, :].astype(F32) + c[at, :].astype(F32)
            out[...] = total.astype(BF16)

    outs = [shape((rows, cols))] * 4
    return call(
        "cut_blocks",
        body,
        table,
        (1,),
        parts,
        [whole(x) for x in parts],
        outs,
        [whole(o) for o in outs],
        16,
    )


def final_sums(table, parts):
    rows, cols = parts[0].shape

    def body(s, a, b, c, d, here, there):
        total = sum(ref[...].astype(F32) for ref in (a, b, c, d)).astype(BF16)
        here[...] = total[: rows // 2]
        there[...] = total[rows // 2 :]

    outs = [shape((rows // 2, cols))] * 2
    return call(
        "final_sums",
        body,
        table,
        (1,),
        parts,
        [whole(x) for x in parts],
        outs,
        [whole(o) for o in outs],
        8,
    )


def finish(table, here, there):
    rows, cols = here[0].shape
    side = cols // 3

    def body(s, *refs):
        out = refs[-1]
        for i, half in enumerate((s[Z], 1 - s[Z])):
            for k in range(2):
                at = pl.ds(pl.multiple_of(half * 2 * side + k * side, side), side)
                out[0, :, at] = refs[2 * i + k][...].astype(F32)

    out = shape((3, rows, 4 * side), F32)
    part = pl.BlockSpec((rows, side), lambda j, s: (0, j))
    spec = pl.BlockSpec((1, rows, 4 * side), lambda j, s: (j, 0, 0))
    return call("finish", body, table, (3,), (*here, *there), [part] * 4, out, spec, 8)


def swaps(pieces, left, right):
    a, c = send(pieces[0], left, 1), send(pieces[2], right, 1)
    b, d = send(pieces[1], left, 3), send(pieces[3], right, 3)
    return [a, b], [c, d]


def device_part(activations, qkv_weight, log_decay, lengths, out_grad):
    tied = lax.optimization_barrier
    tokens = activations.shape[0]
    heads = log_decay.shape[1]
    per = heads // 2
    index = [lax.axis_index(a) for a in ("c0", "c1", "c2", "zl", "co")]
    here_z = index[0]
    fixed = [*index, index[3] * 2 + index[4]]
    table = jnp.stack(fixed).astype(jnp.int32)
    weight = pltpu.with_memory_space_constraint(jnp.transpose(qkv_weight, (1, 0, 2)), pltpu.HBM)

    near = send(activations, "zl", 1)
    side = across(activations)
    core = send(activations, "co", 1)

    live = (jnp.arange(tokens, dtype=jnp.int32) < lengths[0]).astype(F32)
    cumul = jnp.cumsum(log_decay.T * live[None, :], axis=1)
    size = jnp.broadcast_to(lengths.astype(F32)[:, None], (per, tokens))
    info, note = (
        jnp.concatenate([lax.dynamic_slice_in_dim(cumul, z * per, per), size])
        for z in (here_z, 1 - here_z)
    )
    note = send(note, "c0", 1)
    width = per * HEAD
    og_own = lax.dynamic_slice_in_dim(out_grad, here_z * width, width, axis=1)
    og_other = lax.dynamic_slice_in_dim(out_grad, (1 - here_z) * width, width, axis=1)

    acc_own = project(table, [[activations], [core]], (0, 1), weight, None, None)
    near, side, acc_own, note, og_other, info = tied((near, side, acc_own, note, og_other, info))
    far = split(table, side, near)
    far = [send(far[0], "zl", 1), across(far[1])]
    near_core = send(near, "co", 1)
    side_core = send(side, "co", 1)
    qkv_own = project(table, [[near], [near_core]], (2, 3), weight, acc_own, info)
    turned = [turn(table, tied(([[activations], [core], [near], [near_core]], qkv_own))[0])]
    far, side_core, qkv_own, turned = tied((far, side_core, qkv_own, turned))
    far_core = [send(x, "co", 1) for x in far]
    og_pair = send(tied((og_other, far))[0], "c0", 1)
    to_y = shard_states(table, qkv_own, og_own, info, 0, None)
    far_core, to_y = tied((far_core, to_y))
    qkv_pair = project(
        table, [[side], [side_core], far, far_core], (2, 3, 0, 1), weight, None, note
    )
    og_pair, qkv_pair = tied((og_pair, qkv_pair))

    to_y = shard_states(table, qkv_pair, og_pair, note, 1, to_y)
    at_y = [send(to_y[r], "c2", r) for r in (1, 3, 2)]
    qkv_own, _ = tied((qkv_own, to_y[0]))
    local_own = local_grads(table, qkv_own, og_own, info, 0, per, None)
    at_y, local_own = tied((at_y, local_own))
    before, after, prior, later, ring = ring_y(table, [to_y[0], at_y[0], at_y[2], at_y[1]])
    at_x = [send(ring, "c1", r) for r in (1, 3, 2)]
    qkv_pair, _ = tied((qkv_pair, ring))
    local = local_grads(table, qkv_pair, og_pair, note, 0, per // 2, None)
    second, _ = tied(([far, far_core, [side], [side_core]], ring))
    turned.append(turn(table, second))
    at_x, local, turned = tied((at_x, local, turned))
    back = arrivals(table, [ring, at_x[0], at_x[2], at_x[1]], before, after, prior, later)
    states = [send(back[r], "c2", r) for r in (1, 3, 2)]
    local, _ = tied((local, back[0]))
    local = local_grads(table, qkv_pair, og_pair, note, per // 2, per // 2, local)
    states, turned, local = tied((states, turned, local))
    states = [back[0], states[0], states[2], states[1]]

    left_own, right_own, left_pair, right_pair = whole_grads(table, local_own, local, states)
    lefts, rights = (left_own, left_pair), (right_own, right_pair)
    far_piece = weight_part(table, turned, lefts, rights, (2,), True)
    l_half, r_half = swaps(far_piece, "c1", "c2")
    turned, _ = tied((turned, far_piece[0]))
    l_one, l_three, r_one, r_three = weight_part(table, turned, lefts, rights, (1, 3), False)
    l_half, l_one = tied((l_half, l_one))
    l_three, l_one = add_halves(table, l_three, l_one, l_half)
    l_got = [send(l_one, "c1", 1), send(l_three, "c1", 3)]
    r_half, _ = tied((r_half, l_one))
    r_three, r_one = add_halves(table, r_three, r_one, r_half)
    r_got = [send(r_one, "c2", 1), send(r_three, "c2", 3)]
    turned, _ = tied((turned, r_one))
    own = weight_part(table, turned, lefts, rights, (0,), False)
    l_got, own = tied((l_got, own))
    l_cut = cut_blocks(table, Y, (own[0], *l_got))
    r_got, _ = tied((r_got, l_cut[3]))
    r_cut = cut_blocks(table, X, (own[1], *r_got))
    l_got = [send(x, "c2", by) for x, by in zip(l_cut, (1, 3, 2))]
    r_got = [send(x, "c1", by) for x, by in zip(r_cut, (1, 3, 2))]
    l_got, _ = tied((l_got, r_cut[3]))
    l_here, l_there = final_sums(table, (l_cut[3], *l_got))
    r_got, _ = tied((r_got, l_here))
    r_here, r_there = final_sums(table, (r_cut[3], *r_got))
    l_there = send(l_there, "c0", 1)
    l_there, r_here = tied((l_there, r_here))
    there = [l_there, send(r_there, "c0", 1)]
    return jnp.transpose(finish(table, (l_here, r_here), there), (1, 0, 2))


def solution(mesh):
    finer = Mesh(mesh.devices.reshape(2, 4, 4, 2, 2), ("c0", "c1", "c2", "zl", "co"))
    context, tensor = ("c0", "c1", "c2"), ("zl", "co")
    placed = (
        P(context, tensor),
        P(None, None, tensor),
        P(context, tensor),
        P(context),
        P(context, tensor),
    )
    return jax.shard_map(
        device_part,
        mesh=finer,
        in_specs=placed,
        out_specs=P(context, None, tensor),
        check_vma=False,
    )
```

```python
import jax
import jax.numpy as jnp
from jax import lax
from jax.experimental import pallas as pl
from jax.experimental.pallas import tpu as pltpu
from jax.sharding import Mesh
from jax.sharding import PartitionSpec as P

F32 = jnp.float32
BF16 = jnp.bfloat16
HEAD = 128
HEADS = 4
Z, X, Y, ZL, CO, TEN = range(6)
AB_T = (((1,), (1,)), ((), ()))
A_TB = (((0,), (0,)), ((), ()))


def dot(a, b):
    return jnp.dot(a, b, preferred_element_type=F32)


def send(x, axis, by):
    return lax.ppermute(x, axis, [(i, i ^ by) for i in range(lax.axis_size(axis))])


def across(x):
    return lax.ppermute(x, ("c0", "zl"), [(0, 3), (1, 2), (2, 1), (3, 0)])


def whole(x):
    return pl.BlockSpec(x.shape, lambda *_, n=len(x.shape): (0,) * n)


def call(name, body, table, grid, operands, in_specs, outs, out_specs, mib, scratch=(), alias=None):
    return pl.pallas_call(
        body,
        grid_spec=pltpu.PrefetchScalarGridSpec(
            num_scalar_prefetch=1,
            grid=grid,
            in_specs=in_specs,
            out_specs=out_specs,
            scratch_shapes=scratch,
        ),
        out_shape=outs,
        input_output_aliases=alias or {},
        compiler_params=pltpu.CompilerParams(
            dimension_semantics=("arbitrary",) * len(grid), vmem_limit_bytes=mib << 20
        ),
        cost_estimate=pl.CostEstimate(flops=1, bytes_accessed=1, transcendentals=0),
        name=name,
    )(table, *operands)


def shape(dims, kind=BF16):
    return jax.ShapeDtypeStruct(dims, kind)


def joined(refs):
    parts = [ref[...] for ref in refs]
    return parts[0] if len(parts) == 1 else jnp.concatenate(parts, axis=0)


def living(info, dims):
    row = lax.broadcasted_iota(jnp.int32, dims, 0).astype(F32)
    return row < info[HEADS : HEADS + 1, :1]


def project(table, shards, flips, weight, partial, info):
    last = info is not None
    n, counts = len(shards), [len(x) for x in shards]
    flat = [part for x in shards for part in x]
    tokens, width = sum(part.shape[0] for part in shards[0]), flat[0].shape[1]
    cols = weight.shape[2] // 2

    def body(s, *refs):
        out, rest = refs[-1], list(refs)
        acc = None
        for i, count in enumerate(counts):
            rows = joined([rest.pop(0) for _ in range(count)])
            term = dot(rows, refs[len(flat) + i][0])
            acc = term if acc is None else acc + term
        if partial is not None:
            acc += refs[len(flat) + n][0]
        if last:
            acc = jnp.where(living(refs[-2], acc.shape), acc, 0.0)
        out[0] = acc.astype(out.dtype)

    tile = pl.BlockSpec((1, tokens, cols), lambda g, s: (g, 0, 0))
    in_specs = [whole(x) for x in flat]
    for flip in flips:
        in_specs.append(
            pl.BlockSpec((1, width, cols), lambda g, s, flip=flip: (g, s[TEN] ^ flip, s[Z]))
        )
    operands = [*flat, *([weight] * n)]
    if partial is not None:
        in_specs.append(tile)
        operands.append(partial)
    if last:
        in_specs.append(whole(info))
        operands.append(info)
    out = shape((3, tokens, cols), BF16 if last else F32)
    return call("project", body, table, (3,), operands, in_specs, out, tile, 24)


def shard_states(table, qkv, out_grad, cumul, which, so_far):
    tokens = qkv.shape[1]
    scale = HEAD**-0.5

    def body(s, qkv_ref, og_ref, cum_ref, *refs):
        outs = refs[-4:]
        r = pl.program_id(0)
        row = cum_ref[pl.ds(s[Y] ^ r, 1), :]
        total = row[:, tokens - 1 : tokens]
        keys_t = qkv_ref[1].T.astype(F32)
        query_t = qkv_ref[0].T.astype(F32)
        keys_t = (keys_t * jnp.exp(total - row)).astype(BF16)
        query_t = (query_t * (scale * jnp.exp(row))).astype(BF16)
        states = (dot(keys_t, qkv_ref[2]), dot(query_t, og_ref[...]))
        at = lax.broadcasted_iota(jnp.int32, (16, HEAD), 0)
        tail = jnp.broadcast_to(total, (16, HEAD)).astype(BF16)
        for k, out in enumerate(outs):

            @pl.when(r == k)
            def _(k=k, out=out):
                here = s[Z] ^ which
                if so_far is not None:
                    out[...] = refs[k][...]
                for kind in range(2):
                    start = pl.multiple_of((2 * kind + here) * HEAD, HEAD)
                    out[pl.ds(start, HEAD), :] = states[kind].astype(BF16)
                if so_far is None:
                    out[4 * HEAD :, :] = tail
                else:
                    out[4 * HEAD :, :] = jnp.where(at == here, tail, refs[k][4 * HEAD :, :])

    message = shape((4 * HEAD + 16, HEAD))
    operands = [qkv, out_grad, cumul, *(so_far or ())]
    in_specs = [
        pl.BlockSpec((3, tokens, HEAD), lambda r, s: (0, 0, s[Y] ^ r)),
        pl.BlockSpec((tokens, HEAD), lambda r, s: (0, s[Y] ^ r)),
        whole(cumul),
        *[whole(m) for m in so_far or ()],
    ]
    return call(
        "shard_states",
        body,
        table,
        (4,),
        operands,
        in_specs,
        [message] * 4,
        [whole(message)] * 4,
        12,
    )


def in_order(refs, place, held):
    for r, ref in enumerate(refs):
        held[place ^ r] = ref[...]


def spread(pair):
    wide = [jnp.broadcast_to(pair[i : i + 1, :], (HEAD, HEAD)) for i in range(2)]
    return jnp.concatenate(wide, axis=0)


def ring_y(table, messages):
    half = 2 * HEAD

    def body(s, a, b, c, d, before, after, prior, later, out, held):
        in_order((a, b, c, d), s[Y], held)
        totals = [held[t, 2 * half : 2 * half + 16, :].astype(F32)[:2] for t in range(4)]
        run = jnp.zeros((half, HEAD), F32)
        reach = jnp.zeros((2, HEAD), F32)
        for t in range(4):
            before[t] = run
            prior[t] = jnp.exp(reach)
            run = spread(jnp.exp(totals[t])) * run + held[t, :half, :].astype(F32)
            reach = reach + totals[t]
        out[:half, :] = run.astype(BF16)
        total = reach
        run = jnp.zeros((half, HEAD), F32)
        reach = jnp.zeros((2, HEAD), F32)
        for t in range(3, -1, -1):
            after[t] = run
            later[t] = jnp.exp(reach)
            run = spread(jnp.exp(totals[t])) * run + held[t, half : 2 * half, :].astype(F32)
            reach = reach + totals[t]
        out[half : 2 * half, :] = run.astype(BF16)
        high = total.astype(BF16).astype(F32)
        low = total - high
        at = lax.broadcasted_iota(jnp.int32, (16, HEAD), 0)
        tail = jnp.where(at == 0, high[0:1], high[1:2])
        tail = jnp.where(at == 2, low[0:1], tail)
        tail = jnp.where(at == 3, low[1:2], tail)
        out[2 * half :, :] = tail.astype(BF16)

    outs = [
        shape((4, half, HEAD), F32),
        shape((4, half, HEAD), F32),
        shape((4, 2, HEAD), F32),
        shape((4, 2, HEAD), F32),
        shape(messages[0].shape),
    ]
    return call(
        "ring_y",
        body,
        table,
        (1,),
        messages,
        [whole(m) for m in messages],
        outs,
        [whole(o) for o in outs],
        8,
        [pltpu.VMEM((4, *messages[0].shape), BF16)],
    )


def arrivals(table, messages, before, after, prior, later):
    half = 2 * HEAD

    def body(s, a, b, c, d, before_ref, after_ref, prior_ref, later_ref, *rest):
        outs, held, mine, edges = rest[:4], *rest[4:]
        in_order((a, b, c, d), s[X], held)
        tails = [held[t, 2 * half : 2 * half + 16, :].astype(F32) for t in range(4)]
        totals = [tail[0:2] + tail[2:4] for tail in tails]
        ends = []
        for kind, steps in ((0, range(4)), (1, range(3, -1, -1))):
            run = jnp.zeros((half, HEAD), F32)
            reach = jnp.zeros((2, HEAD), F32)
            for t in steps:

                @pl.when(s[X] == t)
                def _(run=run, reach=reach, kind=kind):
                    mine[kind] = run
                    edges[kind] = jnp.exp(reach)

                rows = held[t, kind * half : (kind + 1) * half, :].astype(F32)
                run = spread(jnp.exp(totals[t])) * run + rows
                reach = reach + totals[t]
            ends.append(run.astype(BF16).astype(F32))
        nothing = jnp.zeros((HEAD, HEAD), F32)
        across_up = jnp.concatenate([nothing, ends[0][:HEAD]], axis=0)
        across_down = jnp.concatenate([ends[1][HEAD:], nothing], axis=0)
        start = mine[0] + spread(edges[0]) * across_up
        finish = mine[1] + spread(edges[1]) * across_down
        for r, out in enumerate(outs):
            t = s[Y] ^ r
            out[:half, :] = (before_ref[t] + spread(prior_ref[t]) * start).astype(BF16)
            out[half:, :] = (after_ref[t] + spread(later_ref[t]) * finish).astype(BF16)

    operands = (*messages, before, after, prior, later)
    message = shape((2 * half, HEAD))
    return call(
        "arrivals",
        body,
        table,
        (1,),
        operands,
        [whole(m) for m in operands],
        [message] * 4,
        [whole(message)] * 4,
        8,
        [
            pltpu.VMEM((4, *messages[0].shape), BF16),
            pltpu.VMEM((2, half, HEAD), F32),
            pltpu.VMEM((2, 2, HEAD), F32),
        ],
    )


def column_of(row):
    return jnp.broadcast_to(row, (HEAD, row.shape[1])).T


def local_grads(table, qkv, out_grad, cumul, first, count, so_far):
    tokens = qkv.shape[1]
    scale = HEAD**-0.5
    size = tokens // 2

    def body(s, qkv_ref, og_ref, cum_ref, *refs):
        out, ready = refs[-2:]
        row = cum_ref[pl.ds(pl.program_id(0) + first, 1), :]
        column = column_of(row)
        wide = jnp.concatenate([column] * (size // HEAD), axis=1)
        s_at = lax.broadcasted_iota(jnp.int32, (size, size), 0)
        t_at = lax.broadcasted_iota(jnp.int32, (size, size), 1)
        parts = [slice(0, size), slice(size, tokens)]

        def pair(t, s):
            if t == s:
                gap = row[:, parts[t]] - wide[parts[s], :]
                decay = jnp.exp(jnp.where(s_at <= t_at, gap, -jnp.inf))
            else:
                middle = row[:, size - 1 : size]
                to_middle = jnp.exp(middle - column[parts[s], :])
                decay = jnp.concatenate([to_middle] * (size // HEAD), axis=1)
                decay *= jnp.exp(row[:, parts[t]] - middle)
            q, k, v = qkv_ref[0, parts[t], :], qkv_ref[1, parts[s], :], qkv_ref[2, parts[s], :]
            g = og_ref[parts[t], :]
            scores = lax.dot_general(k, q, AB_T, preferred_element_type=F32)
            grads = lax.dot_general(v, g, AB_T, preferred_element_type=F32)
            prob = (scores * decay).astype(BF16)
            score = (grads * decay).astype(BF16)
            dq = lax.dot_general(score, k, A_TB, preferred_element_type=F32)
            return dq, dot(score, q), dot(prob, g)

        a, b, c = pair(0, 0), pair(1, 0), pair(1, 1)
        live = living(cum_ref, (tokens, HEAD))
        grads = (
            jnp.concatenate([a[0], b[0] + c[0]], axis=0) * scale,
            jnp.concatenate([a[1] + b[1], c[1]], axis=0) * scale,
            jnp.concatenate([a[2] + b[2], c[2]], axis=0) * scale,
        )
        until = jnp.exp(row[:, tokens - 1 : tokens] - column)
        rows = (
            og_ref[...].astype(F32) * (scale * jnp.exp(column)),
            qkv_ref[2].astype(F32) * until,
            qkv_ref[1].astype(F32) * until,
        )
        for j in range(3):
            out[j] = jnp.where(live, grads[j], 0.0).astype(BF16)
            ready[j] = jnp.where(live, rows[j], 0.0).astype(BF16)

    tile = pl.BlockSpec((3, tokens, HEAD), lambda h, s: (0, 0, h + first))
    in_specs = [tile, pl.BlockSpec((tokens, HEAD), lambda h, s: (0, h + first)), whole(cumul)]
    operands = [qkv, out_grad, cumul]
    if so_far is not None:
        in_specs += [pl.BlockSpec(memory_space=pl.ANY)] * 2
        operands += so_far
    return call(
        "local_grads",
        body,
        table,
        (count,),
        operands,
        in_specs,
        [shape(qkv.shape), shape(qkv.shape)],
        [tile, tile],
        12,
        alias=None if so_far is None else {4: 0, 5: 1},
    )


def whole_grads(table, own, pair, states):
    tokens, heads = own[0].shape[1], HEADS

    def body(s, local_a, ready_a, local_b, ready_b, a, b, c, d, *rest):
        outs, held = rest[:4], rest[4]
        i = pl.program_id(0)

        @pl.when(i == 0)
        def _():
            in_order((a, b, c, d), s[Y], held)

        for which, (local_ref, ready_ref) in enumerate(((local_a, ready_a), (local_b, ready_b))):
            for k in range(heads):

                @pl.when(i == which * heads + k)
                def _(k=k, which=which, local_ref=local_ref, ready_ref=ready_ref):
                    base = pl.multiple_of((s[Z] ^ which) * HEAD, HEAD)
                    coming = held[k, pl.ds(base, HEAD), :]
                    later = held[k, pl.ds(2 * HEAD + base, HEAD), :]
                    cross = (
                        lax.dot_general(ready_ref[0], coming, AB_T, preferred_element_type=F32),
                        lax.dot_general(ready_ref[1], later, AB_T, preferred_element_type=F32),
                        dot(ready_ref[2], later),
                    )
                    out = outs[2 * which + k // 2]
                    for j in range(3):
                        start = (2 * j + k % 2) * HEAD
                        total = local_ref[j].astype(F32) + cross[j]
                        out[:, start : start + HEAD] = total.astype(BF16)

    first = pl.BlockSpec((3, tokens, HEAD), lambda i, s: (0, 0, jnp.minimum(i, heads - 1)))
    second = pl.BlockSpec((3, tokens, HEAD), lambda i, s: (0, 0, jnp.maximum(i - heads, 0)))
    side = shape((tokens, 3 * heads * HEAD // 2))
    return call(
        "whole_grads",
        body,
        table,
        (2 * heads,),
        (*own, *pair, *states),
        [first, first, second, second, *[whole(m) for m in states]],
        [side] * 4,
        [whole(side)] * 4,
        16,
        [pltpu.VMEM((4, *states[0].shape), BF16)],
    )


def split(table, first, second):
    tokens, width = first.shape

    def body(s, a, b, out_a, out_b):
        out_a[...] = a[...]
        out_b[...] = b[...]

    halves = [pl.BlockSpec((tokens // 2, width), lambda i, s, k=k: (k, 0)) for k in range(2)]
    out = shape((tokens // 2, width))
    return call("split", body, table, (1,), (first, second), halves, [out] * 2, [whole(out)] * 2, 8)


def turn(table, shards):
    counts = [len(x) for x in shards]
    flat = [part for x in shards for part in x]
    tokens, width = sum(part.shape[0] for part in shards[0]), flat[0].shape[1]
    rows = 4 * width // 32

    def body(s, *refs):
        out, at = refs[-1], 0
        for k, count in enumerate(counts):
            mine, at = refs[at : at + count], at + count

            @pl.when((pl.program_id(0) ^ s[TEN]) == k)
            def _(mine=mine):
                out[...] = joined(mine).T.reshape(out.shape)

    out = shape((16, 2, rows, tokens))
    spec = pl.BlockSpec((8, 1, rows, tokens), lambda i, s: (i % 2, (i // 2) ^ s[Z], 0, 0))
    turned = call("turn", body, table, (4,), flat, [whole(x) for x in flat], out, spec, 12)
    return turned.reshape(4, 4, 2 * rows, tokens)


def weight_part(table, turned, lefts, rights, places, split):
    tokens, cols = lefts[0].shape
    rows = turned[0].shape[2]

    def body(s, own_x, own_y, pair_x, pair_y, left_a, left_b, right_a, right_b, *outs):
        r = pl.program_id(0)
        for side, (a, b, ga, gb) in enumerate(
            ((own_x, pair_x, left_a, left_b), (own_y, pair_y, right_a, right_b))
        ):
            acc = dot(a[...].reshape(4 * rows, tokens), ga[...])
            acc += dot(b[...].reshape(4 * rows, tokens), gb[...])
            acc = acc.astype(BF16)
            if split:
                outs[2 * side][...] = acc[: 2 * rows]
                outs[2 * side + 1][...] = acc[2 * rows :]
                continue
            for k in range(len(places)):

                @pl.when(r == k)
                def _(k=k, acc=acc, side=side):
                    outs[side * len(places) + k][...] = acc

    step = places[1] - places[0] if len(places) > 1 else 0
    by_x = pl.BlockSpec((1, 4, rows, tokens), lambda r, s: (s[X] ^ (places[0] + step * r), 0, 0, 0))
    by_y = pl.BlockSpec((4, 1, rows, tokens), lambda r, s: (0, s[Y] ^ (places[0] + step * r), 0, 0))
    outs = [shape((2 * rows if split else 4 * rows, cols))] * (4 if split else 2 * len(places))
    operands = (turned[0], turned[0], turned[1], turned[1], *lefts, *rights)
    return call(
        "weight_part",
        body,
        table,
        (len(places),),
        operands,
        [by_x, by_y, by_x, by_y, *[whole(x) for x in (*lefts, *rights)]],
        outs,
        [whole(o) for o in outs],
        30,
    )


def add_halves(table, third, first_place, halves):
    up, down = halves
    near_up, near_down = third, first_place
    n, cols = up.shape

    def body(s, a, b, u, d, out_a, out_b):
        out_a[...] = (a[...].astype(F32) + u[...].astype(F32)).astype(BF16)
        out_b[...] = (b[...].astype(F32) + d[...].astype(F32)).astype(BF16)

    steps = 4
    first = pl.BlockSpec((n // steps, cols), lambda i, s: (i, 0))
    second = pl.BlockSpec((n // steps, cols), lambda i, s: (i + steps, 0))
    return call(
        "add_halves",
        body,
        table,
        (steps,),
        (near_up, near_down, up, down),
        [first, second, first, first],
        [shape(near_up.shape), shape(near_down.shape)],
        [first, second],
        12,
        alias={1: 0, 2: 1},
    )


def cut_blocks(table, left, right):
    rows, cols = left[0].shape[0] // 4, left[0].shape[1]

    def body(s, *refs):
        for k, axis in enumerate((Y, X)):
            a, b, c = refs[3 * k : 3 * k + 3]
            for r, out in zip((1, 3, 2, 0), refs[6 + 4 * k : 10 + 4 * k]):
                at = pl.ds(pl.multiple_of((s[axis] ^ r) * rows, rows), rows)
                total = a[at, :].astype(F32) + b[at, :].astype(F32) + c[at, :].astype(F32)
                out[...] = total.astype(BF16)

    outs = [shape((rows, cols))] * 8
    operands = (*left, *right)
    cut = call(
        "cut_blocks",
        body,
        table,
        (1,),
        operands,
        [whole(x) for x in operands],
        outs,
        [whole(o) for o in outs],
        24,
    )
    return cut[:4], cut[4:]


def final_sums(table, parts):
    rows, cols = parts[0].shape

    def body(s, a, b, c, d, here, there):
        total = sum(ref[...].astype(F32) for ref in (a, b, c, d)).astype(BF16)
        here[...] = total[: rows // 2]
        there[...] = total[rows // 2 :]

    outs = [shape((rows // 2, cols))] * 2
    return call(
        "final_sums",
        body,
        table,
        (1,),
        parts,
        [whole(x) for x in parts],
        outs,
        [whole(o) for o in outs],
        8,
    )


def finish(table, here, there):
    rows, cols = here[0].shape
    side = cols // 3

    def body(s, *refs):
        out = refs[-1]
        for i, half in enumerate((s[Z], 1 - s[Z])):
            for k in range(2):
                for j in range(3):
                    at = pl.ds(pl.multiple_of(half * 2 * side + k * side, side), side)
                    out[j, :, at] = refs[2 * i + k][:, j * side : (j + 1) * side].astype(F32)

    out = shape((3, rows, 4 * side), F32)
    operands = (*here, *there)
    return call("finish", body, table, (1,), operands, [whole(x) for x in operands], out, whole(out), 8)


def swaps(pieces, left, right):
    a, c = send(pieces[0], left, 1), send(pieces[2], right, 1)
    b, d = send(pieces[1], left, 3), send(pieces[3], right, 3)
    return [a, b], [c, d]


def device_part(activations, qkv_weight, log_decay, lengths, out_grad):
    tied = lax.optimization_barrier
    tokens = activations.shape[0]
    heads = log_decay.shape[1]
    per = heads // 2
    index = [lax.axis_index(a) for a in ("c0", "c1", "c2", "zl", "co")]
    here_z = index[0]
    fixed = [*index, index[3] * 2 + index[4]]
    table = jnp.stack(fixed).astype(jnp.int32)
    weight = pltpu.with_memory_space_constraint(jnp.transpose(qkv_weight, (1, 0, 2)), pltpu.HBM)

    near = send(activations, "zl", 1)
    side = across(activations)
    core = send(activations, "co", 1)

    live = (jnp.arange(tokens, dtype=jnp.int32) < lengths[0]).astype(F32)
    cumul = jnp.cumsum(log_decay.T * live[None, :], axis=1)
    size = jnp.broadcast_to(lengths.astype(F32)[:, None], (per, tokens))
    info, note = (
        jnp.concatenate([lax.dynamic_slice_in_dim(cumul, z * per, per), size])
        for z in (here_z, 1 - here_z)
    )
    note = send(note, "c0", 1)
    width = per * HEAD
    og_own = lax.dynamic_slice_in_dim(out_grad, here_z * width, width, axis=1)
    og_other = lax.dynamic_slice_in_dim(out_grad, (1 - here_z) * width, width, axis=1)

    acc_own = project(table, [[activations], [core]], (0, 1), weight, None, None)
    near, side, acc_own, note, og_other, info = tied((near, side, acc_own, note, og_other, info))
    far = split(table, side, near)
    far = [send(far[0], "zl", 1), across(far[1])]
    near_core = send(near, "co", 1)
    side_core = send(side, "co", 1)
    qkv_own = project(table, [[near], [near_core]], (2, 3), weight, acc_own, info)
    turned = [turn(table, tied(([[activations], [core], [near], [near_core]], qkv_own))[0])]
    far, side_core, qkv_own, turned = tied((far, side_core, qkv_own, turned))
    far_core = [send(x, "co", 1) for x in far]
    og_pair = send(tied((og_other, far))[0], "c0", 1)
    to_y = shard_states(table, qkv_own, og_own, info, 0, None)
    far_core, to_y = tied((far_core, to_y))
    qkv_pair = project(
        table, [[side], [side_core], far, far_core], (2, 3, 0, 1), weight, None, note
    )
    og_pair, qkv_pair = tied((og_pair, qkv_pair))

    to_y = shard_states(table, qkv_pair, og_pair, note, 1, to_y)
    at_y = [send(to_y[r], "c2", r) for r in (1, 3, 2)]
    qkv_own, _ = tied((qkv_own, to_y[0]))
    local_own = local_grads(table, qkv_own, og_own, info, 0, per, None)
    at_y, local_own = tied((at_y, local_own))
    before, after, prior, later, ring = ring_y(table, [to_y[0], at_y[0], at_y[2], at_y[1]])
    at_x = [send(ring, "c1", r) for r in (1, 3, 2)]
    qkv_pair, _ = tied((qkv_pair, ring))
    local = local_grads(table, qkv_pair, og_pair, note, 0, per // 2, None)
    second, _ = tied(([far, far_core, [side], [side_core]], ring))
    turned.append(turn(table, second))
    at_x, local, turned = tied((at_x, local, turned))
    back = arrivals(table, [ring, at_x[0], at_x[2], at_x[1]], before, after, prior, later)
    states = [send(back[r], "c2", r) for r in (1, 3, 2)]
    local, _ = tied((local, back[0]))
    local = local_grads(table, qkv_pair, og_pair, note, per // 2, per // 2, local)
    states, turned, local = tied((states, turned, local))
    states = [back[0], states[0], states[2], states[1]]

    left_own, right_own, left_pair, right_pair = whole_grads(table, local_own, local, states)
    lefts, rights = (left_own, left_pair), (right_own, right_pair)
    far_piece = weight_part(table, turned, lefts, rights, (2,), True)
    l_half, r_half = swaps(far_piece, "c1", "c2")
    turned, _ = tied((turned, far_piece[0]))
    l_one, l_three, r_one, r_three = weight_part(table, turned, lefts, rights, (1, 3), False)
    l_half, l_one = tied((l_half, l_one))
    l_three, l_one = add_halves(table, l_three, l_one, l_half)
    l_got = [send(l_one, "c1", 1), send(l_three, "c1", 3)]
    r_half, _ = tied((r_half, l_one))
    r_three, r_one = add_halves(table, r_three, r_one, r_half)
    r_got = [send(r_one, "c2", 1), send(r_three, "c2", 3)]
    turned, _ = tied((turned, r_one))
    own = weight_part(table, turned, lefts, rights, (0,), False)
    l_got, own = tied((l_got, own))
    l_cut, r_cut = cut_blocks(table, (own[0], *l_got), (own[1], *r_got))
    l_got = [send(x, "c2", by) for x, by in zip(l_cut, (1, 3, 2))]
    r_got = [send(x, "c1", by) for x, by in zip(r_cut, (1, 3, 2))]
    l_here, l_there = final_sums(table, (l_cut[3], *l_got))
    r_got, _ = tied((r_got, l_here))
    r_here, r_there = final_sums(table, (r_cut[3], *r_got))
    there = [send(x, "c0", 1) for x in (l_there, r_there)]
    return jnp.transpose(finish(table, (l_here, r_here), there), (1, 0, 2))


def solution(mesh):
    finer = Mesh(mesh.devices.reshape(2, 4, 4, 2, 2), ("c0", "c1", "c2", "zl", "co"))
    context, tensor = ("c0", "c1", "c2"), ("zl", "co")
    placed = (
        P(context, tensor),
        P(None, None, tensor),
        P(context, tensor),
        P(context),
        P(context, tensor),
    )
    return jax.shard_map(
        device_part,
        mesh=finer,
        in_specs=placed,
        out_specs=P(context, None, tensor),
        check_vma=False,
    )
```

```python
import jax
import jax.numpy as jnp
from jax import lax
from jax.experimental import pallas as pl
from jax.experimental.pallas import tpu as pltpu
from jax.sharding import Mesh
from jax.sharding import PartitionSpec as P

F32 = jnp.float32
BF16 = jnp.bfloat16
HEAD = 128
HEADS = 4
Z, X, Y, ZL, CO, TEN = range(6)
AB_T = (((1,), (1,)), ((), ()))
A_TB = (((0,), (0,)), ((), ()))


def dot(a, b):
    return jnp.dot(a, b, preferred_element_type=F32)


def send(x, axis, by):
    return lax.ppermute(x, axis, [(i, i ^ by) for i in range(lax.axis_size(axis))])


def across(x):
    return lax.ppermute(x, ("c0", "zl"), [(0, 3), (1, 2), (2, 1), (3, 0)])


def whole(x):
    return pl.BlockSpec(x.shape, lambda *_, n=len(x.shape): (0,) * n)


def call(name, body, table, grid, operands, in_specs, outs, out_specs, mib, scratch=(), alias=None):
    return pl.pallas_call(
        body,
        grid_spec=pltpu.PrefetchScalarGridSpec(
            num_scalar_prefetch=1,
            grid=grid,
            in_specs=in_specs,
            out_specs=out_specs,
            scratch_shapes=scratch,
        ),
        out_shape=outs,
        input_output_aliases=alias or {},
        compiler_params=pltpu.CompilerParams(
            dimension_semantics=("arbitrary",) * len(grid), vmem_limit_bytes=mib << 20
        ),
        cost_estimate=pl.CostEstimate(flops=1, bytes_accessed=1, transcendentals=0),
        name=name,
    )(table, *operands)


def shape(dims, kind=BF16):
    return jax.ShapeDtypeStruct(dims, kind)


def joined(refs):
    parts = [ref[...] for ref in refs]
    return parts[0] if len(parts) == 1 else jnp.concatenate(parts, axis=0)


def living(info, dims):
    row = lax.broadcasted_iota(jnp.int32, dims, 0).astype(F32)
    return row < info[HEADS : HEADS + 1, :1]


def project(table, shards, flips, weight, partial, info):
    last = info is not None
    n, counts = len(shards), [len(x) for x in shards]
    flat = [part for x in shards for part in x]
    tokens, width = sum(part.shape[0] for part in shards[0]), flat[0].shape[1]
    cols = weight.shape[2] // 2

    def body(s, *refs):
        out, rest = refs[-1], list(refs)
        acc = None
        for i, count in enumerate(counts):
            rows = joined([rest.pop(0) for _ in range(count)])
            term = dot(rows, refs[len(flat) + i][0])
            acc = term if acc is None else acc + term
        if partial is not None:
            acc += refs[len(flat) + n][0]
        if last:
            acc = jnp.where(living(refs[-2], acc.shape), acc, 0.0)
        out[0] = acc.astype(out.dtype)

    tile = pl.BlockSpec((1, tokens, cols), lambda g, s: (g, 0, 0))
    in_specs = [whole(x) for x in flat]
    for flip in flips:
        in_specs.append(
            pl.BlockSpec((1, width, cols), lambda g, s, flip=flip: (g, s[TEN] ^ flip, s[Z]))
        )
    operands = [*flat, *([weight] * n)]
    if partial is not None:
        in_specs.append(tile)
        operands.append(partial)
    if last:
        in_specs.append(whole(info))
        operands.append(info)
    out = shape((3, tokens, cols), BF16 if last else F32)
    return call("project", body, table, (3,), operands, in_specs, out, tile, 24)


def shard_states(table, qkv, out_grad, cumul, which, so_far):
    tokens = qkv.shape[1]
    scale = HEAD**-0.5

    def body(s, qkv_ref, og_ref, cum_ref, *refs):
        outs = refs[-4:]
        r = pl.program_id(0)
        row = cum_ref[pl.ds(s[Y] ^ r, 1), :]
        total = row[:, tokens - 1 : tokens]
        keys_t = qkv_ref[1].T.astype(F32)
        query_t = qkv_ref[0].T.astype(F32)
        keys_t = (keys_t * jnp.exp(total - row)).astype(BF16)
        query_t = (query_t * (scale * jnp.exp(row))).astype(BF16)
        states = (dot(keys_t, qkv_ref[2]), dot(query_t, og_ref[...]))
        at = lax.broadcasted_iota(jnp.int32, (16, HEAD), 0)
        tail = jnp.broadcast_to(total, (16, HEAD)).astype(BF16)
        for k, out in enumerate(outs):

            @pl.when(r == k)
            def _(k=k, out=out):
                here = s[Z] ^ which
                if so_far is not None:
                    out[...] = refs[k][...]
                for kind in range(2):
                    start = pl.multiple_of((2 * kind + here) * HEAD, HEAD)
                    out[pl.ds(start, HEAD), :] = states[kind].astype(BF16)
                if so_far is None:
                    out[4 * HEAD :, :] = tail
                else:
                    out[4 * HEAD :, :] = jnp.where(at == here, tail, refs[k][4 * HEAD :, :])

    message = shape((4 * HEAD + 16, HEAD))
    operands = [qkv, out_grad, cumul, *(so_far or ())]
    in_specs = [
        pl.BlockSpec((3, tokens, HEAD), lambda r, s: (0, 0, s[Y] ^ r)),
        pl.BlockSpec((tokens, HEAD), lambda r, s: (0, s[Y] ^ r)),
        whole(cumul),
        *[whole(m) for m in so_far or ()],
    ]
    return call(
        "shard_states",
        body,
        table,
        (4,),
        operands,
        in_specs,
        [message] * 4,
        [whole(message)] * 4,
        12,
    )


def in_order(refs, place, held):
    for r, ref in enumerate(refs):
        held[place ^ r] = ref[...]


def spread(pair):
    wide = [jnp.broadcast_to(pair[i : i + 1, :], (HEAD, HEAD)) for i in range(2)]
    return jnp.concatenate(wide, axis=0)


def ring_y(table, messages):
    half = 2 * HEAD

    def body(s, a, b, c, d, before, after, prior, later, out, held):
        in_order((a, b, c, d), s[Y], held)
        totals = [held[t, 2 * half : 2 * half + 16, :].astype(F32)[:2] for t in range(4)]
        run = jnp.zeros((half, HEAD), F32)
        reach = jnp.zeros((2, HEAD), F32)
        for t in range(4):
            before[t] = run
            prior[t] = jnp.exp(reach)
            run = spread(jnp.exp(totals[t])) * run + held[t, :half, :].astype(F32)
            reach = reach + totals[t]
        out[:half, :] = run.astype(BF16)
        total = reach
        run = jnp.zeros((half, HEAD), F32)
        reach = jnp.zeros((2, HEAD), F32)
        for t in range(3, -1, -1):
            after[t] = run
            later[t] = jnp.exp(reach)
            run = spread(jnp.exp(totals[t])) * run + held[t, half : 2 * half, :].astype(F32)
            reach = reach + totals[t]
        out[half : 2 * half, :] = run.astype(BF16)
        high = total.astype(BF16).astype(F32)
        low = total - high
        at = lax.broadcasted_iota(jnp.int32, (16, HEAD), 0)
        tail = jnp.where(at == 0, high[0:1], high[1:2])
        tail = jnp.where(at == 2, low[0:1], tail)
        tail = jnp.where(at == 3, low[1:2], tail)
        out[2 * half :, :] = tail.astype(BF16)

    outs = [
        shape((4, half, HEAD), F32),
        shape((4, half, HEAD), F32),
        shape((4, 2, HEAD), F32),
        shape((4, 2, HEAD), F32),
        shape(messages[0].shape),
    ]
    return call(
        "ring_y",
        body,
        table,
        (1,),
        messages,
        [whole(m) for m in messages],
        outs,
        [whole(o) for o in outs],
        8,
        [pltpu.VMEM((4, *messages[0].shape), BF16)],
    )


def arrivals(table, messages, before, after, prior, later):
    half = 2 * HEAD

    def body(s, a, b, c, d, before_ref, after_ref, prior_ref, later_ref, *rest):
        outs, held, mine, edges = rest[:4], *rest[4:]
        in_order((a, b, c, d), s[X], held)
        tails = [held[t, 2 * half : 2 * half + 16, :].astype(F32) for t in range(4)]
        totals = [tail[0:2] + tail[2:4] for tail in tails]
        ends = []
        for kind, steps in ((0, range(4)), (1, range(3, -1, -1))):
            run = jnp.zeros((half, HEAD), F32)
            reach = jnp.zeros((2, HEAD), F32)
            for t in steps:

                @pl.when(s[X] == t)
                def _(run=run, reach=reach, kind=kind):
                    mine[kind] = run
                    edges[kind] = jnp.exp(reach)

                rows = held[t, kind * half : (kind + 1) * half, :].astype(F32)
                run = spread(jnp.exp(totals[t])) * run + rows
                reach = reach + totals[t]
            ends.append(run.astype(BF16).astype(F32))
        nothing = jnp.zeros((HEAD, HEAD), F32)
        across_up = jnp.concatenate([nothing, ends[0][:HEAD]], axis=0)
        across_down = jnp.concatenate([ends[1][HEAD:], nothing], axis=0)
        start = mine[0] + spread(edges[0]) * across_up
        finish = mine[1] + spread(edges[1]) * across_down
        for r, out in enumerate(outs):
            t = s[Y] ^ r
            out[:half, :] = (before_ref[t] + spread(prior_ref[t]) * start).astype(BF16)
            out[half:, :] = (after_ref[t] + spread(later_ref[t]) * finish).astype(BF16)

    operands = (*messages, before, after, prior, later)
    message = shape((2 * half, HEAD))
    return call(
        "arrivals",
        body,
        table,
        (1,),
        operands,
        [whole(m) for m in operands],
        [message] * 4,
        [whole(message)] * 4,
        8,
        [
            pltpu.VMEM((4, *messages[0].shape), BF16),
            pltpu.VMEM((2, half, HEAD), F32),
            pltpu.VMEM((2, 2, HEAD), F32),
        ],
    )


def column_of(row):
    return jnp.broadcast_to(row, (HEAD, row.shape[1])).T


def local_grads(table, qkv, out_grad, cumul, first, count, so_far):
    tokens = qkv.shape[1]
    scale = HEAD**-0.5
    size = tokens // 2

    def body(s, qkv_ref, og_ref, cum_ref, *refs):
        out, ready = refs[-2:]
        row = cum_ref[pl.ds(pl.program_id(0) + first, 1), :]
        column = column_of(row)
        wide = jnp.concatenate([column] * (size // HEAD), axis=1)
        s_at = lax.broadcasted_iota(jnp.int32, (size, size), 0)
        t_at = lax.broadcasted_iota(jnp.int32, (size, size), 1)
        parts = [slice(0, size), slice(size, tokens)]

        def pair(t, s):
            if t == s:
                gap = row[:, parts[t]] - wide[parts[s], :]
                decay = jnp.exp(jnp.where(s_at <= t_at, gap, -jnp.inf))
            else:
                middle = row[:, size - 1 : size]
                to_middle = jnp.exp(middle - column[parts[s], :])
                decay = jnp.concatenate([to_middle] * (size // HEAD), axis=1)
                decay *= jnp.exp(row[:, parts[t]] - middle)
            q, k, v = qkv_ref[0, parts[t], :], qkv_ref[1, parts[s], :], qkv_ref[2, parts[s], :]
            g = og_ref[parts[t], :]
            scores = lax.dot_general(k, q, AB_T, preferred_element_type=F32)
            grads = lax.dot_general(v, g, AB_T, preferred_element_type=F32)
            prob = (scores * decay).astype(BF16)
            score = (grads * decay).astype(BF16)
            dq = lax.dot_general(score, k, A_TB, preferred_element_type=F32)
            return dq, dot(score, q), dot(prob, g)

        a, b, c = pair(0, 0), pair(1, 0), pair(1, 1)
        live = living(cum_ref, (tokens, HEAD))
        grads = (
            jnp.concatenate([a[0], b[0] + c[0]], axis=0) * scale,
            jnp.concatenate([a[1] + b[1], c[1]], axis=0) * scale,
            jnp.concatenate([a[2] + b[2], c[2]], axis=0) * scale,
        )
        until = jnp.exp(row[:, tokens - 1 : tokens] - column)
        rows = (
            og_ref[...].astype(F32) * (scale * jnp.exp(column)),
            qkv_ref[2].astype(F32) * until,
            qkv_ref[1].astype(F32) * until,
        )
        for j in range(3):
            out[j] = jnp.where(live, grads[j], 0.0).astype(BF16)
            ready[j] = jnp.where(live, rows[j], 0.0).astype(BF16)

    tile = pl.BlockSpec((3, tokens, HEAD), lambda h, s: (0, 0, h + first))
    in_specs = [tile, pl.BlockSpec((tokens, HEAD), lambda h, s: (0, h + first)), whole(cumul)]
    operands = [qkv, out_grad, cumul]
    if so_far is not None:
        in_specs += [pl.BlockSpec(memory_space=pl.ANY)] * 2
        operands += so_far
    return call(
        "local_grads",
        body,
        table,
        (count,),
        operands,
        in_specs,
        [shape(qkv.shape), shape(qkv.shape)],
        [tile, tile],
        12,
        alias=None if so_far is None else {4: 0, 5: 1},
    )


def whole_grads(table, own, pair, states):
    tokens, heads = own[0].shape[1], HEADS

    def body(s, local_a, ready_a, local_b, ready_b, a, b, c, d, *rest):
        outs, held = rest[:4], rest[4]
        i = pl.program_id(0)

        @pl.when(i == 0)
        def _():
            in_order((a, b, c, d), s[Y], held)

        for which, (local_ref, ready_ref) in enumerate(((local_a, ready_a), (local_b, ready_b))):
            for k in range(heads):

                @pl.when(i == which * heads + k)
                def _(k=k, which=which, local_ref=local_ref, ready_ref=ready_ref):
                    base = pl.multiple_of((s[Z] ^ which) * HEAD, HEAD)
                    coming = held[k, pl.ds(base, HEAD), :]
                    later = held[k, pl.ds(2 * HEAD + base, HEAD), :]
                    cross = (
                        lax.dot_general(ready_ref[0], coming, AB_T, preferred_element_type=F32),
                        lax.dot_general(ready_ref[1], later, AB_T, preferred_element_type=F32),
                        dot(ready_ref[2], later),
                    )
                    out = outs[2 * which + k // 2]
                    for j in range(3):
                        start = (2 * j + k % 2) * HEAD
                        total = local_ref[j].astype(F32) + cross[j]
                        out[:, start : start + HEAD] = total.astype(BF16)

    first = pl.BlockSpec((3, tokens, HEAD), lambda i, s: (0, 0, jnp.minimum(i, heads - 1)))
    second = pl.BlockSpec((3, tokens, HEAD), lambda i, s: (0, 0, jnp.maximum(i - heads, 0)))
    side = shape((tokens, 3 * heads * HEAD // 2))
    return call(
        "whole_grads",
        body,
        table,
        (2 * heads,),
        (*own, *pair, *states),
        [first, first, second, second, *[whole(m) for m in states]],
        [side] * 4,
        [whole(side)] * 4,
        16,
        [pltpu.VMEM((4, *states[0].shape), BF16)],
    )


def split(table, first, second):
    tokens, width = first.shape

    def body(s, a, b, out_a, out_b):
        out_a[...] = a[...]
        out_b[...] = b[...]

    halves = [pl.BlockSpec((tokens // 2, width), lambda i, s, k=k: (k, 0)) for k in range(2)]
    out = shape((tokens // 2, width))
    return call("split", body, table, (1,), (first, second), halves, [out] * 2, [whole(out)] * 2, 8)


def turn(table, shards):
    counts = [len(x) for x in shards]
    flat = [part for x in shards for part in x]
    tokens, width = sum(part.shape[0] for part in shards[0]), flat[0].shape[1]
    rows = 4 * width // 32

    def body(s, *refs):
        out, at = refs[-1], 0
        for k, count in enumerate(counts):
            mine, at = refs[at : at + count], at + count

            @pl.when((pl.program_id(0) ^ s[TEN]) == k)
            def _(mine=mine):
                out[...] = joined(mine).T.reshape(out.shape)

    out = shape((16, 2, rows, tokens))
    spec = pl.BlockSpec((8, 1, rows, tokens), lambda i, s: (i % 2, (i // 2) ^ s[Z], 0, 0))
    turned = call("turn", body, table, (4,), flat, [whole(x) for x in flat], out, spec, 12)
    return turned.reshape(4, 4, 2 * rows, tokens)


def weight_part(table, turned, lefts, rights, places, split):
    tokens, cols = lefts[0].shape
    rows = turned[0].shape[2]

    n = 2 if split else 1

    def body(s, own_x, own_y, pair_x, pair_y, left_a, left_b, right_a, right_b, *outs):
        r = pl.program_id(0)
        count = len(outs) // 2
        for side, (a, b, ga, gb) in enumerate(
            ((own_x, pair_x, left_a, left_b), (own_y, pair_y, right_a, right_b))
        ):
            acc = dot(a[...].reshape(4 * rows // n, tokens), ga[...])
            acc += dot(b[...].reshape(4 * rows // n, tokens), gb[...])
            acc = acc.astype(BF16)
            for k in range(count):

                @pl.when(r == k)
                def _(k=k, acc=acc, side=side):
                    outs[side * count + k][...] = acc

    step = places[1] - places[0] if len(places) > 1 else 0
    if split:
        by_x = pl.BlockSpec((1, 2, rows, tokens), lambda r, s: (s[X] ^ places[0], r, 0, 0))
        by_y = pl.BlockSpec((2, 1, rows, tokens), lambda r, s: (r, s[Y] ^ places[0], 0, 0))
    else:
        by_x = pl.BlockSpec(
            (1, 4, rows, tokens), lambda r, s: (s[X] ^ (places[0] + step * r), 0, 0, 0)
        )
        by_y = pl.BlockSpec(
            (4, 1, rows, tokens), lambda r, s: (0, s[Y] ^ (places[0] + step * r), 0, 0)
        )
    outs = [shape((4 * rows // n, cols))] * (4 if split else 2 * len(places))
    operands = (turned[0], turned[0], turned[1], turned[1], *lefts, *rights)
    return call(
        "weight_part",
        body,
        table,
        (n * len(places),),
        operands,
        [by_x, by_y, by_x, by_y, *[whole(x) for x in (*lefts, *rights)]],
        outs,
        [whole(o) for o in outs],
        30,
    )


def add_halves(table, third, first_place, halves):
    up, down = halves
    near_up, near_down = third, first_place
    n, cols = up.shape

    def body(s, a, b, u, d, out_a, out_b):
        out_a[...] = (a[...].astype(F32) + u[...].astype(F32)).astype(BF16)
        out_b[...] = (b[...].astype(F32) + d[...].astype(F32)).astype(BF16)

    steps = 4
    first = pl.BlockSpec((n // steps, cols), lambda i, s: (i, 0))
    second = pl.BlockSpec((n // steps, cols), lambda i, s: (i + steps, 0))
    return call(
        "add_halves",
        body,
        table,
        (steps,),
        (near_up, near_down, up, down),
        [first, second, first, first],
        [shape(near_up.shape), shape(near_down.shape)],
        [first, second],
        12,
        alias={1: 0, 2: 1},
    )


def cut_blocks(table, left, right):
    rows, cols = left[0].shape[0] // 4, left[0].shape[1]

    def body(s, *refs):
        i = pl.program_id(0)
        for side in range(2):
            a, b, c = (ref[...].astype(F32) for ref in refs[3 * side : 3 * side + 3])
            total = (a + b + c).astype(BF16)
            for k, at in enumerate((0, 2, 1, 3)):

                @pl.when(i == at)
                def _(k=k, side=side, total=total):
                    refs[6 + 4 * side + k][...] = total

    outs = [shape((rows, cols))] * 8
    specs = [
        pl.BlockSpec((rows, cols), lambda i, s, axis=axis: (s[axis] ^ ((i + 1) % 4), 0))
        for axis in (Y, X)
    ]
    cut = call(
        "cut_blocks",
        body,
        table,
        (4,),
        (*left, *right),
        [specs[0]] * 3 + [specs[1]] * 3,
        outs,
        [whole(o) for o in outs],
        24,
    )
    return cut[:4], cut[4:]


def final_sums(table, parts):
    rows, cols = parts[0].shape

    def body(s, a, b, c, d, here, there):
        total = sum(ref[...].astype(F32) for ref in (a, b, c, d)).astype(BF16)
        here[...] = total[: rows // 2]
        there[...] = total[rows // 2 :]

    outs = [shape((rows // 2, cols))] * 2
    return call(
        "final_sums",
        body,
        table,
        (1,),
        parts,
        [whole(x) for x in parts],
        outs,
        [whole(o) for o in outs],
        8,
    )


def finish(table, here, there):
    rows, cols = here[0].shape
    side = cols // 3

    def body(s, *refs):
        out = refs[-1]
        for i, half in enumerate((s[Z], 1 - s[Z])):
            for k in range(2):
                for j in range(3):
                    at = pl.ds(pl.multiple_of(half * 2 * side + k * side, side), side)
                    out[j, :, at] = refs[2 * i + k][:, j * side : (j + 1) * side].astype(F32)

    out = shape((3, rows, 4 * side), F32)
    operands = (*here, *there)
    return call("finish", body, table, (1,), operands, [whole(x) for x in operands], out, whole(out), 8)


def swaps(pieces, left, right):
    a, c = send(pieces[0], left, 1), send(pieces[2], right, 1)
    b, d = send(pieces[1], left, 3), send(pieces[3], right, 3)
    return [a, b], [c, d]


def device_part(activations, qkv_weight, log_decay, lengths, out_grad):
    tied = lax.optimization_barrier
    tokens = activations.shape[0]
    heads = log_decay.shape[1]
    per = heads // 2
    index = [lax.axis_index(a) for a in ("c0", "c1", "c2", "zl", "co")]
    here_z = index[0]
    fixed = [*index, index[3] * 2 + index[4]]
    table = jnp.stack(fixed).astype(jnp.int32)
    weight = pltpu.with_memory_space_constraint(jnp.transpose(qkv_weight, (1, 0, 2)), pltpu.HBM)

    near = send(activations, "zl", 1)
    side = across(activations)
    core = send(activations, "co", 1)

    live = (jnp.arange(tokens, dtype=jnp.int32) < lengths[0]).astype(F32)
    cumul = jnp.cumsum(log_decay.T * live[None, :], axis=1)
    size = jnp.broadcast_to(lengths.astype(F32)[:, None], (per, tokens))
    info, note = (
        jnp.concatenate([lax.dynamic_slice_in_dim(cumul, z * per, per), size])
        for z in (here_z, 1 - here_z)
    )
    note = send(note, "c0", 1)
    width = per * HEAD
    og_own = lax.dynamic_slice_in_dim(out_grad, here_z * width, width, axis=1)
    og_other = lax.dynamic_slice_in_dim(out_grad, (1 - here_z) * width, width, axis=1)

    acc_own = project(table, [[activations], [core]], (0, 1), weight, None, None)
    near, side, acc_own, note, og_other, info = tied((near, side, acc_own, note, og_other, info))
    far = split(table, side, near)
    far = [send(far[0], "zl", 1), across(far[1])]
    near_core = send(near, "co", 1)
    side_core = send(side, "co", 1)
    qkv_own = project(table, [[near], [near_core]], (2, 3), weight, acc_own, info)
    turned = [turn(table, tied(([[activations], [core], [near], [near_core]], qkv_own))[0])]
    far, side_core, qkv_own, turned = tied((far, side_core, qkv_own, turned))
    far_core = [send(x, "co", 1) for x in far]
    og_pair = send(tied((og_other, far))[0], "c0", 1)
    to_y = shard_states(table, qkv_own, og_own, info, 0, None)
    far_core, to_y = tied((far_core, to_y))
    qkv_pair = project(
        table, [[side], [side_core], far, far_core], (2, 3, 0, 1), weight, None, note
    )
    og_pair, qkv_pair = tied((og_pair, qkv_pair))

    to_y = shard_states(table, qkv_pair, og_pair, note, 1, to_y)
    at_y = [send(to_y[r], "c2", r) for r in (1, 3, 2)]
    qkv_own, _ = tied((qkv_own, to_y[0]))
    local_own = local_grads(table, qkv_own, og_own, info, 0, per, None)
    at_y, local_own = tied((at_y, local_own))
    before, after, prior, later, ring = ring_y(table, [to_y[0], at_y[0], at_y[2], at_y[1]])
    at_x = [send(ring, "c1", r) for r in (1, 3, 2)]
    qkv_pair, _ = tied((qkv_pair, ring))
    local = local_grads(table, qkv_pair, og_pair, note, 0, per // 2, None)
    second, _ = tied(([far, far_core, [side], [side_core]], ring))
    turned.append(turn(table, second))
    at_x, local, turned = tied((at_x, local, turned))
    back = arrivals(table, [ring, at_x[0], at_x[2], at_x[1]], before, after, prior, later)
    states = [send(back[r], "c2", r) for r in (1, 3, 2)]
    local, _ = tied((local, back[0]))
    local = local_grads(table, qkv_pair, og_pair, note, per // 2, per // 2, local)
    states, turned, local = tied((states, turned, local))
    states = [back[0], states[0], states[2], states[1]]

    left_own, right_own, left_pair, right_pair = whole_grads(table, local_own, local, states)
    lefts, rights = (left_own, left_pair), (right_own, right_pair)
    far_piece = weight_part(table, turned, lefts, rights, (2,), True)
    l_half, r_half = swaps(far_piece, "c1", "c2")
    turned, _ = tied((turned, far_piece[0]))
    l_one, l_three, r_one, r_three = weight_part(table, turned, lefts, rights, (1, 3), False)
    l_half, l_one = tied((l_half, l_one))
    l_three, l_one = add_halves(table, l_three, l_one, l_half)
    l_got = [send(l_one, "c1", 1), send(l_three, "c1", 3)]
    r_half, _ = tied((r_half, l_one))
    r_three, r_one = add_halves(table, r_three, r_one, r_half)
    r_got = [send(r_one, "c2", 1), send(r_three, "c2", 3)]
    turned, _ = tied((turned, r_one))
    own = weight_part(table, turned, lefts, rights, (0,), False)
    l_got, own = tied((l_got, own))
    l_cut, r_cut = cut_blocks(table, (own[0], *l_got), (own[1], *r_got))
    l_got = [send(x, "c2", by) for x, by in zip(l_cut, (1, 3, 2))]
    r_got = [send(x, "c1", by) for x, by in zip(r_cut, (1, 3, 2))]
    l_here, l_there = final_sums(table, (l_cut[3], *l_got))
    r_got, _ = tied((r_got, l_here))
    r_here, r_there = final_sums(table, (r_cut[3], *r_got))
    there = [send(x, "c0", 1) for x in (l_there, r_there)]
    return jnp.transpose(finish(table, (l_here, r_here), there), (1, 0, 2))


def solution(mesh):
    finer = Mesh(mesh.devices.reshape(2, 4, 4, 2, 2), ("c0", "c1", "c2", "zl", "co"))
    context, tensor = ("c0", "c1", "c2"), ("zl", "co")
    placed = (
        P(context, tensor),
        P(None, None, tensor),
        P(context, tensor),
        P(context),
        P(context, tensor),
    )
    return jax.shard_map(
        device_part,
        mesh=finer,
        in_specs=placed,
        out_specs=P(context, None, tensor),
        check_vma=False,
    )
```

```python
import jax
import jax.numpy as jnp
from jax import lax
from jax.experimental import pallas as pl
from jax.experimental.pallas import tpu as pltpu
from jax.sharding import Mesh
from jax.sharding import PartitionSpec as P

F32 = jnp.float32
BF16 = jnp.bfloat16
HEAD = 128
HEADS = 4
Z, X, Y, ZL, CO, TEN = range(6)
AB_T = (((1,), (1,)), ((), ()))
A_TB = (((0,), (0,)), ((), ()))


def dot(a, b):
    return jnp.dot(a, b, preferred_element_type=F32)


def send(x, axis, by):
    return lax.ppermute(x, axis, [(i, i ^ by) for i in range(lax.axis_size(axis))])


def across(x):
    return lax.ppermute(x, ("c0", "zl"), [(0, 3), (1, 2), (2, 1), (3, 0)])


def whole(x):
    return pl.BlockSpec(x.shape, lambda *_, n=len(x.shape): (0,) * n)


def call(name, body, table, grid, operands, in_specs, outs, out_specs, mib, scratch=(), alias=None):
    return pl.pallas_call(
        body,
        grid_spec=pltpu.PrefetchScalarGridSpec(
            num_scalar_prefetch=1,
            grid=grid,
            in_specs=in_specs,
            out_specs=out_specs,
            scratch_shapes=scratch,
        ),
        out_shape=outs,
        input_output_aliases=alias or {},
        compiler_params=pltpu.CompilerParams(
            dimension_semantics=("arbitrary",) * len(grid), vmem_limit_bytes=mib << 20
        ),
        cost_estimate=pl.CostEstimate(flops=1, bytes_accessed=1, transcendentals=0),
        name=name,
    )(table, *operands)


def shape(dims, kind=BF16):
    return jax.ShapeDtypeStruct(dims, kind)


def joined(refs):
    parts = [ref[...] for ref in refs]
    return parts[0] if len(parts) == 1 else jnp.concatenate(parts, axis=0)


def living(info, dims):
    row = lax.broadcasted_iota(jnp.int32, dims, 0).astype(F32)
    return row < info[HEADS : HEADS + 1, :1]


def project(table, shards, flips, weight, partial, info):
    last = info is not None
    n, counts = len(shards), [len(x) for x in shards]
    flat = [part for x in shards for part in x]
    tokens, width = sum(part.shape[0] for part in shards[0]), flat[0].shape[1]
    cols = weight.shape[2] // 2

    def body(s, *refs):
        out, rest = refs[-1], list(refs)
        acc = None
        for i, count in enumerate(counts):
            rows = joined([rest.pop(0) for _ in range(count)])
            term = dot(rows, refs[len(flat) + i][0])
            acc = term if acc is None else acc + term
        if partial is not None:
            acc += refs[len(flat) + n][0]
        if last:
            acc = jnp.where(living(refs[-2], acc.shape), acc, 0.0)
        out[0] = acc.astype(out.dtype)

    tile = pl.BlockSpec((1, tokens, cols), lambda g, s: (g, 0, 0))
    in_specs = [whole(x) for x in flat]
    for flip in flips:
        in_specs.append(
            pl.BlockSpec((1, width, cols), lambda g, s, flip=flip: (g, s[TEN] ^ flip, s[Z]))
        )
    operands = [*flat, *([weight] * n)]
    if partial is not None:
        in_specs.append(tile)
        operands.append(partial)
    if last:
        in_specs.append(whole(info))
        operands.append(info)
    out = shape((3, tokens, cols), BF16 if last else F32)
    return call("project", body, table, (3,), operands, in_specs, out, tile, 24)


def shard_states(table, qkv, out_grad, cumul, which, so_far):
    tokens = qkv.shape[1]
    scale = HEAD**-0.5

    def body(s, qkv_ref, og_ref, cum_ref, *refs):
        outs = refs[-4:]
        r = pl.program_id(0)
        row = cum_ref[pl.ds(s[Y] ^ r, 1), :]
        total = row[:, tokens - 1 : tokens]
        keys_t = qkv_ref[1].T.astype(F32)
        query_t = qkv_ref[0].T.astype(F32)
        keys_t = (keys_t * jnp.exp(total - row)).astype(BF16)
        query_t = (query_t * (scale * jnp.exp(row))).astype(BF16)
        states = (dot(keys_t, qkv_ref[2]), dot(query_t, og_ref[...]))
        at = lax.broadcasted_iota(jnp.int32, (16, HEAD), 0)
        tail = jnp.broadcast_to(total, (16, HEAD)).astype(BF16)
        for k, out in enumerate(outs):

            @pl.when(r == k)
            def _(k=k, out=out):
                here = s[Z] ^ which
                if so_far is not None:
                    out[...] = refs[k][...]
                for kind in range(2):
                    start = pl.multiple_of((2 * kind + here) * HEAD, HEAD)
                    out[pl.ds(start, HEAD), :] = states[kind].astype(BF16)
                if so_far is None:
                    out[4 * HEAD :, :] = tail
                else:
                    out[4 * HEAD :, :] = jnp.where(at == here, tail, refs[k][4 * HEAD :, :])

    message = shape((4 * HEAD + 16, HEAD))
    operands = [qkv, out_grad, cumul, *(so_far or ())]
    in_specs = [
        pl.BlockSpec((3, tokens, HEAD), lambda r, s: (0, 0, s[Y] ^ r)),
        pl.BlockSpec((tokens, HEAD), lambda r, s: (0, s[Y] ^ r)),
        whole(cumul),
        *[whole(m) for m in so_far or ()],
    ]
    return call(
        "shard_states",
        body,
        table,
        (4,),
        operands,
        in_specs,
        [message] * 4,
        [whole(message)] * 4,
        12,
    )


def in_order(refs, place, held):
    for r, ref in enumerate(refs):
        held[place ^ r] = ref[...]


def spread(pair):
    wide = [jnp.broadcast_to(pair[i : i + 1, :], (HEAD, HEAD)) for i in range(2)]
    return jnp.concatenate(wide, axis=0)


def ring_y(table, messages):
    half = 2 * HEAD

    def body(s, a, b, c, d, before, after, prior, later, out, held):
        in_order((a, b, c, d), s[Y], held)
        totals = [held[t, 2 * half : 2 * half + 16, :].astype(F32)[:2] for t in range(4)]
        run = jnp.zeros((half, HEAD), F32)
        reach = jnp.zeros((2, HEAD), F32)
        for t in range(4):
            before[t] = run
            prior[t] = jnp.exp(reach)
            run = spread(jnp.exp(totals[t])) * run + held[t, :half, :].astype(F32)
            reach = reach + totals[t]
        out[:half, :] = run.astype(BF16)
        total = reach
        run = jnp.zeros((half, HEAD), F32)
        reach = jnp.zeros((2, HEAD), F32)
        for t in range(3, -1, -1):
            after[t] = run
            later[t] = jnp.exp(reach)
            run = spread(jnp.exp(totals[t])) * run + held[t, half : 2 * half, :].astype(F32)
            reach = reach + totals[t]
        out[half : 2 * half, :] = run.astype(BF16)
        high = total.astype(BF16).astype(F32)
        low = total - high
        at = lax.broadcasted_iota(jnp.int32, (16, HEAD), 0)
        tail = jnp.where(at == 0, high[0:1], high[1:2])
        tail = jnp.where(at == 2, low[0:1], tail)
        tail = jnp.where(at == 3, low[1:2], tail)
        out[2 * half :, :] = tail.astype(BF16)

    outs = [
        shape((4, half, HEAD), F32),
        shape((4, half, HEAD), F32),
        shape((4, 2, HEAD), F32),
        shape((4, 2, HEAD), F32),
        shape(messages[0].shape),
    ]
    return call(
        "ring_y",
        body,
        table,
        (1,),
        messages,
        [whole(m) for m in messages],
        outs,
        [whole(o) for o in outs],
        8,
        [pltpu.VMEM((4, *messages[0].shape), BF16)],
    )


def arrivals(table, messages, before, after, prior, later):
    half = 2 * HEAD

    def body(s, a, b, c, d, before_ref, after_ref, prior_ref, later_ref, *rest):
        outs, held, mine, edges = rest[:4], *rest[4:]
        in_order((a, b, c, d), s[X], held)
        tails = [held[t, 2 * half : 2 * half + 16, :].astype(F32) for t in range(4)]
        totals = [tail[0:2] + tail[2:4] for tail in tails]
        ends = []
        for kind, steps in ((0, range(4)), (1, range(3, -1, -1))):
            run = jnp.zeros((half, HEAD), F32)
            reach = jnp.zeros((2, HEAD), F32)
            for t in steps:

                @pl.when(s[X] == t)
                def _(run=run, reach=reach, kind=kind):
                    mine[kind] = run
                    edges[kind] = jnp.exp(reach)

                rows = held[t, kind * half : (kind + 1) * half, :].astype(F32)
                run = spread(jnp.exp(totals[t])) * run + rows
                reach = reach + totals[t]
            ends.append(run.astype(BF16).astype(F32))
        nothing = jnp.zeros((HEAD, HEAD), F32)
        across_up = jnp.concatenate([nothing, ends[0][:HEAD]], axis=0)
        across_down = jnp.concatenate([ends[1][HEAD:], nothing], axis=0)
        start = mine[0] + spread(edges[0]) * across_up
        finish = mine[1] + spread(edges[1]) * across_down
        for r, out in enumerate(outs):
            t = s[Y] ^ r
            out[:half, :] = (before_ref[t] + spread(prior_ref[t]) * start).astype(BF16)
            out[half:, :] = (after_ref[t] + spread(later_ref[t]) * finish).astype(BF16)

    operands = (*messages, before, after, prior, later)
    message = shape((2 * half, HEAD))
    return call(
        "arrivals",
        body,
        table,
        (1,),
        operands,
        [whole(m) for m in operands],
        [message] * 4,
        [whole(message)] * 4,
        8,
        [
            pltpu.VMEM((4, *messages[0].shape), BF16),
            pltpu.VMEM((2, half, HEAD), F32),
            pltpu.VMEM((2, 2, HEAD), F32),
        ],
    )


def column_of(row):
    return jnp.broadcast_to(row, (HEAD, row.shape[1])).T


def local_grads(table, qkv, out_grad, cumul, first, count, so_far):
    tokens = qkv.shape[1]
    scale = HEAD**-0.5
    size = tokens // 2

    def body(s, qkv_ref, og_ref, cum_ref, *refs):
        out, ready = refs[-2:]
        row = cum_ref[pl.ds(pl.program_id(0) + first, 1), :]
        column = column_of(row)
        wide = jnp.concatenate([column] * (size // HEAD), axis=1)
        s_at = lax.broadcasted_iota(jnp.int32, (size, size), 0)
        t_at = lax.broadcasted_iota(jnp.int32, (size, size), 1)
        parts = [slice(0, size), slice(size, tokens)]

        def pair(t, s):
            if t == s:
                gap = row[:, parts[t]] - wide[parts[s], :]
                decay = jnp.exp(jnp.where(s_at <= t_at, gap, -jnp.inf))
            else:
                middle = row[:, size - 1 : size]
                to_middle = jnp.exp(middle - column[parts[s], :])
                decay = jnp.concatenate([to_middle] * (size // HEAD), axis=1)
                decay *= jnp.exp(row[:, parts[t]] - middle)
            q, k, v = qkv_ref[0, parts[t], :], qkv_ref[1, parts[s], :], qkv_ref[2, parts[s], :]
            g = og_ref[parts[t], :]
            scores = lax.dot_general(k, q, AB_T, preferred_element_type=F32)
            grads = lax.dot_general(v, g, AB_T, preferred_element_type=F32)
            prob = (scores * decay).astype(BF16)
            score = (grads * decay).astype(BF16)
            dq = lax.dot_general(score, k, A_TB, preferred_element_type=F32)
            return dq, dot(score, q), dot(prob, g)

        a, b, c = pair(0, 0), pair(1, 0), pair(1, 1)
        live = living(cum_ref, (tokens, HEAD))
        grads = (
            jnp.concatenate([a[0], b[0] + c[0]], axis=0) * scale,
            jnp.concatenate([a[1] + b[1], c[1]], axis=0) * scale,
            jnp.concatenate([a[2] + b[2], c[2]], axis=0) * scale,
        )
        until = jnp.exp(row[:, tokens - 1 : tokens] - column)
        rows = (
            og_ref[...].astype(F32) * (scale * jnp.exp(column)),
            qkv_ref[2].astype(F32) * until,
            qkv_ref[1].astype(F32) * until,
        )
        for j in range(3):
            out[j] = jnp.where(live, grads[j], 0.0).astype(BF16)
            ready[j] = jnp.where(live, rows[j], 0.0).astype(BF16)

    tile = pl.BlockSpec((3, tokens, HEAD), lambda h, s: (0, 0, h + first))
    in_specs = [tile, pl.BlockSpec((tokens, HEAD), lambda h, s: (0, h + first)), whole(cumul)]
    operands = [qkv, out_grad, cumul]
    if so_far is not None:
        in_specs += [pl.BlockSpec(memory_space=pl.ANY)] * 2
        operands += so_far
    return call(
        "local_grads",
        body,
        table,
        (count,),
        operands,
        in_specs,
        [shape(qkv.shape), shape(qkv.shape)],
        [tile, tile],
        12,
        alias=None if so_far is None else {4: 0, 5: 1},
    )


def whole_grads(table, own, pair, states):
    tokens, heads = own[0].shape[1], HEADS

    def body(s, local_a, ready_a, local_b, ready_b, a, b, c, d, *rest):
        outs, held = rest[:4], rest[4]
        i = pl.program_id(0)

        @pl.when(i == 0)
        def _():
            in_order((a, b, c, d), s[Y], held)

        for which, (local_ref, ready_ref) in enumerate(((local_a, ready_a), (local_b, ready_b))):
            for k in range(heads):

                @pl.when(i == which * heads + k)
                def _(k=k, which=which, local_ref=local_ref, ready_ref=ready_ref):
                    base = pl.multiple_of((s[Z] ^ which) * HEAD, HEAD)
                    coming = held[k, pl.ds(base, HEAD), :]
                    later = held[k, pl.ds(2 * HEAD + base, HEAD), :]
                    cross = (
                        lax.dot_general(ready_ref[0], coming, AB_T, preferred_element_type=F32),
                        lax.dot_general(ready_ref[1], later, AB_T, preferred_element_type=F32),
                        dot(ready_ref[2], later),
                    )
                    out = outs[2 * which + k // 2]
                    for j in range(3):
                        start = (2 * j + k % 2) * HEAD
                        total = local_ref[j].astype(F32) + cross[j]
                        out[:, start : start + HEAD] = total.astype(BF16)

    first = pl.BlockSpec((3, tokens, HEAD), lambda i, s: (0, 0, jnp.minimum(i, heads - 1)))
    second = pl.BlockSpec((3, tokens, HEAD), lambda i, s: (0, 0, jnp.maximum(i - heads, 0)))
    side = shape((tokens, 3 * heads * HEAD // 2))
    return call(
        "whole_grads",
        body,
        table,
        (2 * heads,),
        (*own, *pair, *states),
        [first, first, second, second, *[whole(m) for m in states]],
        [side] * 4,
        [whole(side)] * 4,
        16,
        [pltpu.VMEM((4, *states[0].shape), BF16)],
    )


def split(table, first, second):
    tokens, width = first.shape

    def body(s, a, b, out_a, out_b):
        out_a[...] = a[...]
        out_b[...] = b[...]

    halves = [pl.BlockSpec((tokens // 2, width), lambda i, s, k=k: (k, 0)) for k in range(2)]
    out = shape((tokens // 2, width))
    return call("split", body, table, (1,), (first, second), halves, [out] * 2, [whole(out)] * 2, 8)


def turn(table, shards):
    counts = [len(x) for x in shards]
    flat = [part for x in shards for part in x]
    tokens, width = sum(part.shape[0] for part in shards[0]), flat[0].shape[1]
    rows = 4 * width // 32

    def body(s, *refs):
        out, at = refs[-1], 0
        for k, count in enumerate(counts):
            mine, at = refs[at : at + count], at + count

            @pl.when((pl.program_id(0) ^ s[TEN]) == k)
            def _(mine=mine):
                out[...] = joined(mine).T.reshape(out.shape)

    out = shape((16, 2, rows, tokens))
    spec = pl.BlockSpec((8, 1, rows, tokens), lambda i, s: (i % 2, (i // 2) ^ s[Z], 0, 0))
    turned = call("turn", body, table, (4,), flat, [whole(x) for x in flat], out, spec, 12)
    return turned.reshape(4, 4, 2 * rows, tokens)


def weight_part(table, turned, lefts, rights, places, split):
    tokens, cols = lefts[0].shape
    rows = turned[0].shape[2]

    def body(s, own_x, own_y, pair_x, pair_y, left_a, left_b, right_a, right_b, *outs):
        r = pl.program_id(0)
        for side, (a, b, ga, gb) in enumerate(
            ((own_x, pair_x, left_a, left_b), (own_y, pair_y, right_a, right_b))
        ):
            acc = dot(a[...].reshape(4 * rows, tokens), ga[...])
            acc += dot(b[...].reshape(4 * rows, tokens), gb[...])
            acc = acc.astype(BF16)
            if split:
                outs[2 * side][...] = acc[: 2 * rows]
                outs[2 * side + 1][...] = acc[2 * rows :]
                continue
            for k in range(len(places)):

                @pl.when(r == k)
                def _(k=k, acc=acc, side=side):
                    outs[side * len(places) + k][...] = acc

    step = places[1] - places[0] if len(places) > 1 else 0
    by_x = pl.BlockSpec((1, 4, rows, tokens), lambda r, s: (s[X] ^ (places[0] + step * r), 0, 0, 0))
    by_y = pl.BlockSpec((4, 1, rows, tokens), lambda r, s: (0, s[Y] ^ (places[0] + step * r), 0, 0))
    outs = [shape((2 * rows if split else 4 * rows, cols))] * (4 if split else 2 * len(places))
    operands = (turned[0], turned[0], turned[1], turned[1], *lefts, *rights)
    return call(
        "weight_part",
        body,
        table,
        (len(places),),
        operands,
        [by_x, by_y, by_x, by_y, *[whole(x) for x in (*lefts, *rights)]],
        outs,
        [whole(o) for o in outs],
        30,
    )


def add_halves(table, third, first_place, halves):
    up, down = halves
    near_up, near_down = third, first_place
    n, cols = up.shape

    def body(s, a, b, u, d, out_a, out_b):
        out_a[...] = (a[...].astype(F32) + u[...].astype(F32)).astype(BF16)
        out_b[...] = (b[...].astype(F32) + d[...].astype(F32)).astype(BF16)

    steps = 4
    first = pl.BlockSpec((n // steps, cols), lambda i, s: (i, 0))
    second = pl.BlockSpec((n // steps, cols), lambda i, s: (i + steps, 0))
    return call(
        "add_halves",
        body,
        table,
        (steps,),
        (near_up, near_down, up, down),
        [first, second, first, first],
        [shape(near_up.shape), shape(near_down.shape)],
        [first, second],
        12,
        alias={1: 0, 2: 1},
    )


def cut_blocks(table, left, right):
    rows, cols = left[0].shape[0] // 4, left[0].shape[1]

    def body(s, *refs):
        for k, axis in enumerate((Y, X)):
            a, b, c = refs[3 * k : 3 * k + 3]
            for r, out in zip((1, 3, 2, 0), refs[6 + 4 * k : 10 + 4 * k]):
                at = pl.ds(pl.multiple_of((s[axis] ^ r) * rows, rows), rows)
                total = a[at, :].astype(F32) + b[at, :].astype(F32) + c[at, :].astype(F32)
                out[...] = total.astype(BF16)

    outs = [shape((rows, cols))] * 8
    operands = (*left, *right)
    cut = call(
        "cut_blocks",
        body,
        table,
        (1,),
        operands,
        [whole(x) for x in operands],
        outs,
        [whole(o) for o in outs],
        24,
    )
    return cut[:4], cut[4:]


def final_sums(table, parts):
    rows, cols = parts[0].shape

    def body(s, a, b, c, d, here, there):
        total = sum(ref[...].astype(F32) for ref in (a, b, c, d)).astype(BF16)
        here[...] = total[: rows // 2]
        there[...] = total[rows // 2 :]

    outs = [shape((rows // 2, cols))] * 2
    return call(
        "final_sums",
        body,
        table,
        (1,),
        parts,
        [whole(x) for x in parts],
        outs,
        [whole(o) for o in outs],
        8,
    )


def finish(table, here, there):
    rows, cols = here[0].shape
    side = cols // 3

    def body(s, *refs):
        out = refs[-1]
        for i, half in enumerate((s[Z], 1 - s[Z])):
            for k in range(2):
                for j in range(3):
                    at = pl.ds(pl.multiple_of(half * 2 * side + k * side, side), side)
                    out[j, :, at] = refs[2 * i + k][:, j * side : (j + 1) * side].astype(F32)

    out = shape((3, rows, 4 * side), F32)
    operands = (*here, *there)
    return call("finish", body, table, (1,), operands, [whole(x) for x in operands], out, whole(out), 8)


def swaps(pieces, left, right):
    a, c = send(pieces[0], left, 1), send(pieces[2], right, 1)
    b, d = send(pieces[1], left, 3), send(pieces[3], right, 3)
    return [a, b], [c, d]


def device_part(activations, qkv_weight, log_decay, lengths, out_grad):
    tied = lax.optimization_barrier
    tokens = activations.shape[0]
    heads = log_decay.shape[1]
    per = heads // 2
    index = [lax.axis_index(a) for a in ("c0", "c1", "c2", "zl", "co")]
    here_z = index[0]
    fixed = [*index, index[3] * 2 + index[4]]
    table = jnp.stack(fixed).astype(jnp.int32)
    weight = pltpu.with_memory_space_constraint(jnp.transpose(qkv_weight, (1, 0, 2)), pltpu.HBM)

    near = send(activations, "zl", 1)
    side = across(activations)
    core = send(activations, "co", 1)

    live = (jnp.arange(tokens, dtype=jnp.int32) < lengths[0]).astype(F32)
    cumul = jnp.cumsum(log_decay.T * live[None, :], axis=1)
    size = jnp.broadcast_to(lengths.astype(F32)[:, None], (per, tokens))
    info, note = (
        jnp.concatenate([lax.dynamic_slice_in_dim(cumul, z * per, per), size])
        for z in (here_z, 1 - here_z)
    )
    note = send(note, "c0", 1)
    width = per * HEAD
    og_own = lax.dynamic_slice_in_dim(out_grad, here_z * width, width, axis=1)
    og_other = lax.dynamic_slice_in_dim(out_grad, (1 - here_z) * width, width, axis=1)

    acc_own = project(table, [[activations], [core]], (0, 1), weight, None, None)
    near, side, acc_own, note, og_other, info = tied((near, side, acc_own, note, og_other, info))
    far = split(table, side, near)
    far = [send(far[0], "zl", 1), across(far[1])]
    near_core = send(near, "co", 1)
    side_core = send(side, "co", 1)
    qkv_own = project(table, [[near], [near_core]], (2, 3), weight, acc_own, info)
    turned = [turn(table, tied(([[activations], [core], [near], [near_core]], qkv_own))[0])]
    far, side_core, qkv_own, turned = tied((far, side_core, qkv_own, turned))
    far_core = [send(x, "co", 1) for x in far]
    og_pair = send(tied((og_other, far))[0], "c0", 1)
    to_y = shard_states(table, qkv_own, og_own, info, 0, None)
    far_core, to_y = tied((far_core, to_y))
    qkv_pair = project(
        table, [[side], [side_core], far, far_core], (2, 3, 0, 1), weight, None, note
    )
    og_pair, qkv_pair = tied((og_pair, qkv_pair))

    to_y = shard_states(table, qkv_pair, og_pair, note, 1, to_y)
    at_y = [send(to_y[r], "c2", r) for r in (2, 1, 3)]
    qkv_own, _ = tied((qkv_own, to_y[0]))
    local_own = local_grads(table, qkv_own, og_own, info, 0, per, None)
    at_y, local_own = tied((at_y, local_own))
    before, after, prior, later, ring = ring_y(table, [to_y[0], at_y[1], at_y[0], at_y[2]])
    at_x = [send(ring, "c1", r) for r in (1, 3, 2)]
    qkv_pair, _ = tied((qkv_pair, ring))
    local = local_grads(table, qkv_pair, og_pair, note, 0, per // 2, None)
    second, _ = tied(([far, far_core, [side], [side_core]], ring))
    turned.append(turn(table, second))
    at_x, local, turned = tied((at_x, local, turned))
    back = arrivals(table, [ring, at_x[0], at_x[2], at_x[1]], before, after, prior, later)
    states = [send(back[r], "c2", r) for r in (2, 1, 3)]
    local, _ = tied((local, back[0]))
    local = local_grads(table, qkv_pair, og_pair, note, per // 2, per // 2, local)
    states, turned, local = tied((states, turned, local))
    states = [back[0], states[1], states[0], states[2]]

    left_own, right_own, left_pair, right_pair = whole_grads(table, local_own, local, states)
    lefts, rights = (left_own, left_pair), (right_own, right_pair)
    far_piece = weight_part(table, turned, lefts, rights, (2,), True)
    l_half, r_half = swaps(far_piece, "c1", "c2")
    turned, _ = tied((turned, far_piece[0]))
    l_one, l_three, r_one, r_three = weight_part(table, turned, lefts, rights, (1, 3), False)
    l_half, l_one = tied((l_half, l_one))
    l_three, l_one = add_halves(table, l_three, l_one, l_half)
    l_got = [send(l_one, "c1", 1), send(l_three, "c1", 3)]
    r_half, _ = tied((r_half, l_one))
    r_three, r_one = add_halves(table, r_three, r_one, r_half)
    r_got = [send(r_one, "c2", 1), send(r_three, "c2", 3)]
    turned, _ = tied((turned, r_one))
    own = weight_part(table, turned, lefts, rights, (0,), False)
    l_got, own = tied((l_got, own))
    l_cut, r_cut = cut_blocks(table, (own[0], *l_got), (own[1], *r_got))
    l_got = [send(x, "c2", by) for x, by in zip(l_cut, (1, 3, 2))]
    r_got = [send(x, "c1", by) for x, by in zip(r_cut, (1, 3, 2))]
    l_here, l_there = final_sums(table, (l_cut[3], *l_got))
    r_got, _ = tied((r_got, l_here))
    r_here, r_there = final_sums(table, (r_cut[3], *r_got))
    there = [send(x, "c0", 1) for x in (l_there, r_there)]
    return jnp.transpose(finish(table, (l_here, r_here), there), (1, 0, 2))


def solution(mesh):
    finer = Mesh(mesh.devices.reshape(2, 4, 4, 2, 2), ("c0", "c1", "c2", "zl", "co"))
    context, tensor = ("c0", "c1", "c2"), ("zl", "co")
    placed = (
        P(context, tensor),
        P(None, None, tensor),
        P(context, tensor),
        P(context),
        P(context, tensor),
    )
    return jax.shard_map(
        device_part,
        mesh=finer,
        in_specs=placed,
        out_specs=P(context, None, tensor),
        check_vma=False,
    )
```

```python
import jax
import jax.numpy as jnp
from jax import lax
from jax.experimental import pallas as pl
from jax.experimental.pallas import tpu as pltpu
from jax.sharding import Mesh
from jax.sharding import PartitionSpec as P

F32 = jnp.float32
BF16 = jnp.bfloat16
HEAD = 128
HEADS = 4
Z, X, Y, ZL, CO, TEN = range(6)
AB_T = (((1,), (1,)), ((), ()))
A_TB = (((0,), (0,)), ((), ()))


def dot(a, b):
    return jnp.dot(a, b, preferred_element_type=F32)


def send(x, axis, by):
    return lax.ppermute(x, axis, [(i, i ^ by) for i in range(lax.axis_size(axis))])


def across(x):
    return lax.ppermute(x, ("c0", "zl"), [(0, 3), (1, 2), (2, 1), (3, 0)])


def whole(x):
    return pl.BlockSpec(x.shape, lambda *_, n=len(x.shape): (0,) * n)


def call(name, body, table, grid, operands, in_specs, outs, out_specs, mib, scratch=(), alias=None):
    return pl.pallas_call(
        body,
        grid_spec=pltpu.PrefetchScalarGridSpec(
            num_scalar_prefetch=1,
            grid=grid,
            in_specs=in_specs,
            out_specs=out_specs,
            scratch_shapes=scratch,
        ),
        out_shape=outs,
        input_output_aliases=alias or {},
        compiler_params=pltpu.CompilerParams(
            dimension_semantics=("arbitrary",) * len(grid), vmem_limit_bytes=mib << 20
        ),
        cost_estimate=pl.CostEstimate(flops=1, bytes_accessed=1, transcendentals=0),
        name=name,
    )(table, *operands)


def shape(dims, kind=BF16):
    return jax.ShapeDtypeStruct(dims, kind)


def joined(refs):
    parts = [ref[...] for ref in refs]
    return parts[0] if len(parts) == 1 else jnp.concatenate(parts, axis=0)


def living(info, dims):
    row = lax.broadcasted_iota(jnp.int32, dims, 0).astype(F32)
    return row < info[HEADS : HEADS + 1, :1]


def project(table, shards, flips, weight, partial, info):
    last = info is not None
    n, counts = len(shards), [len(x) for x in shards]
    flat = [part for x in shards for part in x]
    tokens, width = sum(part.shape[0] for part in shards[0]), flat[0].shape[1]
    cols = weight.shape[2] // 2

    def body(s, *refs):
        out, rest = refs[-1], list(refs)
        acc = None
        for i, count in enumerate(counts):
            rows = joined([rest.pop(0) for _ in range(count)])
            term = dot(rows, refs[len(flat) + i][0])
            acc = term if acc is None else acc + term
        if partial is not None:
            acc += refs[len(flat) + n][0]
        if last:
            acc = jnp.where(living(refs[-2], acc.shape), acc, 0.0)
        out[0] = acc.astype(out.dtype)

    tile = pl.BlockSpec((1, tokens, cols), lambda g, s: (g, 0, 0))
    in_specs = [whole(x) for x in flat]
    for flip in flips:
        in_specs.append(
            pl.BlockSpec((1, width, cols), lambda g, s, flip=flip: (g, s[TEN] ^ flip, s[Z]))
        )
    operands = [*flat, *([weight] * n)]
    if partial is not None:
        in_specs.append(tile)
        operands.append(partial)
    if last:
        in_specs.append(whole(info))
        operands.append(info)
    out = shape((3, tokens, cols), BF16 if last else F32)
    return call("project", body, table, (3,), operands, in_specs, out, tile, 24)


def shard_states(table, qkv, out_grad, cumul, which, so_far):
    tokens = qkv.shape[1]
    scale = HEAD**-0.5

    def body(s, qkv_ref, og_ref, cum_ref, *refs):
        outs = refs[-4:]
        r = pl.program_id(0)
        row = cum_ref[pl.ds(s[Y] ^ r, 1), :]
        total = row[:, tokens - 1 : tokens]
        keys_t = qkv_ref[1].T.astype(F32)
        query_t = qkv_ref[0].T.astype(F32)
        keys_t = (keys_t * jnp.exp(total - row)).astype(BF16)
        query_t = (query_t * (scale * jnp.exp(row))).astype(BF16)
        states = (dot(keys_t, qkv_ref[2]), dot(query_t, og_ref[...]))
        at = lax.broadcasted_iota(jnp.int32, (16, HEAD), 0)
        tail = jnp.broadcast_to(total, (16, HEAD)).astype(BF16)
        for k, out in enumerate(outs):

            @pl.when(r == k)
            def _(k=k, out=out):
                here = s[Z] ^ which
                if so_far is not None:
                    out[...] = refs[k][...]
                for kind in range(2):
                    start = pl.multiple_of((2 * kind + here) * HEAD, HEAD)
                    out[pl.ds(start, HEAD), :] = states[kind].astype(BF16)
                if so_far is None:
                    out[4 * HEAD :, :] = tail
                else:
                    out[4 * HEAD :, :] = jnp.where(at == here, tail, refs[k][4 * HEAD :, :])

    message = shape((4 * HEAD + 16, HEAD))
    operands = [qkv, out_grad, cumul, *(so_far or ())]
    in_specs = [
        pl.BlockSpec((3, tokens, HEAD), lambda r, s: (0, 0, s[Y] ^ r)),
        pl.BlockSpec((tokens, HEAD), lambda r, s: (0, s[Y] ^ r)),
        whole(cumul),
        *[whole(m) for m in so_far or ()],
    ]
    return call(
        "shard_states",
        body,
        table,
        (4,),
        operands,
        in_specs,
        [message] * 4,
        [whole(message)] * 4,
        12,
    )


def in_order(refs, place, held):
    for r, ref in enumerate(refs):
        held[place ^ r] = ref[...]


def spread(pair):
    wide = [jnp.broadcast_to(pair[i : i + 1, :], (HEAD, HEAD)) for i in range(2)]
    return jnp.concatenate(wide, axis=0)


def ring_y(table, messages):
    half = 2 * HEAD

    def body(s, a, b, c, d, before, after, prior, later, out, held):
        in_order((a, b, c, d), s[Y], held)
        totals = [held[t, 2 * half : 2 * half + 16, :].astype(F32)[:2] for t in range(4)]
        run = jnp.zeros((half, HEAD), F32)
        reach = jnp.zeros((2, HEAD), F32)
        for t in range(4):
            before[t] = run
            prior[t] = jnp.exp(reach)
            run = spread(jnp.exp(totals[t])) * run + held[t, :half, :].astype(F32)
            reach = reach + totals[t]
        out[:half, :] = run.astype(BF16)
        total = reach
        run = jnp.zeros((half, HEAD), F32)
        reach = jnp.zeros((2, HEAD), F32)
        for t in range(3, -1, -1):
            after[t] = run
            later[t] = jnp.exp(reach)
            run = spread(jnp.exp(totals[t])) * run + held[t, half : 2 * half, :].astype(F32)
            reach = reach + totals[t]
        out[half : 2 * half, :] = run.astype(BF16)
        high = total.astype(BF16).astype(F32)
        low = total - high
        at = lax.broadcasted_iota(jnp.int32, (16, HEAD), 0)
        tail = jnp.where(at == 0, high[0:1], high[1:2])
        tail = jnp.where(at == 2, low[0:1], tail)
        tail = jnp.where(at == 3, low[1:2], tail)
        out[2 * half :, :] = tail.astype(BF16)

    outs = [
        shape((4, half, HEAD), F32),
        shape((4, half, HEAD), F32),
        shape((4, 2, HEAD), F32),
        shape((4, 2, HEAD), F32),
        shape(messages[0].shape),
    ]
    return call(
        "ring_y",
        body,
        table,
        (1,),
        messages,
        [whole(m) for m in messages],
        outs,
        [whole(o) for o in outs],
        8,
        [pltpu.VMEM((4, *messages[0].shape), BF16)],
    )


def arrivals(table, messages, before, after, prior, later):
    half = 2 * HEAD

    def body(s, a, b, c, d, before_ref, after_ref, prior_ref, later_ref, *rest):
        outs, held, mine, edges = rest[:4], *rest[4:]
        in_order((a, b, c, d), s[X], held)
        tails = [held[t, 2 * half : 2 * half + 16, :].astype(F32) for t in range(4)]
        totals = [tail[0:2] + tail[2:4] for tail in tails]
        ends = []
        for kind, steps in ((0, range(4)), (1, range(3, -1, -1))):
            run = jnp.zeros((half, HEAD), F32)
            reach = jnp.zeros((2, HEAD), F32)
            for t in steps:

                @pl.when(s[X] == t)
                def _(run=run, reach=reach, kind=kind):
                    mine[kind] = run
                    edges[kind] = jnp.exp(reach)

                rows = held[t, kind * half : (kind + 1) * half, :].astype(F32)
                run = spread(jnp.exp(totals[t])) * run + rows
                reach = reach + totals[t]
            ends.append(run.astype(BF16).astype(F32))
        nothing = jnp.zeros((HEAD, HEAD), F32)
        across_up = jnp.concatenate([nothing, ends[0][:HEAD]], axis=0)
        across_down = jnp.concatenate([ends[1][HEAD:], nothing], axis=0)
        start = mine[0] + spread(edges[0]) * across_up
        finish = mine[1] + spread(edges[1]) * across_down
        for r, out in enumerate(outs):
            t = s[Y] ^ r
            out[:half, :] = (before_ref[t] + spread(prior_ref[t]) * start).astype(BF16)
            out[half:, :] = (after_ref[t] + spread(later_ref[t]) * finish).astype(BF16)

    operands = (*messages, before, after, prior, later)
    message = shape((2 * half, HEAD))
    return call(
        "arrivals",
        body,
        table,
        (1,),
        operands,
        [whole(m) for m in operands],
        [message] * 4,
        [whole(message)] * 4,
        8,
        [
            pltpu.VMEM((4, *messages[0].shape), BF16),
            pltpu.VMEM((2, half, HEAD), F32),
            pltpu.VMEM((2, 2, HEAD), F32),
        ],
    )


def column_of(row):
    return jnp.broadcast_to(row, (HEAD, row.shape[1])).T


def local_grads(table, qkv, out_grad, cumul, first, count, so_far):
    tokens = qkv.shape[1]
    scale = HEAD**-0.5
    size = tokens // 2

    def body(s, qkv_ref, og_ref, cum_ref, *refs):
        out, ready = refs[-2:]
        row = cum_ref[pl.ds(pl.program_id(0) + first, 1), :]
        column = column_of(row)
        wide = jnp.concatenate([column] * (size // HEAD), axis=1)
        s_at = lax.broadcasted_iota(jnp.int32, (size, size), 0)
        t_at = lax.broadcasted_iota(jnp.int32, (size, size), 1)
        parts = [slice(0, size), slice(size, tokens)]

        def pair(t, s):
            if t == s:
                gap = row[:, parts[t]] - wide[parts[s], :]
                decay = jnp.exp(jnp.where(s_at <= t_at, gap, -jnp.inf))
            else:
                middle = row[:, size - 1 : size]
                to_middle = jnp.exp(middle - column[parts[s], :])
                decay = jnp.concatenate([to_middle] * (size // HEAD), axis=1)
                decay *= jnp.exp(row[:, parts[t]] - middle)
            q, k, v = qkv_ref[0, parts[t], :], qkv_ref[1, parts[s], :], qkv_ref[2, parts[s], :]
            g = og_ref[parts[t], :]
            scores = lax.dot_general(k, q, AB_T, preferred_element_type=F32)
            grads = lax.dot_general(v, g, AB_T, preferred_element_type=F32)
            prob = (scores * decay).astype(BF16)
            score = (grads * decay).astype(BF16)
            dq = lax.dot_general(score, k, A_TB, preferred_element_type=F32)
            return dq, dot(score, q), dot(prob, g)

        a, b, c = pair(0, 0), pair(1, 0), pair(1, 1)
        live = living(cum_ref, (tokens, HEAD))
        grads = (
            jnp.concatenate([a[0], b[0] + c[0]], axis=0) * scale,
            jnp.concatenate([a[1] + b[1], c[1]], axis=0) * scale,
            jnp.concatenate([a[2] + b[2], c[2]], axis=0) * scale,
        )
        until = jnp.exp(row[:, tokens - 1 : tokens] - column)
        rows = (
            og_ref[...].astype(F32) * (scale * jnp.exp(column)),
            qkv_ref[2].astype(F32) * until,
            qkv_ref[1].astype(F32) * until,
        )
        for j in range(3):
            out[j] = jnp.where(live, grads[j], 0.0).astype(BF16)
            ready[j] = jnp.where(live, rows[j], 0.0).astype(BF16)

    tile = pl.BlockSpec((3, tokens, HEAD), lambda h, s: (0, 0, h + first))
    in_specs = [tile, pl.BlockSpec((tokens, HEAD), lambda h, s: (0, h + first)), whole(cumul)]
    operands = [qkv, out_grad, cumul]
    if so_far is not None:
        in_specs += [pl.BlockSpec(memory_space=pl.ANY)] * 2
        operands += so_far
    return call(
        "local_grads",
        body,
        table,
        (count,),
        operands,
        in_specs,
        [shape(qkv.shape), shape(qkv.shape)],
        [tile, tile],
        12,
        alias=None if so_far is None else {4: 0, 5: 1},
    )


def whole_grads(table, own, pair, states):
    tokens, heads = own[0].shape[1], HEADS

    def body(s, local_a, ready_a, local_b, ready_b, a, b, c, d, *rest):
        outs, held = rest[:4], rest[4]
        i = pl.program_id(0)

        @pl.when(i == 0)
        def _():
            in_order((a, b, c, d), s[Y], held)

        for which, (local_ref, ready_ref) in enumerate(((local_a, ready_a), (local_b, ready_b))):
            for k in range(heads):

                @pl.when(i == which * heads + k)
                def _(k=k, which=which, local_ref=local_ref, ready_ref=ready_ref):
                    base = pl.multiple_of((s[Z] ^ which) * HEAD, HEAD)
                    coming = held[k, pl.ds(base, HEAD), :]
                    later = held[k, pl.ds(2 * HEAD + base, HEAD), :]
                    cross = (
                        lax.dot_general(ready_ref[0], coming, AB_T, preferred_element_type=F32),
                        lax.dot_general(ready_ref[1], later, AB_T, preferred_element_type=F32),
                        dot(ready_ref[2], later),
                    )
                    out = outs[2 * which + k // 2]
                    for j in range(3):
                        start = (2 * j + k % 2) * HEAD
                        total = local_ref[j].astype(F32) + cross[j]
                        out[:, start : start + HEAD] = total.astype(BF16)

    first = pl.BlockSpec((3, tokens, HEAD), lambda i, s: (0, 0, jnp.minimum(i, heads - 1)))
    second = pl.BlockSpec((3, tokens, HEAD), lambda i, s: (0, 0, jnp.maximum(i - heads, 0)))
    side = shape((tokens, 3 * heads * HEAD // 2))
    return call(
        "whole_grads",
        body,
        table,
        (2 * heads,),
        (*own, *pair, *states),
        [first, first, second, second, *[whole(m) for m in states]],
        [side] * 4,
        [whole(side)] * 4,
        16,
        [pltpu.VMEM((4, *states[0].shape), BF16)],
    )


def split(table, first, second):
    tokens, width = first.shape

    def body(s, a, b, out_a, out_b):
        out_a[...] = a[...]
        out_b[...] = b[...]

    halves = [pl.BlockSpec((tokens // 2, width), lambda i, s, k=k: (k, 0)) for k in range(2)]
    out = shape((tokens // 2, width))
    return call("split", body, table, (1,), (first, second), halves, [out] * 2, [whole(out)] * 2, 8)


def turn(table, shards):
    counts = [len(x) for x in shards]
    flat = [part for x in shards for part in x]
    tokens, width = sum(part.shape[0] for part in shards[0]), flat[0].shape[1]
    rows = 4 * width // 32

    def body(s, *refs):
        out, at = refs[-1], 0
        for k, count in enumerate(counts):
            mine, at = refs[at : at + count], at + count

            @pl.when((pl.program_id(0) ^ s[TEN]) == k)
            def _(mine=mine):
                out[...] = joined(mine).T.reshape(out.shape)

    out = shape((16, 2, rows, tokens))
    spec = pl.BlockSpec((8, 1, rows, tokens), lambda i, s: (i % 2, (i // 2) ^ s[Z], 0, 0))
    turned = call("turn", body, table, (4,), flat, [whole(x) for x in flat], out, spec, 12)
    return turned.reshape(4, 4, 2 * rows, tokens)


def weight_part(table, turned, lefts, rights, places, split):
    tokens, cols = lefts[0].shape
    rows = turned[0].shape[2]

    def body(s, own_x, own_y, pair_x, pair_y, left_a, left_b, right_a, right_b, *outs):
        r = pl.program_id(0)
        for side, (a, b, ga, gb) in enumerate(
            ((own_x, pair_x, left_a, left_b), (own_y, pair_y, right_a, right_b))
        ):
            acc = dot(a[...].reshape(4 * rows, tokens), ga[...])
            acc += dot(b[...].reshape(4 * rows, tokens), gb[...])
            acc = acc.astype(BF16)
            if split:
                outs[2 * side][...] = acc[: 2 * rows]
                outs[2 * side + 1][...] = acc[2 * rows :]
                continue
            for k in range(len(places)):

                @pl.when(r == k)
                def _(k=k, acc=acc, side=side):
                    outs[side * len(places) + k][...] = acc

    step = places[1] - places[0] if len(places) > 1 else 0
    by_x = pl.BlockSpec((1, 4, rows, tokens), lambda r, s: (s[X] ^ (places[0] + step * r), 0, 0, 0))
    by_y = pl.BlockSpec((4, 1, rows, tokens), lambda r, s: (0, s[Y] ^ (places[0] + step * r), 0, 0))
    outs = [shape((2 * rows if split else 4 * rows, cols))] * (4 if split else 2 * len(places))
    operands = (turned[0], turned[0], turned[1], turned[1], *lefts, *rights)
    return call(
        "weight_part",
        body,
        table,
        (len(places),),
        operands,
        [by_x, by_y, by_x, by_y, *[whole(x) for x in (*lefts, *rights)]],
        outs,
        [whole(o) for o in outs],
        30,
    )


def add_halves(table, third, first_place, halves):
    up, down = halves
    near_up, near_down = third, first_place
    n, cols = up.shape

    def body(s, a, b, u, d, out_a, out_b):
        out_a[...] = (a[...].astype(F32) + u[...].astype(F32)).astype(BF16)
        out_b[...] = (b[...].astype(F32) + d[...].astype(F32)).astype(BF16)

    steps = 4
    first = pl.BlockSpec((n // steps, cols), lambda i, s: (i, 0))
    second = pl.BlockSpec((n // steps, cols), lambda i, s: (i + steps, 0))
    return call(
        "add_halves",
        body,
        table,
        (steps,),
        (near_up, near_down, up, down),
        [first, second, first, first],
        [shape(near_up.shape), shape(near_down.shape)],
        [first, second],
        12,
        alias={1: 0, 2: 1},
    )


def cut_blocks(table, left, right):
    rows, cols = left[0].shape[0] // 4, left[0].shape[1]

    def body(s, *refs):
        for k, axis in enumerate((Y, X)):
            a, b, c = refs[3 * k : 3 * k + 3]
            for r, out in zip((1, 3, 2, 0), refs[6 + 4 * k : 10 + 4 * k]):
                at = pl.ds(pl.multiple_of((s[axis] ^ r) * rows, rows), rows)
                total = a[at, :].astype(F32) + b[at, :].astype(F32) + c[at, :].astype(F32)
                out[...] = total.astype(BF16)

    outs = [shape((rows, cols))] * 8
    operands = (*left, *right)
    cut = call(
        "cut_blocks",
        body,
        table,
        (1,),
        operands,
        [whole(x) for x in operands],
        outs,
        [whole(o) for o in outs],
        24,
    )
    return cut[:4], cut[4:]


def final_sums(table, parts):
    rows, cols = parts[0].shape

    def body(s, a, b, c, d, here, there):
        total = sum(ref[...].astype(F32) for ref in (a, b, c, d)).astype(BF16)
        here[...] = total[: rows // 2]
        there[...] = total[rows // 2 :]

    outs = [shape((rows // 2, cols))] * 2
    return call(
        "final_sums",
        body,
        table,
        (1,),
        parts,
        [whole(x) for x in parts],
        outs,
        [whole(o) for o in outs],
        8,
    )


def finish(table, here, there):
    rows, cols = here[0].shape
    side = cols // 3

    def body(s, *refs):
        out = refs[-1]
        for i, half in enumerate((s[Z], 1 - s[Z])):
            for k in range(2):
                for j in range(3):
                    at = pl.ds(pl.multiple_of(half * 2 * side + k * side, side), side)
                    out[j, :, at] = refs[2 * i + k][:, j * side : (j + 1) * side].astype(F32)

    out = shape((3, rows, 4 * side), F32)
    operands = (*here, *there)
    return call("finish", body, table, (1,), operands, [whole(x) for x in operands], out, whole(out), 8)


def swaps(pieces, left, right):
    a, c = send(pieces[0], left, 1), send(pieces[2], right, 1)
    b, d = send(pieces[1], left, 3), send(pieces[3], right, 3)
    return [a, b], [c, d]


def device_part(activations, qkv_weight, log_decay, lengths, out_grad):
    tied = lax.optimization_barrier
    tokens = activations.shape[0]
    heads = log_decay.shape[1]
    per = heads // 2
    index = [lax.axis_index(a) for a in ("c0", "c1", "c2", "zl", "co")]
    here_z = index[0]
    fixed = [*index, index[3] * 2 + index[4]]
    table = jnp.stack(fixed).astype(jnp.int32)
    weight = pltpu.with_memory_space_constraint(jnp.transpose(qkv_weight, (1, 0, 2)), pltpu.HBM)

    near = send(activations, "zl", 1)
    side = across(activations)
    core = send(activations, "co", 1)

    live = (jnp.arange(tokens, dtype=jnp.int32) < lengths[0]).astype(F32)
    cumul = jnp.cumsum(log_decay.T * live[None, :], axis=1)
    size = jnp.broadcast_to(lengths.astype(F32)[:, None], (per, tokens))
    info, note = (
        jnp.concatenate([lax.dynamic_slice_in_dim(cumul, z * per, per), size])
        for z in (here_z, 1 - here_z)
    )
    note = send(note, "c0", 1)
    width = per * HEAD
    og_own = lax.dynamic_slice_in_dim(out_grad, here_z * width, width, axis=1)
    og_other = lax.dynamic_slice_in_dim(out_grad, (1 - here_z) * width, width, axis=1)

    acc_own = project(table, [[activations], [core]], (0, 1), weight, None, None)
    near, side, acc_own, note, og_other, info = tied((near, side, acc_own, note, og_other, info))
    far = split(table, side, near)
    far = [send(far[0], "zl", 1), across(far[1])]
    near_core = send(near, "co", 1)
    side_core = send(side, "co", 1)
    qkv_own = project(table, [[near], [near_core]], (2, 3), weight, acc_own, info)
    turned = [turn(table, tied(([[activations], [core], [near], [near_core]], qkv_own))[0])]
    far, side_core, qkv_own, turned = tied((far, side_core, qkv_own, turned))
    far_core = [send(x, "co", 1) for x in far]
    og_pair = send(tied((og_other, far))[0], "c0", 1)
    to_y = shard_states(table, qkv_own, og_own, info, 0, None)
    far_core, to_y = tied((far_core, to_y))
    qkv_pair = project(
        table, [[side], [side_core], far, far_core], (2, 3, 0, 1), weight, None, note
    )
    og_pair, qkv_pair = tied((og_pair, qkv_pair))

    to_y = shard_states(table, qkv_pair, og_pair, note, 1, to_y)
    at_y = [send(to_y[r], "c2", r) for r in (2, 1, 3)]
    qkv_own, _ = tied((qkv_own, to_y[0]))
    local_own = local_grads(table, qkv_own, og_own, info, 0, per, None)
    at_y, local_own = tied((at_y, local_own))
    before, after, prior, later, ring = ring_y(table, [to_y[0], at_y[1], at_y[0], at_y[2]])
    at_x = [send(ring, "c1", r) for r in (1, 3, 2)]
    qkv_pair, _ = tied((qkv_pair, ring))
    local = local_grads(table, qkv_pair, og_pair, note, 0, per // 2, None)
    at_x, local = tied((at_x, local))
    back = arrivals(table, [ring, at_x[0], at_x[2], at_x[1]], before, after, prior, later)
    states = [send(back[r], "c2", r) for r in (2, 1, 3)]
    local, _ = tied((local, back[0]))
    local = local_grads(table, qkv_pair, og_pair, note, per // 2, per // 2, local)
    second, _ = tied(([far, far_core, [side], [side_core]], back[0]))
    turned.append(turn(table, second))
    states, turned, local = tied((states, turned, local))
    states = [back[0], states[1], states[0], states[2]]

    left_own, right_own, left_pair, right_pair = whole_grads(table, local_own, local, states)
    lefts, rights = (left_own, left_pair), (right_own, right_pair)
    far_piece = weight_part(table, turned, lefts, rights, (2,), True)
    l_half, r_half = swaps(far_piece, "c1", "c2")
    turned, _ = tied((turned, far_piece[0]))
    l_one, l_three, r_one, r_three = weight_part(table, turned, lefts, rights, (1, 3), False)
    l_half, l_one = tied((l_half, l_one))
    l_three, l_one = add_halves(table, l_three, l_one, l_half)
    l_got = [send(l_one, "c1", 1), send(l_three, "c1", 3)]
    r_half, _ = tied((r_half, l_one))
    r_three, r_one = add_halves(table, r_three, r_one, r_half)
    r_got = [send(r_one, "c2", 1), send(r_three, "c2", 3)]
    turned, _ = tied((turned, r_one))
    own = weight_part(table, turned, lefts, rights, (0,), False)
    l_got, own = tied((l_got, own))
    l_cut, r_cut = cut_blocks(table, (own[0], *l_got), (own[1], *r_got))
    l_got = [send(x, "c2", by) for x, by in zip(l_cut, (1, 3, 2))]
    r_got = [send(x, "c1", by) for x, by in zip(r_cut, (1, 3, 2))]
    l_here, l_there = final_sums(table, (l_cut[3], *l_got))
    r_got, _ = tied((r_got, l_here))
    r_here, r_there = final_sums(table, (r_cut[3], *r_got))
    there = [send(x, "c0", 1) for x in (l_there, r_there)]
    return jnp.transpose(finish(table, (l_here, r_here), there), (1, 0, 2))


def solution(mesh):
    finer = Mesh(mesh.devices.reshape(2, 4, 4, 2, 2), ("c0", "c1", "c2", "zl", "co"))
    context, tensor = ("c0", "c1", "c2"), ("zl", "co")
    placed = (
        P(context, tensor),
        P(None, None, tensor),
        P(context, tensor),
        P(context),
        P(context, tensor),
    )
    return jax.shard_map(
        device_part,
        mesh=finer,
        in_specs=placed,
        out_specs=P(context, None, tensor),
        check_vma=False,
    )
```
